32 devices in a mesh: seq: 2 (over x), tp: 4 (over z), dp: 4 (over y, core).
Axes of the slice: x: 2, y: 2, z: 4, core: 2. Of those that a mesh axis runs over, the one named last changes fastest.
Arguments:
- clip_tokens: bfloat16 [2048, 8192], P('tp', ('dp', 'seq')), parts along dimension 1, may hold values from -40 to 40, as said below
- conv_taps: float32 [27, 2048], P(None, 'tp'), may hold values from -3 to 3
- norm_gain: float32 [2048], replicated, may hold values from 0.25 to 1.75
- qkv_weight: bfloat16 [3, 2048, 2048], P(None, 'tp'), may hold values from -1 to 1
- out_weight: bfloat16 [2048, 2048], P('tp'), may hold values from -2 to 2
- tile_mask: int32 [16, 16], replicated, may hold values from 0 to 1, as said below
- stripe_order: int32 [16], replicated, may hold values from 0 to 15, as said below
Outputs:
- attended: bfloat16 [2048, 8192], P('tp', ('dp', 'seq')), parts along dimension 1
The draws below stay inside these ranges and needn't reach their ends.
There are 4 independent parts, one for each index of `dp`. The reference program is written for one: setup_inputs(seed, part) draws one part's arguments, and reference() takes and returns one part's arrays. A program takes and returns all parts, laid end to end along the dimension named above; an argument that names none is the same for every part. Nothing has to cross between parts.
Inputs may be any that keep to these rules, and one draw needn't show every extreme that they name: `clip_tokens`: the clip's values. tile_mask[i, j] is 1 where tiles i and j lie in the same frame, 0 where tile j lies in a later frame than tile i, and 0 or 1 where tile j lies in an earlier frame; a frame is 4 consecutive tiles. `stripe_order`: A permutation of the 16 tiles. Each aligned block of 8 banded positions holds exactly 4 tiles of each aligned block of 8 tile numbers.
All inputs are finite; a program needn't handle non-finite values.
Results may differ from the reference program's by a relative error of at most 0.024.
Values may be sent and summed in bfloat16 or wider, within the bound.
No kernel may reach another device: no remote copies, remote signals or barrier semaphores. Data moves between devices by JAX's collectives and lax.ppermute only.
A program may use at most 64 MiB of HBM per device.

```python
import math
import jax
import jax.numpy as jnp
from jax import lax

D = 2048
HEADS = 16
HEAD = 128
TILE = 128
FH = 16
FW = 32
TOKENS = 2048
TILES_DEV = 8
NT = 16
N_TP = 4


def draw_clip_tokens(key, part):
    key_base, key_token = jax.random.split(jax.random.fold_in(key, 1), 2)
    channel_scale = 10.0 ** (jnp.arange(D, dtype=jnp.float32)[:, None] / D - 0.5)
    token_scale = 10.0 ** (jax.random.uniform(key_token, (1, TOKENS), dtype=jnp.float32) - 0.5)
    base = jnp.clip(jax.random.normal(key_base, (D, TOKENS), dtype=jnp.float32), -4.0, 4.0)
    return (base * channel_scale * token_scale).astype(jnp.bfloat16)


def draw_qkv_weight(key, part):
    key_base = jax.random.fold_in(jax.random.fold_in(key, 3), 0)
    base = jnp.clip(jax.random.normal(key_base, (3, D, D), dtype=jnp.float32), -4.0, 4.0) * D ** (-0.5)
    drawn = base * jnp.array([1.4, 1.4, 1.0], jnp.float32)[:, None, None]
    return jnp.clip(drawn, -1.0, 1.0).astype(jnp.bfloat16)


def draw_tile_mask(key, part):
    tiles_frame = FH * FW // TILE
    frame_of = jnp.arange(NT, dtype=jnp.int32) // tiles_frame
    coins = jax.random.randint(jax.random.fold_in(key, 5), (NT, NT), 0, 2, dtype=jnp.int32)
    same_frame = frame_of[:, None] == frame_of[None, :]
    earlier = frame_of[None, :] < frame_of[:, None]
    return jnp.where(same_frame, 1, jnp.where(earlier, coins, 0)).astype(jnp.int32)


def draw_stripe_order(key, part):
    tiles_dev = TILES_DEV
    seq_count = NT // tiles_dev
    per_source = tiles_dev // seq_count
    keys_first = jax.random.split(jax.random.fold_in(key, 11), seq_count)
    orders = jax.vmap(lambda sub_key: jax.random.permutation(sub_key, tiles_dev))(keys_first).astype(jnp.int32)
    tiles = orders + (jnp.arange(seq_count, dtype=jnp.int32) * tiles_dev)[:, None]
    dealt = tiles.reshape(seq_count, per_source, seq_count)
    blocks = jnp.transpose(dealt, (2, 0, 1)).reshape(seq_count, tiles_dev)
    keys_second = jax.random.split(jax.random.fold_in(key, 12), seq_count)
    shuffles = jax.vmap(lambda sub_key: jax.random.permutation(sub_key, tiles_dev))(keys_second).astype(jnp.int32)
    placed = jnp.take_along_axis(blocks, shuffles, axis=1)
    return placed.reshape(seq_count * tiles_dev).astype(jnp.int32)


def spiked(entries, own_key, source, target, shards_of, factor):
    owner, partner = [(jnp.arange(entries.shape[dim]) // (entries.shape[dim] // shards_of)).reshape([-1 if axis == dim else 1 for axis in range(entries.ndim)]) for dim in (source, target)]
    chosen = jax.random.permutation(own_key, shards_of)[partner]
    strong = (owner == chosen) | (owner == (partner + shards_of // 2) % shards_of)
    return jnp.where(strong, factor * entries, entries)


def steps_of(own_key, shape, pieces, least, largest):
    loudness = 1.0
    for position, blocks in pieces:
        heights = jax.random.uniform(jax.random.fold_in(jax.random.fold_in(own_key, 6), position), (blocks,), jnp.float32, least / len(pieces), largest / len(pieces))
        loudness = loudness * jnp.repeat(jnp.exp(heights), shape[position] // blocks).reshape((-1,) + (1,) * (len(shape) - 1 - position))
    return loudness


def noise(key, shape, deviation, bound, pieces=(), kind=jnp.bfloat16):
    values = deviation * jax.random.normal(key, shape, jnp.float32)
    if pieces:
        values = values * steps_of(key, shape, pieces, -0.22, 0.18)
    return jnp.clip(values, -bound, bound).astype(kind)


def heavy_noise(own_key, shape, scale, reach, cuts, heavy, kind=jnp.bfloat16):
    values = scale * jax.random.normal(own_key, shape, jnp.float32)
    if cuts:
        values = values * steps_of(own_key, shape, cuts, -0.22, 0.18)
    return jnp.clip(spiked(values, jax.random.fold_in(own_key, 3), *heavy), -reach, reach).astype(kind)


def setup_inputs(seed: int = 0, part: int = 0) -> dict:
    key_of = jax.random.split(jax.random.key(seed), 8)
    part_splits = jax.random.split(jax.random.fold_in(key_of[7], part), 8)
    return {
        "clip_tokens": draw_clip_tokens(jax.random.fold_in(jax.random.fold_in(key_of[7], part), 71), part),
        "conv_taps": noise(key_of[1], (27, D), 0.2, 3.0, ((1, 4),), jnp.float32),
        "norm_gain": jnp.clip(1.0 + 0.15 * jax.random.normal(key_of[2], (D,), jnp.float32), 0.25, 1.75),
        "qkv_weight": draw_qkv_weight(jax.random.fold_in(key_of[7], 71), part),
        "out_weight": heavy_noise(key_of[4], (D, D), 0.1, 2.0, ((0, 4),), (0, 1, 4, 2.0)),
        "tile_mask": draw_tile_mask(jax.random.fold_in(key_of[7], 71), part),
        "stripe_order": draw_stripe_order(jax.random.fold_in(key_of[7], 71), part),
    }


EPSILON = 1e-06
MASKED_SCORE = -1e+30

def convolve(clip_tokens, conv_taps):
    frames = TOKENS // (FH * FW)
    volume = clip_tokens.astype(jnp.float32).reshape(D, frames, FH, FW)
    padded = jnp.pad(volume, ((0, 0), (2, 0), (1, 1), (1, 1)))
    summed = jnp.zeros((D, frames, FH, FW), jnp.float32)
    for time_off in range(3):
        for row_off in range(3):
            for col_off in range(3):
                tap_vec = conv_taps[time_off * 9 + row_off * 3 + col_off].astype(jnp.float32)
                summed = summed + tap_vec[:, None, None, None] * padded[:, time_off:time_off + frames, row_off:row_off + FH, col_off:col_off + FW]
    return (clip_tokens.astype(jnp.float32) + summed.reshape(D, TOKENS)).astype(jnp.bfloat16)

def reference(clip_tokens, conv_taps, norm_gain, qkv_weight, out_weight, tile_mask, stripe_order):
    mixed = convolve(clip_tokens, conv_taps)
    widened = mixed.astype(jnp.float32)
    scaled = (widened * norm_gain.astype(jnp.float32)[:, None]).astype(jnp.bfloat16)
    inverse = lax.rsqrt(lax.optimization_barrier(jnp.sum(widened * widened, axis=0)) / D + EPSILON)
    projected = []
    for kind_index in range(3):
        product = jnp.dot(scaled.T, qkv_weight[kind_index].T, preferred_element_type=jnp.float32)
        projected.append((product * inverse[:, None]).astype(jnp.bfloat16))
    tile_of = (jnp.arange(TOKENS) // TILE).astype(jnp.int32)
    allowed = jnp.take(jnp.take(tile_mask, tile_of, axis=0), tile_of, axis=1) > 0
    score_scale = 1.0 / math.sqrt(HEAD)

    def one_head(head_index):
        offset = (head_index * HEAD).astype(jnp.int32)
        queries = lax.dynamic_slice_in_dim(projected[0], offset, HEAD, axis=1)
        key_rows = lax.dynamic_slice_in_dim(projected[1], offset, HEAD, axis=1)
        values = lax.dynamic_slice_in_dim(projected[2], offset, HEAD, axis=1)
        scores = jnp.dot(queries, key_rows.T, preferred_element_type=jnp.float32) * score_scale
        masked = jnp.where(allowed, scores, MASKED_SCORE)
        rowmax = lax.optimization_barrier(jnp.max(masked, axis=1, keepdims=True))
        powers = jnp.where(allowed, jnp.exp(masked - rowmax), 0.0)
        weights = powers.astype(jnp.bfloat16)
        numer = jnp.dot(weights, values, preferred_element_type=jnp.float32)
        return (numer / lax.optimization_barrier(jnp.sum(powers, axis=1, keepdims=True))).astype(jnp.bfloat16)
    heads_out = lax.map(one_head, jnp.arange(HEADS, dtype=jnp.int32))
    joined = jnp.transpose(heads_out, (1, 0, 2)).reshape(TOKENS, D)
    group_cols = D // N_TP

    def add_group(group_index, running):
        offset = (group_index * group_cols).astype(jnp.int32)
        col_block = lax.dynamic_slice_in_dim(joined, offset, group_cols, axis=1)
        row_block = lax.dynamic_slice_in_dim(out_weight, offset, group_cols, axis=0)
        partial_value = jnp.dot(col_block, row_block, preferred_element_type=jnp.float32).astype(jnp.bfloat16)
        return running + partial_value.astype(jnp.float32)
    summed = lax.fori_loop(0, N_TP, add_group, jnp.zeros((TOKENS, D), jnp.float32))
    source = (stripe_order[:, None].astype(jnp.int32) * TILE + jnp.arange(TILE, dtype=jnp.int32)[None, :]).reshape(TOKENS).astype(jnp.int32)
    return jnp.take(summed, source, axis=0).T.astype(jnp.bfloat16)
```

```python
import functools
import math

import jax
import jax.numpy as jnp
from jax import lax
from jax.experimental import pallas as pl
from jax.experimental.pallas import tpu as pltpu
from jax.sharding import PartitionSpec as P

HEAD = 128
TILE = 128
FH = 16
FW = 32
FRAME = FH * FW
TAPS = 27


EPSILON = 1e-06
MASKED_SCORE = -1e30
LOG2E = math.log2(math.e)

VMEM_LIMIT = 48 * 1024 * 1024


def vmem_spec():
    return pl.BlockSpec(memory_space=pltpu.VMEM)


def smem_spec():
    return pl.BlockSpec(memory_space=pltpu.SMEM)


def params(**more):
    return pltpu.CompilerParams(vmem_limit_bytes=VMEM_LIMIT, **more)


def column_shifts(frame, lane):
    column = lane % FW
    left = jnp.where(column > 0, pltpu.roll(frame, 1, 1), 0.0)
    right = jnp.where(column < FW - 1, pltpu.roll(frame, FRAME - 1, 1), 0.0)
    return (left, frame, right)


def row_sum(rows, lane):
    above = jnp.where(lane >= FW, pltpu.roll(rows[0], FW, 1), 0.0)
    below = jnp.where(lane < FRAME - FW, pltpu.roll(rows[2], FRAME - FW, 1), 0.0)
    return rows[1] + above + below


def taps_applied(pairs, taps, lane):
    rows = []
    for row_off in range(3):
        total = None
        for time_off, shifts in pairs:
            for col_off in range(3):
                tap = time_off * 9 + row_off * 3 + col_off
                term = taps[:, tap : tap + 1] * shifts[col_off]
                total = term if total is None else total + term
        rows.append(total)
    return row_sum(rows, lane)


def pack_slots(order_ref, slots_ref, seq_here, tiles_dev, positions):
    half = tiles_dev // 2
    kept = jnp.int32(0)
    sent = jnp.int32(half)
    for position in range(positions):
        tile = order_ref[position]
        mine = tile // tiles_dev == seq_here
        stays = jnp.int32(position // tiles_dev) == seq_here
        slot = jnp.where(stays, kept, sent)

        @pl.when(mine)
        def _(tile=tile, slot=slot):
            slots_ref[tile - seq_here * tiles_dev] = slot

        step = mine.astype(jnp.int32)
        kept = kept + jnp.where(stays, step, 0)
        sent = sent + jnp.where(stays, 0, step)


def conv_body(with_before, seq_ref, order_ref, *refs):
    if with_before:
        tokens_ref, taps_ref, before_ref, part_ref, keep_ref, send_ref, slots_ref, taps_scr, packed = refs
    else:
        tokens_ref, taps_ref, part_ref, keep_ref, send_ref, slots_ref, taps_scr, packed = refs
    channels, tokens = tokens_ref.shape
    tiles_dev = tokens // TILE
    seq_here = seq_ref[0]

    @pl.when(pl.program_id(0) == 0)
    def _():
        pack_slots(order_ref, slots_ref, seq_here, tiles_dev, order_ref.shape[0])

    taps_scr[:, :TAPS] = taps_ref[...].T
    group = 16
    lane = lax.broadcasted_iota(jnp.int32, (group, FRAME), 1)

    def advance(step, carry):
        rows = pl.ds(pl.multiple_of(step * group, group), group)
        taps = taps_scr[rows, :]
        if with_before:
            old = [
                column_shifts(before_ref[rows, f * FRAME : (f + 1) * FRAME].astype(jnp.float32), lane)
                for f in range(2)
            ]
            sums = [
                part_ref[rows, :FRAME] + taps_applied([(0, old[0]), (1, old[1])], taps, lane),
                part_ref[rows, FRAME:] + taps_applied([(0, old[1])], taps, lane),
            ]
        else:
            now = [
                column_shifts(tokens_ref[rows, f * FRAME : (f + 1) * FRAME].astype(jnp.float32), lane)
                for f in range(2)
            ]
            sums = [
                now[0][1] + taps_applied([(2, now[0])], taps, lane),
                now[1][1] + taps_applied([(1, now[0]), (2, now[1])], taps, lane),
            ]
            part_ref[rows, :FRAME] = sums[0]
            part_ref[rows, FRAME:] = sums[1]
        for tile in range(tiles_dev):
            frame, spot = divmod(tile * TILE, FRAME)
            place = pl.ds(pl.multiple_of(slots_ref[tile] * TILE, TILE), TILE)
            packed[rows, place] = sums[frame][:, spot : spot + TILE].astype(jnp.bfloat16)
        return carry

    lax.fori_loop(0, channels // group, advance, 0)
    keep_ref[...] = packed[:, : tokens // 2]
    send_ref[...] = packed[:, tokens // 2 :]


def conv_call(seq_here, stripe_order, tokens, conv_taps, before=None, part=None):
    channels, count = tokens.shape
    block = 128
    wide = pl.BlockSpec((block, count), lambda i, *_: (i, 0))
    slim = pl.BlockSpec((block, count // 2), lambda i, *_: (i, 0))
    taps_spec = pl.BlockSpec((TAPS, block), lambda i, *_: (0, i))
    packed_shape = jax.ShapeDtypeStruct((channels, count // 2), jnp.bfloat16)
    with_before = before is not None
    extra_in, extra_args, out_specs, out_shape = [], [], [slim, slim], [packed_shape, packed_shape]
    if with_before:
        extra_in, extra_args = [wide, wide], [before, part]
    else:
        out_specs = [wide] + out_specs
        out_shape = [jax.ShapeDtypeStruct((channels, count), jnp.float32)] + out_shape
    return pl.pallas_call(
        functools.partial(conv_body, with_before),
        grid_spec=pltpu.PrefetchScalarGridSpec(
            num_scalar_prefetch=2,
            grid=(channels // block,),
            in_specs=[wide, taps_spec] + extra_in,
            out_specs=out_specs,
            scratch_shapes=[
                pltpu.SMEM((count // TILE,), jnp.int32),
                pltpu.VMEM((block, 128), jnp.float32),
                pltpu.VMEM((block, count), jnp.bfloat16),
            ],
        ),
        out_shape=out_shape,
        compiler_params=params(),
        cost_estimate=pl.CostEstimate(
            flops=channels * count * TAPS, bytes_accessed=channels * count * 8, transcendentals=0
        ),
        name="conv_before" if with_before else "conv_here",
    )(seq_here, stripe_order, tokens, conv_taps, *extra_args)


def prepare_body(blocks_ref, gain_ref, qkv_ref, out_ref, qkv_out, out_out):
    qkv_out[...] = (qkv_ref[...].astype(jnp.float32) * gain_ref[...]).astype(jnp.bfloat16)
    out_out[...] = out_ref[...].T


def prepare_weights(blocks, norm_gain, qkv_weight, out_weight):
    kinds, cols, channels = qkv_weight.shape
    count = blocks.shape[0]
    width = channels // count
    return pl.pallas_call(
        prepare_body,
        grid_spec=pltpu.PrefetchScalarGridSpec(
            num_scalar_prefetch=1,
            grid=(count,),
            in_specs=[
                pl.BlockSpec((1, width), lambda j, b: (0, b[j])),
                pl.BlockSpec((kinds * cols, width), lambda j, b: (0, b[j])),
                pl.BlockSpec((cols, width), lambda j, b: (0, b[j])),
            ],
            out_specs=[
                pl.BlockSpec((kinds * cols, width), lambda j, b: (0, j)),
                pl.BlockSpec((width, cols), lambda j, b: (j, 0)),
            ],
        ),
        out_shape=[
            jax.ShapeDtypeStruct((kinds * cols, channels), jnp.bfloat16),
            jax.ShapeDtypeStruct((channels, cols), jnp.bfloat16),
        ],
        compiler_params=params(),
        cost_estimate=pl.CostEstimate(
            flops=kinds * cols * channels, bytes_accessed=16 * cols * channels, transcendentals=0
        ),
        name="prepare_weights",
    )(blocks, norm_gain[None, :], qkv_weight.reshape(kinds * cols, channels), out_weight)


def project_body(query_steps, weight_ref, *refs):
    shards, out_ref, inverse_ref = refs[:-2], refs[-2], refs[-1]
    width = shards[0].shape[0]
    step = pl.program_id(0)

    @pl.when(step == 0)
    def _():
        squares = None
        for shard in shards:
            wide = shard[...].astype(jnp.float32)
            term = jnp.sum(wide * wide, axis=0, keepdims=True)
            squares = term if squares is None else squares + term
        inverse_ref[...] = lax.rsqrt(squares / (width * len(shards)) + EPSILON)

    total = None
    for index, shard in enumerate(shards):
        term = jnp.dot(
            weight_ref[:, index * width : (index + 1) * width],
            shard[...],
            preferred_element_type=jnp.float32,
        )
        total = term if total is None else total + term
    scale = jnp.where(step < query_steps, LOG2E / math.sqrt(HEAD), 1.0)
    out_ref[...] = (total * (inverse_ref[...] * scale)).astype(jnp.bfloat16)


def project_call(weights, shards):
    rows, channels = weights.shape
    width, tokens = shards[0].shape
    block = 256
    whole = pl.BlockSpec((width, tokens), lambda i: (0, 0))
    return pl.pallas_call(
        functools.partial(project_body, rows // 3 // block),
        grid=(rows // block,),
        in_specs=[pl.BlockSpec((block, channels), lambda i: (i, 0))] + [whole] * len(shards),
        out_specs=pl.BlockSpec((block, tokens), lambda i: (i, 0)),
        out_shape=jax.ShapeDtypeStruct((rows, tokens), jnp.bfloat16),
        scratch_shapes=[pltpu.VMEM((1, tokens), jnp.float32)],
        compiler_params=params(),
        cost_estimate=pl.CostEstimate(
            flops=2 * rows * channels * tokens,
            bytes_accessed=2 * (rows * channels + channels * tokens + rows * tokens),
            transcendentals=0,
        ),
        name="project",
    )(weights, *shards)


def tile_lists(order_ref, ids_ref, seq_here, tiles_dev):
    half = tiles_dev // 2
    for block in range(2):
        first = jnp.int32(0)
        second = jnp.int32(0)
        away = (jnp.int32(block) != seq_here).astype(jnp.int32)
        for spot in range(tiles_dev):
            tile = order_ref[block * tiles_dev + spot]
            late = tile // tiles_dev
            rank = jnp.where(late == 0, first, second)
            ids_ref[(2 * late + away) * half + rank] = tile
            first = first + (1 - late)
            second = second + late


def attend_body(chunk, seq_ref, order_ref, mask_ref, query_ref, *refs):
    count = 2 * (chunk + 1)
    keys, values = refs[:count], refs[count : 2 * count]
    out_ref, ids_ref, scores_ref = refs[2 * count], refs[2 * count + 1], refs[2 * count + 2]
    tokens = query_ref.shape[1]
    half = tokens // TILE

    @pl.when(pl.program_id(0) == 0)
    def _():
        tile_lists(order_ref, ids_ref, seq_ref[0], 2 * half)

    query = query_ref[...]
    lane_tile = lax.broadcasted_iota(jnp.int32, (1, tokens), 1) // TILE
    top = None
    for source in range(count):
        block = jnp.dot(keys[source][...].T, query, preferred_element_type=jnp.float32)
        for spot in range(half):
            key_tile = ids_ref[source * half + spot]
            bias = jnp.zeros((1, tokens), jnp.float32)
            for query_spot in range(half):
                query_tile = ids_ref[2 * chunk * half + query_spot]
                blocked = jnp.where(mask_ref[query_tile, key_tile] == 1, 0.0, MASKED_SCORE)
                bias = jnp.where(lane_tile == query_spot, blocked, bias)
            piece = block[spot * TILE : (spot + 1) * TILE, :] + bias
            scores_ref[source * tokens + spot * TILE : source * tokens + (spot + 1) * TILE, :] = piece
            best = jnp.max(piece, axis=0, keepdims=True)
            top = best if top is None else jnp.maximum(top, best)
    denom = None
    weighted = None
    for source in range(count):
        powers = jnp.exp2(scores_ref[source * tokens : (source + 1) * tokens, :] - top)
        summed = jnp.sum(powers, axis=0, keepdims=True)
        term = jnp.dot(
            values[source][...], powers.astype(jnp.bfloat16), preferred_element_type=jnp.float32
        )
        denom = summed if denom is None else denom + summed
        weighted = term if weighted is None else weighted + term
    out_ref[...] = (weighted / denom).astype(jnp.bfloat16)


def attend_call(chunk, seq_here, stripe_order, tile_mask, own, peers):
    rows, tokens = own[0].shape
    heads = rows // 3 // HEAD
    sources = []
    for mine, other in zip(own, peers):
        sources += [(mine, heads, 2 * heads), (other, 0, heads)]

    def spec(start):
        return pl.BlockSpec((HEAD, tokens), lambda h, *_, start=start: (start + h, 0))

    count = len(sources)
    return pl.pallas_call(
        functools.partial(attend_body, chunk),
        grid_spec=pltpu.PrefetchScalarGridSpec(
            num_scalar_prefetch=3,
            grid=(heads,),
            in_specs=[spec(0)] + [spec(k) for _, k, _ in sources] + [spec(v) for _, _, v in sources],
            out_specs=spec(0),
            scratch_shapes=[
                pltpu.SMEM((4 * tokens // TILE,), jnp.int32),
                pltpu.VMEM((count * tokens, tokens), jnp.float32),
            ],
        ),
        out_shape=jax.ShapeDtypeStruct((heads * HEAD, tokens), jnp.bfloat16),
        compiler_params=params(),
        cost_estimate=pl.CostEstimate(
            flops=4 * heads * HEAD * tokens * tokens * count,
            bytes_accessed=2 * heads * HEAD * tokens * (2 + 2 * count),
            transcendentals=heads * tokens * tokens * count,
        ),
        name=f"attend_{chunk}",
    )(
        seq_here,
        stripe_order,
        tile_mask,
        own[chunk],
        *[array for array, _, _ in sources],
        *[array for array, _, _ in sources],
    )


def place_body(seq_ref, order_ref, ends_ref, first_ref, *refs):
    parts, out_ref, second_ref = refs[:4], refs[4], refs[5]
    channels, tokens = first_ref.shape
    tiles_dev = 2 * tokens // TILE
    seq_here = seq_ref[0]
    at_end = ends_ref[0] == 1
    total = (
        parts[0][...].astype(jnp.float32)
        + parts[1][...].astype(jnp.float32)
        + parts[2][...].astype(jnp.float32)
        + jnp.where(at_end, parts[3][...].astype(jnp.float32), 0.0)
    )
    second_ref[...] = total.astype(jnp.bfloat16)
    ranks = [jnp.int32(0), jnp.int32(0)]
    for position in range(tiles_dev):
        late = order_ref[seq_here * tiles_dev + position] // tiles_dev
        spot = pl.ds(pl.multiple_of(jnp.where(late == 0, ranks[0], ranks[1]) * TILE, TILE), TILE)
        here = slice(position * TILE, (position + 1) * TILE)

        @pl.when(late == 0)
        def _(spot=spot, here=here):
            out_ref[:, here] = first_ref[:, spot]

        @pl.when(late == 1)
        def _(spot=spot, here=here):
            out_ref[:, here] = second_ref[:, spot]

        ranks[0] = ranks[0] + (1 - late)
        ranks[1] = ranks[1] + late


def place_call(seq_here, stripe_order, at_end, first, parts):
    channels, tokens = first.shape
    block = 128
    slim = pl.BlockSpec((block, tokens), lambda i, *_: (i, 0))
    return pl.pallas_call(
        place_body,
        grid_spec=pltpu.PrefetchScalarGridSpec(
            num_scalar_prefetch=3,
            grid=(channels // block,),
            in_specs=[slim] * 5,
            out_specs=pl.BlockSpec((block, 2 * tokens), lambda i, *_: (i, 0)),
            scratch_shapes=[pltpu.VMEM((block, tokens), jnp.bfloat16)],
        ),
        out_shape=jax.ShapeDtypeStruct((channels, 2 * tokens), jnp.bfloat16),
        compiler_params=params(),
        cost_estimate=pl.CostEstimate(
            flops=4 * channels * tokens, bytes_accessed=14 * channels * tokens, transcendentals=0
        ),
        name="place",
    )(seq_here, stripe_order, at_end, first, *parts)


FORWARD = [(0, 1), (1, 2), (2, 3), (3, 0)]
BACKWARD = [(1, 0), (2, 1), (3, 2), (0, 3)]
FOLDED = [(0, 1), (1, 3), (3, 2), (2, 0)]
UNFOLDED = [(1, 0), (3, 1), (2, 3), (0, 2)]


def gather_blocks(block, here):
    before = lax.ppermute(block, "tp", FORWARD)
    after = lax.ppermute(block, "tp", BACKWARD)
    relay = jnp.where(here == 2, before, jnp.where(here == 1, after, block))
    across = lax.ppermute(relay, "tp", UNFOLDED)
    return (block, before, after, across)


def plus(a, b, chosen):
    summed = a.astype(jnp.float32) + jnp.where(chosen, b.astype(jnp.float32), 0.0)
    return summed.astype(jnp.bfloat16)


def reduce_blocks(weights, heads_out, here):
    width = weights.shape[0] // 4

    def partial(index):
        block = weights[index * width : (index + 1) * width]
        return jnp.dot(block, heads_out, preferred_element_type=jnp.float32).astype(jnp.bfloat16)

    across = lax.ppermute(partial(3), "tp", FOLDED)
    back = lax.ppermute(plus(partial(1), across, here == 2), "tp", BACKWARD)
    onward = lax.ppermute(plus(partial(2), across, here == 1), "tp", FORWARD)
    return (partial(0), back, onward, across)


def per_device_fast(
    clip_tokens, conv_taps, norm_gain, qkv_weight, out_weight, tile_mask, stripe_order
):
    seq = lax.axis_index("seq")
    here = lax.axis_index("tp")
    seq_here = seq.astype(jnp.int32)[None]
    at_end = ((here == 0) | (here == 3)).astype(jnp.int32)[None]
    blocks = jnp.stack([here, (here + 3) % 4, (here + 1) % 4, (here + 2) % 4]).astype(jnp.int32)

    part, keep_a, send_a = conv_call(seq_here, stripe_order, clip_tokens, conv_taps)
    got_a = lax.ppermute(send_a, "seq", [(0, 1)])
    halo_tokens, _ = lax.optimization_barrier((clip_tokens, send_a))
    before = lax.ppermute(halo_tokens, "seq", [(0, 1)])
    weights, out_t = prepare_weights(blocks, norm_gain, qkv_weight, out_weight)

    tokens_a = jnp.where(seq == 0, keep_a, got_a)
    shards_a = gather_blocks(tokens_a, here)

    keep_b, send_b = conv_call(seq_here, stripe_order, clip_tokens, conv_taps, before, part)
    got_b = lax.ppermute(send_b, "seq", [(1, 0)])
    tokens_b = jnp.where(seq == 1, keep_b, got_b)

    rows = weights.shape[0]
    cols = rows // 3
    swap = [(0, 1), (1, 0)]
    own_a = project_call(weights, shards_a)
    peer_a = lax.ppermute(own_a[cols:], "seq", swap)
    shards_b = gather_blocks(tokens_b, here)
    out_a = attend_call(0, seq_here, stripe_order, tile_mask, [own_a], [peer_a])
    parts_a = reduce_blocks(out_t, out_a, here)
    own_b = project_call(weights, shards_b)
    peer_b = lax.ppermute(own_b[cols:], "seq", swap)
    out_b = attend_call(1, seq_here, stripe_order, tile_mask, [own_a, own_b], [peer_a, peer_b])
    parts_b = reduce_blocks(out_t, out_b, here)
    first = (
        parts_a[0].astype(jnp.float32)
        + parts_a[1].astype(jnp.float32)
        + parts_a[2].astype(jnp.float32)
        + jnp.where(at_end == 1, parts_a[3].astype(jnp.float32), 0.0)
    ).astype(jnp.bfloat16)
    return place_call(seq_here, stripe_order, at_end, first, parts_b)


def passed_along(block, axis, distance):
    devices = range(lax.axis_size(axis))
    route = [(i - distance, i) for i in devices if i - distance in devices]
    return lax.ppermute(block, axis, route)


def from_partner(block, axis, apart):
    count = lax.axis_size(axis)
    route = []
    for low in range(count):
        high = low | 1 << apart
        if high != low and high < count:
            route += [(low, high), (high, low)]
    return lax.ppermute(block, axis, route)


def causal_conv(local_tokens, before, conv_taps):
    channels = local_tokens.shape[0]
    frames = local_tokens.shape[1] // (FH * FW)
    stacked = (
        jnp.concatenate([before, local_tokens], axis=1)
        .astype(jnp.float32)
        .reshape(channels, frames + 2, FH, FW)
    )
    padded = jnp.pad(stacked, ((0, 0), (0, 0), (1, 1), (1, 1)))
    summed = jnp.zeros((channels, frames, FH, FW), jnp.float32)
    for time_off in range(3):
        for row_off in range(3):
            for col_off in range(3):
                tap_vec = conv_taps[time_off * 9 + row_off * 3 + col_off]
                summed = (
                    summed
                    + tap_vec[:, None, None, None]
                    * padded[
                        :,
                        time_off : time_off + frames,
                        row_off : row_off + FH,
                        col_off : col_off + FW,
                    ]
                )
    return (local_tokens.astype(jnp.float32) + summed.reshape(channels, -1)).astype(jnp.bfloat16)


def stripe_tables(stripe_order, tiles_dev):
    seq_count = lax.axis_size("seq")
    seq_here = lax.axis_index("seq")
    per_source = tiles_dev // seq_count
    blocks = stripe_order.reshape(seq_count, tiles_dev)
    owners = blocks // tiles_dev
    is_mine = (owners == seq_here).astype(jnp.int32)
    rank_of = jnp.cumsum(is_mine, axis=1) - 1
    slot_ids = jnp.arange(per_source, dtype=jnp.int32)
    picked = is_mine[:, None, :] * (rank_of[:, None, :] == slot_ids[None, :, None]).astype(
        jnp.int32
    )
    local_tiles = (blocks - seq_here * tiles_dev)[:, None, :]
    send_order = jnp.sum(picked * local_tiles, axis=2).reshape(-1)
    own_row = lax.dynamic_slice_in_dim(stripe_order, seq_here * tiles_dev, tiles_dev)
    sources = own_row // tiles_dev
    position = jnp.arange(tiles_dev, dtype=jnp.int32)
    earlier = (sources[:, None] == sources[None, :]) & (position[None, :] < position[:, None])
    place_order = sources * per_source + jnp.sum(earlier.astype(jnp.int32), axis=1)
    return (send_order, place_order, own_row)


def regroup(values, send_order, place_order):
    leading = values.shape[0]
    trailing = values.shape[2:]
    in_tiles = values.reshape((leading, values.shape[1] // TILE, TILE) + trailing)
    outgoing = jnp.take(in_tiles, send_order, axis=1)
    arrived = lax.all_to_all(outgoing, "seq", split_axis=1, concat_axis=1, tiled=True)
    placed = jnp.take(arrived, place_order, axis=1)
    return placed.reshape(values.shape)


def project(mixed, norm_gain, qkv_weight):
    channels = norm_gain.shape[0]
    widened = lax.all_gather(mixed, "tp", axis=0, tiled=True).astype(jnp.float32)
    scaled = (widened * norm_gain[:, None]).astype(jnp.bfloat16)
    projected = jnp.einsum("ct,khc->kth", scaled, qkv_weight, preferred_element_type=jnp.float32)
    squares = jnp.sum(widened * widened, axis=0)
    projected, squares = (projected, squares)
    inverse = lax.rsqrt(squares / channels + EPSILON)
    return (projected * inverse[None, :, None]).astype(jnp.bfloat16)


def position_mask(tile_mask, stripe_order, own_half):
    tiles_all = tile_mask.shape[0]
    tile_ids = jnp.arange(tiles_all, dtype=jnp.int32)
    own_onehot = (own_half[:, None] == tile_ids[None, :]).astype(jnp.float32)
    order_onehot = (stripe_order[:, None] == tile_ids[None, :]).astype(jnp.float32)
    rows_mask = jnp.dot(
        own_onehot, tile_mask.astype(jnp.float32), preferred_element_type=jnp.float32
    )
    return jnp.dot(rows_mask, order_onehot.T, preferred_element_type=jnp.float32)


def attend(queries_flat, key_values, pos_mask):
    row_count = queries_flat.shape[0]
    heads_dev = queries_flat.shape[1] // HEAD
    queries = queries_flat.reshape(row_count, heads_dev, HEAD)
    score_scale = 1.0 / math.sqrt(HEAD)
    tiles_dev = row_count // TILE
    tile_ids = jnp.arange(pos_mask.shape[1], dtype=jnp.int32)
    initial = (
        jnp.full((heads_dev, row_count), MASKED_SCORE, jnp.float32),
        jnp.zeros((heads_dev, row_count), jnp.float32),
        jnp.zeros((heads_dev, row_count, HEAD), jnp.float32),
    )
    fetched = lax.all_gather(key_values, "seq", axis=1, tiled=True)
    fetched_count = fetched.shape[1]
    key_block = 512

    def advance(block_index, state_now):
        top_score, denom, weighted = state_now
        offset = block_index * key_block
        key_rows = lax.dynamic_slice_in_dim(fetched[0], offset, key_block).reshape(
            key_block, heads_dev, HEAD
        )
        values = lax.dynamic_slice_in_dim(fetched[1], offset, key_block).reshape(
            key_block, heads_dev, HEAD
        )
        tile_pos = (offset + jnp.arange(key_block, dtype=jnp.int32)) // TILE
        onehot = (tile_pos[:, None] == tile_ids[None, :]).astype(jnp.float32)
        tile_allowed = (
            jnp.einsum("qn,kn->qk", pos_mask, onehot, preferred_element_type=jnp.float32) > 0.5
        )
        visible = jnp.broadcast_to(tile_allowed[:, None, :], (tiles_dev, TILE, key_block)).reshape(
            row_count, key_block
        )
        scores = (
            jnp.einsum("qhd,khd->hqk", queries, key_rows, preferred_element_type=jnp.float32)
            * score_scale
        )
        masked = jnp.where(visible[None], scores, MASKED_SCORE)
        new_top = jnp.maximum(top_score, jnp.max(masked, axis=2))
        powers = jnp.where(visible[None], jnp.exp(masked - new_top[:, :, None]), 0.0)
        shrink = jnp.exp(top_score - new_top)
        denom = denom * shrink + jnp.sum(powers, axis=2)
        weighted = weighted * shrink[:, :, None] + jnp.einsum(
            "hqk,khd->hqd", powers.astype(jnp.bfloat16), values, preferred_element_type=jnp.float32
        )
        return (new_top, denom, weighted)

    top_score, denom, weighted = lax.fori_loop(0, fetched_count // key_block, advance, initial)
    finished = (weighted / denom[:, :, None]).astype(jnp.bfloat16)
    return jnp.transpose(finished, (1, 0, 2)).reshape(row_count, heads_dev * HEAD)


def per_device_general(clip_tokens, conv_taps, norm_gain, qkv_weight, out_weight, tile_mask, stripe_order):
    tiles_dev = clip_tokens.shape[1] // TILE
    send_order, place_order, own_row = stripe_tables(stripe_order, tiles_dev)
    before = passed_along(clip_tokens, "seq", 1)
    mixed = causal_conv(clip_tokens, before, conv_taps)
    mixed = regroup(mixed, send_order, place_order)
    projected = project(mixed, norm_gain, qkv_weight)
    row_count = projected.shape[1]
    group_cols = projected.shape[2]
    half_rows = row_count // 2
    side = lax.axis_index("tp") % 2
    mine_first = side == 0
    query_send = lax.dynamic_slice_in_dim(projected[0], (1 - side) * half_rows, half_rows, axis=0)
    query_mine = lax.dynamic_slice_in_dim(projected[0], side * half_rows, half_rows, axis=0)
    kv_mine = projected[1:]
    query_other, kv_other = from_partner((query_send, kv_mine), "tp", 0)
    queries = jnp.where(
        mine_first,
        jnp.concatenate([query_mine, query_other], axis=1),
        jnp.concatenate([query_other, query_mine], axis=1),
    )
    key_values = jnp.where(
        mine_first,
        jnp.concatenate([kv_mine, kv_other], axis=2),
        jnp.concatenate([kv_other, kv_mine], axis=2),
    )
    own_half = lax.dynamic_slice_in_dim(own_row, side * (tiles_dev // 2), tiles_dev // 2)
    pos_mask = position_mask(tile_mask, stripe_order, own_half)
    pair_out = attend(queries, key_values, pos_mask)
    give_cols = lax.dynamic_slice_in_dim(pair_out, (1 - side) * group_cols, group_cols, axis=1)
    keep_cols = lax.dynamic_slice_in_dim(pair_out, side * group_cols, group_cols, axis=1)
    got_cols = from_partner(give_cols, "tp", 0)
    heads_out = jnp.where(
        mine_first,
        jnp.concatenate([keep_cols, got_cols], axis=0),
        jnp.concatenate([got_cols, keep_cols], axis=0),
    )
    return lax.psum_scatter(
        jnp.einsum("qg,gc->cq", heads_out, out_weight, preferred_element_type=jnp.float32).astype(
            jnp.bfloat16
        ),
        "tp",
        scatter_dimension=0,
        tiled=True,
    )


def per_device(clip_tokens, conv_taps, norm_gain, qkv_weight, out_weight, tile_mask, stripe_order):
    arguments = (clip_tokens, conv_taps, norm_gain, qkv_weight, out_weight, tile_mask, stripe_order)
    whole_heads = qkv_weight.shape[1] % HEAD == 0
    two_halves = lax.axis_size("seq") == 2 and clip_tokens.shape[1] == 2 * FRAME
    if whole_heads and two_halves and lax.axis_size("tp") == 4:
        return per_device_fast(*arguments)
    return per_device_general(*arguments)


def solution(mesh):
    in_specs = (
        P("tp", ("dp", "seq")),
        P(None, "tp"),
        P(),
        P(None, "tp", None),
        P("tp", None),
        P(),
        P(),
    )
    out_specs = P("tp", ("dp", "seq"))
    return jax.shard_map(
        per_device, mesh=mesh, in_specs=in_specs, out_specs=out_specs, check_vma=False
    )
```

```python
import functools
import math

import jax
import jax.numpy as jnp
from jax import lax
from jax.experimental import pallas as pl
from jax.experimental.pallas import tpu as pltpu
from jax.sharding import PartitionSpec as P


HEAD = 128
TILE = 128
FH = 16
FW = 32
FRAME = FH * FW
TAPS = 27


EPSILON = 1e-06
MASKED_SCORE = -1e30
LOG2E = math.log2(math.e)

VMEM_LIMIT = 20 * 1024 * 1024
VMEM_WHOLE = 60 * 1024 * 1024


def params(limit=VMEM_LIMIT):
    return pltpu.CompilerParams(vmem_limit_bytes=limit)


def column_shifts(frame, lane):
    column = lane % FW
    left = jnp.where(column > 0, pltpu.roll(frame, 1, 1), 0.0)
    right = jnp.where(column < FW - 1, pltpu.roll(frame, FRAME - 1, 1), 0.0)
    return (left, frame, right)


def row_sum(rows, lane):
    above = jnp.where(lane >= FW, pltpu.roll(rows[0], FW, 1), 0.0)
    below = jnp.where(lane < FRAME - FW, pltpu.roll(rows[2], FRAME - FW, 1), 0.0)
    return rows[1] + above + below


def taps_applied(pairs, taps, lane):
    rows = []
    for row_off in range(3):
        total = None
        for time_off, shifts in pairs:
            for col_off in range(3):
                tap = time_off * 9 + row_off * 3 + col_off
                term = taps[:, tap : tap + 1] * shifts[col_off]
                total = term if total is None else total + term
        rows.append(total)
    return row_sum(rows, lane)


def pack_slots(order_ref, slots_ref, seq_here, tiles_dev, positions):
    half = tiles_dev // 2
    kept = jnp.int32(0)
    sent = jnp.int32(half)
    for position in range(positions):
        tile = order_ref[position]
        mine = tile // tiles_dev == seq_here
        stays = jnp.int32(position // tiles_dev) == seq_here
        slot = jnp.where(stays, kept, sent)

        @pl.when(mine)
        def _(tile=tile, slot=slot):
            slots_ref[tile - seq_here * tiles_dev] = slot

        step = mine.astype(jnp.int32)
        kept = kept + jnp.where(stays, step, 0)
        sent = sent + jnp.where(stays, 0, step)


def conv_body(with_before, seq_ref, order_ref, *refs):
    if with_before:
        tokens_ref, taps_ref, before_ref, part_ref, keep_ref, send_ref, slots_ref, taps_scr, packed = refs
    else:
        tokens_ref, taps_ref, part_ref, keep_ref, send_ref, slots_ref, taps_scr, packed = refs
    channels, tokens = tokens_ref.shape
    tiles_dev = tokens // TILE
    seq_here = seq_ref[0]

    @pl.when(pl.program_id(0) == 0)
    def _():
        pack_slots(order_ref, slots_ref, seq_here, tiles_dev, order_ref.shape[0])

    taps_scr[:, :TAPS] = taps_ref[...].T
    group = 16
    lane = lax.broadcasted_iota(jnp.int32, (group, FRAME), 1)

    def advance(step, carry):
        rows = pl.ds(pl.multiple_of(step * group, group), group)
        taps = taps_scr[rows, :]
        if with_before:
            old = [
                column_shifts(before_ref[rows, f * FRAME : (f + 1) * FRAME].astype(jnp.float32), lane)
                for f in range(2)
            ]
            sums = [
                part_ref[rows, :FRAME] + taps_applied([(0, old[0]), (1, old[1])], taps, lane),
                part_ref[rows, FRAME:] + taps_applied([(0, old[1])], taps, lane),
            ]
        else:
            now = [
                column_shifts(tokens_ref[rows, f * FRAME : (f + 1) * FRAME].astype(jnp.float32), lane)
                for f in range(2)
            ]
            sums = [
                now[0][1] + taps_applied([(2, now[0])], taps, lane),
                now[1][1] + taps_applied([(1, now[0]), (2, now[1])], taps, lane),
            ]
            part_ref[rows, :FRAME] = sums[0]
            part_ref[rows, FRAME:] = sums[1]
        for tile in range(tiles_dev):
            frame, spot = divmod(tile * TILE, FRAME)
            place = pl.ds(pl.multiple_of(slots_ref[tile] * TILE, TILE), TILE)
            packed[rows, place] = sums[frame][:, spot : spot + TILE].astype(jnp.bfloat16)
        return carry

    lax.fori_loop(0, channels // group, advance, 0)
    keep_ref[...] = packed[:, : tokens // 2]
    send_ref[...] = packed[:, tokens // 2 :]


def conv_call(seq_here, stripe_order, tokens, conv_taps, before=None, part=None):
    channels, count = tokens.shape
    block = 128
    wide = pl.BlockSpec((block, count), lambda i, *_: (i, 0))
    slim = pl.BlockSpec((block, count // 2), lambda i, *_: (i, 0))
    taps_spec = pl.BlockSpec((TAPS, block), lambda i, *_: (0, i))
    packed_shape = jax.ShapeDtypeStruct((channels, count // 2), jnp.bfloat16)
    with_before = before is not None
    extra_in, extra_args, out_specs, out_shape = [], [], [slim, slim], [packed_shape, packed_shape]
    if with_before:
        extra_in, extra_args = [wide, wide], [before, part]
    else:
        out_specs = [wide] + out_specs
        out_shape = [jax.ShapeDtypeStruct((channels, count), jnp.float32)] + out_shape
    return pl.pallas_call(
        functools.partial(conv_body, with_before),
        grid_spec=pltpu.PrefetchScalarGridSpec(
            num_scalar_prefetch=2,
            grid=(channels // block,),
            in_specs=[wide, taps_spec] + extra_in,
            out_specs=out_specs,
            scratch_shapes=[
                pltpu.SMEM((count // TILE,), jnp.int32),
                pltpu.VMEM((block, 128), jnp.float32),
                pltpu.VMEM((block, count), jnp.bfloat16),
            ],
        ),
        out_shape=out_shape,
        compiler_params=params(VMEM_LIMIT if with_before else VMEM_WHOLE),
        cost_estimate=pl.CostEstimate(
            flops=channels * count * TAPS, bytes_accessed=channels * count * 8, transcendentals=0
        ),
        name="conv_before" if with_before else "conv_here",
    )(seq_here, stripe_order, tokens, conv_taps, *extra_args)


def prepare_body(blocks_ref, gain_ref, qkv_ref, out_ref, qkv_out, out_out):
    qkv_out[...] = (qkv_ref[...].astype(jnp.float32) * gain_ref[...]).astype(jnp.bfloat16)
    out_out[...] = out_ref[...].T


def prepare_weights(blocks, norm_gain, qkv_weight, out_weight):
    kinds, cols, channels = qkv_weight.shape
    count = blocks.shape[0]
    width = channels // count
    return pl.pallas_call(
        prepare_body,
        grid_spec=pltpu.PrefetchScalarGridSpec(
            num_scalar_prefetch=1,
            grid=(count,),
            in_specs=[
                pl.BlockSpec((1, width), lambda j, b: (0, b[j])),
                pl.BlockSpec((kinds * cols, width), lambda j, b: (0, b[j])),
                pl.BlockSpec((cols, width), lambda j, b: (0, b[j])),
            ],
            out_specs=[
                pl.BlockSpec((kinds * cols, width), lambda j, b: (0, j)),
                pl.BlockSpec((width, cols), lambda j, b: (j, 0)),
            ],
        ),
        out_shape=[
            jax.ShapeDtypeStruct((kinds * cols, channels), jnp.bfloat16),
            jax.ShapeDtypeStruct((channels, cols), jnp.bfloat16),
        ],
        compiler_params=params(),
        cost_estimate=pl.CostEstimate(
            flops=kinds * cols * channels, bytes_accessed=16 * cols * channels, transcendentals=0
        ),
        name="prepare_weights",
    )(blocks, norm_gain[None, :], qkv_weight.reshape(kinds * cols, channels), out_weight)


def project_body(query_steps, weight_ref, *refs):
    shards, out_ref, inverse_ref = refs[:-2], refs[-2], refs[-1]
    width = shards[0].shape[0]
    step = pl.program_id(0)

    @pl.when(step == 0)
    def _():
        squares = None
        for shard in shards:
            wide = shard[...].astype(jnp.float32)
            term = jnp.sum(wide * wide, axis=0, keepdims=True)
            squares = term if squares is None else squares + term
        inverse_ref[...] = lax.rsqrt(squares / (width * len(shards)) + EPSILON)

    total = None
    for index, shard in enumerate(shards):
        term = jnp.dot(
            weight_ref[:, index * width : (index + 1) * width],
            shard[...],
            preferred_element_type=jnp.float32,
        )
        total = term if total is None else total + term
    scale = jnp.where(step < query_steps, LOG2E / math.sqrt(HEAD), 1.0)
    out_ref[...] = (total * (inverse_ref[...] * scale)).astype(jnp.bfloat16)


def project_call(weights, shards):
    rows, channels = weights.shape
    width, tokens = shards[0].shape
    block = 256
    whole = pl.BlockSpec((width, tokens), lambda i: (0, 0))
    return pl.pallas_call(
        functools.partial(project_body, rows // 3 // block),
        grid=(rows // block,),
        in_specs=[pl.BlockSpec((block, channels), lambda i: (i, 0))] + [whole] * len(shards),
        out_specs=pl.BlockSpec((block, tokens), lambda i: (i, 0)),
        out_shape=jax.ShapeDtypeStruct((rows, tokens), jnp.bfloat16),
        scratch_shapes=[pltpu.VMEM((1, tokens), jnp.float32)],
        compiler_params=params(),
        cost_estimate=pl.CostEstimate(
            flops=2 * rows * channels * tokens,
            bytes_accessed=2 * (rows * channels + channels * tokens + rows * tokens),
            transcendentals=0,
        ),
        name="project",
    )(weights, *shards)


def tile_lists(order_ref, ids_ref, seq_here, tiles_dev):
    half = tiles_dev // 2
    for block in range(2):
        first = jnp.int32(0)
        second = jnp.int32(0)
        away = (jnp.int32(block) != seq_here).astype(jnp.int32)
        for spot in range(tiles_dev):
            tile = order_ref[block * tiles_dev + spot]
            late = tile // tiles_dev
            rank = jnp.where(late == 0, first, second)
            ids_ref[(2 * late + away) * half + rank] = tile
            first = first + (1 - late)
            second = second + late


def attend_body(chunk, seq_ref, order_ref, mask_ref, query_ref, *refs):
    count = 2 * (chunk + 1)
    keys, values = refs[:count], refs[count : 2 * count]
    out_ref, ids_ref, scores_ref = refs[2 * count], refs[2 * count + 1], refs[2 * count + 2]
    tokens = query_ref.shape[1]
    half = tokens // TILE

    @pl.when(pl.program_id(0) == 0)
    def _():
        tile_lists(order_ref, ids_ref, seq_ref[0], 2 * half)

    query = query_ref[...]
    lane_tile = lax.broadcasted_iota(jnp.int32, (1, tokens), 1) // TILE
    top = None
    for source in range(count):
        block = jnp.dot(keys[source][...].T, query, preferred_element_type=jnp.float32)
        for spot in range(half):
            key_tile = ids_ref[source * half + spot]
            bias = jnp.zeros((1, tokens), jnp.float32)
            for query_spot in range(half):
                query_tile = ids_ref[2 * chunk * half + query_spot]
                blocked = jnp.where(mask_ref[query_tile, key_tile] == 1, 0.0, MASKED_SCORE)
                bias = jnp.where(lane_tile == query_spot, blocked, bias)
            piece = block[spot * TILE : (spot + 1) * TILE, :] + bias
            scores_ref[source * tokens + spot * TILE : source * tokens + (spot + 1) * TILE, :] = piece
            best = jnp.max(piece, axis=0, keepdims=True)
            top = best if top is None else jnp.maximum(top, best)
    denom = None
    weighted = None
    for source in range(count):
        powers = jnp.exp2(scores_ref[source * tokens : (source + 1) * tokens, :] - top)
        summed = jnp.sum(powers, axis=0, keepdims=True)
        term = jnp.dot(
            values[source][...], powers.astype(jnp.bfloat16), preferred_element_type=jnp.float32
        )
        denom = summed if denom is None else denom + summed
        weighted = term if weighted is None else weighted + term
    out_ref[...] = (weighted / denom).astype(jnp.bfloat16)


def attend_call(chunk, seq_here, stripe_order, tile_mask, own, peers):
    rows, tokens = own[0].shape
    heads = rows // 3 // HEAD
    sources = []
    for mine, other in zip(own, peers):
        sources += [(mine, heads, 2 * heads), (other, 0, heads)]

    def spec(start):
        return pl.BlockSpec((HEAD, tokens), lambda h, *_, start=start: (start + h, 0))

    count = len(sources)
    return pl.pallas_call(
        functools.partial(attend_body, chunk),
        grid_spec=pltpu.PrefetchScalarGridSpec(
            num_scalar_prefetch=3,
            grid=(heads,),
            in_specs=[spec(0)] + [spec(k) for _, k, _ in sources] + [spec(v) for _, _, v in sources],
            out_specs=spec(0),
            scratch_shapes=[
                pltpu.SMEM((4 * tokens // TILE,), jnp.int32),
                pltpu.VMEM((count * tokens, tokens), jnp.float32),
            ],
        ),
        out_shape=jax.ShapeDtypeStruct((heads * HEAD, tokens), jnp.bfloat16),
        compiler_params=params(),
        cost_estimate=pl.CostEstimate(
            flops=4 * heads * HEAD * tokens * tokens * count,
            bytes_accessed=2 * heads * HEAD * tokens * (2 + 2 * count),
            transcendentals=heads * tokens * tokens * count,
        ),
    )(
        seq_here,
        stripe_order,
        tile_mask,
        own[chunk],
        *[array for array, _, _ in sources],
        *[array for array, _, _ in sources],
    )


def place_body(seq_ref, order_ref, ends_ref, first_ref, *refs):
    parts, out_ref, second_ref = refs[:4], refs[4], refs[5]
    _, tokens = first_ref.shape
    tiles_dev = 2 * tokens // TILE
    seq_here = seq_ref[0]
    at_end = ends_ref[0] == 1
    total = (
        parts[0][...].astype(jnp.float32)
        + parts[1][...].astype(jnp.float32)
        + parts[2][...].astype(jnp.float32)
        + jnp.where(at_end, parts[3][...].astype(jnp.float32), 0.0)
    )
    second_ref[...] = total.astype(jnp.bfloat16)
    ranks = [jnp.int32(0), jnp.int32(0)]
    for position in range(tiles_dev):
        late = order_ref[seq_here * tiles_dev + position] // tiles_dev
        spot = pl.ds(pl.multiple_of(jnp.where(late == 0, ranks[0], ranks[1]) * TILE, TILE), TILE)
        here = slice(position * TILE, (position + 1) * TILE)

        @pl.when(late == 0)
        def _(spot=spot, here=here):
            out_ref[:, here] = first_ref[:, spot]

        @pl.when(late == 1)
        def _(spot=spot, here=here):
            out_ref[:, here] = second_ref[:, spot]

        ranks[0] = ranks[0] + (1 - late)
        ranks[1] = ranks[1] + late


def place_call(seq_here, stripe_order, at_end, first, parts):
    channels, tokens = first.shape
    block = 128
    slim = pl.BlockSpec((block, tokens), lambda i, *_: (i, 0))
    return pl.pallas_call(
        place_body,
        grid_spec=pltpu.PrefetchScalarGridSpec(
            num_scalar_prefetch=3,
            grid=(channels // block,),
            in_specs=[slim] * 5,
            out_specs=pl.BlockSpec((block, 2 * tokens), lambda i, *_: (i, 0)),
            scratch_shapes=[pltpu.VMEM((block, tokens), jnp.bfloat16)],
        ),
        out_shape=jax.ShapeDtypeStruct((channels, 2 * tokens), jnp.bfloat16),
        compiler_params=params(),
        cost_estimate=pl.CostEstimate(
            flops=4 * channels * tokens, bytes_accessed=14 * channels * tokens, transcendentals=0
        ),
        name="place",
    )(seq_here, stripe_order, at_end, first, *parts)


FORWARD = [(0, 1), (1, 2), (2, 3), (3, 0)]
BACKWARD = [(1, 0), (2, 1), (3, 2), (0, 3)]
FOLDED = [(0, 1), (1, 3), (3, 2), (2, 0)]
UNFOLDED = [(1, 0), (3, 1), (2, 3), (0, 2)]


def gather_blocks(block, here):
    before = lax.ppermute(block, "tp", FORWARD)
    after = lax.ppermute(block, "tp", BACKWARD)
    relay = jnp.where(here == 2, before, jnp.where(here == 1, after, block))
    across = lax.ppermute(relay, "tp", UNFOLDED)
    return (block, before, after, across)


def plus(a, b, chosen):
    summed = a.astype(jnp.float32) + jnp.where(chosen, b.astype(jnp.float32), 0.0)
    return summed.astype(jnp.bfloat16)


def reduce_blocks(weights, heads_out, here):
    width = weights.shape[0] // 4

    def partial(index):
        block = weights[index * width : (index + 1) * width]
        return jnp.dot(block, heads_out, preferred_element_type=jnp.float32).astype(jnp.bfloat16)

    sent = partial(3)
    across = lax.ppermute(sent, "tp", FOLDED)
    back = lax.ppermute(plus(partial(1), across, here == 2), "tp", BACKWARD)
    onward = lax.ppermute(plus(partial(2), across, here == 1), "tp", FORWARD)
    return (partial(0), back, onward, across)


def per_device_fast(
    clip_tokens, conv_taps, norm_gain, qkv_weight, out_weight, tile_mask, stripe_order
):
    seq = lax.axis_index("seq")
    here = lax.axis_index("tp")
    seq_here = seq.astype(jnp.int32)[None]
    at_end = ((here == 0) | (here == 3)).astype(jnp.int32)[None]
    blocks = jnp.stack([here, (here + 3) % 4, (here + 1) % 4, (here + 2) % 4]).astype(jnp.int32)

    part, keep_a, send_a = conv_call(seq_here, stripe_order, clip_tokens, conv_taps)
    got_a = lax.ppermute(send_a, "seq", [(0, 1)])
    before = lax.ppermute(clip_tokens, "seq", [(0, 1)])
    weights, out_t = prepare_weights(blocks, norm_gain, qkv_weight, out_weight)

    tokens_a = jnp.where(seq == 0, keep_a, got_a)
    shards_a = gather_blocks(tokens_a, here)

    keep_b, send_b = conv_call(seq_here, stripe_order, clip_tokens, conv_taps, before, part)
    got_b = lax.ppermute(send_b, "seq", [(1, 0)])
    tokens_b = jnp.where(seq == 1, keep_b, got_b)

    rows = weights.shape[0]
    cols = rows // 3
    swap = [(0, 1), (1, 0)]
    own_a = project_call(weights, shards_a)
    peer_a = lax.ppermute(own_a[cols:], "seq", swap)
    shards_b = gather_blocks(tokens_b, here)
    out_a = attend_call(0, seq_here, stripe_order, tile_mask, [own_a], [peer_a])
    parts_a = reduce_blocks(out_t, out_a, here)
    own_b = project_call(weights, shards_b)
    peer_b = lax.ppermute(own_b[cols:], "seq", swap)
    out_b = attend_call(1, seq_here, stripe_order, tile_mask, [own_a, own_b], [peer_a, peer_b])
    parts_b = reduce_blocks(out_t, out_b, here)
    first = (
        parts_a[0].astype(jnp.float32)
        + parts_a[1].astype(jnp.float32)
        + parts_a[2].astype(jnp.float32)
        + jnp.where(at_end == 1, parts_a[3].astype(jnp.float32), 0.0)
    ).astype(jnp.bfloat16)
    return place_call(seq_here, stripe_order, at_end, first, parts_b)


def passed_along(block, axis, distance):
    devices = range(lax.axis_size(axis))
    route = [(i - distance, i) for i in devices if i - distance in devices]
    return lax.ppermute(block, axis, route)


def from_partner(block, axis, apart):
    count = lax.axis_size(axis)
    route = []
    for low in range(count):
        high = low | 1 << apart
        if high != low and high < count:
            route += [(low, high), (high, low)]
    return lax.ppermute(block, axis, route)


def causal_conv(local_tokens, before, conv_taps):
    channels = local_tokens.shape[0]
    frames = local_tokens.shape[1] // (FH * FW)
    stacked = (
        jnp.concatenate([before, local_tokens], axis=1)
        .astype(jnp.float32)
        .reshape(channels, frames + 2, FH, FW)
    )
    padded = jnp.pad(stacked, ((0, 0), (0, 0), (1, 1), (1, 1)))
    summed = jnp.zeros((channels, frames, FH, FW), jnp.float32)
    for time_off in range(3):
        for row_off in range(3):
            for col_off in range(3):
                tap_vec = conv_taps[time_off * 9 + row_off * 3 + col_off]
                summed = (
                    summed
                    + tap_vec[:, None, None, None]
                    * padded[
                        :,
                        time_off : time_off + frames,
                        row_off : row_off + FH,
                        col_off : col_off + FW,
                    ]
                )
    return (local_tokens.astype(jnp.float32) + summed.reshape(channels, -1)).astype(jnp.bfloat16)


def stripe_tables(stripe_order, tiles_dev):
    seq_count = lax.axis_size("seq")
    seq_here = lax.axis_index("seq")
    per_source = tiles_dev // seq_count
    blocks = stripe_order.reshape(seq_count, tiles_dev)
    owners = blocks // tiles_dev
    is_mine = (owners == seq_here).astype(jnp.int32)
    rank_of = jnp.cumsum(is_mine, axis=1) - 1
    slot_ids = jnp.arange(per_source, dtype=jnp.int32)
    picked = is_mine[:, None, :] * (rank_of[:, None, :] == slot_ids[None, :, None]).astype(
        jnp.int32
    )
    local_tiles = (blocks - seq_here * tiles_dev)[:, None, :]
    send_order = jnp.sum(picked * local_tiles, axis=2).reshape(-1)
    own_row = lax.dynamic_slice_in_dim(stripe_order, seq_here * tiles_dev, tiles_dev)
    sources = own_row // tiles_dev
    position = jnp.arange(tiles_dev, dtype=jnp.int32)
    earlier = (sources[:, None] == sources[None, :]) & (position[None, :] < position[:, None])
    place_order = sources * per_source + jnp.sum(earlier.astype(jnp.int32), axis=1)
    return (send_order, place_order, own_row)


def regroup(values, send_order, place_order):
    leading = values.shape[0]
    trailing = values.shape[2:]
    in_tiles = values.reshape((leading, values.shape[1] // TILE, TILE) + trailing)
    outgoing = jnp.take(in_tiles, send_order, axis=1)
    arrived = lax.all_to_all(outgoing, "seq", split_axis=1, concat_axis=1, tiled=True)
    placed = jnp.take(arrived, place_order, axis=1)
    return placed.reshape(values.shape)


def project(mixed, norm_gain, qkv_weight):
    channels = norm_gain.shape[0]
    widened = lax.all_gather(mixed, "tp", axis=0, tiled=True).astype(jnp.float32)
    scaled = (widened * norm_gain[:, None]).astype(jnp.bfloat16)
    projected = jnp.einsum("ct,khc->kth", scaled, qkv_weight, preferred_element_type=jnp.float32)
    squares = jnp.sum(widened * widened, axis=0)
    projected, squares = (projected, squares)
    inverse = lax.rsqrt(squares / channels + EPSILON)
    return (projected * inverse[None, :, None]).astype(jnp.bfloat16)


def position_mask(tile_mask, stripe_order, own_half):
    tiles_all = tile_mask.shape[0]
    tile_ids = jnp.arange(tiles_all, dtype=jnp.int32)
    own_onehot = (own_half[:, None] == tile_ids[None, :]).astype(jnp.float32)
    order_onehot = (stripe_order[:, None] == tile_ids[None, :]).astype(jnp.float32)
    rows_mask = jnp.dot(
        own_onehot, tile_mask.astype(jnp.float32), preferred_element_type=jnp.float32
    )
    return jnp.dot(rows_mask, order_onehot.T, preferred_element_type=jnp.float32)


def attend(queries_flat, key_values, pos_mask):
    row_count = queries_flat.shape[0]
    heads_dev = queries_flat.shape[1] // HEAD
    queries = queries_flat.reshape(row_count, heads_dev, HEAD)
    score_scale = 1.0 / math.sqrt(HEAD)
    tiles_dev = row_count // TILE
    tile_ids = jnp.arange(pos_mask.shape[1], dtype=jnp.int32)
    initial = (
        jnp.full((heads_dev, row_count), MASKED_SCORE, jnp.float32),
        jnp.zeros((heads_dev, row_count), jnp.float32),
        jnp.zeros((heads_dev, row_count, HEAD), jnp.float32),
    )
    fetched = lax.all_gather(key_values, "seq", axis=1, tiled=True)
    fetched_count = fetched.shape[1]
    key_block = 512

    def advance(block_index, state_now):
        top_score, denom, weighted = state_now
        offset = block_index * key_block
        key_rows = lax.dynamic_slice_in_dim(fetched[0], offset, key_block).reshape(
            key_block, heads_dev, HEAD
        )
        values = lax.dynamic_slice_in_dim(fetched[1], offset, key_block).reshape(
            key_block, heads_dev, HEAD
        )
        tile_pos = (offset + jnp.arange(key_block, dtype=jnp.int32)) // TILE
        onehot = (tile_pos[:, None] == tile_ids[None, :]).astype(jnp.float32)
        tile_allowed = (
            jnp.einsum("qn,kn->qk", pos_mask, onehot, preferred_element_type=jnp.float32) > 0.5
        )
        visible = jnp.broadcast_to(tile_allowed[:, None, :], (tiles_dev, TILE, key_block)).reshape(
            row_count, key_block
        )
        scores = (
            jnp.einsum("qhd,khd->hqk", queries, key_rows, preferred_element_type=jnp.float32)
            * score_scale
        )
        masked = jnp.where(visible[None], scores, MASKED_SCORE)
        new_top = jnp.maximum(top_score, jnp.max(masked, axis=2))
        powers = jnp.where(visible[None], jnp.exp(masked - new_top[:, :, None]), 0.0)
        shrink = jnp.exp(top_score - new_top)
        denom = denom * shrink + jnp.sum(powers, axis=2)
        weighted = weighted * shrink[:, :, None] + jnp.einsum(
            "hqk,khd->hqd", powers.astype(jnp.bfloat16), values, preferred_element_type=jnp.float32
        )
        return (new_top, denom, weighted)

    _, denom, weighted = lax.fori_loop(0, fetched_count // key_block, advance, initial)
    finished = (weighted / denom[:, :, None]).astype(jnp.bfloat16)
    return jnp.transpose(finished, (1, 0, 2)).reshape(row_count, heads_dev * HEAD)


def per_device_general(clip_tokens, conv_taps, norm_gain, qkv_weight, out_weight, tile_mask, stripe_order):
    tiles_dev = clip_tokens.shape[1] // TILE
    send_order, place_order, own_row = stripe_tables(stripe_order, tiles_dev)
    before = passed_along(clip_tokens, "seq", 1)
    mixed = causal_conv(clip_tokens, before, conv_taps)
    mixed = regroup(mixed, send_order, place_order)
    projected = project(mixed, norm_gain, qkv_weight)
    row_count = projected.shape[1]
    group_cols = projected.shape[2]
    half_rows = row_count // 2
    side = lax.axis_index("tp") % 2
    mine_first = side == 0
    query_send = lax.dynamic_slice_in_dim(projected[0], (1 - side) * half_rows, half_rows, axis=0)
    query_mine = lax.dynamic_slice_in_dim(projected[0], side * half_rows, half_rows, axis=0)
    kv_mine = projected[1:]
    query_other, kv_other = from_partner((query_send, kv_mine), "tp", 0)
    queries = jnp.where(
        mine_first,
        jnp.concatenate([query_mine, query_other], axis=1),
        jnp.concatenate([query_other, query_mine], axis=1),
    )
    key_values = jnp.where(
        mine_first,
        jnp.concatenate([kv_mine, kv_other], axis=2),
        jnp.concatenate([kv_other, kv_mine], axis=2),
    )
    own_half = lax.dynamic_slice_in_dim(own_row, side * (tiles_dev // 2), tiles_dev // 2)
    pos_mask = position_mask(tile_mask, stripe_order, own_half)
    pair_out = attend(queries, key_values, pos_mask)
    give_cols = lax.dynamic_slice_in_dim(pair_out, (1 - side) * group_cols, group_cols, axis=1)
    keep_cols = lax.dynamic_slice_in_dim(pair_out, side * group_cols, group_cols, axis=1)
    got_cols = from_partner(give_cols, "tp", 0)
    heads_out = jnp.where(
        mine_first,
        jnp.concatenate([keep_cols, got_cols], axis=0),
        jnp.concatenate([got_cols, keep_cols], axis=0),
    )
    return lax.psum_scatter(
        jnp.einsum("qg,gc->cq", heads_out, out_weight, preferred_element_type=jnp.float32).astype(
            jnp.bfloat16
        ),
        "tp",
        scatter_dimension=0,
        tiled=True,
    )


def solution(mesh):
    in_specs = (
        P("tp", ("dp", "seq")),
        P(None, "tp"),
        P(),
        P(None, "tp", None),
        P("tp", None),
        P(),
        P(),
    )
    out_specs = P("tp", ("dp", "seq"))

    def run(clip_tokens, conv_taps, norm_gain, qkv_weight, out_weight, tile_mask, stripe_order):
        arguments = (clip_tokens, conv_taps, norm_gain, qkv_weight, out_weight, tile_mask, stripe_order)
        tokens = clip_tokens.shape[1] // (mesh.shape["dp"] * mesh.shape["seq"])
        columns = qkv_weight.shape[1] // mesh.shape["tp"]
        two_halves = mesh.shape["seq"] == 2 and tokens == 2 * FRAME
        fast = two_halves and mesh.shape["tp"] == 4 and columns % HEAD == 0

        def per_device(*local):
            if not fast:
                return per_device_general(*local)
            return per_device_fast(*local)

        step = jax.shard_map(
            per_device, mesh=mesh, in_specs=in_specs, out_specs=out_specs, check_vma=False
        )
        return step(*arguments)

    return run
```

```python
import functools
import math

import jax
import jax.numpy as jnp
from jax import lax
from jax.experimental import pallas as pl
from jax.experimental.pallas import tpu as pltpu
from jax.sharding import PartitionSpec as P


HEAD = 128
TILE = 128
FH = 16
FW = 32
FRAME = FH * FW
TAPS = 27


EPSILON = 1e-06
MASKED_SCORE = -1e30
LOG2E = math.log2(math.e)

VMEM_LIMIT = 20 * 1024 * 1024
VMEM_WHOLE = 60 * 1024 * 1024


def params(limit=VMEM_LIMIT):
    return pltpu.CompilerParams(vmem_limit_bytes=limit)


def column_shifts(frame, lane):
    column = lane % FW
    left = jnp.where(column > 0, pltpu.roll(frame, 1, 1), 0.0)
    right = jnp.where(column < FW - 1, pltpu.roll(frame, FRAME - 1, 1), 0.0)
    return (left, frame, right)


def row_sum(rows, lane):
    above = jnp.where(lane >= FW, pltpu.roll(rows[0], FW, 1), 0.0)
    below = jnp.where(lane < FRAME - FW, pltpu.roll(rows[2], FRAME - FW, 1), 0.0)
    return rows[1] + above + below


def taps_applied(pairs, taps, lane):
    rows = []
    for row_off in range(3):
        total = None
        for time_off, shifts in pairs:
            for col_off in range(3):
                tap = time_off * 9 + row_off * 3 + col_off
                term = taps[:, tap : tap + 1] * shifts[col_off]
                total = term if total is None else total + term
        rows.append(total)
    return row_sum(rows, lane)


def pack_slots(order_ref, slots_ref, seq_here, tiles_dev, positions):
    half = tiles_dev // 2
    kept = jnp.int32(0)
    sent = jnp.int32(half)
    for position in range(positions):
        tile = order_ref[position]
        mine = tile // tiles_dev == seq_here
        stays = jnp.int32(position // tiles_dev) == seq_here
        slot = jnp.where(stays, kept, sent)

        @pl.when(mine)
        def _(tile=tile, slot=slot):
            slots_ref[tile - seq_here * tiles_dev] = slot

        step = mine.astype(jnp.int32)
        kept = kept + jnp.where(stays, step, 0)
        sent = sent + jnp.where(stays, 0, step)


def conv_body(with_before, seq_ref, order_ref, *refs):
    if with_before:
        tokens_ref, taps_ref, before_ref, part_ref, keep_ref, send_ref, slots_ref, taps_scr, packed = refs
    else:
        tokens_ref, taps_ref, part_ref, keep_ref, send_ref, slots_ref, taps_scr, packed = refs
    channels, tokens = tokens_ref.shape
    tiles_dev = tokens // TILE
    seq_here = seq_ref[0]

    @pl.when(pl.program_id(0) == 0)
    def _():
        pack_slots(order_ref, slots_ref, seq_here, tiles_dev, order_ref.shape[0])

    taps_scr[:, :TAPS] = taps_ref[...].T
    group = 16
    part = 8
    lane = lax.broadcasted_iota(jnp.int32, (part, FRAME), 1)

    def frame_of(ref, rows, frame, piece):
        wide = ref[rows, frame * FRAME : (frame + 1) * FRAME].astype(jnp.float32)
        return column_shifts(wide[piece * part : (piece + 1) * part], lane)

    def advance(step, carry):
        start = pl.multiple_of(step * group, group)
        rows = pl.ds(start, group)
        pieces = []
        for piece in range(group // part):
            inner = pl.ds(start + piece * part, part)
            taps = taps_scr[inner, :]
            if with_before:
                old = [frame_of(before_ref, rows, f, piece) for f in range(2)]
                sums = [
                    part_ref[inner, :FRAME] + taps_applied([(0, old[0]), (1, old[1])], taps, lane),
                    part_ref[inner, FRAME:] + taps_applied([(0, old[1])], taps, lane),
                ]
            else:
                now = [frame_of(tokens_ref, rows, f, piece) for f in range(2)]
                sums = [
                    now[0][1] + taps_applied([(2, now[0])], taps, lane),
                    now[1][1] + taps_applied([(1, now[0]), (2, now[1])], taps, lane),
                ]
                part_ref[inner, :FRAME] = sums[0]
                part_ref[inner, FRAME:] = sums[1]
            pieces.append(sums)
        for tile in range(tiles_dev):
            frame, spot = divmod(tile * TILE, FRAME)
            place = pl.ds(pl.multiple_of(slots_ref[tile] * TILE, TILE), TILE)
            joined = jnp.concatenate([sums[frame][:, spot : spot + TILE] for sums in pieces], axis=0)
            packed[rows, place] = joined.astype(jnp.bfloat16)
        return carry

    lax.fori_loop(0, channels // group, advance, 0, unroll=2)
    keep_ref[...] = packed[:, : tokens // 2]
    send_ref[...] = packed[:, tokens // 2 :]


def conv_call(seq_here, stripe_order, tokens, conv_taps, before=None, part=None):
    channels, count = tokens.shape
    block = 128
    wide = pl.BlockSpec((block, count), lambda i, *_: (i, 0))
    slim = pl.BlockSpec((block, count // 2), lambda i, *_: (i, 0))
    taps_spec = pl.BlockSpec((TAPS, block), lambda i, *_: (0, i))
    packed_shape = jax.ShapeDtypeStruct((channels, count // 2), jnp.bfloat16)
    with_before = before is not None
    extra_in, extra_args, out_specs, out_shape = [], [], [slim, slim], [packed_shape, packed_shape]
    if with_before:
        extra_in, extra_args = [wide, wide], [before, part]
    else:
        out_specs = [wide] + out_specs
        out_shape = [jax.ShapeDtypeStruct((channels, count), jnp.float32)] + out_shape
    return pl.pallas_call(
        functools.partial(conv_body, with_before),
        grid_spec=pltpu.PrefetchScalarGridSpec(
            num_scalar_prefetch=2,
            grid=(channels // block,),
            in_specs=[wide, taps_spec] + extra_in,
            out_specs=out_specs,
            scratch_shapes=[
                pltpu.SMEM((count // TILE,), jnp.int32),
                pltpu.VMEM((block, 128), jnp.float32),
                pltpu.VMEM((block, count), jnp.bfloat16),
            ],
        ),
        out_shape=out_shape,
        compiler_params=params(VMEM_LIMIT if with_before else VMEM_WHOLE),
        cost_estimate=pl.CostEstimate(
            flops=channels * count * TAPS, bytes_accessed=channels * count * 8, transcendentals=0
        ),
        name="conv_before" if with_before else "conv_here",
    )(seq_here, stripe_order, tokens, conv_taps, *extra_args)


def prepare_body(blocks_ref, gain_ref, qkv_ref, out_ref, qkv_out, out_out):
    qkv_out[...] = (qkv_ref[...].astype(jnp.float32) * gain_ref[...]).astype(jnp.bfloat16)
    out_out[...] = out_ref[...].T


def prepare_weights(blocks, norm_gain, qkv_weight, out_weight):
    kinds, cols, channels = qkv_weight.shape
    count = blocks.shape[0]
    width = channels // count
    return pl.pallas_call(
        prepare_body,
        grid_spec=pltpu.PrefetchScalarGridSpec(
            num_scalar_prefetch=1,
            grid=(count,),
            in_specs=[
                pl.BlockSpec((1, width), lambda j, b: (0, b[j])),
                pl.BlockSpec((kinds * cols, width), lambda j, b: (0, b[j])),
                pl.BlockSpec((cols, width), lambda j, b: (0, b[j])),
            ],
            out_specs=[
                pl.BlockSpec((kinds * cols, width), lambda j, b: (0, j)),
                pl.BlockSpec((width, cols), lambda j, b: (j, 0)),
            ],
        ),
        out_shape=[
            jax.ShapeDtypeStruct((kinds * cols, channels), jnp.bfloat16),
            jax.ShapeDtypeStruct((channels, cols), jnp.bfloat16),
        ],
        compiler_params=params(VMEM_WHOLE),
        cost_estimate=pl.CostEstimate(
            flops=kinds * cols * channels, bytes_accessed=16 * cols * channels, transcendentals=0
        ),
        name="prepare_weights",
    )(blocks, norm_gain[None, :], qkv_weight.reshape(kinds * cols, channels), out_weight)


def project_body(query_steps, ends_ref, weight_ref, own, before, after, across, far, out_ref, tokens_ref, inverse_ref):
    width = own.shape[0]
    step = pl.program_id(0)

    @pl.when(step == 0)
    def _():
        at_start, at_stop = ends_ref[0] == 1, ends_ref[1] == 1
        squares = None
        shards = (
            own[...],
            jnp.where(at_start, far[...], before[...]),
            jnp.where(at_stop, far[...], after[...]),
            across[...],
        )
        for index, shard in enumerate(shards):
            tokens_ref[index * width : (index + 1) * width, :] = shard
            wide = shard.astype(jnp.float32)
            term = jnp.sum(wide * wide, axis=0, keepdims=True)
            squares = term if squares is None else squares + term
        inverse_ref[...] = lax.rsqrt(squares / (width * len(shards)) + EPSILON)

    total = jnp.dot(weight_ref[...], tokens_ref[...], preferred_element_type=jnp.float32)
    scale = jnp.where(step < query_steps, LOG2E / math.sqrt(HEAD), 1.0)
    out_ref[...] = (total * (inverse_ref[...] * scale)).astype(jnp.bfloat16)


def project_call(ends, weights, shards):
    rows, channels = weights.shape
    width, tokens = shards[0].shape
    block = 256
    whole = pl.BlockSpec((width, tokens), lambda i, *_: (0, 0))
    return pl.pallas_call(
        functools.partial(project_body, rows // 3 // block),
        grid_spec=pltpu.PrefetchScalarGridSpec(
            num_scalar_prefetch=1,
            grid=(rows // block,),
            in_specs=[pl.BlockSpec((block, channels), lambda i, *_: (i, 0))] + [whole] * len(shards),
            out_specs=pl.BlockSpec((block, tokens), lambda i, *_: (i, 0)),
            scratch_shapes=[
                pltpu.VMEM((channels, tokens), jnp.bfloat16),
                pltpu.VMEM((1, tokens), jnp.float32),
            ],
        ),
        out_shape=jax.ShapeDtypeStruct((rows, tokens), jnp.bfloat16),
        compiler_params=params(),
        cost_estimate=pl.CostEstimate(
            flops=2 * rows * channels * tokens,
            bytes_accessed=2 * (rows * channels + channels * tokens + rows * tokens),
            transcendentals=0,
        ),
        name="project",
    )(ends, weights, *shards)


def tile_lists(order_ref, ids_ref, seq_here, tiles_dev):
    half = tiles_dev // 2
    for block in range(2):
        first = jnp.int32(0)
        second = jnp.int32(0)
        away = (jnp.int32(block) != seq_here).astype(jnp.int32)
        for spot in range(tiles_dev):
            tile = order_ref[block * tiles_dev + spot]
            late = tile // tiles_dev
            rank = jnp.where(late == 0, first, second)
            ids_ref[(2 * late + away) * half + rank] = tile
            first = first + (1 - late)
            second = second + late


def attend_body(chunk, sources, goes_on, ends, seq_ref, order_ref, mask_ref, query_ref, *refs):
    count = len(sources)
    keys, values = refs[:count], refs[count : 2 * count]
    refs = refs[2 * count :]
    if goes_on:
        old_stats, old_weighted, refs = refs[0], refs[1], refs[2:]
    if ends:
        out_ref, refs = refs[0], refs[1:]
    else:
        new_stats, new_weighted, refs = refs[0], refs[1], refs[2:]
    ids_ref, scores_ref = refs
    tokens = query_ref.shape[1]
    half = tokens // TILE

    @pl.when(pl.program_id(0) == 0)
    def _():
        tile_lists(order_ref, ids_ref, seq_ref[0], 2 * half)

    query = query_ref[...]
    lane_tile = lax.broadcasted_iota(jnp.int32, (1, tokens), 1) // TILE
    old_top = old_stats[0, 0:1, :] if goes_on else None
    top = old_top
    for index, source in enumerate(sources):
        block = jnp.dot(keys[index][...].T, query, preferred_element_type=jnp.float32)
        for spot in range(half):
            key_tile = ids_ref[source * half + spot]
            bias = jnp.zeros((1, tokens), jnp.float32)
            for query_spot in range(half):
                query_tile = ids_ref[2 * chunk * half + query_spot]
                blocked = jnp.where(mask_ref[query_tile, key_tile] == 1, 0.0, MASKED_SCORE)
                bias = jnp.where(lane_tile == query_spot, blocked, bias)
            piece = block[spot * TILE : (spot + 1) * TILE, :] + bias
            scores_ref[index * tokens + spot * TILE : index * tokens + (spot + 1) * TILE, :] = piece
            best = jnp.max(piece, axis=0, keepdims=True)
            top = best if top is None else jnp.maximum(top, best)
    denom = None
    weighted = None
    if goes_on:
        shrink = jnp.exp2(old_top - top)
        denom = old_stats[0, 1:2, :] * shrink
        weighted = old_weighted[...] * shrink
    for index in range(count):
        powers = jnp.exp2(scores_ref[index * tokens : (index + 1) * tokens, :] - top)
        summed = jnp.sum(powers, axis=0, keepdims=True)
        term = jnp.dot(
            values[index][...], powers.astype(jnp.bfloat16), preferred_element_type=jnp.float32
        )
        denom = summed if denom is None else denom + summed
        weighted = term if weighted is None else weighted + term
    if ends:
        out_ref[...] = (weighted / denom).astype(jnp.bfloat16)
    else:
        new_stats[0, 0:1, :] = top
        new_stats[0, 1:2, :] = denom
        new_weighted[...] = weighted


def attend_call(chunk, tables, query_from, sources, state=None, ends=True):
    rows, tokens = query_from.shape
    heads = rows // 3 // HEAD

    def spec(start):
        return pl.BlockSpec((HEAD, tokens), lambda h, *_, start=start: (start + h, 0))

    count = len(sources)
    stats_spec = pl.BlockSpec((1, 2, tokens), lambda h, *_: (h, 0, 0))
    state_specs = [stats_spec, spec(0)]
    state_shapes = [
        jax.ShapeDtypeStruct((heads, 2, tokens), jnp.float32),
        jax.ShapeDtypeStruct((heads * HEAD, tokens), jnp.float32),
    ]
    goes_on = state is not None
    in_specs = [spec(0)]
    in_specs += [spec(first // HEAD) for _, first, _ in sources]
    in_specs += [spec(first // HEAD + heads) for _, first, _ in sources]
    arguments = [query_from] + [array for array, _, _ in sources] * 2
    if goes_on:
        in_specs += state_specs
        arguments += list(state)
    return pl.pallas_call(
        functools.partial(attend_body, chunk, tuple(s for _, _, s in sources), goes_on, ends),
        grid_spec=pltpu.PrefetchScalarGridSpec(
            num_scalar_prefetch=3,
            grid=(heads,),
            in_specs=in_specs,
            out_specs=spec(0) if ends else state_specs,
            scratch_shapes=[
                pltpu.SMEM((4 * tokens // TILE,), jnp.int32),
                pltpu.VMEM((count * tokens, tokens), jnp.float32),
            ],
        ),
        out_shape=jax.ShapeDtypeStruct((heads * HEAD, tokens), jnp.bfloat16) if ends else state_shapes,
        compiler_params=params(),
        cost_estimate=pl.CostEstimate(
            flops=4 * heads * HEAD * tokens * tokens * count,
            bytes_accessed=2 * heads * HEAD * tokens * (2 + 2 * count),
            transcendentals=heads * tokens * tokens * count,
        ),
    )(*tables, *arguments)


def place_body(seq_ref, order_ref, ends_ref, first_ref, *refs):
    parts, out_ref, second_ref = refs[:5], refs[5], refs[6]
    _, tokens = first_ref.shape
    tiles_dev = 2 * tokens // TILE
    seq_here = seq_ref[0]
    at_end = ends_ref[0] == 1
    total = (
        parts[0][...].astype(jnp.float32)
        + parts[1][...].astype(jnp.float32)
        + parts[2][...].astype(jnp.float32)
        + parts[3][...].astype(jnp.float32)
        + jnp.where(at_end, parts[4][...].astype(jnp.float32), 0.0)
    )
    second_ref[...] = total.astype(jnp.bfloat16)
    ranks = [jnp.int32(0), jnp.int32(0)]
    for position in range(tiles_dev):
        late = order_ref[seq_here * tiles_dev + position] // tiles_dev
        spot = pl.ds(pl.multiple_of(jnp.where(late == 0, ranks[0], ranks[1]) * TILE, TILE), TILE)
        here = slice(position * TILE, (position + 1) * TILE)

        @pl.when(late == 0)
        def _(spot=spot, here=here):
            out_ref[:, here] = first_ref[:, spot]

        @pl.when(late == 1)
        def _(spot=spot, here=here):
            out_ref[:, here] = second_ref[:, spot]

        ranks[0] = ranks[0] + (1 - late)
        ranks[1] = ranks[1] + late


def place_call(seq_here, stripe_order, at_end, first, parts):
    channels, tokens = first.shape
    block = 128
    slim = pl.BlockSpec((block, tokens), lambda i, *_: (i, 0))
    return pl.pallas_call(
        place_body,
        grid_spec=pltpu.PrefetchScalarGridSpec(
            num_scalar_prefetch=3,
            grid=(channels // block,),
            in_specs=[slim] * 6,
            out_specs=pl.BlockSpec((block, 2 * tokens), lambda i, *_: (i, 0)),
            scratch_shapes=[pltpu.VMEM((block, tokens), jnp.bfloat16)],
        ),
        out_shape=jax.ShapeDtypeStruct((channels, 2 * tokens), jnp.bfloat16),
        compiler_params=params(),
        cost_estimate=pl.CostEstimate(
            flops=4 * channels * tokens, bytes_accessed=14 * channels * tokens, transcendentals=0
        ),
        name="place",
    )(seq_here, stripe_order, at_end, first, *parts)


UP = [(0, 1), (1, 2), (2, 3)]
DOWN = [(1, 0), (2, 1), (3, 2)]
ENDS = [(0, 3), (3, 0)]
FOLDED = [(0, 1), (1, 3), (3, 2), (2, 0)]
UNFOLDED = [(1, 0), (3, 1), (2, 3), (0, 2)]


def gather_blocks(block, here):
    before = lax.ppermute(block, "tp", UP)
    after = lax.ppermute(block, "tp", DOWN)
    far = lax.ppermute(block, "tp", ENDS)
    relay = jnp.where(here == 2, before, jnp.where(here == 1, after, block))
    across = lax.ppermute(relay, "tp", UNFOLDED)
    return (block, before, after, across, far)


def plus(a, b, chosen):
    summed = a.astype(jnp.float32) + jnp.where(chosen, b.astype(jnp.float32), 0.0)
    return summed.astype(jnp.bfloat16)


def reduce_blocks(weights, heads_out, here):
    width = weights.shape[0] // 4

    def partial(index):
        block = weights[index * width : (index + 1) * width]
        return jnp.dot(block, heads_out, preferred_element_type=jnp.float32).astype(jnp.bfloat16)

    sent = partial(3)
    across = lax.ppermute(sent, "tp", FOLDED)
    down, up = lax.optimization_barrier((partial(1), partial(2)))
    far = lax.ppermute(jnp.where(here == 0, down, up), "tp", ENDS)
    back = lax.ppermute(plus(down, across, here == 2), "tp", DOWN)
    onward = lax.ppermute(plus(up, across, here == 1), "tp", UP)
    return (partial(0), back, onward, far, across)


def per_device_fast(
    clip_tokens, conv_taps, norm_gain, qkv_weight, out_weight, tile_mask, stripe_order
):
    seq = lax.axis_index("seq")
    here = lax.axis_index("tp")
    seq_here = seq.astype(jnp.int32)[None]
    at_end = ((here == 0) | (here == 3)).astype(jnp.int32)[None]
    ends = jnp.stack([here == 0, here == 3]).astype(jnp.int32)
    blocks = jnp.stack([here, (here + 3) % 4, (here + 1) % 4, (here + 2) % 4]).astype(jnp.int32)
    tables = (seq_here, stripe_order, tile_mask)

    part, keep_a, send_a = conv_call(seq_here, stripe_order, clip_tokens, conv_taps)
    got_a = lax.ppermute(send_a, "seq", [(0, 1)])
    before = lax.ppermute(clip_tokens, "seq", [(0, 1)])
    weights, out_t = prepare_weights(blocks, norm_gain, qkv_weight, out_weight)

    tokens_a = jnp.where(seq == 0, keep_a, got_a)
    shards_a = gather_blocks(tokens_a, here)

    keep_b, send_b = conv_call(seq_here, stripe_order, clip_tokens, conv_taps, before, part)
    got_b = lax.ppermute(send_b, "seq", [(1, 0)])
    tokens_b = jnp.where(seq == 1, keep_b, got_b)

    cols = weights.shape[0] // 3
    swap = [(0, 1), (1, 0)]
    own_a = project_call(ends, weights, shards_a)
    peer_a = lax.ppermute(own_a[cols:], "seq", swap)
    shards_b = gather_blocks(tokens_b, here)
    out_a = attend_call(0, tables, own_a, [(own_a, cols, 0), (peer_a, 0, 1)])
    parts_a = reduce_blocks(out_t, out_a, here)
    own_b = project_call(ends, weights, shards_b)
    peer_b = lax.ppermute(own_b[cols:], "seq", swap)
    near = [(own_a, cols, 0), (peer_a, 0, 1), (own_b, cols, 2)]
    state = attend_call(1, tables, own_b, near, ends=False)
    out_b = attend_call(1, tables, own_b, [(peer_b, 0, 3)], state=state)
    parts_b = reduce_blocks(out_t, out_b, here)
    first = sum(part.astype(jnp.float32) for part in parts_a[:4])
    first = first + jnp.where(at_end == 1, parts_a[4].astype(jnp.float32), 0.0)
    return place_call(seq_here, stripe_order, at_end, first.astype(jnp.bfloat16), parts_b)


def passed_along(block, axis, distance):
    devices = range(lax.axis_size(axis))
    route = [(i - distance, i) for i in devices if i - distance in devices]
    return lax.ppermute(block, axis, route)


def from_partner(block, axis, apart):
    count = lax.axis_size(axis)
    route = []
    for low in range(count):
        high = low | 1 << apart
        if high != low and high < count:
            route += [(low, high), (high, low)]
    return lax.ppermute(block, axis, route)


def causal_conv(local_tokens, before, conv_taps):
    channels = local_tokens.shape[0]
    frames = local_tokens.shape[1] // (FH * FW)
    stacked = (
        jnp.concatenate([before, local_tokens], axis=1)
        .astype(jnp.float32)
        .reshape(channels, frames + 2, FH, FW)
    )
    padded = jnp.pad(stacked, ((0, 0), (0, 0), (1, 1), (1, 1)))
    summed = jnp.zeros((channels, frames, FH, FW), jnp.float32)
    for time_off in range(3):
        for row_off in range(3):
            for col_off in range(3):
                tap_vec = conv_taps[time_off * 9 + row_off * 3 + col_off]
                summed = (
                    summed
                    + tap_vec[:, None, None, None]
                    * padded[
                        :,
                        time_off : time_off + frames,
                        row_off : row_off + FH,
                        col_off : col_off + FW,
                    ]
                )
    return (local_tokens.astype(jnp.float32) + summed.reshape(channels, -1)).astype(jnp.bfloat16)


def stripe_tables(stripe_order, tiles_dev):
    seq_count = lax.axis_size("seq")
    seq_here = lax.axis_index("seq")
    per_source = tiles_dev // seq_count
    blocks = stripe_order.reshape(seq_count, tiles_dev)
    owners = blocks // tiles_dev
    is_mine = (owners == seq_here).astype(jnp.int32)
    rank_of = jnp.cumsum(is_mine, axis=1) - 1
    slot_ids = jnp.arange(per_source, dtype=jnp.int32)
    picked = is_mine[:, None, :] * (rank_of[:, None, :] == slot_ids[None, :, None]).astype(
        jnp.int32
    )
    local_tiles = (blocks - seq_here * tiles_dev)[:, None, :]
    send_order = jnp.sum(picked * local_tiles, axis=2).reshape(-1)
    own_row = lax.dynamic_slice_in_dim(stripe_order, seq_here * tiles_dev, tiles_dev)
    sources = own_row // tiles_dev
    position = jnp.arange(tiles_dev, dtype=jnp.int32)
    earlier = (sources[:, None] == sources[None, :]) & (position[None, :] < position[:, None])
    place_order = sources * per_source + jnp.sum(earlier.astype(jnp.int32), axis=1)
    return (send_order, place_order, own_row)


def regroup(values, send_order, place_order):
    leading = values.shape[0]
    trailing = values.shape[2:]
    in_tiles = values.reshape((leading, values.shape[1] // TILE, TILE) + trailing)
    outgoing = jnp.take(in_tiles, send_order, axis=1)
    arrived = lax.all_to_all(outgoing, "seq", split_axis=1, concat_axis=1, tiled=True)
    placed = jnp.take(arrived, place_order, axis=1)
    return placed.reshape(values.shape)


def project(mixed, norm_gain, qkv_weight):
    channels = norm_gain.shape[0]
    widened = lax.all_gather(mixed, "tp", axis=0, tiled=True).astype(jnp.float32)
    scaled = (widened * norm_gain[:, None]).astype(jnp.bfloat16)
    projected = jnp.einsum("ct,khc->kth", scaled, qkv_weight, preferred_element_type=jnp.float32)
    squares = jnp.sum(widened * widened, axis=0)
    projected, squares = (projected, squares)
    inverse = lax.rsqrt(squares / channels + EPSILON)
    return (projected * inverse[None, :, None]).astype(jnp.bfloat16)


def position_mask(tile_mask, stripe_order, own_half):
    tiles_all = tile_mask.shape[0]
    tile_ids = jnp.arange(tiles_all, dtype=jnp.int32)
    own_onehot = (own_half[:, None] == tile_ids[None, :]).astype(jnp.float32)
    order_onehot = (stripe_order[:, None] == tile_ids[None, :]).astype(jnp.float32)
    rows_mask = jnp.dot(
        own_onehot, tile_mask.astype(jnp.float32), preferred_element_type=jnp.float32
    )
    return jnp.dot(rows_mask, order_onehot.T, preferred_element_type=jnp.float32)


def attend(queries_flat, key_values, pos_mask):
    row_count = queries_flat.shape[0]
    heads_dev = queries_flat.shape[1] // HEAD
    queries = queries_flat.reshape(row_count, heads_dev, HEAD)
    score_scale = 1.0 / math.sqrt(HEAD)
    tiles_dev = row_count // TILE
    tile_ids = jnp.arange(pos_mask.shape[1], dtype=jnp.int32)
    initial = (
        jnp.full((heads_dev, row_count), MASKED_SCORE, jnp.float32),
        jnp.zeros((heads_dev, row_count), jnp.float32),
        jnp.zeros((heads_dev, row_count, HEAD), jnp.float32),
    )
    fetched = lax.all_gather(key_values, "seq", axis=1, tiled=True)
    fetched_count = fetched.shape[1]
    key_block = 512

    def advance(block_index, state_now):
        top_score, denom, weighted = state_now
        offset = block_index * key_block
        key_rows = lax.dynamic_slice_in_dim(fetched[0], offset, key_block).reshape(
            key_block, heads_dev, HEAD
        )
        values = lax.dynamic_slice_in_dim(fetched[1], offset, key_block).reshape(
            key_block, heads_dev, HEAD
        )
        tile_pos = (offset + jnp.arange(key_block, dtype=jnp.int32)) // TILE
        onehot = (tile_pos[:, None] == tile_ids[None, :]).astype(jnp.float32)
        tile_allowed = (
            jnp.einsum("qn,kn->qk", pos_mask, onehot, preferred_element_type=jnp.float32) > 0.5
        )
        visible = jnp.broadcast_to(tile_allowed[:, None, :], (tiles_dev, TILE, key_block)).reshape(
            row_count, key_block
        )
        scores = (
            jnp.einsum("qhd,khd->hqk", queries, key_rows, preferred_element_type=jnp.float32)
            * score_scale
        )
        masked = jnp.where(visible[None], scores, MASKED_SCORE)
        new_top = jnp.maximum(top_score, jnp.max(masked, axis=2))
        powers = jnp.where(visible[None], jnp.exp(masked - new_top[:, :, None]), 0.0)
        shrink = jnp.exp(top_score - new_top)
        denom = denom * shrink + jnp.sum(powers, axis=2)
        weighted = weighted * shrink[:, :, None] + jnp.einsum(
            "hqk,khd->hqd", powers.astype(jnp.bfloat16), values, preferred_element_type=jnp.float32
        )
        return (new_top, denom, weighted)

    _, denom, weighted = lax.fori_loop(0, fetched_count // key_block, advance, initial)
    finished = (weighted / denom[:, :, None]).astype(jnp.bfloat16)
    return jnp.transpose(finished, (1, 0, 2)).reshape(row_count, heads_dev * HEAD)


def per_device_general(clip_tokens, conv_taps, norm_gain, qkv_weight, out_weight, tile_mask, stripe_order):
    tiles_dev = clip_tokens.shape[1] // TILE
    send_order, place_order, own_row = stripe_tables(stripe_order, tiles_dev)
    before = passed_along(clip_tokens, "seq", 1)
    mixed = causal_conv(clip_tokens, before, conv_taps)
    mixed = regroup(mixed, send_order, place_order)
    projected = project(mixed, norm_gain, qkv_weight)
    row_count = projected.shape[1]
    group_cols = projected.shape[2]
    half_rows = row_count // 2
    side = lax.axis_index("tp") % 2
    mine_first = side == 0
    query_send = lax.dynamic_slice_in_dim(projected[0], (1 - side) * half_rows, half_rows, axis=0)
    query_mine = lax.dynamic_slice_in_dim(projected[0], side * half_rows, half_rows, axis=0)
    kv_mine = projected[1:]
    query_other, kv_other = from_partner((query_send, kv_mine), "tp", 0)
    queries = jnp.where(
        mine_first,
        jnp.concatenate([query_mine, query_other], axis=1),
        jnp.concatenate([query_other, query_mine], axis=1),
    )
    key_values = jnp.where(
        mine_first,
        jnp.concatenate([kv_mine, kv_other], axis=2),
        jnp.concatenate([kv_other, kv_mine], axis=2),
    )
    own_half = lax.dynamic_slice_in_dim(own_row, side * (tiles_dev // 2), tiles_dev // 2)
    pos_mask = position_mask(tile_mask, stripe_order, own_half)
    pair_out = attend(queries, key_values, pos_mask)
    give_cols = lax.dynamic_slice_in_dim(pair_out, (1 - side) * group_cols, group_cols, axis=1)
    keep_cols = lax.dynamic_slice_in_dim(pair_out, side * group_cols, group_cols, axis=1)
    got_cols = from_partner(give_cols, "tp", 0)
    heads_out = jnp.where(
        mine_first,
        jnp.concatenate([keep_cols, got_cols], axis=0),
        jnp.concatenate([got_cols, keep_cols], axis=0),
    )
    return lax.psum_scatter(
        jnp.einsum("qg,gc->cq", heads_out, out_weight, preferred_element_type=jnp.float32).astype(
            jnp.bfloat16
        ),
        "tp",
        scatter_dimension=0,
        tiled=True,
    )


def solution(mesh):
    in_specs = (
        P("tp", ("dp", "seq")),
        P(None, "tp"),
        P(),
        P(None, "tp", None),
        P("tp", None),
        P(),
        P(),
    )
    out_specs = P("tp", ("dp", "seq"))

    def run(clip_tokens, conv_taps, norm_gain, qkv_weight, out_weight, tile_mask, stripe_order):
        arguments = (clip_tokens, conv_taps, norm_gain, qkv_weight, out_weight, tile_mask, stripe_order)
        tokens = clip_tokens.shape[1] // (mesh.shape["dp"] * mesh.shape["seq"])
        columns = qkv_weight.shape[1] // mesh.shape["tp"]
        two_halves = mesh.shape["seq"] == 2 and tokens == 2 * FRAME
        fast = two_halves and mesh.shape["tp"] == 4 and columns % HEAD == 0

        def per_device(*local):
            if not fast:
                return per_device_general(*local)
            return per_device_fast(*local)

        step = jax.shard_map(
            per_device, mesh=mesh, in_specs=in_specs, out_specs=out_specs, check_vma=False
        )
        return step(*arguments)

    return run
```

```python
import functools
import math

import jax
import jax.numpy as jnp
from jax import lax
from jax.experimental import pallas as pl
from jax.experimental.pallas import tpu as pltpu
from jax.sharding import PartitionSpec as P


HEAD = 128
TILE = 128
FH = 16
FW = 32
FRAME = FH * FW
TAPS = 27


EPSILON = 1e-06
MASKED_SCORE = -1e30
LOG2E = math.log2(math.e)

VMEM_LIMIT = 20 * 1024 * 1024
VMEM_MOST = 57 * 1024 * 1024
VMEM_WHOLE = 60 * 1024 * 1024


def params(limit=VMEM_LIMIT):
    return pltpu.CompilerParams(vmem_limit_bytes=limit)


def column_shifts(frame, lane):
    column = lane % FW
    left = jnp.where(column > 0, pltpu.roll(frame, 1, 1), 0.0)
    right = jnp.where(column < FW - 1, pltpu.roll(frame, FRAME - 1, 1), 0.0)
    return (left, frame, right)


def row_sum(rows, lane):
    above = jnp.where(lane >= FW, pltpu.roll(rows[0], FW, 1), 0.0)
    below = jnp.where(lane < FRAME - FW, pltpu.roll(rows[2], FRAME - FW, 1), 0.0)
    return rows[1] + above + below


def spread(taps, tap):
    column = jnp.broadcast_to(taps[:, tap : tap + 1], (taps.shape[0], 128))
    return jnp.concatenate([column] * (FRAME // 128), axis=1)


def taps_applied(pairs, taps, lane):
    rows = []
    for row_off in range(3):
        total = None
        for time_off, shifts in pairs:
            for col_off in range(3):
                tap = time_off * 9 + row_off * 3 + col_off
                term = spread(taps, tap) * shifts[col_off]
                total = term if total is None else total + term
        rows.append(total)
    return row_sum(rows, lane)


def pack_slots(order_ref, slots_ref, seq_here, tiles_dev, positions):
    half = tiles_dev // 2
    kept = jnp.int32(0)
    sent = jnp.int32(half)
    for position in range(positions):
        tile = order_ref[position]
        mine = tile // tiles_dev == seq_here
        stays = jnp.int32(position // tiles_dev) == seq_here
        slot = jnp.where(stays, kept, sent)

        @pl.when(mine)
        def _(tile=tile, slot=slot):
            slots_ref[tile - seq_here * tiles_dev] = slot

        step = mine.astype(jnp.int32)
        kept = kept + jnp.where(stays, step, 0)
        sent = sent + jnp.where(stays, 0, step)


def conv_body(with_before, seq_ref, order_ref, *refs):
    if with_before:
        tokens_ref, taps_ref, before_ref, part_ref, keep_ref, send_ref, slots_ref, taps_scr, packed = refs
    else:
        tokens_ref, taps_ref, part_ref, keep_ref, send_ref, slots_ref, taps_scr, packed = refs
    channels, tokens = tokens_ref.shape
    tiles_dev = tokens // TILE
    seq_here = seq_ref[0]

    @pl.when(pl.program_id(0) == 0)
    def _():
        pack_slots(order_ref, slots_ref, seq_here, tiles_dev, order_ref.shape[0])

    taps_scr[:, :TAPS] = taps_ref[...].T
    group = 16
    part = 16
    lane = lax.broadcasted_iota(jnp.int32, (part, FRAME), 1)

    def frame_of(ref, rows, frame, piece):
        wide = ref[rows, frame * FRAME : (frame + 1) * FRAME].astype(jnp.float32)
        return column_shifts(wide[piece * part : (piece + 1) * part], lane)

    def advance(step, carry):
        start = pl.multiple_of(step * group, group)
        rows = pl.ds(start, group)
        pieces = []
        for piece in range(group // part):
            inner = pl.ds(start + piece * part, part)
            taps = taps_scr[inner, :]
            if with_before:
                old = [frame_of(before_ref, rows, f, piece) for f in range(2)]
                sums = [
                    part_ref[inner, :FRAME] + taps_applied([(0, old[0]), (1, old[1])], taps, lane),
                    part_ref[inner, FRAME:] + taps_applied([(0, old[1])], taps, lane),
                ]
            else:
                now = [frame_of(tokens_ref, rows, f, piece) for f in range(2)]
                sums = [
                    now[0][1] + taps_applied([(2, now[0])], taps, lane),
                    now[1][1] + taps_applied([(1, now[0]), (2, now[1])], taps, lane),
                ]
                part_ref[inner, :FRAME] = sums[0]
                part_ref[inner, FRAME:] = sums[1]
            pieces.append(sums)
        for tile in range(tiles_dev):
            frame, spot = divmod(tile * TILE, FRAME)
            place = pl.ds(pl.multiple_of(slots_ref[tile] * TILE, TILE), TILE)
            joined = jnp.concatenate([sums[frame][:, spot : spot + TILE] for sums in pieces], axis=0)
            packed[rows, place] = joined.astype(jnp.bfloat16)
        return carry

    lax.fori_loop(0, channels // group, advance, 0)
    keep_ref[...] = packed[:, : tokens // 2]
    send_ref[...] = packed[:, tokens // 2 :]


def conv_call(seq_here, stripe_order, tokens, conv_taps, before=None, part=None):
    channels, count = tokens.shape
    block = 128
    wide = pl.BlockSpec((block, count), lambda i, *_: (i, 0))
    slim = pl.BlockSpec((block, count // 2), lambda i, *_: (i, 0))
    taps_spec = pl.BlockSpec((TAPS, block), lambda i, *_: (0, i))
    packed_shape = jax.ShapeDtypeStruct((channels, count // 2), jnp.bfloat16)
    with_before = before is not None
    extra_in, extra_args, out_specs, out_shape = [], [], [slim, slim], [packed_shape, packed_shape]
    if with_before:
        extra_in, extra_args = [wide, wide], [before, part]
    else:
        out_specs = [wide] + out_specs
        out_shape = [jax.ShapeDtypeStruct((channels, count), jnp.float32)] + out_shape
    return pl.pallas_call(
        functools.partial(conv_body, with_before),
        grid_spec=pltpu.PrefetchScalarGridSpec(
            num_scalar_prefetch=2,
            grid=(channels // block,),
            in_specs=[wide, taps_spec] + extra_in,
            out_specs=out_specs,
            scratch_shapes=[
                pltpu.SMEM((count // TILE,), jnp.int32),
                pltpu.VMEM((block, 128), jnp.float32),
                pltpu.VMEM((block, count), jnp.bfloat16),
            ],
        ),
        out_shape=out_shape,
        compiler_params=params(VMEM_LIMIT if with_before else VMEM_WHOLE),
        cost_estimate=pl.CostEstimate(
            flops=channels * count * TAPS, bytes_accessed=channels * count * 8, transcendentals=0
        ),
        name="conv",
    )(seq_here, stripe_order, tokens, conv_taps, *extra_args)


def prepare_body(blocks_ref, gain_ref, qkv_ref, out_ref, qkv_out, out_out):
    qkv_out[...] = (qkv_ref[...].astype(jnp.float32) * gain_ref[...]).astype(jnp.bfloat16)
    out_out[...] = out_ref[...].T


def prepare_weights(blocks, norm_gain, qkv_weight, out_weight):
    kinds, cols, channels = qkv_weight.shape
    count = blocks.shape[0]
    width = channels // count
    return pl.pallas_call(
        prepare_body,
        grid_spec=pltpu.PrefetchScalarGridSpec(
            num_scalar_prefetch=1,
            grid=(count,),
            in_specs=[
                pl.BlockSpec((1, width), lambda j, b: (0, b[j])),
                pl.BlockSpec((kinds * cols, width), lambda j, b: (0, b[j])),
                pl.BlockSpec((cols, width), lambda j, b: (0, b[j])),
            ],
            out_specs=[
                pl.BlockSpec((kinds * cols, width), lambda j, b: (0, j)),
                pl.BlockSpec((width, cols), lambda j, b: (j, 0)),
            ],
        ),
        out_shape=[
            jax.ShapeDtypeStruct((kinds * cols, channels), jnp.bfloat16),
            jax.ShapeDtypeStruct((channels, cols), jnp.bfloat16),
        ],
        compiler_params=params(VMEM_WHOLE),
        cost_estimate=pl.CostEstimate(
            flops=kinds * cols * channels, bytes_accessed=16 * cols * channels, transcendentals=0
        ),
        name="prepare",
    )(blocks, norm_gain[None, :], qkv_weight.reshape(kinds * cols, channels), out_weight)


def project_body(query_steps, weight_ref, own, before, after, across, query_ref, pair_ref, tokens_ref, inverse_ref):
    width = own.shape[0]
    step = pl.program_id(0)

    @pl.when(step == 0)
    def _():
        squares = None
        for index, shard in enumerate((own, before, after, across)):
            block = shard[...]
            tokens_ref[index * width : (index + 1) * width, :] = block
            wide = block.astype(jnp.float32)
            term = jnp.sum(wide * wide, axis=0, keepdims=True)
            squares = term if squares is None else squares + term
        inverse_ref[...] = lax.rsqrt(squares / (4 * width) + EPSILON)

    total = jnp.dot(weight_ref[...], tokens_ref[...], preferred_element_type=jnp.float32)

    @pl.when(step < query_steps)
    def _():
        query_ref[...] = (total * (inverse_ref[...] * (LOG2E / math.sqrt(HEAD)))).astype(jnp.bfloat16)

    @pl.when(step >= query_steps)
    def _():
        pair_ref[...] = (total * inverse_ref[...]).astype(jnp.bfloat16)


def project_call(weights, shards):
    rows, channels = weights.shape
    width, tokens = shards[0].shape
    cols = rows // 3
    block = 256
    query_steps = cols // block
    whole = pl.BlockSpec((width, tokens), lambda i: (0, 0))
    return pl.pallas_call(
        functools.partial(project_body, query_steps),
        grid=(rows // block,),
        in_specs=[pl.BlockSpec((block, channels), lambda i: (i, 0))] + [whole] * len(shards),
        out_specs=[
            pl.BlockSpec((block, tokens), lambda i: (jnp.minimum(i, query_steps - 1), 0)),
            pl.BlockSpec((block, tokens), lambda i: (jnp.maximum(i - query_steps, 0), 0)),
        ],
        scratch_shapes=[
            pltpu.VMEM((channels, tokens), jnp.bfloat16),
            pltpu.VMEM((1, tokens), jnp.float32),
        ],
        out_shape=[
            jax.ShapeDtypeStruct((cols, tokens), jnp.bfloat16),
            jax.ShapeDtypeStruct((2 * cols, tokens), jnp.bfloat16),
        ],
        compiler_params=params(VMEM_MOST),
        cost_estimate=pl.CostEstimate(
            flops=2 * rows * channels * tokens,
            bytes_accessed=2 * (rows * channels + channels * tokens + rows * tokens),
            transcendentals=0,
        ),
        name="project",
    )(weights, *shards)


def tile_lists(order_ref, ids_ref, seq_here, tiles_dev):
    half = tiles_dev // 2
    for block in range(2):
        first = jnp.int32(0)
        second = jnp.int32(0)
        away = (jnp.int32(block) != seq_here).astype(jnp.int32)
        for spot in range(tiles_dev):
            tile = order_ref[block * tiles_dev + spot]
            late = tile // tiles_dev
            rank = jnp.where(late == 0, first, second)
            ids_ref[(2 * late + away) * half + rank] = tile
            first = first + (1 - late)
            second = second + late


def attend_body(chunk, sources, goes_on, ends, seq_ref, order_ref, mask_ref, query_ref, *refs):
    count = len(sources)
    keys, values = refs[:count], refs[count : 2 * count]
    refs = refs[2 * count :]
    if goes_on:
        old_stats, old_weighted, refs = refs[0], refs[1], refs[2:]
    if ends:
        out_ref, refs = refs[0], refs[1:]
    else:
        new_stats, new_weighted, refs = refs[0], refs[1], refs[2:]
    ids_ref, scores_ref = refs
    tokens = query_ref.shape[1]
    half = tokens // TILE

    @pl.when(pl.program_id(0) == 0)
    def _():
        tile_lists(order_ref, ids_ref, seq_ref[0], 2 * half)

    query = query_ref[...]
    lane_tile = lax.broadcasted_iota(jnp.int32, (1, tokens), 1) // TILE
    old_top = old_stats[0, 0:1, :] if goes_on else None
    top = old_top
    for index, source in enumerate(sources):
        block = jnp.dot(keys[index][...].T, query, preferred_element_type=jnp.float32)
        for spot in range(half):
            key_tile = ids_ref[source * half + spot]
            bias = jnp.zeros((1, tokens), jnp.float32)
            for query_spot in range(half):
                query_tile = ids_ref[2 * chunk * half + query_spot]
                blocked = jnp.where(mask_ref[query_tile, key_tile] == 1, 0.0, MASKED_SCORE)
                bias = jnp.where(lane_tile == query_spot, blocked, bias)
            piece = block[spot * TILE : (spot + 1) * TILE, :] + bias
            scores_ref[index * tokens + spot * TILE : index * tokens + (spot + 1) * TILE, :] = piece
            best = jnp.max(piece, axis=0, keepdims=True)
            top = best if top is None else jnp.maximum(top, best)
    denom = None
    weighted = None
    if goes_on:
        shrink = jnp.exp2(old_top - top)
        denom = old_stats[0, 1:2, :] * shrink
        weighted = old_weighted[...] * shrink
    for index in range(count):
        powers = jnp.exp2(scores_ref[index * tokens : (index + 1) * tokens, :] - top)
        summed = jnp.sum(powers, axis=0, keepdims=True)
        term = jnp.dot(
            values[index][...], powers.astype(jnp.bfloat16), preferred_element_type=jnp.float32
        )
        denom = summed if denom is None else denom + summed
        weighted = term if weighted is None else weighted + term
    if ends:
        out_ref[...] = (weighted / denom).astype(jnp.bfloat16)
    else:
        new_stats[0, 0:1, :] = top
        new_stats[0, 1:2, :] = denom
        new_weighted[...] = weighted


def attend_call(chunk, tables, queries, sources, state=None, ends=True):
    rows, tokens = queries.shape
    heads = rows // HEAD

    def spec(start):
        return pl.BlockSpec((HEAD, tokens), lambda h, *_, start=start: (start + h, 0))

    count = len(sources)
    stats_spec = pl.BlockSpec((1, 2, tokens), lambda h, *_: (h, 0, 0))
    state_specs = [stats_spec, spec(0)]
    state_shapes = [
        jax.ShapeDtypeStruct((heads, 2, tokens), jnp.float32),
        jax.ShapeDtypeStruct((rows, tokens), jnp.float32),
    ]
    goes_on = state is not None
    in_specs = [spec(0)] + [spec(0)] * count + [spec(heads)] * count
    arguments = [queries] + [array for array, _ in sources] * 2
    if goes_on:
        in_specs += state_specs
        arguments += list(state)
    return pl.pallas_call(
        functools.partial(attend_body, chunk, tuple(s for _, s in sources), goes_on, ends),
        grid_spec=pltpu.PrefetchScalarGridSpec(
            num_scalar_prefetch=3,
            grid=(heads,),
            in_specs=in_specs,
            out_specs=spec(0) if ends else state_specs,
            scratch_shapes=[
                pltpu.SMEM((4 * tokens // TILE,), jnp.int32),
                pltpu.VMEM((count * tokens, tokens), jnp.float32),
            ],
        ),
        out_shape=jax.ShapeDtypeStruct((rows, tokens), jnp.bfloat16) if ends else state_shapes,
        compiler_params=params(),
        cost_estimate=pl.CostEstimate(
            flops=4 * rows * tokens * tokens * count,
            bytes_accessed=2 * rows * tokens * (2 + 2 * count),
            transcendentals=heads * tokens * tokens * count,
        ),
        name="attend",
    )(*tables, *arguments)


def place_body(seq_ref, order_ref, ends_ref, first_ref, *refs):
    parts, out_ref, second_ref = refs[:4], refs[4], refs[5]
    _, tokens = first_ref.shape
    tiles_dev = 2 * tokens // TILE
    seq_here = seq_ref[0]
    at_end = ends_ref[0] == 1
    total = (
        parts[0][...].astype(jnp.float32)
        + parts[1][...].astype(jnp.float32)
        + parts[2][...].astype(jnp.float32)
        + jnp.where(at_end, parts[3][...].astype(jnp.float32), 0.0)
    )
    second_ref[...] = total.astype(jnp.bfloat16)
    ranks = [jnp.int32(0), jnp.int32(0)]
    for position in range(tiles_dev):
        late = order_ref[seq_here * tiles_dev + position] // tiles_dev
        spot = pl.ds(pl.multiple_of(jnp.where(late == 0, ranks[0], ranks[1]) * TILE, TILE), TILE)
        here = slice(position * TILE, (position + 1) * TILE)

        @pl.when(late == 0)
        def _(spot=spot, here=here):
            out_ref[:, here] = first_ref[:, spot]

        @pl.when(late == 1)
        def _(spot=spot, here=here):
            out_ref[:, here] = second_ref[:, spot]

        ranks[0] = ranks[0] + (1 - late)
        ranks[1] = ranks[1] + late


def place_call(seq_here, stripe_order, at_end, first, parts):
    channels, tokens = first.shape
    block = 128
    slim = pl.BlockSpec((block, tokens), lambda i, *_: (i, 0))
    return pl.pallas_call(
        place_body,
        grid_spec=pltpu.PrefetchScalarGridSpec(
            num_scalar_prefetch=3,
            grid=(channels // block,),
            in_specs=[slim] * 5,
            out_specs=pl.BlockSpec((block, 2 * tokens), lambda i, *_: (i, 0)),
            scratch_shapes=[pltpu.VMEM((block, tokens), jnp.bfloat16)],
        ),
        out_shape=jax.ShapeDtypeStruct((channels, 2 * tokens), jnp.bfloat16),
        compiler_params=params(),
        cost_estimate=pl.CostEstimate(
            flops=4 * channels * tokens, bytes_accessed=14 * channels * tokens, transcendentals=0
        ),
        name="place",
    )(seq_here, stripe_order, at_end, first, *parts)


FORWARD = [(0, 1), (1, 2), (2, 3), (3, 0)]
BACKWARD = [(1, 0), (2, 1), (3, 2), (0, 3)]
FOLDED = [(0, 1), (1, 3), (3, 2), (2, 0)]
UNFOLDED = [(1, 0), (3, 1), (2, 3), (0, 2)]


def gather_blocks(block, here):
    before = lax.ppermute(block, "tp", FORWARD)
    after = lax.ppermute(block, "tp", BACKWARD)
    relay = jnp.where(here == 2, before, jnp.where(here == 1, after, block))
    across = lax.ppermute(relay, "tp", UNFOLDED)
    return (block, before, after, across)


def plus(a, b, chosen):
    summed = a.astype(jnp.float32) + jnp.where(chosen, b.astype(jnp.float32), 0.0)
    return summed.astype(jnp.bfloat16)


def reduce_blocks(weights, heads_out, here):
    width = weights.shape[0] // 4

    def partial(index):
        block = weights[index * width : (index + 1) * width]
        return jnp.dot(block, heads_out, preferred_element_type=jnp.float32).astype(jnp.bfloat16)

    sent = partial(3)
    across = lax.ppermute(sent, "tp", FOLDED)
    down, up = lax.optimization_barrier((partial(1), partial(2)))
    back = lax.ppermute(plus(down, across, here == 2), "tp", BACKWARD)
    onward = lax.ppermute(plus(up, across, here == 1), "tp", FORWARD)
    return (partial(0), back, onward, across)


def per_device_fast(
    clip_tokens, conv_taps, norm_gain, qkv_weight, out_weight, tile_mask, stripe_order
):
    seq = lax.axis_index("seq")
    here = lax.axis_index("tp")
    seq_here = seq.astype(jnp.int32)[None]
    at_end = ((here == 0) | (here == 3)).astype(jnp.int32)[None]
    blocks = jnp.stack([here, (here + 3) % 4, (here + 1) % 4, (here + 2) % 4]).astype(jnp.int32)
    tables = (seq_here, stripe_order, tile_mask)

    part, keep_a, send_a = conv_call(seq_here, stripe_order, clip_tokens, conv_taps)
    got_a = lax.ppermute(send_a, "seq", [(0, 1)])
    before = lax.ppermute(clip_tokens, "seq", [(0, 1)])
    weights, out_t = prepare_weights(blocks, norm_gain, qkv_weight, out_weight)

    tokens_a = jnp.where(seq == 0, keep_a, got_a)
    shards_a = gather_blocks(tokens_a, here)

    keep_b, send_b = conv_call(seq_here, stripe_order, clip_tokens, conv_taps, before, part)
    got_b = lax.ppermute(send_b, "seq", [(1, 0)])
    tokens_b = jnp.where(seq == 1, keep_b, got_b)

    swap = [(0, 1), (1, 0)]
    query_a, pair_a = project_call(weights, shards_a)
    peer_a = lax.ppermute(pair_a, "seq", swap)
    shards_b = gather_blocks(tokens_b, here)
    out_a = attend_call(0, tables, query_a, [(pair_a, 0), (peer_a, 1)])
    parts_a = reduce_blocks(out_t, out_a, here)
    query_b, pair_b = project_call(weights, shards_b)
    peer_b = lax.ppermute(pair_b, "seq", swap)
    near = [(pair_a, 0), (peer_a, 1), (pair_b, 2)]
    state = attend_call(1, tables, query_b, near, ends=False)
    out_b = attend_call(1, tables, query_b, [(peer_b, 3)], state=state)
    parts_b = reduce_blocks(out_t, out_b, here)
    first = sum(part.astype(jnp.float32) for part in parts_a[:3])
    first = first + jnp.where(at_end == 1, parts_a[3].astype(jnp.float32), 0.0)
    return place_call(seq_here, stripe_order, at_end, first.astype(jnp.bfloat16), parts_b)


def passed_along(block, axis, distance):
    devices = range(lax.axis_size(axis))
    route = [(i - distance, i) for i in devices if i - distance in devices]
    return lax.ppermute(block, axis, route)


def from_partner(block, axis, apart):
    count = lax.axis_size(axis)
    route = []
    for low in range(count):
        high = low | 1 << apart
        if high != low and high < count:
            route += [(low, high), (high, low)]
    return lax.ppermute(block, axis, route)


def causal_conv(local_tokens, before, conv_taps):
    channels = local_tokens.shape[0]
    frames = local_tokens.shape[1] // (FH * FW)
    stacked = (
        jnp.concatenate([before, local_tokens], axis=1)
        .astype(jnp.float32)
        .reshape(channels, frames + 2, FH, FW)
    )
    padded = jnp.pad(stacked, ((0, 0), (0, 0), (1, 1), (1, 1)))
    summed = jnp.zeros((channels, frames, FH, FW), jnp.float32)
    for time_off in range(3):
        for row_off in range(3):
            for col_off in range(3):
                tap_vec = conv_taps[time_off * 9 + row_off * 3 + col_off]
                summed = (
                    summed
                    + tap_vec[:, None, None, None]
                    * padded[
                        :,
                        time_off : time_off + frames,
                        row_off : row_off + FH,
                        col_off : col_off + FW,
                    ]
                )
    return (local_tokens.astype(jnp.float32) + summed.reshape(channels, -1)).astype(jnp.bfloat16)


def stripe_tables(stripe_order, tiles_dev):
    seq_count = lax.axis_size("seq")
    seq_here = lax.axis_index("seq")
    per_source = tiles_dev // seq_count
    blocks = stripe_order.reshape(seq_count, tiles_dev)
    owners = blocks // tiles_dev
    is_mine = (owners == seq_here).astype(jnp.int32)
    rank_of = jnp.cumsum(is_mine, axis=1) - 1
    slot_ids = jnp.arange(per_source, dtype=jnp.int32)
    picked = is_mine[:, None, :] * (rank_of[:, None, :] == slot_ids[None, :, None]).astype(
        jnp.int32
    )
    local_tiles = (blocks - seq_here * tiles_dev)[:, None, :]
    send_order = jnp.sum(picked * local_tiles, axis=2).reshape(-1)
    own_row = lax.dynamic_slice_in_dim(stripe_order, seq_here * tiles_dev, tiles_dev)
    sources = own_row // tiles_dev
    position = jnp.arange(tiles_dev, dtype=jnp.int32)
    earlier = (sources[:, None] == sources[None, :]) & (position[None, :] < position[:, None])
    place_order = sources * per_source + jnp.sum(earlier.astype(jnp.int32), axis=1)
    return (send_order, place_order, own_row)


def regroup(values, send_order, place_order):
    leading = values.shape[0]
    trailing = values.shape[2:]
    in_tiles = values.reshape((leading, values.shape[1] // TILE, TILE) + trailing)
    outgoing = jnp.take(in_tiles, send_order, axis=1)
    arrived = lax.all_to_all(outgoing, "seq", split_axis=1, concat_axis=1, tiled=True)
    placed = jnp.take(arrived, place_order, axis=1)
    return placed.reshape(values.shape)


def project(mixed, norm_gain, qkv_weight):
    channels = norm_gain.shape[0]
    widened = lax.all_gather(mixed, "tp", axis=0, tiled=True).astype(jnp.float32)
    scaled = (widened * norm_gain[:, None]).astype(jnp.bfloat16)
    projected = jnp.einsum("ct,khc->kth", scaled, qkv_weight, preferred_element_type=jnp.float32)
    squares = jnp.sum(widened * widened, axis=0)
    projected, squares = (projected, squares)
    inverse = lax.rsqrt(squares / channels + EPSILON)
    return (projected * inverse[None, :, None]).astype(jnp.bfloat16)


def position_mask(tile_mask, stripe_order, own_half):
    tiles_all = tile_mask.shape[0]
    tile_ids = jnp.arange(tiles_all, dtype=jnp.int32)
    own_onehot = (own_half[:, None] == tile_ids[None, :]).astype(jnp.float32)
    order_onehot = (stripe_order[:, None] == tile_ids[None, :]).astype(jnp.float32)
    rows_mask = jnp.dot(
        own_onehot, tile_mask.astype(jnp.float32), preferred_element_type=jnp.float32
    )
    return jnp.dot(rows_mask, order_onehot.T, preferred_element_type=jnp.float32)


def attend(queries_flat, key_values, pos_mask):
    row_count = queries_flat.shape[0]
    heads_dev = queries_flat.shape[1] // HEAD
    queries = queries_flat.reshape(row_count, heads_dev, HEAD)
    score_scale = 1.0 / math.sqrt(HEAD)
    tiles_dev = row_count // TILE
    tile_ids = jnp.arange(pos_mask.shape[1], dtype=jnp.int32)
    initial = (
        jnp.full((heads_dev, row_count), MASKED_SCORE, jnp.float32),
        jnp.zeros((heads_dev, row_count), jnp.float32),
        jnp.zeros((heads_dev, row_count, HEAD), jnp.float32),
    )
    fetched = lax.all_gather(key_values, "seq", axis=1, tiled=True)
    fetched_count = fetched.shape[1]
    key_block = 512

    def advance(block_index, state_now):
        top_score, denom, weighted = state_now
        offset = block_index * key_block
        key_rows = lax.dynamic_slice_in_dim(fetched[0], offset, key_block).reshape(
            key_block, heads_dev, HEAD
        )
        values = lax.dynamic_slice_in_dim(fetched[1], offset, key_block).reshape(
            key_block, heads_dev, HEAD
        )
        tile_pos = (offset + jnp.arange(key_block, dtype=jnp.int32)) // TILE
        onehot = (tile_pos[:, None] == tile_ids[None, :]).astype(jnp.float32)
        tile_allowed = (
            jnp.einsum("qn,kn->qk", pos_mask, onehot, preferred_element_type=jnp.float32) > 0.5
        )
        visible = jnp.broadcast_to(tile_allowed[:, None, :], (tiles_dev, TILE, key_block)).reshape(
            row_count, key_block
        )
        scores = (
            jnp.einsum("qhd,khd->hqk", queries, key_rows, preferred_element_type=jnp.float32)
            * score_scale
        )
        masked = jnp.where(visible[None], scores, MASKED_SCORE)
        new_top = jnp.maximum(top_score, jnp.max(masked, axis=2))
        powers = jnp.where(visible[None], jnp.exp(masked - new_top[:, :, None]), 0.0)
        shrink = jnp.exp(top_score - new_top)
        denom = denom * shrink + jnp.sum(powers, axis=2)
        weighted = weighted * shrink[:, :, None] + jnp.einsum(
            "hqk,khd->hqd", powers.astype(jnp.bfloat16), values, preferred_element_type=jnp.float32
        )
        return (new_top, denom, weighted)

    _, denom, weighted = lax.fori_loop(0, fetched_count // key_block, advance, initial)
    finished = (weighted / denom[:, :, None]).astype(jnp.bfloat16)
    return jnp.transpose(finished, (1, 0, 2)).reshape(row_count, heads_dev * HEAD)


def per_device_general(clip_tokens, conv_taps, norm_gain, qkv_weight, out_weight, tile_mask, stripe_order):
    tiles_dev = clip_tokens.shape[1] // TILE
    send_order, place_order, own_row = stripe_tables(stripe_order, tiles_dev)
    before = passed_along(clip_tokens, "seq", 1)
    mixed = causal_conv(clip_tokens, before, conv_taps)
    mixed = regroup(mixed, send_order, place_order)
    projected = project(mixed, norm_gain, qkv_weight)
    row_count = projected.shape[1]
    group_cols = projected.shape[2]
    half_rows = row_count // 2
    side = lax.axis_index("tp") % 2
    mine_first = side == 0
    query_send = lax.dynamic_slice_in_dim(projected[0], (1 - side) * half_rows, half_rows, axis=0)
    query_mine = lax.dynamic_slice_in_dim(projected[0], side * half_rows, half_rows, axis=0)
    kv_mine = projected[1:]
    query_other, kv_other = from_partner((query_send, kv_mine), "tp", 0)
    queries = jnp.where(
        mine_first,
        jnp.concatenate([query_mine, query_other], axis=1),
        jnp.concatenate([query_other, query_mine], axis=1),
    )
    key_values = jnp.where(
        mine_first,
        jnp.concatenate([kv_mine, kv_other], axis=2),
        jnp.concatenate([kv_other, kv_mine], axis=2),
    )
    own_half = lax.dynamic_slice_in_dim(own_row, side * (tiles_dev // 2), tiles_dev // 2)
    pos_mask = position_mask(tile_mask, stripe_order, own_half)
    pair_out = attend(queries, key_values, pos_mask)
    give_cols = lax.dynamic_slice_in_dim(pair_out, (1 - side) * group_cols, group_cols, axis=1)
    keep_cols = lax.dynamic_slice_in_dim(pair_out, side * group_cols, group_cols, axis=1)
    got_cols = from_partner(give_cols, "tp", 0)
    heads_out = jnp.where(
        mine_first,
        jnp.concatenate([keep_cols, got_cols], axis=0),
        jnp.concatenate([got_cols, keep_cols], axis=0),
    )
    return lax.psum_scatter(
        jnp.einsum("qg,gc->cq", heads_out, out_weight, preferred_element_type=jnp.float32).astype(
            jnp.bfloat16
        ),
        "tp",
        scatter_dimension=0,
        tiled=True,
    )


def solution(mesh):
    in_specs = (
        P("tp", ("dp", "seq")),
        P(None, "tp"),
        P(),
        P(None, "tp", None),
        P("tp", None),
        P(),
        P(),
    )
    out_specs = P("tp", ("dp", "seq"))

    def run(clip_tokens, conv_taps, norm_gain, qkv_weight, out_weight, tile_mask, stripe_order):
        arguments = (clip_tokens, conv_taps, norm_gain, qkv_weight, out_weight, tile_mask, stripe_order)
        tokens = clip_tokens.shape[1] // (mesh.shape["dp"] * mesh.shape["seq"])
        columns = qkv_weight.shape[1] // mesh.shape["tp"]
        two_halves = mesh.shape["seq"] == 2 and tokens == 2 * FRAME
        fast = two_halves and mesh.shape["tp"] == 4 and columns % HEAD == 0

        def per_device(*local):
            if not fast:
                return per_device_general(*local)
            return per_device_fast(*local)

        step = jax.shard_map(
            per_device, mesh=mesh, in_specs=in_specs, out_specs=out_specs, check_vma=False
        )
        return step(*arguments)

    return run
```

```python
import functools
import math

import jax
import jax.numpy as jnp
from jax import lax
from jax.experimental import pallas as pl
from jax.experimental.pallas import tpu as pltpu
from jax.sharding import PartitionSpec as P


HEAD = 128
TILE = 128
FH = 16
FW = 32
FRAME = FH * FW
TAPS = 27


EPSILON = 1e-06
MASKED_SCORE = -1e30
LOG2E = math.log2(math.e)

VMEM_LIMIT = 20 * 1024 * 1024
VMEM_WHOLE = 60 * 1024 * 1024


def vmem_spec():
    return pl.BlockSpec(memory_space=pltpu.VMEM)


def smem_spec():
    return pl.BlockSpec(memory_space=pltpu.SMEM)


def params(limit=VMEM_LIMIT):
    return pltpu.CompilerParams(vmem_limit_bytes=limit)


def shift_matrix(row_off, col_offs, rows):
    shape = (rows, TILE * len(col_offs))
    source = lax.broadcasted_iota(jnp.int32, shape, 0)
    target = lax.broadcasted_iota(jnp.int32, shape, 1)
    lane = target % TILE
    col_off = jnp.zeros(shape, jnp.int32)
    for index, offset in enumerate(col_offs):
        col_off = jnp.where(target // TILE == index, offset, col_off)
    base = TILE if row_off < 0 else 0
    wanted = lane + row_off * FW + col_off + base
    column = lane % FW + col_off
    inside = (column >= 0) & (column < FW)
    return jnp.where((source == wanted) & inside, 1.0, 0.0).astype(jnp.bfloat16)


def shift_pieces(source_ref, shifted, matrices):
    channels, tokens = source_ref.shape
    pieces = tokens // TILE
    per_frame = FRAME // TILE
    nothing = jnp.zeros((channels, TILE), jnp.bfloat16)

    def piece(index):
        return source_ref[:, index * TILE : (index + 1) * TILE]

    above, here, below = [], [], []
    for index in range(pieces):
        first, last = index % per_frame == 0, index % per_frame == per_frame - 1
        now = piece(index)
        here.append(now)
        above.append(jnp.concatenate([nothing if first else piece(index - 1), now], axis=1))
        below.append(jnp.concatenate([now, nothing if last else piece(index + 1)], axis=1))
    for out, matrix, parts in zip(shifted, matrices, (above, here, below)):
        out[...] = jnp.dot(
            jnp.concatenate(parts, axis=0), matrix[...], preferred_element_type=jnp.float32
        )


def pack_slots(order_ref, slots_ref, seq_here, tiles_dev, positions):
    half = tiles_dev // 2
    kept = jnp.int32(0)
    sent = jnp.int32(half)
    for position in range(positions):
        tile = order_ref[position]
        mine = tile // tiles_dev == seq_here
        stays = jnp.int32(position // tiles_dev) == seq_here
        slot = jnp.where(stays, kept, sent)

        @pl.when(mine)
        def _(tile=tile, slot=slot):
            slots_ref[tile - seq_here * tiles_dev] = slot

        step = mine.astype(jnp.int32)
        kept = kept + jnp.where(stays, step, 0)
        sent = sent + jnp.where(stays, 0, step)


def conv_body(with_before, seq_ref, order_ref, *refs):
    tokens_ref, taps_ref, part_ref, keep_ref, send_ref, *refs = refs
    slots_ref, taps_scr, packed, *refs = refs
    shifted, matrices = refs[:3], refs[3:]
    channels, tokens = tokens_ref.shape
    tiles_dev = tokens // TILE
    per_frame = FRAME // TILE
    seq_here = seq_ref[0]

    @pl.when(pl.program_id(0) == 0)
    def _():
        pack_slots(order_ref, slots_ref, seq_here, tiles_dev, order_ref.shape[0])
        matrices[0][...] = shift_matrix(-1, (-1, 0, 1), 2 * TILE)
        matrices[1][...] = shift_matrix(0, (-1, 1), TILE)
        matrices[2][...] = shift_matrix(1, (-1, 0, 1), 2 * TILE)

    taps_scr[:, :TAPS] = taps_ref[...].T
    shift_pieces(tokens_ref, shifted, matrices)
    group = 16
    reads = ((0, 0, 0), (0, 1, 1), (1, 1, 0)) if with_before else ((2, 0, 0), (2, 1, 1), (1, 0, 1))

    def advance(step, carry):
        start = pl.multiple_of(step * group, group)
        rows = pl.ds(start, group)
        taps = taps_scr[rows, :]
        centre = [
            tokens_ref[rows, tile * TILE : (tile + 1) * TILE].astype(jnp.float32)
            for tile in range(tiles_dev)
        ]
        if with_before:
            sums = [part_ref[rows, tile * TILE : (tile + 1) * TILE] for tile in range(tiles_dev)]
        else:
            sums = list(centre)

        def value(tile, row_off, col_off):
            if row_off == 1 and col_off == 1:
                return centre[tile]
            column = col_off // 2 if row_off == 1 else col_off
            lines = pl.ds(tile * channels + start, group)
            return shifted[row_off][lines, column * TILE : (column + 1) * TILE]

        for time_off, read, written in reads:
            for row_off in range(3):
                for col_off in range(3):
                    tap = time_off * 9 + row_off * 3 + col_off
                    weight = jnp.broadcast_to(taps[:, tap : tap + 1], (group, TILE))
                    for spot in range(per_frame):
                        out = written * per_frame + spot
                        sums[out] = sums[out] + weight * value(read * per_frame + spot, row_off, col_off)
        for tile in range(tiles_dev):
            if not with_before:
                part_ref[rows, tile * TILE : (tile + 1) * TILE] = sums[tile]
            place = pl.ds(pl.multiple_of(slots_ref[tile] * TILE, TILE), TILE)
            packed[rows, place] = sums[tile].astype(jnp.bfloat16)
        return carry

    lax.fori_loop(0, channels // group, advance, 0)
    keep_ref[...] = packed[:, : tokens // 2]
    send_ref[...] = packed[:, tokens // 2 :]


def conv_call(seq_here, stripe_order, tokens, conv_taps, part=None):
    channels, count = tokens.shape
    block = 128
    wide = pl.BlockSpec((block, count), lambda i, *_: (i, 0))
    slim = pl.BlockSpec((block, count // 2), lambda i, *_: (i, 0))
    taps_spec = pl.BlockSpec((TAPS, block), lambda i, *_: (0, i))
    packed_shape = jax.ShapeDtypeStruct((channels, count // 2), jnp.bfloat16)
    with_before = part is not None
    out_specs, out_shape = [slim, slim], [packed_shape, packed_shape]
    if not with_before:
        out_specs = [wide] + out_specs
        out_shape = [jax.ShapeDtypeStruct((channels, count), jnp.float32)] + out_shape
    lines = block * (count // TILE)
    return pl.pallas_call(
        functools.partial(conv_body, with_before),
        grid_spec=pltpu.PrefetchScalarGridSpec(
            num_scalar_prefetch=2,
            grid=(channels // block,),
            in_specs=[wide, taps_spec] + [wide] * with_before,
            out_specs=out_specs,
            scratch_shapes=[
                pltpu.SMEM((count // TILE,), jnp.int32),
                pltpu.VMEM((block, 128), jnp.float32),
                pltpu.VMEM((block, count), jnp.bfloat16),
                pltpu.VMEM((lines, 3 * TILE), jnp.float32),
                pltpu.VMEM((lines, 2 * TILE), jnp.float32),
                pltpu.VMEM((lines, 3 * TILE), jnp.float32),
                pltpu.VMEM((2 * TILE, 3 * TILE), jnp.bfloat16),
                pltpu.VMEM((TILE, 2 * TILE), jnp.bfloat16),
                pltpu.VMEM((2 * TILE, 3 * TILE), jnp.bfloat16),
            ],
        ),
        out_shape=out_shape,
        compiler_params=params(VMEM_LIMIT if with_before else VMEM_WHOLE),
        cost_estimate=pl.CostEstimate(
            flops=channels * count * TAPS, bytes_accessed=channels * count * 8, transcendentals=0
        ),
        name="conv",
    )(seq_here, stripe_order, tokens, conv_taps, *([part] if with_before else []))


def prepare_body(blocks_ref, gain_ref, qkv_ref, out_ref, qkv_out, out_out):
    qkv_out[...] = (qkv_ref[...].astype(jnp.float32) * gain_ref[...]).astype(jnp.bfloat16)
    out_out[...] = out_ref[...].T


def prepare_weights(blocks, norm_gain, qkv_weight, out_weight):
    kinds, cols, channels = qkv_weight.shape
    count = blocks.shape[0]
    width = channels // count
    return pl.pallas_call(
        prepare_body,
        grid_spec=pltpu.PrefetchScalarGridSpec(
            num_scalar_prefetch=1,
            grid=(count,),
            in_specs=[
                pl.BlockSpec((1, width), lambda j, b: (0, b[j])),
                pl.BlockSpec((kinds * cols, width), lambda j, b: (0, b[j])),
                pl.BlockSpec((cols, width), lambda j, b: (0, b[j])),
            ],
            out_specs=[
                pl.BlockSpec((kinds * cols, width), lambda j, b: (0, j)),
                pl.BlockSpec((width, cols), lambda j, b: (j, 0)),
            ],
        ),
        out_shape=[
            jax.ShapeDtypeStruct((kinds * cols, channels), jnp.bfloat16),
            jax.ShapeDtypeStruct((channels, cols), jnp.bfloat16),
        ],
        compiler_params=params(VMEM_WHOLE),
        cost_estimate=pl.CostEstimate(
            flops=kinds * cols * channels, bytes_accessed=16 * cols * channels, transcendentals=0
        ),
        name="prepare",
    )(blocks, norm_gain[None, :], qkv_weight.reshape(kinds * cols, channels), out_weight)


def fetches(source, target, semaphores):
    block = target.shape[0] // semaphores.shape[0]
    return [
        pltpu.make_async_copy(
            source.at[index * block : (index + 1) * block],
            target.at[index * block : (index + 1) * block],
            semaphores.at[index],
        )
        for index in range(semaphores.shape[0])
    ]


def project_body(weight_hbm, own, before, after, across, query_ref, pair_ref, weight_ref, tokens_ref, arrived):
    copies = fetches(weight_hbm, weight_ref, arrived)
    for copy in copies:
        copy.start()
    width = own.shape[0]
    cols = query_ref.shape[0]
    squares = None
    for index, shard in enumerate((own, before, after, across)):
        block = shard[...]
        tokens_ref[index * width : (index + 1) * width, :] = block
        wide = block.astype(jnp.float32)
        term = jnp.sum(wide * wide, axis=0, keepdims=True)
        squares = term if squares is None else squares + term
    inverse = lax.rsqrt(squares / (4 * width) + EPSILON)
    rows = weight_ref.shape[0] // len(copies)
    for index, copy in enumerate(copies):
        copy.wait()
        here = slice(index * rows, (index + 1) * rows)
        total = jnp.dot(weight_ref[here, :], tokens_ref[...], preferred_element_type=jnp.float32)
        if index * rows < cols:
            query_ref[here, :] = (total * (inverse * (LOG2E / math.sqrt(HEAD)))).astype(jnp.bfloat16)
        else:
            there = slice(index * rows - cols, (index + 1) * rows - cols)
            pair_ref[there, :] = (total * inverse).astype(jnp.bfloat16)


def project_call(weights, shards):
    rows, channels = weights.shape
    tokens = shards[0].shape[1]
    cols = rows // 3
    return pl.pallas_call(
        project_body,
        in_specs=[pl.BlockSpec(memory_space=pltpu.HBM)] + [vmem_spec()] * len(shards),
        out_specs=[vmem_spec(), vmem_spec()],
        scratch_shapes=[
            pltpu.VMEM((rows, channels), jnp.bfloat16),
            pltpu.VMEM((channels, tokens), jnp.bfloat16),
            pltpu.SemaphoreType.DMA((6,)),
        ],
        out_shape=[
            jax.ShapeDtypeStruct((cols, tokens), jnp.bfloat16),
            jax.ShapeDtypeStruct((2 * cols, tokens), jnp.bfloat16),
        ],
        compiler_params=params(),
        cost_estimate=pl.CostEstimate(
            flops=2 * rows * channels * tokens,
            bytes_accessed=2 * (rows * channels + channels * tokens + rows * tokens),
            transcendentals=0,
        ),
        name="project",
    )(weights, *shards)


def tile_lists(order_ref, ids_ref, seq_here, tiles_dev):
    half = tiles_dev // 2
    for block in range(2):
        first = jnp.int32(0)
        second = jnp.int32(0)
        away = (jnp.int32(block) != seq_here).astype(jnp.int32)
        for spot in range(tiles_dev):
            tile = order_ref[block * tiles_dev + spot]
            late = tile // tiles_dev
            rank = jnp.where(late == 0, first, second)
            ids_ref[(2 * late + away) * half + rank] = tile
            first = first + (1 - late)
            second = second + late


def attend_body(chunk, sources, goes_on, ends, seq_ref, order_ref, mask_ref, query_ref, *refs):
    count = len(sources)
    pairs, refs = refs[:count], refs[count:]
    if goes_on:
        old_stats, old_weighted, *refs = refs
    if ends:
        weight_hbm, *refs = refs
        partial_refs, refs = refs[:4], refs[4:]
        ids_ref, bias_ref, scores_ref, heads_ref, weight_ref, arrived = refs
        copies = fetches(weight_hbm, weight_ref, arrived)
        for copy in copies:
            copy.start()
    else:
        new_stats, new_weighted, ids_ref, bias_ref, scores_ref = refs
    cols, tokens = query_ref.shape
    half = tokens // TILE
    tile_lists(order_ref, ids_ref, seq_ref[0], 2 * half)
    lane_tile = lax.broadcasted_iota(jnp.int32, (1, tokens), 1) // TILE
    for index, source in enumerate(sources):
        for spot in range(half):
            key_tile = ids_ref[source * half + spot]
            bias = jnp.zeros((1, tokens), jnp.float32)
            for query_spot in range(half):
                query_tile = ids_ref[2 * chunk * half + query_spot]
                blocked = jnp.where(mask_ref[query_tile, key_tile] == 1, 0.0, MASKED_SCORE)
                bias = jnp.where(lane_tile == query_spot, blocked, bias)
            bias_ref[index * half + spot : index * half + spot + 1, :] = bias

    def one_head(head, carry):
        rows = pl.ds(pl.multiple_of(head * HEAD, HEAD), HEAD)
        value_rows = pl.ds(pl.multiple_of(cols + head * HEAD, HEAD), HEAD)
        query = query_ref[rows, :]
        old_top = old_stats[head, 0:1, :] if goes_on else None
        top = old_top
        for index in range(count):
            block = jnp.dot(pairs[index][rows, :].T, query, preferred_element_type=jnp.float32)
            for spot in range(half):
                line = index * half + spot
                piece = block[spot * TILE : (spot + 1) * TILE, :] + bias_ref[line : line + 1, :]
                scores_ref[line * TILE : (line + 1) * TILE, :] = piece
                best = jnp.max(piece, axis=0, keepdims=True)
                top = best if top is None else jnp.maximum(top, best)
        denom = None
        weighted = None
        if goes_on:
            shrink = jnp.exp2(old_top - top)
            denom = old_stats[head, 1:2, :] * shrink
            weighted = old_weighted[rows, :] * shrink
        for index in range(count):
            powers = jnp.exp2(scores_ref[index * tokens : (index + 1) * tokens, :] - top)
            summed = jnp.sum(powers, axis=0, keepdims=True)
            term = jnp.dot(
                pairs[index][value_rows, :],
                powers.astype(jnp.bfloat16),
                preferred_element_type=jnp.float32,
            )
            denom = summed if denom is None else denom + summed
            weighted = term if weighted is None else weighted + term
        if ends:
            heads_ref[rows, :] = (weighted / denom).astype(jnp.bfloat16)
        else:
            new_stats[head, 0:1, :] = top
            new_stats[head, 1:2, :] = denom
            new_weighted[rows, :] = weighted
        return carry

    lax.fori_loop(0, cols // HEAD, one_head, 0)
    if ends:
        width = weight_ref.shape[0] // 4
        for copy in copies:
            copy.wait()
        for index, out in enumerate(partial_refs):
            block = weight_ref[index * width : (index + 1) * width, :]
            out[...] = jnp.dot(
                block, heads_ref[...], preferred_element_type=jnp.float32
            ).astype(jnp.bfloat16)


def attend_call(chunk, tables, queries, sources, state=None, out_t=None):
    cols, tokens = queries.shape
    heads = cols // HEAD
    count = len(sources)
    half = tokens // TILE
    goes_on, ends = state is not None, out_t is not None
    arguments = [queries] + [array for array, _ in sources] + (list(state) if goes_on else [])
    in_specs = [vmem_spec()] * len(arguments)
    scratch = [
        pltpu.SMEM((4 * half,), jnp.int32),
        pltpu.VMEM((count * half, tokens), jnp.float32),
        pltpu.VMEM((count * tokens, tokens), jnp.float32),
    ]
    if ends:
        in_specs += [pl.BlockSpec(memory_space=pltpu.HBM)]
        arguments += [out_t]
        shapes = [jax.ShapeDtypeStruct((out_t.shape[0] // 4, tokens), jnp.bfloat16)] * 4
        scratch += [
            pltpu.VMEM((cols, tokens), jnp.bfloat16),
            pltpu.VMEM(out_t.shape, jnp.bfloat16),
            pltpu.SemaphoreType.DMA((4,)),
        ]
    else:
        shapes = [
            jax.ShapeDtypeStruct((heads, 2, tokens), jnp.float32),
            jax.ShapeDtypeStruct((cols, tokens), jnp.float32),
        ]
    return pl.pallas_call(
        functools.partial(attend_body, chunk, tuple(s for _, s in sources), goes_on, ends),
        in_specs=[smem_spec()] * 3 + in_specs,
        out_specs=[vmem_spec()] * len(shapes),
        scratch_shapes=scratch,
        out_shape=shapes,
        compiler_params=params(),
        cost_estimate=pl.CostEstimate(
            flops=4 * cols * tokens * tokens * count,
            bytes_accessed=2 * cols * tokens * (2 + 2 * count),
            transcendentals=heads * tokens * tokens * count,
        ),
        name="attend",
    )(*tables, *arguments)


def place_body(seq_ref, order_ref, ends_ref, first_ref, *refs):
    parts, out_ref, second_ref = refs[:4], refs[4], refs[5]
    _, tokens = first_ref.shape
    tiles_dev = 2 * tokens // TILE
    seq_here = seq_ref[0]
    at_end = ends_ref[0] == 1
    total = (
        parts[0][...].astype(jnp.float32)
        + parts[1][...].astype(jnp.float32)
        + parts[2][...].astype(jnp.float32)
        + jnp.where(at_end, parts[3][...].astype(jnp.float32), 0.0)
    )
    second_ref[...] = total.astype(jnp.bfloat16)
    ranks = [jnp.int32(0), jnp.int32(0)]
    for position in range(tiles_dev):
        late = order_ref[seq_here * tiles_dev + position] // tiles_dev
        spot = pl.ds(pl.multiple_of(jnp.where(late == 0, ranks[0], ranks[1]) * TILE, TILE), TILE)
        here = slice(position * TILE, (position + 1) * TILE)

        @pl.when(late == 0)
        def _(spot=spot, here=here):
            out_ref[:, here] = first_ref[:, spot]

        @pl.when(late == 1)
        def _(spot=spot, here=here):
            out_ref[:, here] = second_ref[:, spot]

        ranks[0] = ranks[0] + (1 - late)
        ranks[1] = ranks[1] + late


def place_call(seq_here, stripe_order, at_end, first, parts):
    channels, tokens = first.shape
    block = 128
    slim = pl.BlockSpec((block, tokens), lambda i, *_: (i, 0))
    return pl.pallas_call(
        place_body,
        grid_spec=pltpu.PrefetchScalarGridSpec(
            num_scalar_prefetch=3,
            grid=(channels // block,),
            in_specs=[slim] * 5,
            out_specs=pl.BlockSpec((block, 2 * tokens), lambda i, *_: (i, 0)),
            scratch_shapes=[pltpu.VMEM((block, tokens), jnp.bfloat16)],
        ),
        out_shape=jax.ShapeDtypeStruct((channels, 2 * tokens), jnp.bfloat16),
        compiler_params=params(),
        cost_estimate=pl.CostEstimate(
            flops=4 * channels * tokens, bytes_accessed=14 * channels * tokens, transcendentals=0
        ),
        name="place",
    )(seq_here, stripe_order, at_end, first, *parts)


FORWARD = [(0, 1), (1, 2), (2, 3), (3, 0)]
BACKWARD = [(1, 0), (2, 1), (3, 2), (0, 3)]
FOLDED = [(0, 1), (1, 3), (3, 2), (2, 0)]
UNFOLDED = [(1, 0), (3, 1), (2, 3), (0, 2)]


def gather_blocks(block, here):
    before = lax.ppermute(block, "tp", FORWARD)
    after = lax.ppermute(block, "tp", BACKWARD)
    relay = jnp.where(here == 2, before, jnp.where(here == 1, after, block))
    across = lax.ppermute(relay, "tp", UNFOLDED)
    return (block, before, after, across)


def plus(a, b, chosen):
    summed = a.astype(jnp.float32) + jnp.where(chosen, b.astype(jnp.float32), 0.0)
    return summed.astype(jnp.bfloat16)


def reduce_blocks(partials, here):
    own, down, up, sent = partials
    across = lax.ppermute(sent, "tp", FOLDED)
    back = lax.ppermute(plus(down, across, here == 2), "tp", BACKWARD)
    onward = lax.ppermute(plus(up, across, here == 1), "tp", FORWARD)
    return (own, back, onward, across)


def per_device_fast(
    clip_tokens, conv_taps, norm_gain, qkv_weight, out_weight, tile_mask, stripe_order
):
    seq = lax.axis_index("seq")
    here = lax.axis_index("tp")
    seq_here = seq.astype(jnp.int32)[None]
    at_end = ((here == 0) | (here == 3)).astype(jnp.int32)[None]
    blocks = jnp.stack([here, (here + 3) % 4, (here + 1) % 4, (here + 2) % 4]).astype(jnp.int32)
    tables = (seq_here, stripe_order, tile_mask)

    part, keep_a, send_a = conv_call(seq_here, stripe_order, clip_tokens, conv_taps)
    got_a = lax.ppermute(send_a, "seq", [(0, 1)])
    before = lax.ppermute(clip_tokens, "seq", [(0, 1)])
    weights, out_t = prepare_weights(blocks, norm_gain, qkv_weight, out_weight)

    tokens_a = jnp.where(seq == 0, keep_a, got_a)
    shards_a = gather_blocks(tokens_a, here)

    keep_b, send_b = conv_call(seq_here, stripe_order, before, conv_taps, part)
    got_b = lax.ppermute(send_b, "seq", [(1, 0)])
    tokens_b = jnp.where(seq == 1, keep_b, got_b)

    swap = [(0, 1), (1, 0)]
    query_a, pair_a = project_call(weights, shards_a)
    peer_a = lax.ppermute(pair_a, "seq", swap)
    shards_b = gather_blocks(tokens_b, here)
    partials_a = attend_call(0, tables, query_a, [(pair_a, 0), (peer_a, 1)], out_t=out_t)
    parts_a = reduce_blocks(partials_a, here)
    query_b, pair_b = project_call(weights, shards_b)
    peer_b = lax.ppermute(pair_b, "seq", swap)
    near = [(pair_a, 0), (peer_a, 1), (pair_b, 2)]
    state = attend_call(1, tables, query_b, near)
    partials_b = attend_call(1, tables, query_b, [(peer_b, 3)], state=state, out_t=out_t)
    parts_b = reduce_blocks(partials_b, here)
    first = sum(part.astype(jnp.float32) for part in parts_a[:3])
    first = first + jnp.where(at_end == 1, parts_a[3].astype(jnp.float32), 0.0)
    return place_call(seq_here, stripe_order, at_end, first.astype(jnp.bfloat16), parts_b)


def passed_along(block, axis, distance):
    devices = range(lax.axis_size(axis))
    route = [(i - distance, i) for i in devices if i - distance in devices]
    return lax.ppermute(block, axis, route)


def from_partner(block, axis, apart):
    count = lax.axis_size(axis)
    route = []
    for low in range(count):
        high = low | 1 << apart
        if high != low and high < count:
            route += [(low, high), (high, low)]
    return lax.ppermute(block, axis, route)


def causal_conv(local_tokens, before, conv_taps):
    channels = local_tokens.shape[0]
    frames = local_tokens.shape[1] // (FH * FW)
    stacked = (
        jnp.concatenate([before, local_tokens], axis=1)
        .astype(jnp.float32)
        .reshape(channels, frames + 2, FH, FW)
    )
    padded = jnp.pad(stacked, ((0, 0), (0, 0), (1, 1), (1, 1)))
    summed = jnp.zeros((channels, frames, FH, FW), jnp.float32)
    for time_off in range(3):
        for row_off in range(3):
            for col_off in range(3):
                tap_vec = conv_taps[time_off * 9 + row_off * 3 + col_off]
                summed = (
                    summed
                    + tap_vec[:, None, None, None]
                    * padded[
                        :,
                        time_off : time_off + frames,
                        row_off : row_off + FH,
                        col_off : col_off + FW,
                    ]
                )
    return (local_tokens.astype(jnp.float32) + summed.reshape(channels, -1)).astype(jnp.bfloat16)


def stripe_tables(stripe_order, tiles_dev):
    seq_count = lax.axis_size("seq")
    seq_here = lax.axis_index("seq")
    per_source = tiles_dev // seq_count
    blocks = stripe_order.reshape(seq_count, tiles_dev)
    owners = blocks // tiles_dev
    is_mine = (owners == seq_here).astype(jnp.int32)
    rank_of = jnp.cumsum(is_mine, axis=1) - 1
    slot_ids = jnp.arange(per_source, dtype=jnp.int32)
    picked = is_mine[:, None, :] * (rank_of[:, None, :] == slot_ids[None, :, None]).astype(
        jnp.int32
    )
    local_tiles = (blocks - seq_here * tiles_dev)[:, None, :]
    send_order = jnp.sum(picked * local_tiles, axis=2).reshape(-1)
    own_row = lax.dynamic_slice_in_dim(stripe_order, seq_here * tiles_dev, tiles_dev)
    sources = own_row // tiles_dev
    position = jnp.arange(tiles_dev, dtype=jnp.int32)
    earlier = (sources[:, None] == sources[None, :]) & (position[None, :] < position[:, None])
    place_order = sources * per_source + jnp.sum(earlier.astype(jnp.int32), axis=1)
    return (send_order, place_order, own_row)


def regroup(values, send_order, place_order):
    leading = values.shape[0]
    trailing = values.shape[2:]
    in_tiles = values.reshape((leading, values.shape[1] // TILE, TILE) + trailing)
    outgoing = jnp.take(in_tiles, send_order, axis=1)
    arrived = lax.all_to_all(outgoing, "seq", split_axis=1, concat_axis=1, tiled=True)
    placed = jnp.take(arrived, place_order, axis=1)
    return placed.reshape(values.shape)


def project(mixed, norm_gain, qkv_weight):
    channels = norm_gain.shape[0]
    widened = lax.all_gather(mixed, "tp", axis=0, tiled=True).astype(jnp.float32)
    scaled = (widened * norm_gain[:, None]).astype(jnp.bfloat16)
    projected = jnp.einsum("ct,khc->kth", scaled, qkv_weight, preferred_element_type=jnp.float32)
    squares = jnp.sum(widened * widened, axis=0)
    projected, squares = (projected, squares)
    inverse = lax.rsqrt(squares / channels + EPSILON)
    return (projected * inverse[None, :, None]).astype(jnp.bfloat16)


def position_mask(tile_mask, stripe_order, own_half):
    tiles_all = tile_mask.shape[0]
    tile_ids = jnp.arange(tiles_all, dtype=jnp.int32)
    own_onehot = (own_half[:, None] == tile_ids[None, :]).astype(jnp.float32)
    order_onehot = (stripe_order[:, None] == tile_ids[None, :]).astype(jnp.float32)
    rows_mask = jnp.dot(
        own_onehot, tile_mask.astype(jnp.float32), preferred_element_type=jnp.float32
    )
    return jnp.dot(rows_mask, order_onehot.T, preferred_element_type=jnp.float32)


def attend(queries_flat, key_values, pos_mask):
    row_count = queries_flat.shape[0]
    heads_dev = queries_flat.shape[1] // HEAD
    queries = queries_flat.reshape(row_count, heads_dev, HEAD)
    score_scale = 1.0 / math.sqrt(HEAD)
    tiles_dev = row_count // TILE
    tile_ids = jnp.arange(pos_mask.shape[1], dtype=jnp.int32)
    initial = (
        jnp.full((heads_dev, row_count), MASKED_SCORE, jnp.float32),
        jnp.zeros((heads_dev, row_count), jnp.float32),
        jnp.zeros((heads_dev, row_count, HEAD), jnp.float32),
    )
    fetched = lax.all_gather(key_values, "seq", axis=1, tiled=True)
    fetched_count = fetched.shape[1]
    key_block = 512

    def advance(block_index, state_now):
        top_score, denom, weighted = state_now
        offset = block_index * key_block
        key_rows = lax.dynamic_slice_in_dim(fetched[0], offset, key_block).reshape(
            key_block, heads_dev, HEAD
        )
        values = lax.dynamic_slice_in_dim(fetched[1], offset, key_block).reshape(
            key_block, heads_dev, HEAD
        )
        tile_pos = (offset + jnp.arange(key_block, dtype=jnp.int32)) // TILE
        onehot = (tile_pos[:, None] == tile_ids[None, :]).astype(jnp.float32)
        tile_allowed = (
            jnp.einsum("qn,kn->qk", pos_mask, onehot, preferred_element_type=jnp.float32) > 0.5
        )
        visible = jnp.broadcast_to(tile_allowed[:, None, :], (tiles_dev, TILE, key_block)).reshape(
            row_count, key_block
        )
        scores = (
            jnp.einsum("qhd,khd->hqk", queries, key_rows, preferred_element_type=jnp.float32)
            * score_scale
        )
        masked = jnp.where(visible[None], scores, MASKED_SCORE)
        new_top = jnp.maximum(top_score, jnp.max(masked, axis=2))
        powers = jnp.where(visible[None], jnp.exp(masked - new_top[:, :, None]), 0.0)
        shrink = jnp.exp(top_score - new_top)
        denom = denom * shrink + jnp.sum(powers, axis=2)
        weighted = weighted * shrink[:, :, None] + jnp.einsum(
            "hqk,khd->hqd", powers.astype(jnp.bfloat16), values, preferred_element_type=jnp.float32
        )
        return (new_top, denom, weighted)

    _, denom, weighted = lax.fori_loop(0, fetched_count // key_block, advance, initial)
    finished = (weighted / denom[:, :, None]).astype(jnp.bfloat16)
    return jnp.transpose(finished, (1, 0, 2)).reshape(row_count, heads_dev * HEAD)


def per_device_general(clip_tokens, conv_taps, norm_gain, qkv_weight, out_weight, tile_mask, stripe_order):
    tiles_dev = clip_tokens.shape[1] // TILE
    send_order, place_order, own_row = stripe_tables(stripe_order, tiles_dev)
    before = passed_along(clip_tokens, "seq", 1)
    mixed = causal_conv(clip_tokens, before, conv_taps)
    mixed = regroup(mixed, send_order, place_order)
    projected = project(mixed, norm_gain, qkv_weight)
    row_count = projected.shape[1]
    group_cols = projected.shape[2]
    half_rows = row_count // 2
    side = lax.axis_index("tp") % 2
    mine_first = side == 0
    query_send = lax.dynamic_slice_in_dim(projected[0], (1 - side) * half_rows, half_rows, axis=0)
    query_mine = lax.dynamic_slice_in_dim(projected[0], side * half_rows, half_rows, axis=0)
    kv_mine = projected[1:]
    query_other, kv_other = from_partner((query_send, kv_mine), "tp", 0)
    queries = jnp.where(
        mine_first,
        jnp.concatenate([query_mine, query_other], axis=1),
        jnp.concatenate([query_other, query_mine], axis=1),
    )
    key_values = jnp.where(
        mine_first,
        jnp.concatenate([kv_mine, kv_other], axis=2),
        jnp.concatenate([kv_other, kv_mine], axis=2),
    )
    own_half = lax.dynamic_slice_in_dim(own_row, side * (tiles_dev // 2), tiles_dev // 2)
    pos_mask = position_mask(tile_mask, stripe_order, own_half)
    pair_out = attend(queries, key_values, pos_mask)
    give_cols = lax.dynamic_slice_in_dim(pair_out, (1 - side) * group_cols, group_cols, axis=1)
    keep_cols = lax.dynamic_slice_in_dim(pair_out, side * group_cols, group_cols, axis=1)
    got_cols = from_partner(give_cols, "tp", 0)
    heads_out = jnp.where(
        mine_first,
        jnp.concatenate([keep_cols, got_cols], axis=0),
        jnp.concatenate([got_cols, keep_cols], axis=0),
    )
    return lax.psum_scatter(
        jnp.einsum("qg,gc->cq", heads_out, out_weight, preferred_element_type=jnp.float32).astype(
            jnp.bfloat16
        ),
        "tp",
        scatter_dimension=0,
        tiled=True,
    )


def solution(mesh):
    in_specs = (
        P("tp", ("dp", "seq")),
        P(None, "tp"),
        P(),
        P(None, "tp", None),
        P("tp", None),
        P(),
        P(),
    )
    out_specs = P("tp", ("dp", "seq"))

    def run(clip_tokens, conv_taps, norm_gain, qkv_weight, out_weight, tile_mask, stripe_order):
        arguments = (clip_tokens, conv_taps, norm_gain, qkv_weight, out_weight, tile_mask, stripe_order)
        tokens = clip_tokens.shape[1] // (mesh.shape["dp"] * mesh.shape["seq"])
        columns = qkv_weight.shape[1] // mesh.shape["tp"]
        two_halves = mesh.shape["seq"] == 2 and tokens == 2 * FRAME
        fast = two_halves and mesh.shape["tp"] == 4 and columns % HEAD == 0

        def per_device(*local):
            if not fast:
                return per_device_general(*local)
            return per_device_fast(*local)

        step = jax.shard_map(
            per_device, mesh=mesh, in_specs=in_specs, out_specs=out_specs, check_vma=False
        )
        return step(*arguments)

    return run
```

```python
import functools
import math

import jax
import jax.numpy as jnp
from jax import lax
from jax.experimental import pallas as pl
from jax.experimental.pallas import tpu as pltpu
from jax.sharding import PartitionSpec as P


HEAD = 128
TILE = 128
FH = 16
FW = 32
FRAME = FH * FW
TAPS = 27


EPSILON = 1e-06
MASKED_SCORE = -1e30
LOG2E = math.log2(math.e)

VMEM_LIMIT = 20 * 1024 * 1024
VMEM_FIRST = 52 * 1024 * 1024


def vmem_spec():
    return pl.BlockSpec(memory_space=pltpu.VMEM)


def smem_spec():
    return pl.BlockSpec(memory_space=pltpu.SMEM)


def params(limit=VMEM_LIMIT):
    return pltpu.CompilerParams(vmem_limit_bytes=limit)


def fetches(source, target, semaphores):
    block = target.shape[0] // semaphores.shape[0]
    return [
        pltpu.make_async_copy(
            source.at[index * block : (index + 1) * block],
            target.at[index * block : (index + 1) * block],
            semaphores.at[index],
        )
        for index in range(semaphores.shape[0])
    ]


def column_shifts(pieces, column):
    right = [jnp.where(column > 0, pltpu.roll(piece, 1, 1), 0.0) for piece in pieces]
    left = [jnp.where(column < FW - 1, pltpu.roll(piece, TILE - 1, 1), 0.0) for piece in pieces]
    return (right, pieces, left)


def rows_joined(rows, lane):
    down = [pltpu.roll(piece, FW, 1) for piece in rows[0]]
    up = [pltpu.roll(piece, TILE - FW, 1) for piece in rows[2]]
    joined = []
    for spot, middle in enumerate(rows[1]):
        before = down[spot - 1] if spot > 0 else 0.0
        after = up[spot + 1] if spot + 1 < len(up) else 0.0
        above = jnp.where(lane < FW, before, down[spot])
        below = jnp.where(lane >= TILE - FW, after, up[spot])
        joined.append(middle + (above + below))
    return joined


def pack_slots(order_ref, slots_ref, seq_here, tiles_dev, positions):
    half = tiles_dev // 2
    kept = jnp.int32(0)
    sent = jnp.int32(half)
    for position in range(positions):
        tile = order_ref[position]
        mine = tile // tiles_dev == seq_here
        stays = jnp.int32(position // tiles_dev) == seq_here
        slot = jnp.where(stays, kept, sent)

        @pl.when(mine)
        def _(tile=tile, slot=slot):
            slots_ref[tile - seq_here * tiles_dev] = slot

        step = mine.astype(jnp.int32)
        kept = kept + jnp.where(stays, step, 0)
        sent = sent + jnp.where(stays, 0, step)


GROUP = 16
CHUNKS = 4
PIECES = 2


def conv_body(with_before, first_row, seq_ref, order_ref, tokens_ref, taps_ref, part_ref, keep_ref, send_ref, *refs):
    if with_before:
        slots_ref, taps_scr, packed = refs
        source_ref = tokens_ref
    else:
        source_ref, slots_ref, taps_scr, packed, arrived = refs
    channels, tokens = packed.shape
    tiles_dev = tokens // TILE
    per_frame = FRAME // TILE
    if not with_before:
        copies = fetches(tokens_ref.at[first_row : first_row + channels], source_ref, arrived)
        for copy in copies:
            copy.start()
    pack_slots(order_ref, slots_ref, seq_ref[0], tiles_dev, order_ref.shape[0])
    for first in range(0, channels, TILE):
        from_row = first_row + first
        taps_scr[first : first + TILE, :TAPS] = taps_ref[:, from_row : from_row + TILE].T
    lane = lax.broadcasted_iota(jnp.int32, (GROUP, TILE), 1)
    column = lane % FW
    if with_before:
        reads = ([(0, 0), (1, 1)], [(0, 1)])
    else:
        reads = ([(2, 0)], [(1, 0), (2, 1)])

    def advance(step, carry):
        rows = pl.ds(pl.multiple_of(step * GROUP, GROUP), GROUP)
        taps = taps_scr[rows, :]
        shifts = []
        for frame in range(2):
            pieces = []
            for spot in range(per_frame):
                tile = frame * per_frame + spot
                pieces.append(source_ref[rows, tile * TILE : (tile + 1) * TILE].astype(jnp.float32))
            shifts.append(column_shifts(pieces, column))
        for frame in range(2):
            sums = []
            for row_off in range(3):
                line = [None] * per_frame
                for time_off, read in reads[frame]:
                    for col_off in range(3):
                        tap = time_off * 9 + row_off * 3 + col_off
                        weight = jnp.broadcast_to(taps[:, tap : tap + 1], (GROUP, TILE))
                        for spot in range(per_frame):
                            term = weight * shifts[read][col_off][spot]
                            line[spot] = term if line[spot] is None else line[spot] + term
                sums.append(line)
            for spot, value in enumerate(rows_joined(sums, lane)):
                tile = frame * per_frame + spot
                here = slice(tile * TILE, (tile + 1) * TILE)
                if with_before:
                    value = value + part_ref[rows, here]
                else:
                    value = value + shifts[frame][1][spot]
                    part_ref[rows, here] = value
                place = pl.ds(pl.multiple_of(slots_ref[tile] * TILE, TILE), TILE)
                packed[rows, place] = value.astype(jnp.bfloat16)
        keep_ref[rows, :] = packed[rows, : tokens // 2]
        send_ref[rows, :] = packed[rows, tokens // 2 :]
        return carry

    steps = channels // GROUP
    if with_before:
        lax.fori_loop(0, steps, advance, 0)
    else:
        each = steps // CHUNKS

        def chunk(index, carry):
            begin = index * each * GROUP
            pltpu.make_async_copy(
                tokens_ref.at[pl.ds(first_row + begin, each * GROUP)],
                source_ref.at[pl.ds(begin, each * GROUP)],
                arrived.at[index],
            ).wait()
            return lax.fori_loop(index * each, (index + 1) * each, advance, carry)

        lax.fori_loop(0, CHUNKS, chunk, 0)


def conv_call(seq_here, stripe_order, tokens, conv_taps, piece, part=None):
    count = tokens.shape[1]
    channels = conv_taps.shape[1] // PIECES
    packed_shape = jax.ShapeDtypeStruct((channels, count // 2), jnp.bfloat16)
    with_before = part is not None
    out_shape = [packed_shape, packed_shape]
    scratch = [
        pltpu.SMEM((count // TILE,), jnp.int32),
        pltpu.VMEM((channels, 128), jnp.float32),
        pltpu.VMEM((channels, count), jnp.bfloat16),
    ]
    in_specs = [smem_spec(), smem_spec(), vmem_spec(), vmem_spec(), vmem_spec()]
    if not with_before:
        in_specs = [smem_spec(), smem_spec(), pl.BlockSpec(memory_space=pl.ANY), vmem_spec()]
        sum_shape = jax.ShapeDtypeStruct((channels, count), jnp.float32)
        out_shape = [sum_shape] + out_shape + [jax.ShapeDtypeStruct((channels, count), jnp.bfloat16)]
        scratch += [pltpu.SemaphoreType.DMA((CHUNKS,))]
    return pl.pallas_call(
        functools.partial(conv_body, with_before, piece * channels),
        in_specs=in_specs,
        out_specs=[vmem_spec()] * len(out_shape),
        scratch_shapes=scratch,
        out_shape=out_shape,
        compiler_params=params(VMEM_LIMIT if with_before else VMEM_FIRST),
        cost_estimate=pl.CostEstimate(
            flops=channels * count * TAPS, bytes_accessed=channels * count * 8, transcendentals=0
        ),
        name="conv",
    )(seq_here, stripe_order, tokens, conv_taps, *([part] if with_before else []))


def prepare_body(blocks_ref, gain_ref, qkv_ref, out_ref, qkv_out, out_out):
    qkv_out[...] = (qkv_ref[...].astype(jnp.float32) * gain_ref[...]).astype(jnp.bfloat16)
    out_out[...] = out_ref[...].T


def prepare_weights(blocks, norm_gain, qkv_weight, out_weight):
    kinds, cols, channels = qkv_weight.shape
    count = blocks.shape[0]
    width = channels // count
    return pl.pallas_call(
        prepare_body,
        grid_spec=pltpu.PrefetchScalarGridSpec(
            num_scalar_prefetch=1,
            grid=(count,),
            in_specs=[
                pl.BlockSpec((1, width), lambda j, b: (0, b[j])),
                pl.BlockSpec((kinds * cols, width), lambda j, b: (0, b[j])),
                pl.BlockSpec((cols, width), lambda j, b: (0, b[j])),
            ],
            out_specs=[
                pl.BlockSpec((kinds * cols, width), lambda j, b: (0, j)),
                pl.BlockSpec((width, cols), lambda j, b: (j, 0)),
            ],
        ),
        out_shape=[
            jax.ShapeDtypeStruct((kinds * cols, channels), jnp.bfloat16),
            jax.ShapeDtypeStruct((channels, cols), jnp.bfloat16),
        ],
        compiler_params=params(),
        cost_estimate=pl.CostEstimate(
            flops=kinds * cols * channels, bytes_accessed=16 * cols * channels, transcendentals=0
        ),
        name="prepare",
    )(blocks, norm_gain[None, :], qkv_weight.reshape(kinds * cols, channels), out_weight)


def project_body(weight_ref, *refs):
    shards, (query_ref, pair_ref, tokens_ref) = refs[:-3], refs[-3:]
    width = shards[0].shape[0]
    cols = query_ref.shape[0]
    squares = None
    for index, shard in enumerate(shards):
        block = shard[...]
        tokens_ref[index * width : (index + 1) * width, :] = block
        wide = block.astype(jnp.float32)
        term = jnp.sum(wide * wide, axis=0, keepdims=True)
        squares = term if squares is None else squares + term
    inverse = lax.rsqrt(squares / (len(shards) * width) + EPSILON)
    rows = 256
    for index in range(weight_ref.shape[0] // rows):
        here = slice(index * rows, (index + 1) * rows)
        total = jnp.dot(weight_ref[here, :], tokens_ref[...], preferred_element_type=jnp.float32)
        if index * rows < cols:
            query_ref[here, :] = (total * (inverse * (LOG2E / math.sqrt(HEAD)))).astype(jnp.bfloat16)
        else:
            there = slice(index * rows - cols, (index + 1) * rows - cols)
            pair_ref[there, :] = (total * inverse).astype(jnp.bfloat16)


def project_call(weights, shards):
    rows, channels = weights.shape
    tokens = shards[0].shape[1]
    cols = rows // 3
    return pl.pallas_call(
        project_body,
        in_specs=[vmem_spec()] * (1 + len(shards)),
        out_specs=[vmem_spec(), vmem_spec()],
        scratch_shapes=[pltpu.VMEM((channels, tokens), jnp.bfloat16)],
        out_shape=[
            jax.ShapeDtypeStruct((cols, tokens), jnp.bfloat16),
            jax.ShapeDtypeStruct((2 * cols, tokens), jnp.bfloat16),
        ],
        compiler_params=params(),
        cost_estimate=pl.CostEstimate(
            flops=2 * rows * channels * tokens,
            bytes_accessed=2 * (rows * channels + channels * tokens + rows * tokens),
            transcendentals=0,
        ),
        name="project",
    )(weights, *shards)


def tile_lists(order_ref, ids_ref, seq_here, tiles_dev):
    half = tiles_dev // 2
    for block in range(2):
        first = jnp.int32(0)
        second = jnp.int32(0)
        away = (jnp.int32(block) != seq_here).astype(jnp.int32)
        for spot in range(tiles_dev):
            tile = order_ref[block * tiles_dev + spot]
            late = tile // tiles_dev
            rank = jnp.where(late == 0, first, second)
            ids_ref[(2 * late + away) * half + rank] = tile
            first = first + (1 - late)
            second = second + late


def attend_body(chunk, sources, goes_on, ends, seq_ref, order_ref, mask_ref, query_ref, *refs):
    count = len(sources)
    pairs, refs = refs[:count], refs[count:]
    if goes_on:
        old_stats, old_weighted, *refs = refs
    if ends:
        weight_hbm, *refs = refs
        partial_refs, refs = refs[: 4 * PIECES], refs[4 * PIECES :]
        ids_ref, bias_ref, scores_ref, heads_ref, weight_ref, arrived = refs
        copies = fetches(weight_hbm, weight_ref, arrived)
        for copy in copies:
            copy.start()
    else:
        new_stats, new_weighted, ids_ref, bias_ref, scores_ref = refs
    cols, tokens = query_ref.shape
    half = tokens // TILE
    tile_lists(order_ref, ids_ref, seq_ref[0], 2 * half)
    lane_tile = lax.broadcasted_iota(jnp.int32, (1, tokens), 1) // TILE
    for index, source in enumerate(sources):
        for spot in range(half):
            key_tile = ids_ref[source * half + spot]
            bias = jnp.zeros((1, tokens), jnp.float32)
            for query_spot in range(half):
                query_tile = ids_ref[2 * chunk * half + query_spot]
                blocked = jnp.where(mask_ref[query_tile, key_tile] == 1, 0.0, MASKED_SCORE)
                bias = jnp.where(lane_tile == query_spot, blocked, bias)
            bias_ref[index * half + spot : index * half + spot + 1, :] = bias

    def one_head(head, carry):
        rows = pl.ds(pl.multiple_of(head * HEAD, HEAD), HEAD)
        value_rows = pl.ds(pl.multiple_of(cols + head * HEAD, HEAD), HEAD)
        query = query_ref[rows, :]
        old_top = old_stats[head, 0:1, :] if goes_on else None
        top = old_top
        for index in range(count):
            block = jnp.dot(pairs[index][rows, :].T, query, preferred_element_type=jnp.float32)
            for spot in range(half):
                line = index * half + spot
                piece = block[spot * TILE : (spot + 1) * TILE, :] + bias_ref[line : line + 1, :]
                scores_ref[line * TILE : (line + 1) * TILE, :] = piece
                best = jnp.max(piece, axis=0, keepdims=True)
                top = best if top is None else jnp.maximum(top, best)
        denom = None
        weighted = None
        if goes_on:
            shrink = jnp.exp2(old_top - top)
            denom = old_stats[head, 1:2, :] * shrink
            weighted = old_weighted[rows, :] * shrink
        for index in range(count):
            powers = jnp.exp2(scores_ref[index * tokens : (index + 1) * tokens, :] - top)
            summed = jnp.sum(powers, axis=0, keepdims=True)
            term = jnp.dot(
                pairs[index][value_rows, :],
                powers.astype(jnp.bfloat16),
                preferred_element_type=jnp.float32,
            )
            denom = summed if denom is None else denom + summed
            weighted = term if weighted is None else weighted + term
        if ends:
            heads_ref[rows, :] = (weighted / denom).astype(jnp.bfloat16)
        else:
            new_stats[head, 0:1, :] = top
            new_stats[head, 1:2, :] = denom
            new_weighted[rows, :] = weighted
        return carry

    lax.fori_loop(0, cols // HEAD, one_head, 0)
    if ends:
        width = weight_ref.shape[0] // (4 * PIECES)
        for copy in copies:
            copy.wait()
        for index, out in enumerate(partial_refs):
            block = weight_ref[index * width : (index + 1) * width, :]
            out[...] = jnp.dot(
                block, heads_ref[...], preferred_element_type=jnp.float32
            ).astype(jnp.bfloat16)


def attend_call(chunk, tables, queries, sources, state=None, out_t=None):
    cols, tokens = queries.shape
    heads = cols // HEAD
    count = len(sources)
    half = tokens // TILE
    goes_on, ends = state is not None, out_t is not None
    arguments = [queries] + [array for array, _ in sources] + (list(state) if goes_on else [])
    in_specs = [vmem_spec()] * len(arguments)
    scratch = [
        pltpu.SMEM((4 * half,), jnp.int32),
        pltpu.VMEM((count * half, tokens), jnp.float32),
        pltpu.VMEM((count * tokens, tokens), jnp.float32),
    ]
    if ends:
        in_specs += [pl.BlockSpec(memory_space=pltpu.HBM)]
        arguments += [out_t]
        width = out_t.shape[0] // (4 * PIECES)
        shapes = [jax.ShapeDtypeStruct((width, tokens), jnp.bfloat16)] * (4 * PIECES)
        scratch += [
            pltpu.VMEM((cols, tokens), jnp.bfloat16),
            pltpu.VMEM(out_t.shape, jnp.bfloat16),
            pltpu.SemaphoreType.DMA((4,)),
        ]
    else:
        shapes = [
            jax.ShapeDtypeStruct((heads, 2, tokens), jnp.float32),
            jax.ShapeDtypeStruct((cols, tokens), jnp.float32),
        ]
    return pl.pallas_call(
        functools.partial(attend_body, chunk, tuple(s for _, s in sources), goes_on, ends),
        in_specs=[smem_spec()] * 3 + in_specs,
        out_specs=[vmem_spec()] * len(shapes),
        scratch_shapes=scratch,
        out_shape=shapes,
        compiler_params=params(),
        cost_estimate=pl.CostEstimate(
            flops=4 * cols * tokens * tokens * count,
            bytes_accessed=2 * cols * tokens * (2 + 2 * count),
            transcendentals=heads * tokens * tokens * count,
        ),
        name="attend",
    )(*tables, *arguments)


def summed(own, back, onward, across, at_end):
    total = own.astype(jnp.float32) + back.astype(jnp.float32) + onward.astype(jnp.float32)
    return (total + jnp.where(at_end, across.astype(jnp.float32), 0.0)).astype(jnp.bfloat16)


def place_body(seq_ref, order_ref, ends_ref, *refs):
    firsts, refs = refs[:PIECES], refs[PIECES:]
    parts, (out_ref, second_ref) = refs[:-2], refs[-2:]
    width, tokens = firsts[0].shape
    tiles_dev = 2 * tokens // TILE
    at_end = ends_ref[0] == 1
    for piece in range(PIECES):
        addends = [parts[4 * piece + index][...] for index in range(4)]
        second_ref[piece * width : (piece + 1) * width, :] = summed(*addends, at_end)
    ranks = [jnp.int32(0), jnp.int32(0)]
    for position in range(tiles_dev):
        late = order_ref[seq_ref[0] * tiles_dev + position] // tiles_dev
        spot = pl.ds(pl.multiple_of(jnp.where(late == 0, ranks[0], ranks[1]) * TILE, TILE), TILE)
        here = slice(position * TILE, (position + 1) * TILE)

        @pl.when(late == 0)
        def _(spot=spot, here=here):
            for piece in range(PIECES):
                out_ref[piece * width : (piece + 1) * width, here] = firsts[piece][:, spot]

        @pl.when(late == 1)
        def _(spot=spot, here=here):
            out_ref[:, here] = second_ref[:, spot]

        ranks[0] = ranks[0] + (1 - late)
        ranks[1] = ranks[1] + late


def place_call(seq_here, stripe_order, at_end, firsts, parts):
    width, tokens = firsts[0].shape
    channels = width * PIECES
    return pl.pallas_call(
        place_body,
        in_specs=[smem_spec()] * 3 + [vmem_spec()] * (5 * PIECES),
        out_specs=vmem_spec(),
        scratch_shapes=[pltpu.VMEM((channels, tokens), jnp.bfloat16)],
        out_shape=jax.ShapeDtypeStruct((channels, 2 * tokens), jnp.bfloat16),
        compiler_params=params(),
        cost_estimate=pl.CostEstimate(
            flops=4 * channels * tokens, bytes_accessed=14 * channels * tokens, transcendentals=0
        ),
        name="place",
    )(seq_here, stripe_order, at_end, *firsts, *[part for piece in parts for part in piece])


FORWARD = [(0, 1), (1, 2), (2, 3), (3, 0)]
BACKWARD = [(1, 0), (2, 1), (3, 2), (0, 3)]
FOLDED = [(0, 1), (1, 3), (3, 2), (2, 0)]
UNFOLDED = [(1, 0), (3, 1), (2, 3), (0, 2)]


def gather_blocks(block, here):
    before = lax.ppermute(block, "tp", FORWARD)
    after = lax.ppermute(block, "tp", BACKWARD)
    relay = jnp.where(here == 2, before, jnp.where(here == 1, after, block))
    across = lax.ppermute(relay, "tp", UNFOLDED)
    return (block, before, after, across)


def plus(a, b, chosen):
    summed = a.astype(jnp.float32) + jnp.where(chosen, b.astype(jnp.float32), 0.0)
    return summed.astype(jnp.bfloat16)


def reduce_blocks(partials, here):
    own, down, up, sent = partials
    across = lax.ppermute(sent, "tp", FOLDED)
    back = lax.ppermute(plus(down, across, here == 2), "tp", BACKWARD)
    onward = lax.ppermute(plus(up, across, here == 1), "tp", FORWARD)
    return (own, back, onward, across)


def per_device_fast(
    clip_tokens, conv_taps, norm_gain, qkv_weight, out_weight, tile_mask, stripe_order
):
    seq = lax.axis_index("seq")
    here = lax.axis_index("tp")
    seq_here = seq.astype(jnp.int32)[None]
    at_end = ((here == 0) | (here == 3)).astype(jnp.int32)[None]
    blocks = jnp.stack([here, (here + 3) % 4, (here + 1) % 4, (here + 2) % 4]).astype(jnp.int32)
    tables = (seq_here, stripe_order, tile_mask)
    pieces = range(PIECES)

    def gathered(blocks_here):
        by_piece = [gather_blocks(block, here) for block in blocks_here]
        return [by_piece[p][owner] for owner in range(4) for p in pieces]

    def reduced(partials):
        return [reduce_blocks(partials[p::PIECES], here) for p in pieces]

    begun = [conv_call(seq_here, stripe_order, clip_tokens, conv_taps, p) for p in pieces]
    tokens_a, before = [], []
    for _, keep, send, tokens in begun:
        got = lax.ppermute(send, "seq", [(0, 1)])
        tokens_a.append(jnp.where(seq == 0, keep, got))
        before.append(lax.ppermute(tokens, "seq", [(0, 1)]))
    weights, out_t = prepare_weights(blocks, norm_gain, qkv_weight, out_weight)
    shards_a = gathered(tokens_a)

    tokens_b = []
    for p in pieces:
        keep, send = conv_call(seq_here, stripe_order, before[p], conv_taps, p, begun[p][0])
        got = lax.ppermute(send, "seq", [(1, 0)])
        tokens_b.append(jnp.where(seq == 1, keep, got))

    swap = [(0, 1), (1, 0)]
    query_a, pair_a = project_call(weights, shards_a)
    peer_a = lax.ppermute(pair_a, "seq", swap)
    shards_b = gathered(tokens_b)
    partials_a = attend_call(0, tables, query_a, [(pair_a, 0), (peer_a, 1)], out_t=out_t)
    parts_a = reduced(partials_a)
    query_b, pair_b = project_call(weights, shards_b)
    peer_b = lax.ppermute(pair_b, "seq", swap)
    near = [(pair_a, 0), (peer_a, 1), (pair_b, 2)]
    state = attend_call(1, tables, query_b, near)
    partials_b = attend_call(1, tables, query_b, [(peer_b, 3)], state=state, out_t=out_t)
    parts_b = reduced(partials_b)
    firsts = [summed(*part, at_end == 1) for part in parts_a]
    return place_call(seq_here, stripe_order, at_end, firsts, parts_b)


def passed_along(block, axis, distance):
    devices = range(lax.axis_size(axis))
    route = [(i - distance, i) for i in devices if i - distance in devices]
    return lax.ppermute(block, axis, route)


def from_partner(block, axis, apart):
    count = lax.axis_size(axis)
    route = []
    for low in range(count):
        high = low | 1 << apart
        if high != low and high < count:
            route += [(low, high), (high, low)]
    return lax.ppermute(block, axis, route)


def causal_conv(local_tokens, before, conv_taps):
    channels = local_tokens.shape[0]
    frames = local_tokens.shape[1] // (FH * FW)
    stacked = (
        jnp.concatenate([before, local_tokens], axis=1)
        .astype(jnp.float32)
        .reshape(channels, frames + 2, FH, FW)
    )
    padded = jnp.pad(stacked, ((0, 0), (0, 0), (1, 1), (1, 1)))
    summed = jnp.zeros((channels, frames, FH, FW), jnp.float32)
    for time_off in range(3):
        for row_off in range(3):
            for col_off in range(3):
                tap_vec = conv_taps[time_off * 9 + row_off * 3 + col_off]
                summed = (
                    summed
                    + tap_vec[:, None, None, None]
                    * padded[
                        :,
                        time_off : time_off + frames,
                        row_off : row_off + FH,
                        col_off : col_off + FW,
                    ]
                )
    return (local_tokens.astype(jnp.float32) + summed.reshape(channels, -1)).astype(jnp.bfloat16)


def stripe_tables(stripe_order, tiles_dev):
    seq_count = lax.axis_size("seq")
    seq_here = lax.axis_index("seq")
    per_source = tiles_dev // seq_count
    blocks = stripe_order.reshape(seq_count, tiles_dev)
    owners = blocks // tiles_dev
    is_mine = (owners == seq_here).astype(jnp.int32)
    rank_of = jnp.cumsum(is_mine, axis=1) - 1
    slot_ids = jnp.arange(per_source, dtype=jnp.int32)
    picked = is_mine[:, None, :] * (rank_of[:, None, :] == slot_ids[None, :, None]).astype(
        jnp.int32
    )
    local_tiles = (blocks - seq_here * tiles_dev)[:, None, :]
    send_order = jnp.sum(picked * local_tiles, axis=2).reshape(-1)
    own_row = lax.dynamic_slice_in_dim(stripe_order, seq_here * tiles_dev, tiles_dev)
    sources = own_row // tiles_dev
    position = jnp.arange(tiles_dev, dtype=jnp.int32)
    earlier = (sources[:, None] == sources[None, :]) & (position[None, :] < position[:, None])
    place_order = sources * per_source + jnp.sum(earlier.astype(jnp.int32), axis=1)
    return (send_order, place_order, own_row)


def regroup(values, send_order, place_order):
    leading = values.shape[0]
    trailing = values.shape[2:]
    in_tiles = values.reshape((leading, values.shape[1] // TILE, TILE) + trailing)
    outgoing = jnp.take(in_tiles, send_order, axis=1)
    arrived = lax.all_to_all(outgoing, "seq", split_axis=1, concat_axis=1, tiled=True)
    placed = jnp.take(arrived, place_order, axis=1)
    return placed.reshape(values.shape)


def project(mixed, norm_gain, qkv_weight):
    channels = norm_gain.shape[0]
    widened = lax.all_gather(mixed, "tp", axis=0, tiled=True).astype(jnp.float32)
    scaled = (widened * norm_gain[:, None]).astype(jnp.bfloat16)
    projected = jnp.einsum("ct,khc->kth", scaled, qkv_weight, preferred_element_type=jnp.float32)
    squares = jnp.sum(widened * widened, axis=0)
    projected, squares = (projected, squares)
    inverse = lax.rsqrt(squares / channels + EPSILON)
    return (projected * inverse[None, :, None]).astype(jnp.bfloat16)


def position_mask(tile_mask, stripe_order, own_half):
    tiles_all = tile_mask.shape[0]
    tile_ids = jnp.arange(tiles_all, dtype=jnp.int32)
    own_onehot = (own_half[:, None] == tile_ids[None, :]).astype(jnp.float32)
    order_onehot = (stripe_order[:, None] == tile_ids[None, :]).astype(jnp.float32)
    rows_mask = jnp.dot(
        own_onehot, tile_mask.astype(jnp.float32), preferred_element_type=jnp.float32
    )
    return jnp.dot(rows_mask, order_onehot.T, preferred_element_type=jnp.float32)


def attend(queries_flat, key_values, pos_mask):
    row_count = queries_flat.shape[0]
    heads_dev = queries_flat.shape[1] // HEAD
    queries = queries_flat.reshape(row_count, heads_dev, HEAD)
    score_scale = 1.0 / math.sqrt(HEAD)
    tiles_dev = row_count // TILE
    tile_ids = jnp.arange(pos_mask.shape[1], dtype=jnp.int32)
    initial = (
        jnp.full((heads_dev, row_count), MASKED_SCORE, jnp.float32),
        jnp.zeros((heads_dev, row_count), jnp.float32),
        jnp.zeros((heads_dev, row_count, HEAD), jnp.float32),
    )
    fetched = lax.all_gather(key_values, "seq", axis=1, tiled=True)
    fetched_count = fetched.shape[1]
    key_block = 512

    def advance(block_index, state_now):
        top_score, denom, weighted = state_now
        offset = block_index * key_block
        key_rows = lax.dynamic_slice_in_dim(fetched[0], offset, key_block).reshape(
            key_block, heads_dev, HEAD
        )
        values = lax.dynamic_slice_in_dim(fetched[1], offset, key_block).reshape(
            key_block, heads_dev, HEAD
        )
        tile_pos = (offset + jnp.arange(key_block, dtype=jnp.int32)) // TILE
        onehot = (tile_pos[:, None] == tile_ids[None, :]).astype(jnp.float32)
        tile_allowed = (
            jnp.einsum("qn,kn->qk", pos_mask, onehot, preferred_element_type=jnp.float32) > 0.5
        )
        visible = jnp.broadcast_to(tile_allowed[:, None, :], (tiles_dev, TILE, key_block)).reshape(
            row_count, key_block
        )
        scores = (
            jnp.einsum("qhd,khd->hqk", queries, key_rows, preferred_element_type=jnp.float32)
            * score_scale
        )
        masked = jnp.where(visible[None], scores, MASKED_SCORE)
        new_top = jnp.maximum(top_score, jnp.max(masked, axis=2))
        powers = jnp.where(visible[None], jnp.exp(masked - new_top[:, :, None]), 0.0)
        shrink = jnp.exp(top_score - new_top)
        denom = denom * shrink + jnp.sum(powers, axis=2)
        weighted = weighted * shrink[:, :, None] + jnp.einsum(
            "hqk,khd->hqd", powers.astype(jnp.bfloat16), values, preferred_element_type=jnp.float32
        )
        return (new_top, denom, weighted)

    _, denom, weighted = lax.fori_loop(0, fetched_count // key_block, advance, initial)
    finished = (weighted / denom[:, :, None]).astype(jnp.bfloat16)
    return jnp.transpose(finished, (1, 0, 2)).reshape(row_count, heads_dev * HEAD)


def per_device_general(clip_tokens, conv_taps, norm_gain, qkv_weight, out_weight, tile_mask, stripe_order):
    tiles_dev = clip_tokens.shape[1] // TILE
    send_order, place_order, own_row = stripe_tables(stripe_order, tiles_dev)
    before = passed_along(clip_tokens, "seq", 1)
    mixed = causal_conv(clip_tokens, before, conv_taps)
    mixed = regroup(mixed, send_order, place_order)
    projected = project(mixed, norm_gain, qkv_weight)
    row_count = projected.shape[1]
    group_cols = projected.shape[2]
    half_rows = row_count // 2
    side = lax.axis_index("tp") % 2
    mine_first = side == 0
    query_send = lax.dynamic_slice_in_dim(projected[0], (1 - side) * half_rows, half_rows, axis=0)
    query_mine = lax.dynamic_slice_in_dim(projected[0], side * half_rows, half_rows, axis=0)
    kv_mine = projected[1:]
    query_other, kv_other = from_partner((query_send, kv_mine), "tp", 0)
    queries = jnp.where(
        mine_first,
        jnp.concatenate([query_mine, query_other], axis=1),
        jnp.concatenate([query_other, query_mine], axis=1),
    )
    key_values = jnp.where(
        mine_first,
        jnp.concatenate([kv_mine, kv_other], axis=2),
        jnp.concatenate([kv_other, kv_mine], axis=2),
    )
    own_half = lax.dynamic_slice_in_dim(own_row, side * (tiles_dev // 2), tiles_dev // 2)
    pos_mask = position_mask(tile_mask, stripe_order, own_half)
    pair_out = attend(queries, key_values, pos_mask)
    give_cols = lax.dynamic_slice_in_dim(pair_out, (1 - side) * group_cols, group_cols, axis=1)
    keep_cols = lax.dynamic_slice_in_dim(pair_out, side * group_cols, group_cols, axis=1)
    got_cols = from_partner(give_cols, "tp", 0)
    heads_out = jnp.where(
        mine_first,
        jnp.concatenate([keep_cols, got_cols], axis=0),
        jnp.concatenate([got_cols, keep_cols], axis=0),
    )
    return lax.psum_scatter(
        jnp.einsum("qg,gc->cq", heads_out, out_weight, preferred_element_type=jnp.float32).astype(
            jnp.bfloat16
        ),
        "tp",
        scatter_dimension=0,
        tiled=True,
    )


def solution(mesh):
    in_specs = (
        P("tp", ("dp", "seq")),
        P(None, "tp"),
        P(),
        P(None, "tp", None),
        P("tp", None),
        P(),
        P(),
    )
    out_specs = P("tp", ("dp", "seq"))

    def run(clip_tokens, conv_taps, norm_gain, qkv_weight, out_weight, tile_mask, stripe_order):
        arguments = (clip_tokens, conv_taps, norm_gain, qkv_weight, out_weight, tile_mask, stripe_order)
        tokens = clip_tokens.shape[1] // (mesh.shape["dp"] * mesh.shape["seq"])
        columns = qkv_weight.shape[1] // mesh.shape["tp"]
        two_halves = mesh.shape["seq"] == 2 and tokens == 2 * FRAME
        fast = two_halves and mesh.shape["tp"] == 4 and columns % HEAD == 0

        def per_device(*local):
            if not fast:
                return per_device_general(*local)
            return per_device_fast(*local)

        step = jax.shard_map(
            per_device, mesh=mesh, in_specs=in_specs, out_specs=out_specs, check_vma=False
        )
        return step(*arguments)

    return run
```

```python
import functools
import math

import jax
import jax.numpy as jnp
from jax import lax
from jax.experimental import pallas as pl
from jax.experimental.pallas import tpu as pltpu
from jax.sharding import PartitionSpec as P


HEAD = 128
TILE = 128
FH = 16
FW = 32
FRAME = FH * FW
TAPS = 27


EPSILON = 1e-06
MASKED_SCORE = -1e30
LOG2E = math.log2(math.e)

VMEM_LIMIT = 20 * 1024 * 1024
VMEM_FIRST = 52 * 1024 * 1024


def vmem_spec():
    return pl.BlockSpec(memory_space=pltpu.VMEM)


def smem_spec():
    return pl.BlockSpec(memory_space=pltpu.SMEM)


def params(limit=VMEM_LIMIT):
    return pltpu.CompilerParams(vmem_limit_bytes=limit)


def fetches(source, target, semaphores):
    block = target.shape[0] // semaphores.shape[0]
    return [
        pltpu.make_async_copy(
            source.at[index * block : (index + 1) * block],
            target.at[index * block : (index + 1) * block],
            semaphores.at[index],
        )
        for index in range(semaphores.shape[0])
    ]


def column_shifts(pieces, column):
    right = [jnp.where(column > 0, pltpu.roll(piece, 1, 1), 0.0) for piece in pieces]
    left = [jnp.where(column < FW - 1, pltpu.roll(piece, TILE - 1, 1), 0.0) for piece in pieces]
    return (right, pieces, left)


def rows_joined(rows, lane):
    down = [pltpu.roll(piece, FW, 1) for piece in rows[0]]
    up = [pltpu.roll(piece, TILE - FW, 1) for piece in rows[2]]
    joined = []
    for spot, middle in enumerate(rows[1]):
        before = down[spot - 1] if spot > 0 else 0.0
        after = up[spot + 1] if spot + 1 < len(up) else 0.0
        above = jnp.where(lane < FW, before, down[spot])
        below = jnp.where(lane >= TILE - FW, after, up[spot])
        joined.append(middle + (above + below))
    return joined


def pack_slots(order_ref, slots_ref, seq_here, tiles_dev, positions):
    half = tiles_dev // 2
    kept = jnp.int32(0)
    sent = jnp.int32(half)
    for position in range(positions):
        tile = order_ref[position]
        mine = tile // tiles_dev == seq_here
        stays = jnp.int32(position // tiles_dev) == seq_here
        slot = jnp.where(stays, kept, sent)

        @pl.when(mine)
        def _(tile=tile, slot=slot):
            slots_ref[tile - seq_here * tiles_dev] = slot

        step = mine.astype(jnp.int32)
        kept = kept + jnp.where(stays, step, 0)
        sent = sent + jnp.where(stays, 0, step)


GROUP = 16
CHUNKS = 4
PIECES = 2


def conv_body(with_before, first_row, seq_ref, order_ref, tokens_ref, taps_ref, part_ref, keep_ref, send_ref, *refs):
    if with_before:
        slots_ref, taps_scr, packed = refs
        source_ref = tokens_ref
    else:
        source_ref, slots_ref, taps_scr, packed, arrived = refs
    channels, tokens = packed.shape
    tiles_dev = tokens // TILE
    per_frame = FRAME // TILE
    if not with_before:
        copies = fetches(tokens_ref.at[first_row : first_row + channels], source_ref, arrived)
        for copy in copies:
            copy.start()
    pack_slots(order_ref, slots_ref, seq_ref[0], tiles_dev, order_ref.shape[0])
    for first in range(0, channels, TILE):
        from_row = first_row + first
        taps_scr[first : first + TILE, :TAPS] = taps_ref[:, from_row : from_row + TILE].T
    lane = lax.broadcasted_iota(jnp.int32, (GROUP, TILE), 1)
    column = lane % FW
    if with_before:
        reads = ([(0, 0), (1, 1)], [(0, 1)])
    else:
        reads = ([(2, 0)], [(1, 0), (2, 1)])

    def advance(step, carry, base=0):
        rows = pl.ds(pl.multiple_of(base + step * GROUP, GROUP), GROUP)
        taps = taps_scr[rows, :]
        shifts = []
        for frame in range(2):
            pieces = []
            for spot in range(per_frame):
                tile = frame * per_frame + spot
                pieces.append(source_ref[rows, tile * TILE : (tile + 1) * TILE].astype(jnp.float32))
            shifts.append(column_shifts(pieces, column))
        for frame in range(2):
            sums = []
            for row_off in range(3):
                line = [None] * per_frame
                for time_off, read in reads[frame]:
                    for col_off in range(3):
                        tap = time_off * 9 + row_off * 3 + col_off
                        weight = jnp.broadcast_to(taps[:, tap : tap + 1], (GROUP, TILE))
                        for spot in range(per_frame):
                            term = weight * shifts[read][col_off][spot]
                            line[spot] = term if line[spot] is None else line[spot] + term
                sums.append(line)
            for spot, value in enumerate(rows_joined(sums, lane)):
                tile = frame * per_frame + spot
                here = slice(tile * TILE, (tile + 1) * TILE)
                if with_before:
                    value = value + part_ref[rows, here]
                else:
                    value = value + shifts[frame][1][spot]
                    part_ref[rows, here] = value
                place = pl.ds(pl.multiple_of(slots_ref[tile] * TILE, TILE), TILE)
                packed[rows, place] = value.astype(jnp.bfloat16)
        return carry

    steps = channels // GROUP
    if with_before:
        lax.fori_loop(0, steps, advance, 0, unroll=2)
    else:
        each = steps // CHUNKS

        def chunk(index, carry):
            begin = index * each * GROUP
            pltpu.make_async_copy(
                tokens_ref.at[pl.ds(first_row + begin, each * GROUP)],
                source_ref.at[pl.ds(begin, each * GROUP)],
                arrived.at[index],
            ).wait()
            later = functools.partial(advance, base=begin)
            return lax.fori_loop(0, each, later, carry, unroll=2)

        lax.fori_loop(0, CHUNKS, chunk, 0)
    keep_ref[...] = packed[:, : tokens // 2]
    send_ref[...] = packed[:, tokens // 2 :]


def conv_call(seq_here, stripe_order, tokens, conv_taps, piece, part=None):
    count = tokens.shape[1]
    channels = conv_taps.shape[1] // PIECES
    packed_shape = jax.ShapeDtypeStruct((channels, count // 2), jnp.bfloat16)
    with_before = part is not None
    out_shape = [packed_shape, packed_shape]
    scratch = [
        pltpu.SMEM((count // TILE,), jnp.int32),
        pltpu.VMEM((channels, 128), jnp.float32),
        pltpu.VMEM((channels, count), jnp.bfloat16),
    ]
    in_specs = [smem_spec(), smem_spec(), vmem_spec(), vmem_spec(), vmem_spec()]
    if not with_before:
        in_specs = [smem_spec(), smem_spec(), pl.BlockSpec(memory_space=pl.ANY), vmem_spec()]
        sum_shape = jax.ShapeDtypeStruct((channels, count), jnp.float32)
        out_shape = [sum_shape] + out_shape + [jax.ShapeDtypeStruct((channels, count), jnp.bfloat16)]
        scratch += [pltpu.SemaphoreType.DMA((CHUNKS,))]
    return pl.pallas_call(
        functools.partial(conv_body, with_before, piece * channels),
        in_specs=in_specs,
        out_specs=[vmem_spec()] * len(out_shape),
        scratch_shapes=scratch,
        out_shape=out_shape,
        compiler_params=params(VMEM_LIMIT if with_before else VMEM_FIRST),
        cost_estimate=pl.CostEstimate(
            flops=channels * count * TAPS, bytes_accessed=channels * count * 8, transcendentals=0
        ),
        name="conv",
    )(seq_here, stripe_order, tokens, conv_taps, *([part] if with_before else []))


def prepare_body(blocks_ref, out_ref, out_out):
    out_out[...] = out_ref[...].T


def prepare_out(blocks, out_weight):
    cols, channels = out_weight.shape
    count = blocks.shape[0]
    width = channels // count
    return pl.pallas_call(
        prepare_body,
        grid_spec=pltpu.PrefetchScalarGridSpec(
            num_scalar_prefetch=1,
            grid=(count,),
            in_specs=[pl.BlockSpec((cols, width), lambda j, b: (0, b[j]))],
            out_specs=pl.BlockSpec((width, cols), lambda j, b: (j, 0)),
        ),
        out_shape=jax.ShapeDtypeStruct((channels, cols), jnp.bfloat16),
        compiler_params=params(),
        cost_estimate=pl.CostEstimate(
            flops=cols * channels, bytes_accessed=4 * cols * channels, transcendentals=0
        ),
        name="prepare",
    )(blocks, out_weight)


def project_body(blocks_ref, weight_ref, gains_ref, *refs):
    shards, (query_ref, pair_ref, tokens_ref) = refs[:-3], refs[-3:]
    width, tokens = shards[0].shape
    cols = query_ref.shape[0]
    lines = 128
    squares = jnp.zeros((1, tokens), jnp.float32)
    for index, shard in enumerate(shards):
        owner, piece = divmod(index, PIECES)
        start = (blocks_ref[owner] * PIECES + piece) * width
        for first in range(0, width, lines):
            there = pl.ds(pl.multiple_of(start + first, lines), lines)
            wide = shard[first : first + lines, :].astype(jnp.float32)
            squares = squares + jnp.sum(wide * wide, axis=0, keepdims=True)
            gain = jnp.concatenate([gains_ref[there, :]] * (tokens // 128), axis=1)
            tokens_ref[there, :] = (wide * gain).astype(jnp.bfloat16)
    inverse = lax.rsqrt(squares / (len(shards) * width) + EPSILON)
    rows = 256
    for index in range(weight_ref.shape[0] // rows):
        here = slice(index * rows, (index + 1) * rows)
        total = jnp.dot(weight_ref[here, :], tokens_ref[...], preferred_element_type=jnp.float32)
        if index * rows < cols:
            query_ref[here, :] = (total * (inverse * (LOG2E / math.sqrt(HEAD)))).astype(jnp.bfloat16)
        else:
            there = slice(index * rows - cols, (index + 1) * rows - cols)
            pair_ref[there, :] = (total * inverse).astype(jnp.bfloat16)


def project_call(blocks, weights, gains, shards):
    rows, channels = weights.shape
    tokens = shards[0].shape[1]
    cols = rows // 3
    return pl.pallas_call(
        project_body,
        in_specs=[smem_spec()] + [vmem_spec()] * (2 + len(shards)),
        out_specs=[vmem_spec(), vmem_spec()],
        scratch_shapes=[pltpu.VMEM((channels, tokens), jnp.bfloat16)],
        out_shape=[
            jax.ShapeDtypeStruct((cols, tokens), jnp.bfloat16),
            jax.ShapeDtypeStruct((2 * cols, tokens), jnp.bfloat16),
        ],
        compiler_params=params(),
        cost_estimate=pl.CostEstimate(
            flops=2 * rows * channels * tokens,
            bytes_accessed=2 * (rows * channels + channels * tokens + rows * tokens),
            transcendentals=0,
        ),
        name="project",
    )(blocks, weights, gains, *shards)


def tile_lists(order_ref, ids_ref, seq_here, tiles_dev):
    half = tiles_dev // 2
    for block in range(2):
        first = jnp.int32(0)
        second = jnp.int32(0)
        away = (jnp.int32(block) != seq_here).astype(jnp.int32)
        for spot in range(tiles_dev):
            tile = order_ref[block * tiles_dev + spot]
            late = tile // tiles_dev
            rank = jnp.where(late == 0, first, second)
            ids_ref[(2 * late + away) * half + rank] = tile
            first = first + (1 - late)
            second = second + late


def attend_body(chunk, sources, goes_on, ends, seq_ref, order_ref, mask_ref, query_ref, *refs):
    count = len(sources)
    pairs, refs = refs[:count], refs[count:]
    if goes_on:
        old_stats, old_weighted, *refs = refs
    if ends:
        weight_hbm, *refs = refs
        partial_refs, refs = refs[: 4 * PIECES], refs[4 * PIECES :]
        ids_ref, bias_ref, scores_ref, heads_ref, weight_ref, arrived = refs
        copies = fetches(weight_hbm, weight_ref, arrived)
        for copy in copies:
            copy.start()
    else:
        new_stats, new_weighted, ids_ref, bias_ref, scores_ref = refs
    cols, tokens = query_ref.shape
    half = tokens // TILE
    tile_lists(order_ref, ids_ref, seq_ref[0], 2 * half)
    lane_tile = lax.broadcasted_iota(jnp.int32, (1, tokens), 1) // TILE
    for index, source in enumerate(sources):
        for spot in range(half):
            key_tile = ids_ref[source * half + spot]
            bias = jnp.zeros((1, tokens), jnp.float32)
            for query_spot in range(half):
                query_tile = ids_ref[2 * chunk * half + query_spot]
                blocked = jnp.where(mask_ref[query_tile, key_tile] == 1, 0.0, MASKED_SCORE)
                bias = jnp.where(lane_tile == query_spot, blocked, bias)
            bias_ref[index * half + spot : index * half + spot + 1, :] = bias

    def one_head(head, carry):
        rows = pl.ds(pl.multiple_of(head * HEAD, HEAD), HEAD)
        value_rows = pl.ds(pl.multiple_of(cols + head * HEAD, HEAD), HEAD)
        query = query_ref[rows, :]
        old_top = old_stats[head, 0:1, :] if goes_on else None
        top = old_top
        for index in range(count):
            block = jnp.dot(pairs[index][rows, :].T, query, preferred_element_type=jnp.float32)
            for spot in range(half):
                line = index * half + spot
                piece = block[spot * TILE : (spot + 1) * TILE, :] + bias_ref[line : line + 1, :]
                scores_ref[line * TILE : (line + 1) * TILE, :] = piece
                best = jnp.max(piece, axis=0, keepdims=True)
                top = best if top is None else jnp.maximum(top, best)
        denom = None
        weighted = None
        if goes_on:
            shrink = jnp.exp2(old_top - top)
            denom = old_stats[head, 1:2, :] * shrink
            weighted = old_weighted[rows, :] * shrink
        for index in range(count):
            powers = jnp.exp2(scores_ref[index * tokens : (index + 1) * tokens, :] - top)
            summed = jnp.sum(powers, axis=0, keepdims=True)
            term = jnp.dot(
                pairs[index][value_rows, :],
                powers.astype(jnp.bfloat16),
                preferred_element_type=jnp.float32,
            )
            denom = summed if denom is None else denom + summed
            weighted = term if weighted is None else weighted + term
        if ends:
            heads_ref[rows, :] = (weighted / denom).astype(jnp.bfloat16)
        else:
            new_stats[head, 0:1, :] = top
            new_stats[head, 1:2, :] = denom
            new_weighted[rows, :] = weighted
        return carry

    lax.fori_loop(0, cols // HEAD, one_head, 0)
    if ends:
        width = weight_ref.shape[0] // (4 * PIECES)
        for copy in copies:
            copy.wait()
        for index, out in enumerate(partial_refs):
            block = weight_ref[index * width : (index + 1) * width, :]
            out[...] = jnp.dot(
                block, heads_ref[...], preferred_element_type=jnp.float32
            ).astype(jnp.bfloat16)


def attend_call(chunk, tables, queries, sources, state=None, out_t=None):
    cols, tokens = queries.shape
    heads = cols // HEAD
    count = len(sources)
    half = tokens // TILE
    goes_on, ends = state is not None, out_t is not None
    arguments = [queries] + [array for array, _ in sources] + (list(state) if goes_on else [])
    in_specs = [vmem_spec()] * len(arguments)
    scratch = [
        pltpu.SMEM((4 * half,), jnp.int32),
        pltpu.VMEM((count * half, tokens), jnp.float32),
        pltpu.VMEM((count * tokens, tokens), jnp.float32),
    ]
    if ends:
        in_specs += [pl.BlockSpec(memory_space=pltpu.HBM)]
        arguments += [out_t]
        width = out_t.shape[0] // (4 * PIECES)
        shapes = [jax.ShapeDtypeStruct((width, tokens), jnp.bfloat16)] * (4 * PIECES)
        scratch += [
            pltpu.VMEM((cols, tokens), jnp.bfloat16),
            pltpu.VMEM(out_t.shape, jnp.bfloat16),
            pltpu.SemaphoreType.DMA((4,)),
        ]
    else:
        shapes = [
            jax.ShapeDtypeStruct((heads, 2, tokens), jnp.float32),
            jax.ShapeDtypeStruct((cols, tokens), jnp.float32),
        ]
    return pl.pallas_call(
        functools.partial(attend_body, chunk, tuple(s for _, s in sources), goes_on, ends),
        in_specs=[smem_spec()] * 3 + in_specs,
        out_specs=[vmem_spec()] * len(shapes),
        scratch_shapes=scratch,
        out_shape=shapes,
        compiler_params=params(),
        cost_estimate=pl.CostEstimate(
            flops=4 * cols * tokens * tokens * count,
            bytes_accessed=2 * cols * tokens * (2 + 2 * count),
            transcendentals=heads * tokens * tokens * count,
        ),
        name="attend",
    )(*tables, *arguments)


def summed(own, back, onward, across, at_end):
    total = own.astype(jnp.float32) + back.astype(jnp.float32) + onward.astype(jnp.float32)
    return (total + jnp.where(at_end, across.astype(jnp.float32), 0.0)).astype(jnp.bfloat16)


def place_body(seq_ref, order_ref, ends_ref, *refs):
    firsts, refs = refs[:PIECES], refs[PIECES:]
    parts, (out_ref, second_ref) = refs[:-2], refs[-2:]
    width, tokens = firsts[0].shape
    tiles_dev = 2 * tokens // TILE
    at_end = ends_ref[0] == 1
    for piece in range(PIECES):
        addends = [parts[4 * piece + index][...] for index in range(4)]
        second_ref[piece * width : (piece + 1) * width, :] = summed(*addends, at_end)
    ranks = [jnp.int32(0), jnp.int32(0)]
    for position in range(tiles_dev):
        late = order_ref[seq_ref[0] * tiles_dev + position] // tiles_dev
        spot = pl.ds(pl.multiple_of(jnp.where(late == 0, ranks[0], ranks[1]) * TILE, TILE), TILE)
        here = slice(position * TILE, (position + 1) * TILE)

        @pl.when(late == 0)
        def _(spot=spot, here=here):
            for piece in range(PIECES):
                out_ref[piece * width : (piece + 1) * width, here] = firsts[piece][:, spot]

        @pl.when(late == 1)
        def _(spot=spot, here=here):
            out_ref[:, here] = second_ref[:, spot]

        ranks[0] = ranks[0] + (1 - late)
        ranks[1] = ranks[1] + late


def place_call(seq_here, stripe_order, at_end, firsts, parts):
    width, tokens = firsts[0].shape
    channels = width * PIECES
    return pl.pallas_call(
        place_body,
        in_specs=[smem_spec()] * 3 + [vmem_spec()] * (5 * PIECES),
        out_specs=vmem_spec(),
        scratch_shapes=[pltpu.VMEM((channels, tokens), jnp.bfloat16)],
        out_shape=jax.ShapeDtypeStruct((channels, 2 * tokens), jnp.bfloat16),
        compiler_params=params(),
        cost_estimate=pl.CostEstimate(
            flops=4 * channels * tokens, bytes_accessed=14 * channels * tokens, transcendentals=0
        ),
        name="place",
    )(seq_here, stripe_order, at_end, *firsts, *[part for piece in parts for part in piece])


FORWARD = [(0, 1), (1, 2), (2, 3), (3, 0)]
BACKWARD = [(1, 0), (2, 1), (3, 2), (0, 3)]
FOLDED = [(0, 1), (1, 3), (3, 2), (2, 0)]
UNFOLDED = [(1, 0), (3, 1), (2, 3), (0, 2)]


def gather_blocks(block, here):
    before = lax.ppermute(block, "tp", FORWARD)
    after = lax.ppermute(block, "tp", BACKWARD)
    relay = jnp.where(here == 2, before, jnp.where(here == 1, after, block))
    across = lax.ppermute(relay, "tp", UNFOLDED)
    return (block, before, after, across)


def plus(a, b, chosen):
    summed = a.astype(jnp.float32) + jnp.where(chosen, b.astype(jnp.float32), 0.0)
    return summed.astype(jnp.bfloat16)


def reduce_blocks(partials, here):
    own, down, up, sent = partials
    across = lax.ppermute(sent, "tp", FOLDED)
    back = lax.ppermute(plus(down, across, here == 2), "tp", BACKWARD)
    onward = lax.ppermute(plus(up, across, here == 1), "tp", FORWARD)
    return (own, back, onward, across)


def per_device_fast(
    clip_tokens, conv_taps, norm_gain, qkv_weight, out_weight, tile_mask, stripe_order
):
    seq = lax.axis_index("seq")
    here = lax.axis_index("tp")
    seq_here = seq.astype(jnp.int32)[None]
    at_end = ((here == 0) | (here == 3)).astype(jnp.int32)[None]
    blocks = jnp.stack([here, (here + 3) % 4, (here + 1) % 4, (here + 2) % 4]).astype(jnp.int32)
    tables = (seq_here, stripe_order, tile_mask)
    pieces = range(PIECES)

    def gathered(blocks_here):
        by_piece = [gather_blocks(block, here) for block in blocks_here]
        return [by_piece[p][owner] for owner in range(4) for p in pieces]

    def reduced(partials):
        return [reduce_blocks(partials[p::PIECES], here) for p in pieces]

    begun = [conv_call(seq_here, stripe_order, clip_tokens, conv_taps, p) for p in pieces]
    tokens_a, before = [], []
    for _, keep, send, tokens in begun:
        got = lax.ppermute(send, "seq", [(0, 1)])
        tokens_a.append(jnp.where(seq == 0, keep, got))
        before.append(lax.ppermute(tokens, "seq", [(0, 1)]))
    kinds, cols, channels = qkv_weight.shape
    weights = qkv_weight.reshape(kinds * cols, channels)
    gains = jnp.broadcast_to(norm_gain[:, None], (channels, 128))
    out_t = prepare_out(blocks, out_weight)
    shards_a = gathered(tokens_a)

    tokens_b = []
    for p in pieces:
        keep, send = conv_call(seq_here, stripe_order, before[p], conv_taps, p, begun[p][0])
        got = lax.ppermute(send, "seq", [(1, 0)])
        tokens_b.append(jnp.where(seq == 1, keep, got))

    swap = [(0, 1), (1, 0)]
    query_a, pair_a = project_call(blocks, weights, gains, shards_a)
    peer_a = lax.ppermute(pair_a, "seq", swap)
    shards_b = gathered(tokens_b)
    partials_a = attend_call(0, tables, query_a, [(pair_a, 0), (peer_a, 1)], out_t=out_t)
    parts_a = reduced(partials_a)
    query_b, pair_b = project_call(blocks, weights, gains, shards_b)
    peer_b = lax.ppermute(pair_b, "seq", swap)
    near = [(pair_a, 0), (peer_a, 1), (pair_b, 2)]
    state = attend_call(1, tables, query_b, near)
    partials_b = attend_call(1, tables, query_b, [(peer_b, 3)], state=state, out_t=out_t)
    parts_b = reduced(partials_b)
    firsts = [summed(*part, at_end == 1) for part in parts_a]
    return place_call(seq_here, stripe_order, at_end, firsts, parts_b)


def passed_along(block, axis, distance):
    devices = range(lax.axis_size(axis))
    route = [(i - distance, i) for i in devices if i - distance in devices]
    return lax.ppermute(block, axis, route)


def from_partner(block, axis, apart):
    count = lax.axis_size(axis)
    route = []
    for low in range(count):
        high = low | 1 << apart
        if high != low and high < count:
            route += [(low, high), (high, low)]
    return lax.ppermute(block, axis, route)


def causal_conv(local_tokens, before, conv_taps):
    channels = local_tokens.shape[0]
    frames = local_tokens.shape[1] // (FH * FW)
    stacked = (
        jnp.concatenate([before, local_tokens], axis=1)
        .astype(jnp.float32)
        .reshape(channels, frames + 2, FH, FW)
    )
    padded = jnp.pad(stacked, ((0, 0), (0, 0), (1, 1), (1, 1)))
    summed = jnp.zeros((channels, frames, FH, FW), jnp.float32)
    for time_off in range(3):
        for row_off in range(3):
            for col_off in range(3):
                tap_vec = conv_taps[time_off * 9 + row_off * 3 + col_off]
                summed = (
                    summed
                    + tap_vec[:, None, None, None]
                    * padded[
                        :,
                        time_off : time_off + frames,
                        row_off : row_off + FH,
                        col_off : col_off + FW,
                    ]
                )
    return (local_tokens.astype(jnp.float32) + summed.reshape(channels, -1)).astype(jnp.bfloat16)


def stripe_tables(stripe_order, tiles_dev):
    seq_count = lax.axis_size("seq")
    seq_here = lax.axis_index("seq")
    per_source = tiles_dev // seq_count
    blocks = stripe_order.reshape(seq_count, tiles_dev)
    owners = blocks // tiles_dev
    is_mine = (owners == seq_here).astype(jnp.int32)
    rank_of = jnp.cumsum(is_mine, axis=1) - 1
    slot_ids = jnp.arange(per_source, dtype=jnp.int32)
    picked = is_mine[:, None, :] * (rank_of[:, None, :] == slot_ids[None, :, None]).astype(
        jnp.int32
    )
    local_tiles = (blocks - seq_here * tiles_dev)[:, None, :]
    send_order = jnp.sum(picked * local_tiles, axis=2).reshape(-1)
    own_row = lax.dynamic_slice_in_dim(stripe_order, seq_here * tiles_dev, tiles_dev)
    sources = own_row // tiles_dev
    position = jnp.arange(tiles_dev, dtype=jnp.int32)
    earlier = (sources[:, None] == sources[None, :]) & (position[None, :] < position[:, None])
    place_order = sources * per_source + jnp.sum(earlier.astype(jnp.int32), axis=1)
    return (send_order, place_order, own_row)


def regroup(values, send_order, place_order):
    leading = values.shape[0]
    trailing = values.shape[2:]
    in_tiles = values.reshape((leading, values.shape[1] // TILE, TILE) + trailing)
    outgoing = jnp.take(in_tiles, send_order, axis=1)
    arrived = lax.all_to_all(outgoing, "seq", split_axis=1, concat_axis=1, tiled=True)
    placed = jnp.take(arrived, place_order, axis=1)
    return placed.reshape(values.shape)


def project(mixed, norm_gain, qkv_weight):
    channels = norm_gain.shape[0]
    widened = lax.all_gather(mixed, "tp", axis=0, tiled=True).astype(jnp.float32)
    scaled = (widened * norm_gain[:, None]).astype(jnp.bfloat16)
    projected = jnp.einsum("ct,khc->kth", scaled, qkv_weight, preferred_element_type=jnp.float32)
    squares = jnp.sum(widened * widened, axis=0)
    projected, squares = (projected, squares)
    inverse = lax.rsqrt(squares / channels + EPSILON)
    return (projected * inverse[None, :, None]).astype(jnp.bfloat16)


def position_mask(tile_mask, stripe_order, own_half):
    tiles_all = tile_mask.shape[0]
    tile_ids = jnp.arange(tiles_all, dtype=jnp.int32)
    own_onehot = (own_half[:, None] == tile_ids[None, :]).astype(jnp.float32)
    order_onehot = (stripe_order[:, None] == tile_ids[None, :]).astype(jnp.float32)
    rows_mask = jnp.dot(
        own_onehot, tile_mask.astype(jnp.float32), preferred_element_type=jnp.float32
    )
    return jnp.dot(rows_mask, order_onehot.T, preferred_element_type=jnp.float32)


def attend(queries_flat, key_values, pos_mask):
    row_count = queries_flat.shape[0]
    heads_dev = queries_flat.shape[1] // HEAD
    queries = queries_flat.reshape(row_count, heads_dev, HEAD)
    score_scale = 1.0 / math.sqrt(HEAD)
    tiles_dev = row_count // TILE
    tile_ids = jnp.arange(pos_mask.shape[1], dtype=jnp.int32)
    initial = (
        jnp.full((heads_dev, row_count), MASKED_SCORE, jnp.float32),
        jnp.zeros((heads_dev, row_count), jnp.float32),
        jnp.zeros((heads_dev, row_count, HEAD), jnp.float32),
    )
    fetched = lax.all_gather(key_values, "seq", axis=1, tiled=True)
    fetched_count = fetched.shape[1]
    key_block = 512

    def advance(block_index, state_now):
        top_score, denom, weighted = state_now
        offset = block_index * key_block
        key_rows = lax.dynamic_slice_in_dim(fetched[0], offset, key_block).reshape(
            key_block, heads_dev, HEAD
        )
        values = lax.dynamic_slice_in_dim(fetched[1], offset, key_block).reshape(
            key_block, heads_dev, HEAD
        )
        tile_pos = (offset + jnp.arange(key_block, dtype=jnp.int32)) // TILE
        onehot = (tile_pos[:, None] == tile_ids[None, :]).astype(jnp.float32)
        tile_allowed = (
            jnp.einsum("qn,kn->qk", pos_mask, onehot, preferred_element_type=jnp.float32) > 0.5
        )
        visible = jnp.broadcast_to(tile_allowed[:, None, :], (tiles_dev, TILE, key_block)).reshape(
            row_count, key_block
        )
        scores = (
            jnp.einsum("qhd,khd->hqk", queries, key_rows, preferred_element_type=jnp.float32)
            * score_scale
        )
        masked = jnp.where(visible[None], scores, MASKED_SCORE)
        new_top = jnp.maximum(top_score, jnp.max(masked, axis=2))
        powers = jnp.where(visible[None], jnp.exp(masked - new_top[:, :, None]), 0.0)
        shrink = jnp.exp(top_score - new_top)
        denom = denom * shrink + jnp.sum(powers, axis=2)
        weighted = weighted * shrink[:, :, None] + jnp.einsum(
            "hqk,khd->hqd", powers.astype(jnp.bfloat16), values, preferred_element_type=jnp.float32
        )
        return (new_top, denom, weighted)

    _, denom, weighted = lax.fori_loop(0, fetched_count // key_block, advance, initial)
    finished = (weighted / denom[:, :, None]).astype(jnp.bfloat16)
    return jnp.transpose(finished, (1, 0, 2)).reshape(row_count, heads_dev * HEAD)


def per_device_general(clip_tokens, conv_taps, norm_gain, qkv_weight, out_weight, tile_mask, stripe_order):
    tiles_dev = clip_tokens.shape[1] // TILE
    send_order, place_order, own_row = stripe_tables(stripe_order, tiles_dev)
    before = passed_along(clip_tokens, "seq", 1)
    mixed = causal_conv(clip_tokens, before, conv_taps)
    mixed = regroup(mixed, send_order, place_order)
    projected = project(mixed, norm_gain, qkv_weight)
    row_count = projected.shape[1]
    group_cols = projected.shape[2]
    half_rows = row_count // 2
    side = lax.axis_index("tp") % 2
    mine_first = side == 0
    query_send = lax.dynamic_slice_in_dim(projected[0], (1 - side) * half_rows, half_rows, axis=0)
    query_mine = lax.dynamic_slice_in_dim(projected[0], side * half_rows, half_rows, axis=0)
    kv_mine = projected[1:]
    query_other, kv_other = from_partner((query_send, kv_mine), "tp", 0)
    queries = jnp.where(
        mine_first,
        jnp.concatenate([query_mine, query_other], axis=1),
        jnp.concatenate([query_other, query_mine], axis=1),
    )
    key_values = jnp.where(
        mine_first,
        jnp.concatenate([kv_mine, kv_other], axis=2),
        jnp.concatenate([kv_other, kv_mine], axis=2),
    )
    own_half = lax.dynamic_slice_in_dim(own_row, side * (tiles_dev // 2), tiles_dev // 2)
    pos_mask = position_mask(tile_mask, stripe_order, own_half)
    pair_out = attend(queries, key_values, pos_mask)
    give_cols = lax.dynamic_slice_in_dim(pair_out, (1 - side) * group_cols, group_cols, axis=1)
    keep_cols = lax.dynamic_slice_in_dim(pair_out, side * group_cols, group_cols, axis=1)
    got_cols = from_partner(give_cols, "tp", 0)
    heads_out = jnp.where(
        mine_first,
        jnp.concatenate([keep_cols, got_cols], axis=0),
        jnp.concatenate([got_cols, keep_cols], axis=0),
    )
    return lax.psum_scatter(
        jnp.einsum("qg,gc->cq", heads_out, out_weight, preferred_element_type=jnp.float32).astype(
            jnp.bfloat16
        ),
        "tp",
        scatter_dimension=0,
        tiled=True,
    )


def solution(mesh):
    in_specs = (
        P("tp", ("dp", "seq")),
        P(None, "tp"),
        P(),
        P(None, "tp", None),
        P("tp", None),
        P(),
        P(),
    )
    out_specs = P("tp", ("dp", "seq"))

    def run(clip_tokens, conv_taps, norm_gain, qkv_weight, out_weight, tile_mask, stripe_order):
        arguments = (clip_tokens, conv_taps, norm_gain, qkv_weight, out_weight, tile_mask, stripe_order)
        tokens = clip_tokens.shape[1] // (mesh.shape["dp"] * mesh.shape["seq"])
        columns = qkv_weight.shape[1] // mesh.shape["tp"]
        two_halves = mesh.shape["seq"] == 2 and tokens == 2 * FRAME
        fast = two_halves and mesh.shape["tp"] == 4 and columns % HEAD == 0

        def per_device(*local):
            if not fast:
                return per_device_general(*local)
            return per_device_fast(*local)

        step = jax.shard_map(
            per_device, mesh=mesh, in_specs=in_specs, out_specs=out_specs, check_vma=False
        )
        return step(*arguments)

    return run
```

```python
import functools
import math

import jax
import jax.numpy as jnp
from jax import lax
from jax.experimental import pallas as pl
from jax.experimental.pallas import tpu as pltpu
from jax.sharding import PartitionSpec as P


HEAD = 128
TILE = 128
FH = 16
FW = 32
FRAME = FH * FW
TAPS = 27


EPSILON = 1e-06
MASKED_SCORE = -1e30
LOG2E = math.log2(math.e)

VMEM_LIMIT = 20 * 1024 * 1024
VMEM_FIRST = 52 * 1024 * 1024
VMEM_PROJECT = 55 * 1024 * 1024


def vmem_spec():
    return pl.BlockSpec(memory_space=pltpu.VMEM)


def smem_spec():
    return pl.BlockSpec(memory_space=pltpu.SMEM)


def params(limit=VMEM_LIMIT):
    return pltpu.CompilerParams(vmem_limit_bytes=limit)


def fetches(source, target, semaphores):
    block = target.shape[0] // semaphores.shape[0]
    return [
        pltpu.make_async_copy(
            source.at[index * block : (index + 1) * block],
            target.at[index * block : (index + 1) * block],
            semaphores.at[index],
        )
        for index in range(semaphores.shape[0])
    ]


def column_shifts(pieces, column):
    right = [jnp.where(column > 0, pltpu.roll(piece, 1, 1), 0.0) for piece in pieces]
    left = [jnp.where(column < FW - 1, pltpu.roll(piece, TILE - 1, 1), 0.0) for piece in pieces]
    return (right, pieces, left)


def rows_joined(rows, lane):
    down = [pltpu.roll(piece, FW, 1) for piece in rows[0]]
    up = [pltpu.roll(piece, TILE - FW, 1) for piece in rows[2]]
    joined = []
    for spot, middle in enumerate(rows[1]):
        before = down[spot - 1] if spot > 0 else 0.0
        after = up[spot + 1] if spot + 1 < len(up) else 0.0
        above = jnp.where(lane < FW, before, down[spot])
        below = jnp.where(lane >= TILE - FW, after, up[spot])
        joined.append(middle + (above + below))
    return joined


def pack_slots(order_ref, slots_ref, seq_here, tiles_dev, positions):
    half = tiles_dev // 2
    kept = jnp.int32(0)
    sent = jnp.int32(half)
    for position in range(positions):
        tile = order_ref[position]
        mine = tile // tiles_dev == seq_here
        stays = jnp.int32(position // tiles_dev) == seq_here
        slot = jnp.where(stays, kept, sent)

        @pl.when(mine)
        def _(tile=tile, slot=slot):
            slots_ref[tile - seq_here * tiles_dev] = slot

        step = mine.astype(jnp.int32)
        kept = kept + jnp.where(stays, step, 0)
        sent = sent + jnp.where(stays, 0, step)


GROUP = 16
CHUNKS = 4
PIECES = 2


def conv_body(with_before, first_row, seq_ref, order_ref, tokens_ref, taps_ref, part_ref, keep_ref, send_ref, *refs):
    if with_before:
        slots_ref, taps_scr, packed = refs
        source_ref = tokens_ref
    else:
        source_ref, slots_ref, taps_scr, packed, arrived = refs
    channels, tokens = packed.shape
    tiles_dev = tokens // TILE
    per_frame = FRAME // TILE
    if not with_before:
        copies = fetches(tokens_ref.at[first_row : first_row + channels], source_ref, arrived)
        for copy in copies:
            copy.start()
    pack_slots(order_ref, slots_ref, seq_ref[0], tiles_dev, order_ref.shape[0])
    for first in range(0, channels, TILE):
        from_row = first_row + first
        taps_scr[first : first + TILE, :TAPS] = taps_ref[:, from_row : from_row + TILE].T
    lane = lax.broadcasted_iota(jnp.int32, (GROUP, TILE), 1)
    column = lane % FW
    if with_before:
        reads = ([(0, 0), (1, 1)], [(0, 1)])
    else:
        reads = ([(2, 0)], [(1, 0), (2, 1)])

    def advance(step, carry, base=0):
        rows = pl.ds(pl.multiple_of(base + step * GROUP, GROUP), GROUP)
        taps = taps_scr[rows, :]
        shifts = []
        for frame in range(2):
            pieces = []
            for spot in range(per_frame):
                tile = frame * per_frame + spot
                pieces.append(source_ref[rows, tile * TILE : (tile + 1) * TILE].astype(jnp.float32))
            shifts.append(column_shifts(pieces, column))
        for frame in range(2):
            sums = []
            for row_off in range(3):
                line = [None] * per_frame
                for time_off, read in reads[frame]:
                    for col_off in range(3):
                        tap = time_off * 9 + row_off * 3 + col_off
                        weight = jnp.broadcast_to(taps[:, tap : tap + 1], (GROUP, TILE))
                        for spot in range(per_frame):
                            term = weight * shifts[read][col_off][spot]
                            line[spot] = term if line[spot] is None else line[spot] + term
                sums.append(line)
            for spot, value in enumerate(rows_joined(sums, lane)):
                tile = frame * per_frame + spot
                here = slice(tile * TILE, (tile + 1) * TILE)
                if with_before:
                    value = value + part_ref[rows, here]
                else:
                    value = value + shifts[frame][1][spot]
                    part_ref[rows, here] = value
                place = pl.ds(pl.multiple_of(slots_ref[tile] * TILE, TILE), TILE)
                packed[rows, place] = value.astype(jnp.bfloat16)
        return carry

    steps = channels // GROUP
    if with_before:
        lax.fori_loop(0, steps, advance, 0, unroll=2)
    else:
        each = steps // CHUNKS

        def chunk(index, carry):
            begin = index * each * GROUP
            pltpu.make_async_copy(
                tokens_ref.at[pl.ds(first_row + begin, each * GROUP)],
                source_ref.at[pl.ds(begin, each * GROUP)],
                arrived.at[index],
            ).wait()
            later = functools.partial(advance, base=begin)
            return lax.fori_loop(0, each, later, carry, unroll=2)

        lax.fori_loop(0, CHUNKS, chunk, 0)
    keep_ref[...] = packed[:, : tokens // 2]
    send_ref[...] = packed[:, tokens // 2 :]


def conv_call(seq_here, stripe_order, tokens, conv_taps, piece, part=None):
    count = tokens.shape[1]
    channels = conv_taps.shape[1] // PIECES
    packed_shape = jax.ShapeDtypeStruct((channels, count // 2), jnp.bfloat16)
    with_before = part is not None
    out_shape = [packed_shape, packed_shape]
    scratch = [
        pltpu.SMEM((count // TILE,), jnp.int32),
        pltpu.VMEM((channels, 128), jnp.float32),
        pltpu.VMEM((channels, count), jnp.bfloat16),
    ]
    in_specs = [smem_spec(), smem_spec(), vmem_spec(), vmem_spec(), vmem_spec()]
    if not with_before:
        in_specs = [smem_spec(), smem_spec(), pl.BlockSpec(memory_space=pl.ANY), vmem_spec()]
        sum_shape = jax.ShapeDtypeStruct((channels, count), jnp.float32)
        out_shape = [sum_shape] + out_shape + [jax.ShapeDtypeStruct((channels, count), jnp.bfloat16)]
        scratch += [pltpu.SemaphoreType.DMA((CHUNKS,))]
    return pl.pallas_call(
        functools.partial(conv_body, with_before, piece * channels),
        in_specs=in_specs,
        out_specs=[vmem_spec()] * len(out_shape),
        scratch_shapes=scratch,
        out_shape=out_shape,
        compiler_params=params(VMEM_LIMIT if with_before else VMEM_FIRST),
        cost_estimate=pl.CostEstimate(
            flops=channels * count * TAPS, bytes_accessed=channels * count * 8, transcendentals=0
        ),
        name="conv",
    )(seq_here, stripe_order, tokens, conv_taps, *([part] if with_before else []))


def prepare_body(blocks_ref, out_ref, out_out):
    out_out[...] = out_ref[...].T


def prepare_out(blocks, out_weight):
    cols, channels = out_weight.shape
    count = blocks.shape[0]
    width = channels // count
    return pl.pallas_call(
        prepare_body,
        grid_spec=pltpu.PrefetchScalarGridSpec(
            num_scalar_prefetch=1,
            grid=(count,),
            in_specs=[pl.BlockSpec((cols, width), lambda j, b: (0, b[j]))],
            out_specs=pl.BlockSpec((width, cols), lambda j, b: (j, 0)),
        ),
        out_shape=jax.ShapeDtypeStruct((channels, cols), jnp.bfloat16),
        compiler_params=params(),
        cost_estimate=pl.CostEstimate(
            flops=cols * channels, bytes_accessed=4 * cols * channels, transcendentals=0
        ),
        name="prepare",
    )(blocks, out_weight)


def project_body(blocks_ref, weight_hbm, gains_ref, *refs):
    shards, (query_ref, pair_ref, weight_ref, tokens_ref, arrived) = refs[:-5], refs[-5:]
    copies = fetches(weight_hbm, weight_ref, arrived)
    for copy in copies:
        copy.start()
    width, tokens = shards[0].shape
    cols = query_ref.shape[0]
    lines = 128
    squares = jnp.zeros((1, tokens), jnp.float32)
    for index, shard in enumerate(shards):
        owner, piece = divmod(index, PIECES)
        start = (blocks_ref[owner] * PIECES + piece) * width
        for first in range(0, width, lines):
            there = pl.ds(pl.multiple_of(start + first, lines), lines)
            wide = shard[first : first + lines, :].astype(jnp.float32)
            squares = squares + jnp.sum(wide * wide, axis=0, keepdims=True)
            gain = jnp.concatenate([gains_ref[there, :]] * (tokens // 128), axis=1)
            tokens_ref[there, :] = (wide * gain).astype(jnp.bfloat16)
    inverse = lax.rsqrt(squares / (len(shards) * width) + EPSILON)
    rows = weight_ref.shape[0] // len(copies)
    for index, copy in enumerate(copies):
        copy.wait()
        here = slice(index * rows, (index + 1) * rows)
        total = jnp.dot(weight_ref[here, :], tokens_ref[...], preferred_element_type=jnp.float32)
        if index * rows < cols:
            query_ref[here, :] = (total * (inverse * (LOG2E / math.sqrt(HEAD)))).astype(jnp.bfloat16)
        else:
            there = slice(index * rows - cols, (index + 1) * rows - cols)
            pair_ref[there, :] = (total * inverse).astype(jnp.bfloat16)


def project_call(blocks, weights, gains, shards):
    rows, channels = weights.shape
    tokens = shards[0].shape[1]
    cols = rows // 3
    return pl.pallas_call(
        project_body,
        in_specs=[smem_spec(), pl.BlockSpec(memory_space=pl.ANY)] + [vmem_spec()] * (1 + len(shards)),
        out_specs=[vmem_spec(), vmem_spec()],
        scratch_shapes=[
            pltpu.VMEM((rows, channels), jnp.bfloat16),
            pltpu.VMEM((channels, tokens), jnp.bfloat16),
            pltpu.SemaphoreType.DMA((6,)),
        ],
        out_shape=[
            jax.ShapeDtypeStruct((cols, tokens), jnp.bfloat16),
            jax.ShapeDtypeStruct((2 * cols, tokens), jnp.bfloat16),
        ],
        compiler_params=params(VMEM_PROJECT),
        cost_estimate=pl.CostEstimate(
            flops=2 * rows * channels * tokens,
            bytes_accessed=2 * (rows * channels + channels * tokens + rows * tokens),
            transcendentals=0,
        ),
        name="project",
    )(blocks, weights, gains, *shards)


def tile_lists(order_ref, ids_ref, seq_here, tiles_dev):
    half = tiles_dev // 2
    for block in range(2):
        first = jnp.int32(0)
        second = jnp.int32(0)
        away = (jnp.int32(block) != seq_here).astype(jnp.int32)
        for spot in range(tiles_dev):
            tile = order_ref[block * tiles_dev + spot]
            late = tile // tiles_dev
            rank = jnp.where(late == 0, first, second)
            ids_ref[(2 * late + away) * half + rank] = tile
            first = first + (1 - late)
            second = second + late


def attend_body(chunk, sources, goes_on, ends, seq_ref, order_ref, mask_ref, query_ref, *refs):
    count = len(sources)
    pairs, refs = refs[:count], refs[count:]
    if goes_on:
        old_stats, old_weighted, *refs = refs
    if ends:
        weight_hbm, *refs = refs
        partial_refs, refs = refs[: 4 * PIECES], refs[4 * PIECES :]
        ids_ref, bias_ref, scores_ref, heads_ref, weight_ref, arrived = refs
        copies = fetches(weight_hbm, weight_ref, arrived)
        for copy in copies:
            copy.start()
    else:
        new_stats, new_weighted, ids_ref, bias_ref, scores_ref = refs
    cols, tokens = query_ref.shape
    half = tokens // TILE
    tile_lists(order_ref, ids_ref, seq_ref[0], 2 * half)
    lane_tile = lax.broadcasted_iota(jnp.int32, (1, tokens), 1) // TILE
    for index, source in enumerate(sources):
        for spot in range(half):
            key_tile = ids_ref[source * half + spot]
            bias = jnp.zeros((1, tokens), jnp.float32)
            for query_spot in range(half):
                query_tile = ids_ref[2 * chunk * half + query_spot]
                blocked = jnp.where(mask_ref[query_tile, key_tile] == 1, 0.0, MASKED_SCORE)
                bias = jnp.where(lane_tile == query_spot, blocked, bias)
            bias_ref[index * half + spot : index * half + spot + 1, :] = bias

    def one_head(head, carry):
        rows = pl.ds(pl.multiple_of(head * HEAD, HEAD), HEAD)
        value_rows = pl.ds(pl.multiple_of(cols + head * HEAD, HEAD), HEAD)
        query = query_ref[rows, :]
        old_top = old_stats[head, 0:1, :] if goes_on else None
        top = old_top
        for index in range(count):
            block = jnp.dot(pairs[index][rows, :].T, query, preferred_element_type=jnp.float32)
            for spot in range(half):
                line = index * half + spot
                piece = block[spot * TILE : (spot + 1) * TILE, :] + bias_ref[line : line + 1, :]
                scores_ref[line * TILE : (line + 1) * TILE, :] = piece
                best = jnp.max(piece, axis=0, keepdims=True)
                top = best if top is None else jnp.maximum(top, best)
        denom = None
        weighted = None
        if goes_on:
            shrink = jnp.exp2(old_top - top)
            denom = old_stats[head, 1:2, :] * shrink
            weighted = old_weighted[rows, :] * shrink
        for index in range(count):
            powers = jnp.exp2(scores_ref[index * tokens : (index + 1) * tokens, :] - top)
            summed = jnp.sum(powers, axis=0, keepdims=True)
            term = jnp.dot(
                pairs[index][value_rows, :],
                powers.astype(jnp.bfloat16),
                preferred_element_type=jnp.float32,
            )
            denom = summed if denom is None else denom + summed
            weighted = term if weighted is None else weighted + term
        if ends:
            heads_ref[rows, :] = (weighted / denom).astype(jnp.bfloat16)
        else:
            new_stats[head, 0:1, :] = top
            new_stats[head, 1:2, :] = denom
            new_weighted[rows, :] = weighted
        return carry

    lax.fori_loop(0, cols // HEAD, one_head, 0)
    if ends:
        width = weight_ref.shape[0] // (4 * PIECES)
        for copy in copies:
            copy.wait()
        for index, out in enumerate(partial_refs):
            block = weight_ref[index * width : (index + 1) * width, :]
            out[...] = jnp.dot(
                block, heads_ref[...], preferred_element_type=jnp.float32
            ).astype(jnp.bfloat16)


def attend_call(chunk, tables, queries, sources, state=None, out_t=None):
    cols, tokens = queries.shape
    heads = cols // HEAD
    count = len(sources)
    half = tokens // TILE
    goes_on, ends = state is not None, out_t is not None
    arguments = [queries] + [array for array, _ in sources] + (list(state) if goes_on else [])
    in_specs = [vmem_spec()] * len(arguments)
    scratch = [
        pltpu.SMEM((4 * half,), jnp.int32),
        pltpu.VMEM((count * half, tokens), jnp.float32),
        pltpu.VMEM((count * tokens, tokens), jnp.float32),
    ]
    if ends:
        in_specs += [pl.BlockSpec(memory_space=pltpu.HBM)]
        arguments += [out_t]
        width = out_t.shape[0] // (4 * PIECES)
        shapes = [jax.ShapeDtypeStruct((width, tokens), jnp.bfloat16)] * (4 * PIECES)
        scratch += [
            pltpu.VMEM((cols, tokens), jnp.bfloat16),
            pltpu.VMEM(out_t.shape, jnp.bfloat16),
            pltpu.SemaphoreType.DMA((4,)),
        ]
    else:
        shapes = [
            jax.ShapeDtypeStruct((heads, 2, tokens), jnp.float32),
            jax.ShapeDtypeStruct((cols, tokens), jnp.float32),
        ]
    return pl.pallas_call(
        functools.partial(attend_body, chunk, tuple(s for _, s in sources), goes_on, ends),
        in_specs=[smem_spec()] * 3 + in_specs,
        out_specs=[vmem_spec()] * len(shapes),
        scratch_shapes=scratch,
        out_shape=shapes,
        compiler_params=params(),
        cost_estimate=pl.CostEstimate(
            flops=4 * cols * tokens * tokens * count,
            bytes_accessed=2 * cols * tokens * (2 + 2 * count),
            transcendentals=heads * tokens * tokens * count,
        ),
        name="attend",
    )(*tables, *arguments)


def summed(own, back, onward, across, at_end):
    total = own.astype(jnp.float32) + back.astype(jnp.float32) + onward.astype(jnp.float32)
    return (total + jnp.where(at_end, across.astype(jnp.float32), 0.0)).astype(jnp.bfloat16)


def place_body(seq_ref, order_ref, ends_ref, *refs):
    firsts, refs = refs[:PIECES], refs[PIECES:]
    parts, (out_ref, second_ref) = refs[:-2], refs[-2:]
    width, tokens = firsts[0].shape
    tiles_dev = 2 * tokens // TILE
    at_end = ends_ref[0] == 1
    for piece in range(PIECES):
        addends = [parts[4 * piece + index][...] for index in range(4)]
        second_ref[piece * width : (piece + 1) * width, :] = summed(*addends, at_end)
    ranks = [jnp.int32(0), jnp.int32(0)]
    for position in range(tiles_dev):
        late = order_ref[seq_ref[0] * tiles_dev + position] // tiles_dev
        spot = pl.ds(pl.multiple_of(jnp.where(late == 0, ranks[0], ranks[1]) * TILE, TILE), TILE)
        here = slice(position * TILE, (position + 1) * TILE)

        @pl.when(late == 0)
        def _(spot=spot, here=here):
            for piece in range(PIECES):
                out_ref[piece * width : (piece + 1) * width, here] = firsts[piece][:, spot]

        @pl.when(late == 1)
        def _(spot=spot, here=here):
            out_ref[:, here] = second_ref[:, spot]

        ranks[0] = ranks[0] + (1 - late)
        ranks[1] = ranks[1] + late


def place_call(seq_here, stripe_order, at_end, firsts, parts):
    width, tokens = firsts[0].shape
    channels = width * PIECES
    return pl.pallas_call(
        place_body,
        in_specs=[smem_spec()] * 3 + [vmem_spec()] * (5 * PIECES),
        out_specs=vmem_spec(),
        scratch_shapes=[pltpu.VMEM((channels, tokens), jnp.bfloat16)],
        out_shape=jax.ShapeDtypeStruct((channels, 2 * tokens), jnp.bfloat16),
        compiler_params=params(),
        cost_estimate=pl.CostEstimate(
            flops=4 * channels * tokens, bytes_accessed=14 * channels * tokens, transcendentals=0
        ),
        name="place",
    )(seq_here, stripe_order, at_end, *firsts, *[part for piece in parts for part in piece])


FORWARD = [(0, 1), (1, 2), (2, 3), (3, 0)]
BACKWARD = [(1, 0), (2, 1), (3, 2), (0, 3)]
FOLDED = [(0, 1), (1, 3), (3, 2), (2, 0)]
UNFOLDED = [(1, 0), (3, 1), (2, 3), (0, 2)]


def gather_blocks(block, here):
    before = lax.ppermute(block, "tp", FORWARD)
    after = lax.ppermute(block, "tp", BACKWARD)
    relay = jnp.where(here == 2, before, jnp.where(here == 1, after, block))
    across = lax.ppermute(relay, "tp", UNFOLDED)
    return (block, before, after, across)


def plus(a, b, chosen):
    summed = a.astype(jnp.float32) + jnp.where(chosen, b.astype(jnp.float32), 0.0)
    return summed.astype(jnp.bfloat16)


def reduce_blocks(partials, here):
    own, down, up, sent = partials
    across = lax.ppermute(sent, "tp", FOLDED)
    back = lax.ppermute(plus(down, across, here == 2), "tp", BACKWARD)
    onward = lax.ppermute(plus(up, across, here == 1), "tp", FORWARD)
    return (own, back, onward, across)


def per_device_fast(
    clip_tokens, conv_taps, norm_gain, qkv_weight, out_weight, tile_mask, stripe_order
):
    seq = lax.axis_index("seq")
    here = lax.axis_index("tp")
    seq_here = seq.astype(jnp.int32)[None]
    at_end = ((here == 0) | (here == 3)).astype(jnp.int32)[None]
    blocks = jnp.stack([here, (here + 3) % 4, (here + 1) % 4, (here + 2) % 4]).astype(jnp.int32)
    tables = (seq_here, stripe_order, tile_mask)
    pieces = range(PIECES)

    def gathered(blocks_here):
        by_piece = [gather_blocks(block, here) for block in blocks_here]
        return [by_piece[p][owner] for owner in range(4) for p in pieces]

    def reduced(partials):
        return [reduce_blocks(partials[p::PIECES], here) for p in pieces]

    begun = [conv_call(seq_here, stripe_order, clip_tokens, conv_taps, p) for p in pieces]
    tokens_a, before = [], []
    for _, keep, send, tokens in begun:
        got = lax.ppermute(send, "seq", [(0, 1)])
        tokens_a.append(jnp.where(seq == 0, keep, got))
        before.append(lax.ppermute(tokens, "seq", [(0, 1)]))
    kinds, cols, channels = qkv_weight.shape
    weights = qkv_weight.reshape(kinds * cols, channels)
    gains = jnp.broadcast_to(norm_gain[:, None], (channels, 128))
    out_t = prepare_out(blocks, out_weight)
    shards_a = gathered(tokens_a)

    tokens_b = []
    for p in pieces:
        keep, send = conv_call(seq_here, stripe_order, before[p], conv_taps, p, begun[p][0])
        got = lax.ppermute(send, "seq", [(1, 0)])
        tokens_b.append(jnp.where(seq == 1, keep, got))

    swap = [(0, 1), (1, 0)]
    query_a, pair_a = project_call(blocks, weights, gains, shards_a)
    peer_a = lax.ppermute(pair_a, "seq", swap)
    shards_b = gathered(tokens_b)
    partials_a = attend_call(0, tables, query_a, [(pair_a, 0), (peer_a, 1)], out_t=out_t)
    parts_a = reduced(partials_a)
    query_b, pair_b = project_call(blocks, weights, gains, shards_b)
    peer_b = lax.ppermute(pair_b, "seq", swap)
    near = [(pair_a, 0), (peer_a, 1), (pair_b, 2)]
    state = attend_call(1, tables, query_b, near)
    partials_b = attend_call(1, tables, query_b, [(peer_b, 3)], state=state, out_t=out_t)
    parts_b = reduced(partials_b)
    firsts = [summed(*part, at_end == 1) for part in parts_a]
    return place_call(seq_here, stripe_order, at_end, firsts, parts_b)


def passed_along(block, axis, distance):
    devices = range(lax.axis_size(axis))
    route = [(i - distance, i) for i in devices if i - distance in devices]
    return lax.ppermute(block, axis, route)


def from_partner(block, axis, apart):
    count = lax.axis_size(axis)
    route = []
    for low in range(count):
        high = low | 1 << apart
        if high != low and high < count:
            route += [(low, high), (high, low)]
    return lax.ppermute(block, axis, route)


def causal_conv(local_tokens, before, conv_taps):
    channels = local_tokens.shape[0]
    frames = local_tokens.shape[1] // (FH * FW)
    stacked = (
        jnp.concatenate([before, local_tokens], axis=1)
        .astype(jnp.float32)
        .reshape(channels, frames + 2, FH, FW)
    )
    padded = jnp.pad(stacked, ((0, 0), (0, 0), (1, 1), (1, 1)))
    summed = jnp.zeros((channels, frames, FH, FW), jnp.float32)
    for time_off in range(3):
        for row_off in range(3):
            for col_off in range(3):
                tap_vec = conv_taps[time_off * 9 + row_off * 3 + col_off]
                summed = (
                    summed
                    + tap_vec[:, None, None, None]
                    * padded[
                        :,
                        time_off : time_off + frames,
                        row_off : row_off + FH,
                        col_off : col_off + FW,
                    ]
                )
    return (local_tokens.astype(jnp.float32) + summed.reshape(channels, -1)).astype(jnp.bfloat16)


def stripe_tables(stripe_order, tiles_dev):
    seq_count = lax.axis_size("seq")
    seq_here = lax.axis_index("seq")
    per_source = tiles_dev // seq_count
    blocks = stripe_order.reshape(seq_count, tiles_dev)
    owners = blocks // tiles_dev
    is_mine = (owners == seq_here).astype(jnp.int32)
    rank_of = jnp.cumsum(is_mine, axis=1) - 1
    slot_ids = jnp.arange(per_source, dtype=jnp.int32)
    picked = is_mine[:, None, :] * (rank_of[:, None, :] == slot_ids[None, :, None]).astype(
        jnp.int32
    )
    local_tiles = (blocks - seq_here * tiles_dev)[:, None, :]
    send_order = jnp.sum(picked * local_tiles, axis=2).reshape(-1)
    own_row = lax.dynamic_slice_in_dim(stripe_order, seq_here * tiles_dev, tiles_dev)
    sources = own_row // tiles_dev
    position = jnp.arange(tiles_dev, dtype=jnp.int32)
    earlier = (sources[:, None] == sources[None, :]) & (position[None, :] < position[:, None])
    place_order = sources * per_source + jnp.sum(earlier.astype(jnp.int32), axis=1)
    return (send_order, place_order, own_row)


def regroup(values, send_order, place_order):
    leading = values.shape[0]
    trailing = values.shape[2:]
    in_tiles = values.reshape((leading, values.shape[1] // TILE, TILE) + trailing)
    outgoing = jnp.take(in_tiles, send_order, axis=1)
    arrived = lax.all_to_all(outgoing, "seq", split_axis=1, concat_axis=1, tiled=True)
    placed = jnp.take(arrived, place_order, axis=1)
    return placed.reshape(values.shape)


def project(mixed, norm_gain, qkv_weight):
    channels = norm_gain.shape[0]
    widened = lax.all_gather(mixed, "tp", axis=0, tiled=True).astype(jnp.float32)
    scaled = (widened * norm_gain[:, None]).astype(jnp.bfloat16)
    projected = jnp.einsum("ct,khc->kth", scaled, qkv_weight, preferred_element_type=jnp.float32)
    squares = jnp.sum(widened * widened, axis=0)
    projected, squares = (projected, squares)
    inverse = lax.rsqrt(squares / channels + EPSILON)
    return (projected * inverse[None, :, None]).astype(jnp.bfloat16)


def position_mask(tile_mask, stripe_order, own_half):
    tiles_all = tile_mask.shape[0]
    tile_ids = jnp.arange(tiles_all, dtype=jnp.int32)
    own_onehot = (own_half[:, None] == tile_ids[None, :]).astype(jnp.float32)
    order_onehot = (stripe_order[:, None] == tile_ids[None, :]).astype(jnp.float32)
    rows_mask = jnp.dot(
        own_onehot, tile_mask.astype(jnp.float32), preferred_element_type=jnp.float32
    )
    return jnp.dot(rows_mask, order_onehot.T, preferred_element_type=jnp.float32)


def attend(queries_flat, key_values, pos_mask):
    row_count = queries_flat.shape[0]
    heads_dev = queries_flat.shape[1] // HEAD
    queries = queries_flat.reshape(row_count, heads_dev, HEAD)
    score_scale = 1.0 / math.sqrt(HEAD)
    tiles_dev = row_count // TILE
    tile_ids = jnp.arange(pos_mask.shape[1], dtype=jnp.int32)
    initial = (
        jnp.full((heads_dev, row_count), MASKED_SCORE, jnp.float32),
        jnp.zeros((heads_dev, row_count), jnp.float32),
        jnp.zeros((heads_dev, row_count, HEAD), jnp.float32),
    )
    fetched = lax.all_gather(key_values, "seq", axis=1, tiled=True)
    fetched_count = fetched.shape[1]
    key_block = 512

    def advance(block_index, state_now):
        top_score, denom, weighted = state_now
        offset = block_index * key_block
        key_rows = lax.dynamic_slice_in_dim(fetched[0], offset, key_block).reshape(
            key_block, heads_dev, HEAD
        )
        values = lax.dynamic_slice_in_dim(fetched[1], offset, key_block).reshape(
            key_block, heads_dev, HEAD
        )
        tile_pos = (offset + jnp.arange(key_block, dtype=jnp.int32)) // TILE
        onehot = (tile_pos[:, None] == tile_ids[None, :]).astype(jnp.float32)
        tile_allowed = (
            jnp.einsum("qn,kn->qk", pos_mask, onehot, preferred_element_type=jnp.float32) > 0.5
        )
        visible = jnp.broadcast_to(tile_allowed[:, None, :], (tiles_dev, TILE, key_block)).reshape(
            row_count, key_block
        )
        scores = (
            jnp.einsum("qhd,khd->hqk", queries, key_rows, preferred_element_type=jnp.float32)
            * score_scale
        )
        masked = jnp.where(visible[None], scores, MASKED_SCORE)
        new_top = jnp.maximum(top_score, jnp.max(masked, axis=2))
        powers = jnp.where(visible[None], jnp.exp(masked - new_top[:, :, None]), 0.0)
        shrink = jnp.exp(top_score - new_top)
        denom = denom * shrink + jnp.sum(powers, axis=2)
        weighted = weighted * shrink[:, :, None] + jnp.einsum(
            "hqk,khd->hqd", powers.astype(jnp.bfloat16), values, preferred_element_type=jnp.float32
        )
        return (new_top, denom, weighted)

    _, denom, weighted = lax.fori_loop(0, fetched_count // key_block, advance, initial)
    finished = (weighted / denom[:, :, None]).astype(jnp.bfloat16)
    return jnp.transpose(finished, (1, 0, 2)).reshape(row_count, heads_dev * HEAD)


def per_device_general(clip_tokens, conv_taps, norm_gain, qkv_weight, out_weight, tile_mask, stripe_order):
    tiles_dev = clip_tokens.shape[1] // TILE
    send_order, place_order, own_row = stripe_tables(stripe_order, tiles_dev)
    before = passed_along(clip_tokens, "seq", 1)
    mixed = causal_conv(clip_tokens, before, conv_taps)
    mixed = regroup(mixed, send_order, place_order)
    projected = project(mixed, norm_gain, qkv_weight)
    row_count = projected.shape[1]
    group_cols = projected.shape[2]
    half_rows = row_count // 2
    side = lax.axis_index("tp") % 2
    mine_first = side == 0
    query_send = lax.dynamic_slice_in_dim(projected[0], (1 - side) * half_rows, half_rows, axis=0)
    query_mine = lax.dynamic_slice_in_dim(projected[0], side * half_rows, half_rows, axis=0)
    kv_mine = projected[1:]
    query_other, kv_other = from_partner((query_send, kv_mine), "tp", 0)
    queries = jnp.where(
        mine_first,
        jnp.concatenate([query_mine, query_other], axis=1),
        jnp.concatenate([query_other, query_mine], axis=1),
    )
    key_values = jnp.where(
        mine_first,
        jnp.concatenate([kv_mine, kv_other], axis=2),
        jnp.concatenate([kv_other, kv_mine], axis=2),
    )
    own_half = lax.dynamic_slice_in_dim(own_row, side * (tiles_dev // 2), tiles_dev // 2)
    pos_mask = position_mask(tile_mask, stripe_order, own_half)
    pair_out = attend(queries, key_values, pos_mask)
    give_cols = lax.dynamic_slice_in_dim(pair_out, (1 - side) * group_cols, group_cols, axis=1)
    keep_cols = lax.dynamic_slice_in_dim(pair_out, side * group_cols, group_cols, axis=1)
    got_cols = from_partner(give_cols, "tp", 0)
    heads_out = jnp.where(
        mine_first,
        jnp.concatenate([keep_cols, got_cols], axis=0),
        jnp.concatenate([got_cols, keep_cols], axis=0),
    )
    return lax.psum_scatter(
        jnp.einsum("qg,gc->cq", heads_out, out_weight, preferred_element_type=jnp.float32).astype(
            jnp.bfloat16
        ),
        "tp",
        scatter_dimension=0,
        tiled=True,
    )


def solution(mesh):
    in_specs = (
        P("tp", ("dp", "seq")),
        P(None, "tp"),
        P(),
        P(None, "tp", None),
        P("tp", None),
        P(),
        P(),
    )
    out_specs = P("tp", ("dp", "seq"))

    def run(clip_tokens, conv_taps, norm_gain, qkv_weight, out_weight, tile_mask, stripe_order):
        arguments = (clip_tokens, conv_taps, norm_gain, qkv_weight, out_weight, tile_mask, stripe_order)
        tokens = clip_tokens.shape[1] // (mesh.shape["dp"] * mesh.shape["seq"])
        columns = qkv_weight.shape[1] // mesh.shape["tp"]
        two_halves = mesh.shape["seq"] == 2 and tokens == 2 * FRAME
        fast = two_halves and mesh.shape["tp"] == 4 and columns % HEAD == 0

        def per_device(*local):
            if not fast:
                return per_device_general(*local)
            return per_device_fast(*local)

        step = jax.shard_map(
            per_device, mesh=mesh, in_specs=in_specs, out_specs=out_specs, check_vma=False
        )
        return step(*arguments)

    return run
```

```python
import functools
import math

import jax
import jax.numpy as jnp
from jax import lax
from jax.experimental import pallas as pl
from jax.experimental.pallas import tpu as pltpu
from jax.sharding import PartitionSpec as P


HEAD = 128
TILE = 128
FH = 16
FW = 32
FRAME = FH * FW
TAPS = 27


EPSILON = 1e-06
MASKED_SCORE = -1e30
LOG2E = math.log2(math.e)

VMEM_LIMIT = 14 * 1024 * 1024


def vmem_spec():
    return pl.BlockSpec(memory_space=pltpu.VMEM)


def off_chip_spec():
    return pl.BlockSpec(memory_space=pltpu.HBM)


def off_chip(array):
    return pltpu.with_memory_space_constraint(array, pltpu.HBM)


def smem_spec():
    return pl.BlockSpec(memory_space=pltpu.SMEM)


def params(limit=VMEM_LIMIT):
    return pltpu.CompilerParams(vmem_limit_bytes=limit)


def fetches(source, target, semaphores):
    block = target.shape[0] // semaphores.shape[0]
    return [
        pltpu.make_async_copy(
            source.at[index * block : (index + 1) * block],
            target.at[index * block : (index + 1) * block],
            semaphores.at[index],
        )
        for index in range(semaphores.shape[0])
    ]


def column_shifts(pieces, column):
    right = [jnp.where(column > 0, pltpu.roll(piece, 1, 1), 0.0) for piece in pieces]
    left = [jnp.where(column < FW - 1, pltpu.roll(piece, TILE - 1, 1), 0.0) for piece in pieces]
    return (right, pieces, left)


def rows_joined(rows, lane):
    down = [pltpu.roll(piece, FW, 1) for piece in rows[0]]
    up = [pltpu.roll(piece, TILE - FW, 1) for piece in rows[2]]
    joined = []
    for spot, middle in enumerate(rows[1]):
        before = down[spot - 1] if spot > 0 else 0.0
        after = up[spot + 1] if spot + 1 < len(up) else 0.0
        above = jnp.where(lane < FW, before, down[spot])
        below = jnp.where(lane >= TILE - FW, after, up[spot])
        joined.append(middle + (above + below))
    return joined


def pack_slots(order_ref, slots_ref, seq_here, tiles_dev, positions):
    half = tiles_dev // 2
    kept = jnp.int32(0)
    sent = jnp.int32(half)
    for position in range(positions):
        tile = order_ref[position]
        mine = tile // tiles_dev == seq_here
        stays = jnp.int32(position // tiles_dev) == seq_here
        slot = jnp.where(stays, kept, sent)

        @pl.when(mine)
        def _(tile=tile, slot=slot):
            slots_ref[tile - seq_here * tiles_dev] = slot

        step = mine.astype(jnp.int32)
        kept = kept + jnp.where(stays, step, 0)
        sent = sent + jnp.where(stays, 0, step)


GROUP = 16
CHUNKS = 4
PIECES = 2


def conv_body(with_before, first_row, seq_ref, order_ref, tokens_ref, taps_ref, part_ref, keep_ref, send_ref, *refs):
    if with_before:
        slots_ref, taps_scr, packed = refs
        source_ref = tokens_ref
    else:
        source_ref, slots_ref, taps_scr, packed, arrived, taps_in, taps_arrived = refs
    channels, tokens = packed.shape
    tiles_dev = tokens // TILE
    per_frame = FRAME // TILE
    if not with_before:
        taps_copy = pltpu.make_async_copy(
            taps_ref.at[:, first_row : first_row + channels], taps_in, taps_arrived
        )
        taps_copy.start()
        copies = fetches(tokens_ref.at[first_row : first_row + channels], source_ref, arrived)
        for copy in copies:
            copy.start()
    pack_slots(order_ref, slots_ref, seq_ref[0], tiles_dev, order_ref.shape[0])
    if not with_before:
        taps_copy.wait()
    for first in range(0, channels, TILE):
        wide = taps_ref[:, first_row + first : first_row + first + TILE] if with_before else taps_in[:, first : first + TILE]
        taps_scr[first : first + TILE, :TAPS] = wide.T
    lane = lax.broadcasted_iota(jnp.int32, (GROUP, TILE), 1)
    column = lane % FW
    if with_before:
        reads = ([(0, 0), (1, 1)], [(0, 1)])
    else:
        reads = ([(2, 0)], [(1, 0), (2, 1)])

    def advance(step, carry, base=0):
        rows = pl.ds(pl.multiple_of(base + step * GROUP, GROUP), GROUP)
        taps = taps_scr[rows, :]
        shifts = []
        for frame in range(2):
            pieces = []
            for spot in range(per_frame):
                tile = frame * per_frame + spot
                pieces.append(source_ref[rows, tile * TILE : (tile + 1) * TILE].astype(jnp.float32))
            shifts.append(column_shifts(pieces, column))
        for frame in range(2):
            sums = []
            for row_off in range(3):
                line = [None] * per_frame
                for time_off, read in reads[frame]:
                    for col_off in range(3):
                        tap = time_off * 9 + row_off * 3 + col_off
                        weight = jnp.broadcast_to(taps[:, tap : tap + 1], (GROUP, TILE))
                        for spot in range(per_frame):
                            term = weight * shifts[read][col_off][spot]
                            line[spot] = term if line[spot] is None else line[spot] + term
                sums.append(line)
            for spot, value in enumerate(rows_joined(sums, lane)):
                tile = frame * per_frame + spot
                here = slice(tile * TILE, (tile + 1) * TILE)
                if with_before:
                    value = value + part_ref[rows, here]
                else:
                    value = value + shifts[frame][1][spot]
                    part_ref[rows, here] = value
                place = pl.ds(pl.multiple_of(slots_ref[tile] * TILE, TILE), TILE)
                packed[rows, place] = value.astype(jnp.bfloat16)
        return carry

    steps = channels // GROUP
    if with_before:
        lax.fori_loop(0, steps, advance, 0, unroll=2)
    else:
        each = steps // CHUNKS

        def chunk(index, carry):
            begin = index * each * GROUP
            pltpu.make_async_copy(
                tokens_ref.at[pl.ds(first_row + begin, each * GROUP)],
                source_ref.at[pl.ds(begin, each * GROUP)],
                arrived.at[index],
            ).wait()
            later = functools.partial(advance, base=begin)
            return lax.fori_loop(0, each, later, carry, unroll=2)

        lax.fori_loop(0, CHUNKS, chunk, 0)
    keep_ref[...] = packed[:, : tokens // 2]
    send_ref[...] = packed[:, tokens // 2 :]


def conv_call(seq_here, stripe_order, tokens, conv_taps, piece, part=None):
    count = tokens.shape[1]
    channels = conv_taps.shape[1] // PIECES
    packed_shape = jax.ShapeDtypeStruct((channels, count // 2), jnp.bfloat16)
    with_before = part is not None
    out_shape = [packed_shape, packed_shape]
    scratch = [
        pltpu.SMEM((count // TILE,), jnp.int32),
        pltpu.VMEM((channels, 128), jnp.float32),
        pltpu.VMEM((channels, count), jnp.bfloat16),
    ]
    in_specs = [smem_spec(), smem_spec(), vmem_spec(), vmem_spec(), vmem_spec()]
    if not with_before:
        in_specs = [smem_spec(), smem_spec(), off_chip_spec(), off_chip_spec()]
        tokens, conv_taps, stripe_order = (off_chip(a) for a in (tokens, conv_taps, stripe_order))
        sum_shape = jax.ShapeDtypeStruct((channels, count), jnp.float32)
        out_shape = [sum_shape] + out_shape + [jax.ShapeDtypeStruct((channels, count), jnp.bfloat16)]
        scratch += [
            pltpu.SemaphoreType.DMA((CHUNKS,)),
            pltpu.VMEM((TAPS, channels), jnp.float32),
            pltpu.SemaphoreType.DMA,
        ]
    return pl.pallas_call(
        functools.partial(conv_body, with_before, piece * channels),
        in_specs=in_specs,
        out_specs=[vmem_spec()] * len(out_shape),
        scratch_shapes=scratch,
        out_shape=out_shape,
        compiler_params=params(),
        cost_estimate=pl.CostEstimate(
            flops=channels * count * TAPS, bytes_accessed=channels * count * 8, transcendentals=0
        ),
        name="conv",
    )(seq_here, stripe_order, tokens, conv_taps, *([part] if with_before else []))


def prepare_body(blocks_ref, out_ref, out_out):
    out_out[...] = out_ref[...].T


def prepare_out(blocks, out_weight):
    cols, channels = out_weight.shape
    count = blocks.shape[0]
    width = channels // count
    return pl.pallas_call(
        prepare_body,
        grid_spec=pltpu.PrefetchScalarGridSpec(
            num_scalar_prefetch=1,
            grid=(count,),
            in_specs=[pl.BlockSpec((cols, width), lambda j, b: (0, b[j]))],
            out_specs=pl.BlockSpec((width, cols), lambda j, b: (j, 0)),
        ),
        out_shape=jax.ShapeDtypeStruct((channels, cols), jnp.bfloat16),
        compiler_params=params(),
        cost_estimate=pl.CostEstimate(
            flops=cols * channels, bytes_accessed=4 * cols * channels, transcendentals=0
        ),
        name="prepare",
    )(blocks, out_weight)


def project_body(blocks_ref, weight_hbm, gains_ref, *refs):
    shards, (query_ref, pair_ref, weight_ref, tokens_ref, arrived) = refs[:-5], refs[-5:]
    copies = fetches(weight_hbm, weight_ref, arrived)
    for copy in copies[:2]:
        copy.start()
    width, tokens = shards[0].shape
    cols = query_ref.shape[0]
    lines = 128
    squares = jnp.zeros((1, tokens), jnp.float32)
    for index, shard in enumerate(shards):
        owner, piece = divmod(index, PIECES)
        start = (blocks_ref[owner] * PIECES + piece) * width
        for first in range(0, width, lines):
            there = pl.ds(pl.multiple_of(start + first, lines), lines)
            wide = shard[first : first + lines, :].astype(jnp.float32)
            squares = squares + jnp.sum(wide * wide, axis=0, keepdims=True)
            gain = jnp.concatenate([gains_ref[there, :]] * (tokens // 128), axis=1)
            tokens_ref[there, :] = (wide * gain).astype(jnp.bfloat16)
    inverse = lax.rsqrt(squares / (len(shards) * width) + EPSILON)
    rows = weight_ref.shape[0] // len(copies)
    for index, copy in enumerate(copies):
        copy.wait()
        if index + 2 < len(copies):
            copies[index + 2].start()
        here = slice(index * rows, (index + 1) * rows)
        total = jnp.dot(weight_ref[here, :], tokens_ref[...], preferred_element_type=jnp.float32)
        if index * rows < cols:
            query_ref[here, :] = (total * (inverse * (LOG2E / math.sqrt(HEAD)))).astype(jnp.bfloat16)
        else:
            there = slice(index * rows - cols, (index + 1) * rows - cols)
            pair_ref[there, :] = (total * inverse).astype(jnp.bfloat16)


def project_call(blocks, weights, gains, shards):
    rows, channels = weights.shape
    tokens = shards[0].shape[1]
    cols = rows // 3
    return pl.pallas_call(
        project_body,
        in_specs=[smem_spec(), off_chip_spec()] + [vmem_spec()] * (1 + len(shards)),
        out_specs=[vmem_spec(), vmem_spec()],
        scratch_shapes=[
            pltpu.VMEM((rows, channels), jnp.bfloat16),
            pltpu.VMEM((channels, tokens), jnp.bfloat16),
            pltpu.SemaphoreType.DMA((6,)),
        ],
        out_shape=[
            jax.ShapeDtypeStruct((cols, tokens), jnp.bfloat16),
            jax.ShapeDtypeStruct((2 * cols, tokens), jnp.bfloat16),
        ],
        compiler_params=params(),
        cost_estimate=pl.CostEstimate(
            flops=2 * rows * channels * tokens,
            bytes_accessed=2 * (rows * channels + channels * tokens + rows * tokens),
            transcendentals=0,
        ),
        name="project",
    )(blocks, off_chip(weights), gains, *shards)


def tile_lists(order_ref, ids_ref, seq_here, tiles_dev):
    half = tiles_dev // 2
    for block in range(2):
        first = jnp.int32(0)
        second = jnp.int32(0)
        away = (jnp.int32(block) != seq_here).astype(jnp.int32)
        for spot in range(tiles_dev):
            tile = order_ref[block * tiles_dev + spot]
            late = tile // tiles_dev
            rank = jnp.where(late == 0, first, second)
            ids_ref[(2 * late + away) * half + rank] = tile
            first = first + (1 - late)
            second = second + late


def attend_body(chunk, sources, goes_on, ends, seq_ref, order_ref, mask_ref, query_ref, *refs):
    count = len(sources)
    pairs, refs = refs[:count], refs[count:]
    if goes_on:
        old_stats, old_weighted, *refs = refs
    if ends:
        weight_hbm, *refs = refs
        partial_refs, refs = refs[: 4 * PIECES], refs[4 * PIECES :]
        ids_ref, bias_ref, scores_ref, heads_ref, weight_ref, arrived = refs
        copies = fetches(weight_hbm, weight_ref, arrived)
        for copy in copies:
            copy.start()
    else:
        new_stats, new_weighted, ids_ref, bias_ref, scores_ref = refs
    cols, tokens = query_ref.shape
    half = tokens // TILE
    tile_lists(order_ref, ids_ref, seq_ref[0], 2 * half)
    lane_tile = lax.broadcasted_iota(jnp.int32, (1, tokens), 1) // TILE
    for index, source in enumerate(sources):
        for spot in range(half):
            key_tile = ids_ref[source * half + spot]
            bias = jnp.zeros((1, tokens), jnp.float32)
            for query_spot in range(half):
                query_tile = ids_ref[2 * chunk * half + query_spot]
                blocked = jnp.where(mask_ref[query_tile, key_tile] == 1, 0.0, MASKED_SCORE)
                bias = jnp.where(lane_tile == query_spot, blocked, bias)
            bias_ref[index * half + spot : index * half + spot + 1, :] = bias

    def one_head(head, carry):
        rows = pl.ds(pl.multiple_of(head * HEAD, HEAD), HEAD)
        value_rows = pl.ds(pl.multiple_of(cols + head * HEAD, HEAD), HEAD)
        query = query_ref[rows, :]
        old_top = old_stats[head, 0:1, :] if goes_on else None
        top = old_top
        for index in range(count):
            block = jnp.dot(pairs[index][rows, :].T, query, preferred_element_type=jnp.float32)
            for spot in range(half):
                line = index * half + spot
                piece = block[spot * TILE : (spot + 1) * TILE, :] + bias_ref[line : line + 1, :]
                scores_ref[line * TILE : (line + 1) * TILE, :] = piece
                best = jnp.max(piece, axis=0, keepdims=True)
                top = best if top is None else jnp.maximum(top, best)
        denom = None
        weighted = None
        if goes_on:
            shrink = jnp.exp2(old_top - top)
            denom = old_stats[head, 1:2, :] * shrink
            weighted = old_weighted[rows, :] * shrink
        for index in range(count):
            powers = jnp.exp2(scores_ref[index * tokens : (index + 1) * tokens, :] - top)
            summed = jnp.sum(powers, axis=0, keepdims=True)
            term = jnp.dot(
                pairs[index][value_rows, :],
                powers.astype(jnp.bfloat16),
                preferred_element_type=jnp.float32,
            )
            denom = summed if denom is None else denom + summed
            weighted = term if weighted is None else weighted + term
        if ends:
            heads_ref[rows, :] = (weighted / denom).astype(jnp.bfloat16)
        else:
            new_stats[head, 0:1, :] = top
            new_stats[head, 1:2, :] = denom
            new_weighted[rows, :] = weighted
        return carry

    lax.fori_loop(0, cols // HEAD, one_head, 0)
    if ends:
        width = weight_ref.shape[0] // (4 * PIECES)
        for copy in copies:
            copy.wait()
        for index, out in enumerate(partial_refs):
            block = weight_ref[index * width : (index + 1) * width, :]
            out[...] = jnp.dot(
                block, heads_ref[...], preferred_element_type=jnp.float32
            ).astype(jnp.bfloat16)


def attend_call(chunk, tables, queries, sources, state=None, out_t=None):
    cols, tokens = queries.shape
    heads = cols // HEAD
    count = len(sources)
    half = tokens // TILE
    goes_on, ends = state is not None, out_t is not None
    arguments = [queries] + [array for array, _ in sources] + (list(state) if goes_on else [])
    in_specs = [vmem_spec()] * len(arguments)
    scratch = [
        pltpu.SMEM((4 * half,), jnp.int32),
        pltpu.VMEM((count * half, tokens), jnp.float32),
        pltpu.VMEM((count * tokens, tokens), jnp.float32),
    ]
    if ends:
        in_specs += [off_chip_spec()]
        arguments += [out_t]
        width = out_t.shape[0] // (4 * PIECES)
        shapes = [jax.ShapeDtypeStruct((width, tokens), jnp.bfloat16)] * (4 * PIECES)
        scratch += [
            pltpu.VMEM((cols, tokens), jnp.bfloat16),
            pltpu.VMEM(out_t.shape, jnp.bfloat16),
            pltpu.SemaphoreType.DMA((4,)),
        ]
    else:
        shapes = [
            jax.ShapeDtypeStruct((heads, 2, tokens), jnp.float32),
            jax.ShapeDtypeStruct((cols, tokens), jnp.float32),
        ]
    return pl.pallas_call(
        functools.partial(attend_body, chunk, tuple(s for _, s in sources), goes_on, ends),
        in_specs=[smem_spec()] * 3 + in_specs,
        out_specs=[vmem_spec()] * len(shapes),
        scratch_shapes=scratch,
        out_shape=shapes,
        compiler_params=params(),
        cost_estimate=pl.CostEstimate(
            flops=4 * cols * tokens * tokens * count,
            bytes_accessed=2 * cols * tokens * (2 + 2 * count),
            transcendentals=heads * tokens * tokens * count,
        ),
        name="attend",
    )(*tables, *arguments)


def summed(own, back, onward, across, at_end):
    total = own.astype(jnp.float32) + back.astype(jnp.float32) + onward.astype(jnp.float32)
    return (total + jnp.where(at_end, across.astype(jnp.float32), 0.0)).astype(jnp.bfloat16)


def place_body(seq_ref, order_ref, ends_ref, *refs):
    firsts, refs = refs[:PIECES], refs[PIECES:]
    parts, (out_ref, second_ref) = refs[:-2], refs[-2:]
    width, tokens = firsts[0].shape
    tiles_dev = 2 * tokens // TILE
    at_end = ends_ref[0] == 1
    for piece in range(PIECES):
        addends = [parts[4 * piece + index][...] for index in range(4)]
        second_ref[piece * width : (piece + 1) * width, :] = summed(*addends, at_end)
    ranks = [jnp.int32(0), jnp.int32(0)]
    for position in range(tiles_dev):
        late = order_ref[seq_ref[0] * tiles_dev + position] // tiles_dev
        spot = pl.ds(pl.multiple_of(jnp.where(late == 0, ranks[0], ranks[1]) * TILE, TILE), TILE)
        here = slice(position * TILE, (position + 1) * TILE)

        @pl.when(late == 0)
        def _(spot=spot, here=here):
            for piece in range(PIECES):
                out_ref[piece * width : (piece + 1) * width, here] = firsts[piece][:, spot]

        @pl.when(late == 1)
        def _(spot=spot, here=here):
            out_ref[:, here] = second_ref[:, spot]

        ranks[0] = ranks[0] + (1 - late)
        ranks[1] = ranks[1] + late


def place_call(seq_here, stripe_order, at_end, firsts, parts):
    width, tokens = firsts[0].shape
    channels = width * PIECES
    return pl.pallas_call(
        place_body,
        in_specs=[smem_spec()] * 3 + [vmem_spec()] * (5 * PIECES),
        out_specs=vmem_spec(),
        scratch_shapes=[pltpu.VMEM((channels, tokens), jnp.bfloat16)],
        out_shape=jax.ShapeDtypeStruct((channels, 2 * tokens), jnp.bfloat16),
        compiler_params=params(),
        cost_estimate=pl.CostEstimate(
            flops=4 * channels * tokens, bytes_accessed=14 * channels * tokens, transcendentals=0
        ),
        name="place",
    )(seq_here, stripe_order, at_end, *firsts, *[part for piece in parts for part in piece])


FORWARD = [(0, 1), (1, 2), (2, 3), (3, 0)]
BACKWARD = [(1, 0), (2, 1), (3, 2), (0, 3)]
FOLDED = [(0, 1), (1, 3), (3, 2), (2, 0)]
UNFOLDED = [(1, 0), (3, 1), (2, 3), (0, 2)]


def gather_blocks(block, here):
    before = lax.ppermute(block, "tp", FORWARD)
    after = lax.ppermute(block, "tp", BACKWARD)
    relay = jnp.where(here == 2, before, jnp.where(here == 1, after, block))
    across = lax.ppermute(relay, "tp", UNFOLDED)
    return (block, before, after, across)


def plus(a, b, chosen):
    summed = a.astype(jnp.float32) + jnp.where(chosen, b.astype(jnp.float32), 0.0)
    return summed.astype(jnp.bfloat16)


def reduce_blocks(partials, here):
    own, down, up, sent = partials
    across = lax.ppermute(sent, "tp", FOLDED)
    back = lax.ppermute(plus(down, across, here == 2), "tp", BACKWARD)
    onward = lax.ppermute(plus(up, across, here == 1), "tp", FORWARD)
    return (own, back, onward, across)


def per_device_fast(
    clip_tokens, conv_taps, norm_gain, qkv_weight, out_weight, tile_mask, stripe_order
):
    seq = lax.axis_index("seq")
    here = lax.axis_index("tp")
    seq_here = seq.astype(jnp.int32)[None]
    at_end = ((here == 0) | (here == 3)).astype(jnp.int32)[None]
    blocks = jnp.stack([here, (here + 3) % 4, (here + 1) % 4, (here + 2) % 4]).astype(jnp.int32)
    tables = (seq_here, stripe_order, tile_mask)
    pieces = range(PIECES)

    def gathered(blocks_here):
        by_piece = [gather_blocks(block, here) for block in blocks_here]
        return [by_piece[p][owner] for owner in range(4) for p in pieces]

    def reduced(partials):
        return [reduce_blocks(partials[p::PIECES], here) for p in pieces]

    begun = [conv_call(seq_here, stripe_order, clip_tokens, conv_taps, p) for p in pieces]
    tokens_a, before = [], []
    for _, keep, send, tokens in begun:
        got = lax.ppermute(send, "seq", [(0, 1)])
        tokens_a.append(jnp.where(seq == 0, keep, got))
        before.append(lax.ppermute(tokens, "seq", [(0, 1)]))
    kinds, cols, channels = qkv_weight.shape
    weights = qkv_weight.reshape(kinds * cols, channels)
    gains = jnp.broadcast_to(norm_gain[:, None], (channels, 128))
    out_t = prepare_out(blocks, out_weight)
    shards_a = gathered(tokens_a)

    tokens_b = []
    for p in pieces:
        keep, send = conv_call(seq_here, stripe_order, before[p], conv_taps, p, begun[p][0])
        got = lax.ppermute(send, "seq", [(1, 0)])
        tokens_b.append(jnp.where(seq == 1, keep, got))

    swap = [(0, 1), (1, 0)]
    query_a, pair_a = project_call(blocks, weights, gains, shards_a)
    peer_a = lax.ppermute(pair_a, "seq", swap)
    shards_b = gathered(tokens_b)
    partials_a = attend_call(0, tables, query_a, [(pair_a, 0), (peer_a, 1)], out_t=out_t)
    parts_a = reduced(partials_a)
    query_b, pair_b = project_call(blocks, weights, gains, shards_b)
    peer_b = lax.ppermute(pair_b, "seq", swap)
    near = [(pair_a, 0), (peer_a, 1), (pair_b, 2)]
    state = attend_call(1, tables, query_b, near)
    partials_b = attend_call(1, tables, query_b, [(peer_b, 3)], state=state, out_t=out_t)
    parts_b = reduced(partials_b)
    firsts = [summed(*part, at_end == 1) for part in parts_a]
    return place_call(seq_here, stripe_order, at_end, firsts, parts_b)


def passed_along(block, axis, distance):
    devices = range(lax.axis_size(axis))
    route = [(i - distance, i) for i in devices if i - distance in devices]
    return lax.ppermute(block, axis, route)


def from_partner(block, axis, apart):
    count = lax.axis_size(axis)
    route = []
    for low in range(count):
        high = low | 1 << apart
        if high != low and high < count:
            route += [(low, high), (high, low)]
    return lax.ppermute(block, axis, route)


def causal_conv(local_tokens, before, conv_taps):
    channels = local_tokens.shape[0]
    frames = local_tokens.shape[1] // (FH * FW)
    stacked = (
        jnp.concatenate([before, local_tokens], axis=1)
        .astype(jnp.float32)
        .reshape(channels, frames + 2, FH, FW)
    )
    padded = jnp.pad(stacked, ((0, 0), (0, 0), (1, 1), (1, 1)))
    summed = jnp.zeros((channels, frames, FH, FW), jnp.float32)
    for time_off in range(3):
        for row_off in range(3):
            for col_off in range(3):
                tap_vec = conv_taps[time_off * 9 + row_off * 3 + col_off]
                summed = (
                    summed
                    + tap_vec[:, None, None, None]
                    * padded[
                        :,
                        time_off : time_off + frames,
                        row_off : row_off + FH,
                        col_off : col_off + FW,
                    ]
                )
    return (local_tokens.astype(jnp.float32) + summed.reshape(channels, -1)).astype(jnp.bfloat16)


def stripe_tables(stripe_order, tiles_dev):
    seq_count = lax.axis_size("seq")
    seq_here = lax.axis_index("seq")
    per_source = tiles_dev // seq_count
    blocks = stripe_order.reshape(seq_count, tiles_dev)
    owners = blocks // tiles_dev
    is_mine = (owners == seq_here).astype(jnp.int32)
    rank_of = jnp.cumsum(is_mine, axis=1) - 1
    slot_ids = jnp.arange(per_source, dtype=jnp.int32)
    picked = is_mine[:, None, :] * (rank_of[:, None, :] == slot_ids[None, :, None]).astype(
        jnp.int32
    )
    local_tiles = (blocks - seq_here * tiles_dev)[:, None, :]
    send_order = jnp.sum(picked * local_tiles, axis=2).reshape(-1)
    own_row = lax.dynamic_slice_in_dim(stripe_order, seq_here * tiles_dev, tiles_dev)
    sources = own_row // tiles_dev
    position = jnp.arange(tiles_dev, dtype=jnp.int32)
    earlier = (sources[:, None] == sources[None, :]) & (position[None, :] < position[:, None])
    place_order = sources * per_source + jnp.sum(earlier.astype(jnp.int32), axis=1)
    return (send_order, place_order, own_row)


def regroup(values, send_order, place_order):
    leading = values.shape[0]
    trailing = values.shape[2:]
    in_tiles = values.reshape((leading, values.shape[1] // TILE, TILE) + trailing)
    outgoing = jnp.take(in_tiles, send_order, axis=1)
    arrived = lax.all_to_all(outgoing, "seq", split_axis=1, concat_axis=1, tiled=True)
    placed = jnp.take(arrived, place_order, axis=1)
    return placed.reshape(values.shape)


def project(mixed, norm_gain, qkv_weight):
    channels = norm_gain.shape[0]
    widened = lax.all_gather(mixed, "tp", axis=0, tiled=True).astype(jnp.float32)
    scaled = (widened * norm_gain[:, None]).astype(jnp.bfloat16)
    projected = jnp.einsum("ct,khc->kth", scaled, qkv_weight, preferred_element_type=jnp.float32)
    squares = jnp.sum(widened * widened, axis=0)
    projected, squares = (projected, squares)
    inverse = lax.rsqrt(squares / channels + EPSILON)
    return (projected * inverse[None, :, None]).astype(jnp.bfloat16)


def position_mask(tile_mask, stripe_order, own_half):
    tiles_all = tile_mask.shape[0]
    tile_ids = jnp.arange(tiles_all, dtype=jnp.int32)
    own_onehot = (own_half[:, None] == tile_ids[None, :]).astype(jnp.float32)
    order_onehot = (stripe_order[:, None] == tile_ids[None, :]).astype(jnp.float32)
    rows_mask = jnp.dot(
        own_onehot, tile_mask.astype(jnp.float32), preferred_element_type=jnp.float32
    )
    return jnp.dot(rows_mask, order_onehot.T, preferred_element_type=jnp.float32)


def attend(queries_flat, key_values, pos_mask):
    row_count = queries_flat.shape[0]
    heads_dev = queries_flat.shape[1] // HEAD
    queries = queries_flat.reshape(row_count, heads_dev, HEAD)
    score_scale = 1.0 / math.sqrt(HEAD)
    tiles_dev = row_count // TILE
    tile_ids = jnp.arange(pos_mask.shape[1], dtype=jnp.int32)
    initial = (
        jnp.full((heads_dev, row_count), MASKED_SCORE, jnp.float32),
        jnp.zeros((heads_dev, row_count), jnp.float32),
        jnp.zeros((heads_dev, row_count, HEAD), jnp.float32),
    )
    fetched = lax.all_gather(key_values, "seq", axis=1, tiled=True)
    fetched_count = fetched.shape[1]
    key_block = 512

    def advance(block_index, state_now):
        top_score, denom, weighted = state_now
        offset = block_index * key_block
        key_rows = lax.dynamic_slice_in_dim(fetched[0], offset, key_block).reshape(
            key_block, heads_dev, HEAD
        )
        values = lax.dynamic_slice_in_dim(fetched[1], offset, key_block).reshape(
            key_block, heads_dev, HEAD
        )
        tile_pos = (offset + jnp.arange(key_block, dtype=jnp.int32)) // TILE
        onehot = (tile_pos[:, None] == tile_ids[None, :]).astype(jnp.float32)
        tile_allowed = (
            jnp.einsum("qn,kn->qk", pos_mask, onehot, preferred_element_type=jnp.float32) > 0.5
        )
        visible = jnp.broadcast_to(tile_allowed[:, None, :], (tiles_dev, TILE, key_block)).reshape(
            row_count, key_block
        )
        scores = (
            jnp.einsum("qhd,khd->hqk", queries, key_rows, preferred_element_type=jnp.float32)
            * score_scale
        )
        masked = jnp.where(visible[None], scores, MASKED_SCORE)
        new_top = jnp.maximum(top_score, jnp.max(masked, axis=2))
        powers = jnp.where(visible[None], jnp.exp(masked - new_top[:, :, None]), 0.0)
        shrink = jnp.exp(top_score - new_top)
        denom = denom * shrink + jnp.sum(powers, axis=2)
        weighted = weighted * shrink[:, :, None] + jnp.einsum(
            "hqk,khd->hqd", powers.astype(jnp.bfloat16), values, preferred_element_type=jnp.float32
        )
        return (new_top, denom, weighted)

    _, denom, weighted = lax.fori_loop(0, fetched_count // key_block, advance, initial)
    finished = (weighted / denom[:, :, None]).astype(jnp.bfloat16)
    return jnp.transpose(finished, (1, 0, 2)).reshape(row_count, heads_dev * HEAD)


def per_device_general(clip_tokens, conv_taps, norm_gain, qkv_weight, out_weight, tile_mask, stripe_order):
    tiles_dev = clip_tokens.shape[1] // TILE
    send_order, place_order, own_row = stripe_tables(stripe_order, tiles_dev)
    before = passed_along(clip_tokens, "seq", 1)
    mixed = causal_conv(clip_tokens, before, conv_taps)
    mixed = regroup(mixed, send_order, place_order)
    projected = project(mixed, norm_gain, qkv_weight)
    row_count = projected.shape[1]
    group_cols = projected.shape[2]
    half_rows = row_count // 2
    side = lax.axis_index("tp") % 2
    mine_first = side == 0
    query_send = lax.dynamic_slice_in_dim(projected[0], (1 - side) * half_rows, half_rows, axis=0)
    query_mine = lax.dynamic_slice_in_dim(projected[0], side * half_rows, half_rows, axis=0)
    kv_mine = projected[1:]
    query_other, kv_other = from_partner((query_send, kv_mine), "tp", 0)
    queries = jnp.where(
        mine_first,
        jnp.concatenate([query_mine, query_other], axis=1),
        jnp.concatenate([query_other, query_mine], axis=1),
    )
    key_values = jnp.where(
        mine_first,
        jnp.concatenate([kv_mine, kv_other], axis=2),
        jnp.concatenate([kv_other, kv_mine], axis=2),
    )
    own_half = lax.dynamic_slice_in_dim(own_row, side * (tiles_dev // 2), tiles_dev // 2)
    pos_mask = position_mask(tile_mask, stripe_order, own_half)
    pair_out = attend(queries, key_values, pos_mask)
    give_cols = lax.dynamic_slice_in_dim(pair_out, (1 - side) * group_cols, group_cols, axis=1)
    keep_cols = lax.dynamic_slice_in_dim(pair_out, side * group_cols, group_cols, axis=1)
    got_cols = from_partner(give_cols, "tp", 0)
    heads_out = jnp.where(
        mine_first,
        jnp.concatenate([keep_cols, got_cols], axis=0),
        jnp.concatenate([got_cols, keep_cols], axis=0),
    )
    return lax.psum_scatter(
        jnp.einsum("qg,gc->cq", heads_out, out_weight, preferred_element_type=jnp.float32).astype(
            jnp.bfloat16
        ),
        "tp",
        scatter_dimension=0,
        tiled=True,
    )


def solution(mesh):
    in_specs = (
        P("tp", ("dp", "seq")),
        P(None, "tp"),
        P(),
        P(None, "tp", None),
        P("tp", None),
        P(),
        P(),
    )
    out_specs = P("tp", ("dp", "seq"))

    def run(clip_tokens, conv_taps, norm_gain, qkv_weight, out_weight, tile_mask, stripe_order):
        arguments = (clip_tokens, conv_taps, norm_gain, qkv_weight, out_weight, tile_mask, stripe_order)
        tokens = clip_tokens.shape[1] // (mesh.shape["dp"] * mesh.shape["seq"])
        columns = qkv_weight.shape[1] // mesh.shape["tp"]
        two_halves = mesh.shape["seq"] == 2 and tokens == 2 * FRAME
        fast = two_halves and mesh.shape["tp"] == 4 and columns % HEAD == 0

        def per_device(*local):
            if not fast:
                return per_device_general(*local)
            return per_device_fast(*local)

        step = jax.shard_map(
            per_device, mesh=mesh, in_specs=in_specs, out_specs=out_specs, check_vma=False
        )
        return step(*arguments)

    return run
```

```python
import functools
import math

import jax
import jax.numpy as jnp
from jax import lax
from jax.experimental import pallas as pl
from jax.experimental.pallas import tpu as pltpu
from jax.sharding import PartitionSpec as P


HEAD = 128
TILE = 128
FH = 16
FW = 32
FRAME = FH * FW
TAPS = 27


EPSILON = 1e-06
MASKED_SCORE = -1e30
LOG2E = math.log2(math.e)

VMEM_LIMIT = 14 * 1024 * 1024


def vmem_spec():
    return pl.BlockSpec(memory_space=pltpu.VMEM)


def off_chip_spec():
    return pl.BlockSpec(memory_space=pltpu.HBM)


def off_chip(array):
    return pltpu.with_memory_space_constraint(array, pltpu.HBM)


def smem_spec():
    return pl.BlockSpec(memory_space=pltpu.SMEM)


def params(limit=VMEM_LIMIT):
    return pltpu.CompilerParams(vmem_limit_bytes=limit)


def fetches(source, target, semaphores):
    block = target.shape[0] // semaphores.shape[0]
    return [
        pltpu.make_async_copy(
            source.at[index * block : (index + 1) * block],
            target.at[index * block : (index + 1) * block],
            semaphores.at[index],
        )
        for index in range(semaphores.shape[0])
    ]


def column_shifts(pieces, column):
    right = [jnp.where(column > 0, pltpu.roll(piece, 1, 1), 0.0) for piece in pieces]
    left = [jnp.where(column < FW - 1, pltpu.roll(piece, TILE - 1, 1), 0.0) for piece in pieces]
    return (right, pieces, left)


def rows_joined(rows, lane):
    down = [pltpu.roll(piece, FW, 1) for piece in rows[0]]
    up = [pltpu.roll(piece, TILE - FW, 1) for piece in rows[2]]
    joined = []
    for spot, middle in enumerate(rows[1]):
        before = down[spot - 1] if spot > 0 else 0.0
        after = up[spot + 1] if spot + 1 < len(up) else 0.0
        above = jnp.where(lane < FW, before, down[spot])
        below = jnp.where(lane >= TILE - FW, after, up[spot])
        joined.append(middle + (above + below))
    return joined


def pack_slots(order_ref, slots_ref, seq_here, tiles_dev, positions):
    half = tiles_dev // 2
    kept = jnp.int32(0)
    sent = jnp.int32(half)
    for position in range(positions):
        tile = order_ref[position]
        mine = tile // tiles_dev == seq_here
        stays = jnp.int32(position // tiles_dev) == seq_here
        slot = jnp.where(stays, kept, sent)

        @pl.when(mine)
        def _(tile=tile, slot=slot):
            slots_ref[tile - seq_here * tiles_dev] = slot

        step = mine.astype(jnp.int32)
        kept = kept + jnp.where(stays, step, 0)
        sent = sent + jnp.where(stays, 0, step)


GROUP = 16
CHUNKS = 4
PIECES = 2


def conv_body(with_before, first_row, seq_ref, order_ref, tokens_ref, taps_ref, part_ref, keep_ref, send_ref, *refs):
    if with_before:
        slots_ref, taps_scr, packed = refs
        source_ref = tokens_ref
    else:
        copy_ref, slots_ref, taps_scr, packed, source_ref, arrived, taps_in, taps_arrived, left = refs
    channels, tokens = packed.shape
    tiles_dev = tokens // TILE
    per_frame = FRAME // TILE
    if not with_before:
        taps_copy = pltpu.make_async_copy(
            taps_ref.at[:, first_row : first_row + channels], taps_in, taps_arrived
        )
        taps_copy.start()
        copies = fetches(tokens_ref.at[first_row : first_row + channels], source_ref, arrived)
        for copy in copies:
            copy.start()
    pack_slots(order_ref, slots_ref, seq_ref[0], tiles_dev, order_ref.shape[0])
    if not with_before:
        taps_copy.wait()
    for first in range(0, channels, TILE):
        wide = taps_ref[:, first_row + first : first_row + first + TILE] if with_before else taps_in[:, first : first + TILE]
        taps_scr[first : first + TILE, :TAPS] = wide.T
    lane = lax.broadcasted_iota(jnp.int32, (GROUP, TILE), 1)
    column = lane % FW
    if with_before:
        reads = ([(0, 0), (1, 1)], [(0, 1)])
    else:
        reads = ([(2, 0)], [(1, 0), (2, 1)])

    def advance(step, carry, base=0):
        rows = pl.ds(pl.multiple_of(base + step * GROUP, GROUP), GROUP)
        taps = taps_scr[rows, :]
        shifts = []
        for frame in range(2):
            pieces = []
            for spot in range(per_frame):
                tile = frame * per_frame + spot
                pieces.append(source_ref[rows, tile * TILE : (tile + 1) * TILE].astype(jnp.float32))
            shifts.append(column_shifts(pieces, column))
        for frame in range(2):
            sums = []
            for row_off in range(3):
                line = [None] * per_frame
                for time_off, read in reads[frame]:
                    for col_off in range(3):
                        tap = time_off * 9 + row_off * 3 + col_off
                        weight = jnp.broadcast_to(taps[:, tap : tap + 1], (GROUP, TILE))
                        for spot in range(per_frame):
                            term = weight * shifts[read][col_off][spot]
                            line[spot] = term if line[spot] is None else line[spot] + term
                sums.append(line)
            for spot, value in enumerate(rows_joined(sums, lane)):
                tile = frame * per_frame + spot
                here = slice(tile * TILE, (tile + 1) * TILE)
                if with_before:
                    value = value + part_ref[rows, here]
                else:
                    value = value + shifts[frame][1][spot]
                    part_ref[rows, here] = value
                place = pl.ds(pl.multiple_of(slots_ref[tile] * TILE, TILE), TILE)
                packed[rows, place] = value.astype(jnp.bfloat16)
        return carry

    steps = channels // GROUP
    if with_before:
        lax.fori_loop(0, steps, advance, 0, unroll=2)
    else:
        each = steps // CHUNKS

        def leaving(begin, index):
            block = pl.ds(begin, each * GROUP)
            return pltpu.make_async_copy(source_ref.at[block], copy_ref.at[block], left.at[index])

        def chunk(index, carry):
            begin = index * each * GROUP
            pltpu.make_async_copy(
                tokens_ref.at[pl.ds(first_row + begin, each * GROUP)],
                source_ref.at[pl.ds(begin, each * GROUP)],
                arrived.at[index],
            ).wait()
            leaving(begin, index).start()
            later = functools.partial(advance, base=begin)
            return lax.fori_loop(0, each, later, carry, unroll=2)

        lax.fori_loop(0, CHUNKS, chunk, 0)
        for index in range(CHUNKS):
            leaving(index * each * GROUP, index).wait()
    keep_ref[...] = packed[:, : tokens // 2]
    send_ref[...] = packed[:, tokens // 2 :]


def conv_call(seq_here, stripe_order, tokens, conv_taps, piece, part=None):
    count = tokens.shape[1]
    channels = conv_taps.shape[1] // PIECES
    packed_shape = jax.ShapeDtypeStruct((channels, count // 2), jnp.bfloat16)
    with_before = part is not None
    out_shape = [packed_shape, packed_shape]
    out_specs = [vmem_spec()] * 2
    scratch = [
        pltpu.SMEM((count // TILE,), jnp.int32),
        pltpu.VMEM((channels, 128), jnp.float32),
        pltpu.VMEM((channels, count), jnp.bfloat16),
    ]
    in_specs = [smem_spec(), smem_spec(), vmem_spec(), vmem_spec(), vmem_spec()]
    if not with_before:
        in_specs = [smem_spec(), smem_spec(), off_chip_spec(), off_chip_spec()]
        tokens = off_chip(tokens)
        sum_shape = jax.ShapeDtypeStruct((channels, count), jnp.float32)
        out_shape = [sum_shape] + out_shape + [pltpu.HBM((channels, count), jnp.bfloat16)]
        out_specs = [vmem_spec()] * 3 + [off_chip_spec()]
        scratch += [
            pltpu.VMEM((channels, count), jnp.bfloat16),
            pltpu.SemaphoreType.DMA((CHUNKS,)),
            pltpu.VMEM((TAPS, channels), jnp.float32),
            pltpu.SemaphoreType.DMA,
            pltpu.SemaphoreType.DMA((CHUNKS,)),
        ]
    return pl.pallas_call(
        functools.partial(conv_body, with_before, piece * channels),
        in_specs=in_specs,
        out_specs=out_specs,
        scratch_shapes=scratch,
        out_shape=out_shape,
        compiler_params=params(),
        cost_estimate=pl.CostEstimate(
            flops=channels * count * TAPS, bytes_accessed=channels * count * 8, transcendentals=0
        ),
        name="conv",
    )(seq_here, stripe_order, tokens, conv_taps, *([part] if with_before else []))


def prepare_body(blocks_ref, out_ref, out_out):
    out_out[...] = out_ref[...].T


def prepare_out(blocks, out_weight):
    cols, channels = out_weight.shape
    count = blocks.shape[0]
    width = channels // count
    return pl.pallas_call(
        prepare_body,
        grid_spec=pltpu.PrefetchScalarGridSpec(
            num_scalar_prefetch=1,
            grid=(count,),
            in_specs=[pl.BlockSpec((cols, width), lambda j, b: (0, b[j]))],
            out_specs=pl.BlockSpec((width, cols), lambda j, b: (j, 0)),
        ),
        out_shape=jax.ShapeDtypeStruct((channels, cols), jnp.bfloat16),
        compiler_params=params(),
        cost_estimate=pl.CostEstimate(
            flops=cols * channels, bytes_accessed=4 * cols * channels, transcendentals=0
        ),
        name="prepare",
    )(blocks, out_weight)


def project_body(blocks_ref, weight_hbm, gains_ref, *refs):
    shards, (query_ref, pair_ref, weight_ref, tokens_ref, arrived) = refs[:-5], refs[-5:]
    copies = fetches(weight_hbm, weight_ref, arrived)
    ahead, behind = copies[: len(copies) // 2], copies[len(copies) // 2 :]
    for copy in ahead:
        copy.start()
    width, tokens = shards[0].shape
    cols = query_ref.shape[0]
    lines = 128
    squares = jnp.zeros((1, tokens), jnp.float32)
    for index, shard in enumerate(shards):
        owner, piece = divmod(index, PIECES)
        start = (blocks_ref[owner] * PIECES + piece) * width
        for first in range(0, width, lines):
            there = pl.ds(pl.multiple_of(start + first, lines), lines)
            wide = shard[first : first + lines, :].astype(jnp.float32)
            squares = squares + jnp.sum(wide * wide, axis=0, keepdims=True)
            gain = jnp.concatenate([gains_ref[there, :]] * (tokens // 128), axis=1)
            tokens_ref[there, :] = (wide * gain).astype(jnp.bfloat16)
    inverse = lax.rsqrt(squares / (len(shards) * width) + EPSILON)
    rows = 256
    halfway = weight_ref.shape[0] // 2
    for first in range(0, weight_ref.shape[0], rows):
        if first == 0:
            for copy in ahead:
                copy.wait()
            for copy in behind:
                copy.start()
        if first == halfway:
            for copy in behind:
                copy.wait()
        here = slice(first, first + rows)
        total = jnp.dot(weight_ref[here, :], tokens_ref[...], preferred_element_type=jnp.float32)
        if first < cols:
            query_ref[here, :] = (total * (inverse * (LOG2E / math.sqrt(HEAD)))).astype(jnp.bfloat16)
        else:
            there = slice(first - cols, first - cols + rows)
            pair_ref[there, :] = (total * inverse).astype(jnp.bfloat16)


def project_call(blocks, weights, gains, shards):
    rows, channels = weights.shape
    tokens = shards[0].shape[1]
    cols = rows // 3
    return pl.pallas_call(
        project_body,
        in_specs=[smem_spec(), off_chip_spec()] + [vmem_spec()] * (1 + len(shards)),
        out_specs=[vmem_spec(), vmem_spec()],
        scratch_shapes=[
            pltpu.VMEM((rows, channels), jnp.bfloat16),
            pltpu.VMEM((channels, tokens), jnp.bfloat16),
            pltpu.SemaphoreType.DMA((6,)),
        ],
        out_shape=[
            jax.ShapeDtypeStruct((cols, tokens), jnp.bfloat16),
            jax.ShapeDtypeStruct((2 * cols, tokens), jnp.bfloat16),
        ],
        compiler_params=params(),
        cost_estimate=pl.CostEstimate(
            flops=2 * rows * channels * tokens,
            bytes_accessed=2 * (rows * channels + channels * tokens + rows * tokens),
            transcendentals=0,
        ),
        name="project",
    )(blocks, off_chip(weights), gains, *shards)


def tile_lists(order_ref, ids_ref, seq_here, tiles_dev):
    half = tiles_dev // 2
    for block in range(2):
        first = jnp.int32(0)
        second = jnp.int32(0)
        away = (jnp.int32(block) != seq_here).astype(jnp.int32)
        for spot in range(tiles_dev):
            tile = order_ref[block * tiles_dev + spot]
            late = tile // tiles_dev
            rank = jnp.where(late == 0, first, second)
            ids_ref[(2 * late + away) * half + rank] = tile
            first = first + (1 - late)
            second = second + late


def attend_body(chunk, sources, goes_on, ends, seq_ref, order_ref, mask_ref, query_ref, *refs):
    count = len(sources)
    pairs, refs = refs[:count], refs[count:]
    if goes_on:
        old_stats, old_weighted, *refs = refs
    if ends:
        weight_hbm, *refs = refs
        partial_refs, refs = refs[: 4 * PIECES], refs[4 * PIECES :]
        ids_ref, bias_ref, scores_ref, heads_ref, weight_ref, arrived = refs
        copies = fetches(weight_hbm, weight_ref, arrived)
        for copy in copies:
            copy.start()
    else:
        new_stats, new_weighted, ids_ref, bias_ref, scores_ref = refs
    cols, tokens = query_ref.shape
    half = tokens // TILE
    tile_lists(order_ref, ids_ref, seq_ref[0], 2 * half)
    lane_tile = lax.broadcasted_iota(jnp.int32, (1, tokens), 1) // TILE
    for index, source in enumerate(sources):
        for spot in range(half):
            key_tile = ids_ref[source * half + spot]
            bias = jnp.zeros((1, tokens), jnp.float32)
            for query_spot in range(half):
                query_tile = ids_ref[2 * chunk * half + query_spot]
                blocked = jnp.where(mask_ref[query_tile, key_tile] == 1, 0.0, MASKED_SCORE)
                bias = jnp.where(lane_tile == query_spot, blocked, bias)
            bias_ref[index * half + spot : index * half + spot + 1, :] = bias

    def one_head(head, carry):
        rows = pl.ds(pl.multiple_of(head * HEAD, HEAD), HEAD)
        value_rows = pl.ds(pl.multiple_of(cols + head * HEAD, HEAD), HEAD)
        query = query_ref[rows, :]
        old_top = old_stats[head, 0:1, :] if goes_on else None
        top = old_top
        for index in range(count):
            block = jnp.dot(pairs[index][rows, :].T, query, preferred_element_type=jnp.float32)
            for spot in range(half):
                line = index * half + spot
                piece = block[spot * TILE : (spot + 1) * TILE, :] + bias_ref[line : line + 1, :]
                scores_ref[line * TILE : (line + 1) * TILE, :] = piece
                best = jnp.max(piece, axis=0, keepdims=True)
                top = best if top is None else jnp.maximum(top, best)
        denom = None
        weighted = None
        if goes_on:
            shrink = jnp.exp2(old_top - top)
            denom = old_stats[head, 1:2, :] * shrink
            weighted = old_weighted[rows, :] * shrink
        for index in range(count):
            powers = jnp.exp2(scores_ref[index * tokens : (index + 1) * tokens, :] - top)
            summed = jnp.sum(powers, axis=0, keepdims=True)
            term = jnp.dot(
                pairs[index][value_rows, :],
                powers.astype(jnp.bfloat16),
                preferred_element_type=jnp.float32,
            )
            denom = summed if denom is None else denom + summed
            weighted = term if weighted is None else weighted + term
        if ends:
            heads_ref[rows, :] = (weighted / denom).astype(jnp.bfloat16)
        else:
            new_stats[head, 0:1, :] = top
            new_stats[head, 1:2, :] = denom
            new_weighted[rows, :] = weighted
        return carry

    lax.fori_loop(0, cols // HEAD, one_head, 0)
    if ends:
        width = weight_ref.shape[0] // (4 * PIECES)
        for copy in copies:
            copy.wait()
        for index, out in enumerate(partial_refs):
            block = weight_ref[index * width : (index + 1) * width, :]
            out[...] = jnp.dot(
                block, heads_ref[...], preferred_element_type=jnp.float32
            ).astype(jnp.bfloat16)


def attend_call(chunk, tables, queries, sources, state=None, out_t=None):
    cols, tokens = queries.shape
    heads = cols // HEAD
    count = len(sources)
    half = tokens // TILE
    goes_on, ends = state is not None, out_t is not None
    arguments = [queries] + [array for array, _ in sources] + (list(state) if goes_on else [])
    in_specs = [vmem_spec()] * len(arguments)
    scratch = [
        pltpu.SMEM((4 * half,), jnp.int32),
        pltpu.VMEM((count * half, tokens), jnp.float32),
        pltpu.VMEM((count * tokens, tokens), jnp.float32),
    ]
    if ends:
        in_specs += [off_chip_spec()]
        arguments += [out_t]
        width = out_t.shape[0] // (4 * PIECES)
        shapes = [jax.ShapeDtypeStruct((width, tokens), jnp.bfloat16)] * (4 * PIECES)
        scratch += [
            pltpu.VMEM((cols, tokens), jnp.bfloat16),
            pltpu.VMEM(out_t.shape, jnp.bfloat16),
            pltpu.SemaphoreType.DMA((4,)),
        ]
    else:
        shapes = [
            jax.ShapeDtypeStruct((heads, 2, tokens), jnp.float32),
            jax.ShapeDtypeStruct((cols, tokens), jnp.float32),
        ]
    return pl.pallas_call(
        functools.partial(attend_body, chunk, tuple(s for _, s in sources), goes_on, ends),
        in_specs=[smem_spec()] * 3 + in_specs,
        out_specs=[vmem_spec()] * len(shapes),
        scratch_shapes=scratch,
        out_shape=shapes,
        compiler_params=params(),
        cost_estimate=pl.CostEstimate(
            flops=4 * cols * tokens * tokens * count,
            bytes_accessed=2 * cols * tokens * (2 + 2 * count),
            transcendentals=heads * tokens * tokens * count,
        ),
        name="attend",
    )(*tables, *arguments)


def summed(own, back, onward, across, at_end):
    total = own.astype(jnp.float32) + back.astype(jnp.float32) + onward.astype(jnp.float32)
    return (total + jnp.where(at_end, across.astype(jnp.float32), 0.0)).astype(jnp.bfloat16)


def place_body(seq_ref, order_ref, ends_ref, *refs):
    firsts, refs = refs[:PIECES], refs[PIECES:]
    parts, (out_ref, second_ref) = refs[:-2], refs[-2:]
    width, tokens = firsts[0].shape
    tiles_dev = 2 * tokens // TILE
    at_end = ends_ref[0] == 1
    for piece in range(PIECES):
        addends = [parts[4 * piece + index][...] for index in range(4)]
        second_ref[piece * width : (piece + 1) * width, :] = summed(*addends, at_end)
    ranks = [jnp.int32(0), jnp.int32(0)]
    for position in range(tiles_dev):
        late = order_ref[seq_ref[0] * tiles_dev + position] // tiles_dev
        spot = pl.ds(pl.multiple_of(jnp.where(late == 0, ranks[0], ranks[1]) * TILE, TILE), TILE)
        here = slice(position * TILE, (position + 1) * TILE)

        @pl.when(late == 0)
        def _(spot=spot, here=here):
            for piece in range(PIECES):
                out_ref[piece * width : (piece + 1) * width, here] = firsts[piece][:, spot]

        @pl.when(late == 1)
        def _(spot=spot, here=here):
            out_ref[:, here] = second_ref[:, spot]

        ranks[0] = ranks[0] + (1 - late)
        ranks[1] = ranks[1] + late


def place_call(seq_here, stripe_order, at_end, firsts, parts):
    width, tokens = firsts[0].shape
    channels = width * PIECES
    return pl.pallas_call(
        place_body,
        in_specs=[smem_spec()] * 3 + [vmem_spec()] * (5 * PIECES),
        out_specs=vmem_spec(),
        scratch_shapes=[pltpu.VMEM((channels, tokens), jnp.bfloat16)],
        out_shape=jax.ShapeDtypeStruct((channels, 2 * tokens), jnp.bfloat16),
        compiler_params=params(),
        cost_estimate=pl.CostEstimate(
            flops=4 * channels * tokens, bytes_accessed=14 * channels * tokens, transcendentals=0
        ),
        name="place",
    )(seq_here, stripe_order, at_end, *firsts, *[part for piece in parts for part in piece])


FORWARD = [(0, 1), (1, 2), (2, 3), (3, 0)]
BACKWARD = [(1, 0), (2, 1), (3, 2), (0, 3)]
FOLDED = [(0, 1), (1, 3), (3, 2), (2, 0)]
UNFOLDED = [(1, 0), (3, 1), (2, 3), (0, 2)]


def gather_blocks(block, here):
    before = lax.ppermute(block, "tp", FORWARD)
    after = lax.ppermute(block, "tp", BACKWARD)
    relay = jnp.where(here == 2, before, jnp.where(here == 1, after, block))
    across = lax.ppermute(relay, "tp", UNFOLDED)
    return (block, before, after, across)


def plus(a, b, chosen):
    summed = a.astype(jnp.float32) + jnp.where(chosen, b.astype(jnp.float32), 0.0)
    return summed.astype(jnp.bfloat16)


def reduce_blocks(partials, here):
    own, down, up, sent = partials
    across = lax.ppermute(sent, "tp", FOLDED)
    back = lax.ppermute(plus(down, across, here == 2), "tp", BACKWARD)
    onward = lax.ppermute(plus(up, across, here == 1), "tp", FORWARD)
    return (own, back, onward, across)


def per_device_fast(
    clip_tokens, conv_taps, norm_gain, qkv_weight, out_weight, tile_mask, stripe_order
):
    tables = (conv_taps, stripe_order, tile_mask)
    conv_taps, stripe_order, tile_mask = (off_chip(table) for table in tables)
    seq = lax.axis_index("seq")
    here = lax.axis_index("tp")
    seq_here = seq.astype(jnp.int32)[None]
    at_end = ((here == 0) | (here == 3)).astype(jnp.int32)[None]
    blocks = jnp.stack([here, (here + 3) % 4, (here + 1) % 4, (here + 2) % 4]).astype(jnp.int32)
    tables = (seq_here, stripe_order, tile_mask)
    pieces = range(PIECES)

    def gathered(blocks_here):
        by_piece = [gather_blocks(block, here) for block in blocks_here]
        return [by_piece[p][owner] for owner in range(4) for p in pieces]

    def reduced(partials):
        return [reduce_blocks(partials[p::PIECES], here) for p in pieces]

    begun = [conv_call(seq_here, stripe_order, clip_tokens, conv_taps, p) for p in pieces]
    tokens_a, before = [], []
    for _, keep, send, tokens in begun:
        got = lax.ppermute(send, "seq", [(0, 1)])
        tokens_a.append(jnp.where(seq == 0, keep, got))
        before.append(lax.ppermute(tokens, "seq", [(0, 1)]))
    kinds, cols, channels = qkv_weight.shape
    weights = qkv_weight.reshape(kinds * cols, channels)
    gains = jnp.broadcast_to(norm_gain[:, None], (channels, 128))
    out_t = prepare_out(blocks, out_weight)
    shards_a = gathered(tokens_a)

    tokens_b = []
    for p in pieces:
        keep, send = conv_call(seq_here, stripe_order, before[p], conv_taps, p, begun[p][0])
        got = lax.ppermute(send, "seq", [(1, 0)])
        tokens_b.append(jnp.where(seq == 1, keep, got))

    swap = [(0, 1), (1, 0)]
    query_a, pair_a = project_call(blocks, weights, gains, shards_a)
    peer_a = lax.ppermute(pair_a, "seq", swap)
    shards_b = gathered(tokens_b)
    partials_a = attend_call(0, tables, query_a, [(pair_a, 0), (peer_a, 1)], out_t=out_t)
    parts_a = reduced(partials_a)
    query_b, pair_b = project_call(blocks, weights, gains, shards_b)
    peer_b = lax.ppermute(pair_b, "seq", swap)
    near = [(pair_a, 0), (peer_a, 1), (pair_b, 2)]
    state = attend_call(1, tables, query_b, near)
    partials_b = attend_call(1, tables, query_b, [(peer_b, 3)], state=state, out_t=out_t)
    parts_b = reduced(partials_b)
    firsts = [summed(*part, at_end == 1) for part in parts_a]
    return place_call(seq_here, stripe_order, at_end, firsts, parts_b)


def passed_along(block, axis, distance):
    devices = range(lax.axis_size(axis))
    route = [(i - distance, i) for i in devices if i - distance in devices]
    return lax.ppermute(block, axis, route)


def from_partner(block, axis, apart):
    count = lax.axis_size(axis)
    route = []
    for low in range(count):
        high = low | 1 << apart
        if high != low and high < count:
            route += [(low, high), (high, low)]
    return lax.ppermute(block, axis, route)


def causal_conv(local_tokens, before, conv_taps):
    channels = local_tokens.shape[0]
    frames = local_tokens.shape[1] // (FH * FW)
    stacked = (
        jnp.concatenate([before, local_tokens], axis=1)
        .astype(jnp.float32)
        .reshape(channels, frames + 2, FH, FW)
    )
    padded = jnp.pad(stacked, ((0, 0), (0, 0), (1, 1), (1, 1)))
    summed = jnp.zeros((channels, frames, FH, FW), jnp.float32)
    for time_off in range(3):
        for row_off in range(3):
            for col_off in range(3):
                tap_vec = conv_taps[time_off * 9 + row_off * 3 + col_off]
                summed = (
                    summed
                    + tap_vec[:, None, None, None]
                    * padded[
                        :,
                        time_off : time_off + frames,
                        row_off : row_off + FH,
                        col_off : col_off + FW,
                    ]
                )
    return (local_tokens.astype(jnp.float32) + summed.reshape(channels, -1)).astype(jnp.bfloat16)


def stripe_tables(stripe_order, tiles_dev):
    seq_count = lax.axis_size("seq")
    seq_here = lax.axis_index("seq")
    per_source = tiles_dev // seq_count
    blocks = stripe_order.reshape(seq_count, tiles_dev)
    owners = blocks // tiles_dev
    is_mine = (owners == seq_here).astype(jnp.int32)
    rank_of = jnp.cumsum(is_mine, axis=1) - 1
    slot_ids = jnp.arange(per_source, dtype=jnp.int32)
    picked = is_mine[:, None, :] * (rank_of[:, None, :] == slot_ids[None, :, None]).astype(
        jnp.int32
    )
    local_tiles = (blocks - seq_here * tiles_dev)[:, None, :]
    send_order = jnp.sum(picked * local_tiles, axis=2).reshape(-1)
    own_row = lax.dynamic_slice_in_dim(stripe_order, seq_here * tiles_dev, tiles_dev)
    sources = own_row // tiles_dev
    position = jnp.arange(tiles_dev, dtype=jnp.int32)
    earlier = (sources[:, None] == sources[None, :]) & (position[None, :] < position[:, None])
    place_order = sources * per_source + jnp.sum(earlier.astype(jnp.int32), axis=1)
    return (send_order, place_order, own_row)


def regroup(values, send_order, place_order):
    leading = values.shape[0]
    trailing = values.shape[2:]
    in_tiles = values.reshape((leading, values.shape[1] // TILE, TILE) + trailing)
    outgoing = jnp.take(in_tiles, send_order, axis=1)
    arrived = lax.all_to_all(outgoing, "seq", split_axis=1, concat_axis=1, tiled=True)
    placed = jnp.take(arrived, place_order, axis=1)
    return placed.reshape(values.shape)


def project(mixed, norm_gain, qkv_weight):
    channels = norm_gain.shape[0]
    widened = lax.all_gather(mixed, "tp", axis=0, tiled=True).astype(jnp.float32)
    scaled = (widened * norm_gain[:, None]).astype(jnp.bfloat16)
    projected = jnp.einsum("ct,khc->kth", scaled, qkv_weight, preferred_element_type=jnp.float32)
    squares = jnp.sum(widened * widened, axis=0)
    projected, squares = (projected, squares)
    inverse = lax.rsqrt(squares / channels + EPSILON)
    return (projected * inverse[None, :, None]).astype(jnp.bfloat16)


def position_mask(tile_mask, stripe_order, own_half):
    tiles_all = tile_mask.shape[0]
    tile_ids = jnp.arange(tiles_all, dtype=jnp.int32)
    own_onehot = (own_half[:, None] == tile_ids[None, :]).astype(jnp.float32)
    order_onehot = (stripe_order[:, None] == tile_ids[None, :]).astype(jnp.float32)
    rows_mask = jnp.dot(
        own_onehot, tile_mask.astype(jnp.float32), preferred_element_type=jnp.float32
    )
    return jnp.dot(rows_mask, order_onehot.T, preferred_element_type=jnp.float32)


def attend(queries_flat, key_values, pos_mask):
    row_count = queries_flat.shape[0]
    heads_dev = queries_flat.shape[1] // HEAD
    queries = queries_flat.reshape(row_count, heads_dev, HEAD)
    score_scale = 1.0 / math.sqrt(HEAD)
    tiles_dev = row_count // TILE
    tile_ids = jnp.arange(pos_mask.shape[1], dtype=jnp.int32)
    initial = (
        jnp.full((heads_dev, row_count), MASKED_SCORE, jnp.float32),
        jnp.zeros((heads_dev, row_count), jnp.float32),
        jnp.zeros((heads_dev, row_count, HEAD), jnp.float32),
    )
    fetched = lax.all_gather(key_values, "seq", axis=1, tiled=True)
    fetched_count = fetched.shape[1]
    key_block = 512

    def advance(block_index, state_now):
        top_score, denom, weighted = state_now
        offset = block_index * key_block
        key_rows = lax.dynamic_slice_in_dim(fetched[0], offset, key_block).reshape(
            key_block, heads_dev, HEAD
        )
        values = lax.dynamic_slice_in_dim(fetched[1], offset, key_block).reshape(
            key_block, heads_dev, HEAD
        )
        tile_pos = (offset + jnp.arange(key_block, dtype=jnp.int32)) // TILE
        onehot = (tile_pos[:, None] == tile_ids[None, :]).astype(jnp.float32)
        tile_allowed = (
            jnp.einsum("qn,kn->qk", pos_mask, onehot, preferred_element_type=jnp.float32) > 0.5
        )
        visible = jnp.broadcast_to(tile_allowed[:, None, :], (tiles_dev, TILE, key_block)).reshape(
            row_count, key_block
        )
        scores = (
            jnp.einsum("qhd,khd->hqk", queries, key_rows, preferred_element_type=jnp.float32)
            * score_scale
        )
        masked = jnp.where(visible[None], scores, MASKED_SCORE)
        new_top = jnp.maximum(top_score, jnp.max(masked, axis=2))
        powers = jnp.where(visible[None], jnp.exp(masked - new_top[:, :, None]), 0.0)
        shrink = jnp.exp(top_score - new_top)
        denom = denom * shrink + jnp.sum(powers, axis=2)
        weighted = weighted * shrink[:, :, None] + jnp.einsum(
            "hqk,khd->hqd", powers.astype(jnp.bfloat16), values, preferred_element_type=jnp.float32
        )
        return (new_top, denom, weighted)

    _, denom, weighted = lax.fori_loop(0, fetched_count // key_block, advance, initial)
    finished = (weighted / denom[:, :, None]).astype(jnp.bfloat16)
    return jnp.transpose(finished, (1, 0, 2)).reshape(row_count, heads_dev * HEAD)


def per_device_general(clip_tokens, conv_taps, norm_gain, qkv_weight, out_weight, tile_mask, stripe_order):
    tiles_dev = clip_tokens.shape[1] // TILE
    send_order, place_order, own_row = stripe_tables(stripe_order, tiles_dev)
    before = passed_along(clip_tokens, "seq", 1)
    mixed = causal_conv(clip_tokens, before, conv_taps)
    mixed = regroup(mixed, send_order, place_order)
    projected = project(mixed, norm_gain, qkv_weight)
    row_count = projected.shape[1]
    group_cols = projected.shape[2]
    half_rows = row_count // 2
    side = lax.axis_index("tp") % 2
    mine_first = side == 0
    query_send = lax.dynamic_slice_in_dim(projected[0], (1 - side) * half_rows, half_rows, axis=0)
    query_mine = lax.dynamic_slice_in_dim(projected[0], side * half_rows, half_rows, axis=0)
    kv_mine = projected[1:]
    query_other, kv_other = from_partner((query_send, kv_mine), "tp", 0)
    queries = jnp.where(
        mine_first,
        jnp.concatenate([query_mine, query_other], axis=1),
        jnp.concatenate([query_other, query_mine], axis=1),
    )
    key_values = jnp.where(
        mine_first,
        jnp.concatenate([kv_mine, kv_other], axis=2),
        jnp.concatenate([kv_other, kv_mine], axis=2),
    )
    own_half = lax.dynamic_slice_in_dim(own_row, side * (tiles_dev // 2), tiles_dev // 2)
    pos_mask = position_mask(tile_mask, stripe_order, own_half)
    pair_out = attend(queries, key_values, pos_mask)
    give_cols = lax.dynamic_slice_in_dim(pair_out, (1 - side) * group_cols, group_cols, axis=1)
    keep_cols = lax.dynamic_slice_in_dim(pair_out, side * group_cols, group_cols, axis=1)
    got_cols = from_partner(give_cols, "tp", 0)
    heads_out = jnp.where(
        mine_first,
        jnp.concatenate([keep_cols, got_cols], axis=0),
        jnp.concatenate([got_cols, keep_cols], axis=0),
    )
    return lax.psum_scatter(
        jnp.einsum("qg,gc->cq", heads_out, out_weight, preferred_element_type=jnp.float32).astype(
            jnp.bfloat16
        ),
        "tp",
        scatter_dimension=0,
        tiled=True,
    )


def solution(mesh):
    in_specs = (
        P("tp", ("dp", "seq")),
        P(None, "tp"),
        P(),
        P(None, "tp", None),
        P("tp", None),
        P(),
        P(),
    )
    out_specs = P("tp", ("dp", "seq"))

    def run(clip_tokens, conv_taps, norm_gain, qkv_weight, out_weight, tile_mask, stripe_order):
        arguments = (clip_tokens, conv_taps, norm_gain, qkv_weight, out_weight, tile_mask, stripe_order)
        tokens = clip_tokens.shape[1] // (mesh.shape["dp"] * mesh.shape["seq"])
        columns = qkv_weight.shape[1] // mesh.shape["tp"]
        two_halves = mesh.shape["seq"] == 2 and tokens == 2 * FRAME
        fast = two_halves and mesh.shape["tp"] == 4 and columns % HEAD == 0

        def per_device(*local):
            if not fast:
                return per_device_general(*local)
            return per_device_fast(*local)

        step = jax.shard_map(
            per_device, mesh=mesh, in_specs=in_specs, out_specs=out_specs, check_vma=False
        )
        return step(*arguments)

    return run
```

```python
import functools
import math

import jax
import jax.numpy as jnp
from jax import lax
from jax.experimental import pallas as pl
from jax.experimental.pallas import tpu as pltpu
from jax.sharding import PartitionSpec as P


HEAD = 128
TILE = 128
FH = 16
FW = 32
FRAME = FH * FW
TAPS = 27


EPSILON = 1e-06
MASKED_SCORE = -1e30
LOG2E = math.log2(math.e)

VMEM_LIMIT = 14 * 1024 * 1024


def vmem_spec():
    return pl.BlockSpec(memory_space=pltpu.VMEM)


def off_chip_spec():
    return pl.BlockSpec(memory_space=pltpu.HBM)


def off_chip(array):
    return pltpu.with_memory_space_constraint(array, pltpu.HBM)


def smem_spec():
    return pl.BlockSpec(memory_space=pltpu.SMEM)


def params(limit=VMEM_LIMIT):
    return pltpu.CompilerParams(vmem_limit_bytes=limit)


def fetches(source, target, semaphores):
    block = target.shape[0] // semaphores.shape[0]
    return [
        pltpu.make_async_copy(
            source.at[index * block : (index + 1) * block],
            target.at[index * block : (index + 1) * block],
            semaphores.at[index],
        )
        for index in range(semaphores.shape[0])
    ]


def column_shifts(pieces, column):
    right = [jnp.where(column > 0, pltpu.roll(piece, 1, 1), 0.0) for piece in pieces]
    left = [jnp.where(column < FW - 1, pltpu.roll(piece, TILE - 1, 1), 0.0) for piece in pieces]
    return (right, pieces, left)


def rows_joined(rows, lane):
    down = [pltpu.roll(piece, FW, 1) for piece in rows[0]]
    up = [pltpu.roll(piece, TILE - FW, 1) for piece in rows[2]]
    joined = []
    for spot, middle in enumerate(rows[1]):
        before = down[spot - 1] if spot > 0 else 0.0
        after = up[spot + 1] if spot + 1 < len(up) else 0.0
        above = jnp.where(lane < FW, before, down[spot])
        below = jnp.where(lane >= TILE - FW, after, up[spot])
        joined.append(middle + (above + below))
    return joined


def pack_slots(order_ref, slots_ref, seq_here, tiles_dev, positions):
    half = tiles_dev // 2
    kept = jnp.int32(0)
    sent = jnp.int32(half)
    for position in range(positions):
        tile = order_ref[position]
        mine = tile // tiles_dev == seq_here
        stays = jnp.int32(position // tiles_dev) == seq_here
        slot = jnp.where(stays, kept, sent)

        @pl.when(mine)
        def _(tile=tile, slot=slot):
            slots_ref[tile - seq_here * tiles_dev] = slot

        step = mine.astype(jnp.int32)
        kept = kept + jnp.where(stays, step, 0)
        sent = sent + jnp.where(stays, 0, step)


GROUP = 16
CHUNKS = 4
PIECES = 2


def conv_body(with_before, first_row, seq_ref, order_ref, tokens_ref, taps_ref, part_ref, keep_ref, send_ref, *refs):
    if with_before:
        slots_ref, taps_scr, packed = refs
        source_ref = tokens_ref
    else:
        copy_ref, slots_ref, taps_scr, packed, source_ref, arrived, taps_in, taps_arrived, left = refs
    channels, tokens = packed.shape
    tiles_dev = tokens // TILE
    per_frame = FRAME // TILE
    if not with_before:
        taps_copy = pltpu.make_async_copy(
            taps_ref.at[:, first_row : first_row + channels], taps_in, taps_arrived
        )
        taps_copy.start()
        copies = fetches(tokens_ref.at[first_row : first_row + channels], source_ref, arrived)
        for copy in copies:
            copy.start()
    pack_slots(order_ref, slots_ref, seq_ref[0], tiles_dev, order_ref.shape[0])
    if not with_before:
        taps_copy.wait()
    for first in range(0, channels, TILE):
        wide = taps_ref[:, first_row + first : first_row + first + TILE] if with_before else taps_in[:, first : first + TILE]
        taps_scr[first : first + TILE, :TAPS] = wide.T
    lane = lax.broadcasted_iota(jnp.int32, (GROUP, TILE), 1)
    column = lane % FW
    if with_before:
        reads = ([(0, 0), (1, 1)], [(0, 1)])
    else:
        reads = ([(2, 0)], [(1, 0), (2, 1)])

    def advance(step, carry, base=0):
        rows = pl.ds(pl.multiple_of(base + step * GROUP, GROUP), GROUP)
        taps = taps_scr[rows, :]
        shifts = []
        for frame in range(2):
            pieces = []
            for spot in range(per_frame):
                tile = frame * per_frame + spot
                pieces.append(source_ref[rows, tile * TILE : (tile + 1) * TILE].astype(jnp.float32))
            shifts.append(column_shifts(pieces, column))
        for frame in range(2):
            sums = []
            for row_off in range(3):
                line = [None] * per_frame
                for time_off, read in reads[frame]:
                    for col_off in range(3):
                        tap = time_off * 9 + row_off * 3 + col_off
                        weight = jnp.broadcast_to(taps[:, tap : tap + 1], (GROUP, TILE))
                        for spot in range(per_frame):
                            term = weight * shifts[read][col_off][spot]
                            line[spot] = term if line[spot] is None else line[spot] + term
                sums.append(line)
            for spot, value in enumerate(rows_joined(sums, lane)):
                tile = frame * per_frame + spot
                here = slice(tile * TILE, (tile + 1) * TILE)
                if with_before:
                    value = value + part_ref[rows, here]
                else:
                    value = value + shifts[frame][1][spot]
                    part_ref[rows, here] = value
                place = pl.ds(pl.multiple_of(slots_ref[tile] * TILE, TILE), TILE)
                packed[rows, place] = value.astype(jnp.bfloat16)
        return carry

    steps = channels // GROUP
    if with_before:
        lax.fori_loop(0, steps, advance, 0, unroll=2)
    else:
        each = steps // CHUNKS

        def leaving(begin, index):
            block = pl.ds(begin, each * GROUP)
            return pltpu.make_async_copy(source_ref.at[block], copy_ref.at[block], left.at[index])

        def chunk(index, carry):
            begin = index * each * GROUP
            pltpu.make_async_copy(
                tokens_ref.at[pl.ds(first_row + begin, each * GROUP)],
                source_ref.at[pl.ds(begin, each * GROUP)],
                arrived.at[index],
            ).wait()
            leaving(begin, index).start()
            later = functools.partial(advance, base=begin)
            return lax.fori_loop(0, each, later, carry, unroll=2)

        lax.fori_loop(0, CHUNKS, chunk, 0)
        for index in range(CHUNKS):
            leaving(index * each * GROUP, index).wait()
    keep_ref[...] = packed[:, : tokens // 2]
    send_ref[...] = packed[:, tokens // 2 :]


def conv_call(seq_here, stripe_order, tokens, conv_taps, piece, part=None):
    count = tokens.shape[1]
    channels = conv_taps.shape[1] // PIECES
    packed_shape = jax.ShapeDtypeStruct((channels, count // 2), jnp.bfloat16)
    with_before = part is not None
    out_shape = [packed_shape, packed_shape]
    out_specs = [vmem_spec()] * 2
    scratch = [
        pltpu.SMEM((count // TILE,), jnp.int32),
        pltpu.VMEM((channels, 128), jnp.float32),
        pltpu.VMEM((channels, count), jnp.bfloat16),
    ]
    in_specs = [smem_spec(), smem_spec(), vmem_spec(), vmem_spec(), vmem_spec()]
    if not with_before:
        in_specs = [smem_spec(), smem_spec(), off_chip_spec(), off_chip_spec()]
        tokens = off_chip(tokens)
        sum_shape = jax.ShapeDtypeStruct((channels, count), jnp.float32)
        out_shape = [sum_shape] + out_shape + [pltpu.HBM((channels, count), jnp.bfloat16)]
        out_specs = [vmem_spec()] * 3 + [off_chip_spec()]
        scratch += [
            pltpu.VMEM((channels, count), jnp.bfloat16),
            pltpu.SemaphoreType.DMA((CHUNKS,)),
            pltpu.VMEM((TAPS, channels), jnp.float32),
            pltpu.SemaphoreType.DMA,
            pltpu.SemaphoreType.DMA((CHUNKS,)),
        ]
    return pl.pallas_call(
        functools.partial(conv_body, with_before, piece * channels),
        in_specs=in_specs,
        out_specs=out_specs,
        scratch_shapes=scratch,
        out_shape=out_shape,
        compiler_params=params(),
        cost_estimate=pl.CostEstimate(
            flops=channels * count * TAPS, bytes_accessed=channels * count * 8, transcendentals=0
        ),
        name="conv",
    )(seq_here, stripe_order, tokens, conv_taps, *([part] if with_before else []))


def prepare_body(blocks_ref, out_ref, out_out):
    out_out[...] = out_ref[...].T


def prepare_out(blocks, out_weight):
    cols, channels = out_weight.shape
    count = blocks.shape[0]
    width = channels // count
    return pl.pallas_call(
        prepare_body,
        grid_spec=pltpu.PrefetchScalarGridSpec(
            num_scalar_prefetch=1,
            grid=(count,),
            in_specs=[pl.BlockSpec((cols, width), lambda j, b: (0, b[j]))],
            out_specs=pl.BlockSpec((width, cols), lambda j, b: (j, 0)),
        ),
        out_shape=jax.ShapeDtypeStruct((channels, cols), jnp.bfloat16),
        compiler_params=params(),
        cost_estimate=pl.CostEstimate(
            flops=cols * channels, bytes_accessed=4 * cols * channels, transcendentals=0
        ),
        name="prepare",
    )(blocks, out_weight)


ROWS = 256


def products(weight_ref, tokens_ref, scale, copies, out_ref):
    for index, copy in enumerate(copies):
        copy.wait()
        here = slice(index * ROWS, (index + 1) * ROWS)
        total = jnp.dot(weight_ref[here, :], tokens_ref[...], preferred_element_type=jnp.float32)
        out_ref[here, :] = (total * scale).astype(jnp.bfloat16)


def pair_body(blocks_ref, weight_hbm, gains_ref, *refs):
    shards, (pair_ref, tokens_ref, inverse_ref, weight_ref, arrived) = refs[:-5], refs[-5:]
    rows = weight_ref.shape[0]
    skipped = weight_hbm.shape[0] - rows
    copies = fetches(weight_hbm.at[skipped : skipped + rows], weight_ref, arrived)
    for copy in copies:
        copy.start()
    width, tokens = shards[0].shape
    lines = 128
    squares = jnp.zeros((1, tokens), jnp.float32)
    for index, shard in enumerate(shards):
        owner, piece = divmod(index, PIECES)
        start = (blocks_ref[owner] * PIECES + piece) * width
        for first in range(0, width, lines):
            there = pl.ds(pl.multiple_of(start + first, lines), lines)
            wide = shard[first : first + lines, :].astype(jnp.float32)
            squares = squares + jnp.sum(wide * wide, axis=0, keepdims=True)
            gain = jnp.concatenate([gains_ref[there, :]] * (tokens // 128), axis=1)
            tokens_ref[there, :] = (wide * gain).astype(jnp.bfloat16)
    inverse = lax.rsqrt(squares / (len(shards) * width) + EPSILON)
    inverse_ref[...] = inverse
    products(weight_ref, tokens_ref, inverse, copies, pair_ref)


def query_body(weight_hbm, tokens_ref, inverse_ref, query_ref, weight_ref, arrived):
    copies = fetches(weight_hbm.at[: weight_ref.shape[0]], weight_ref, arrived)
    for copy in copies:
        copy.start()
    products(weight_ref, tokens_ref, inverse_ref[...] * (LOG2E / math.sqrt(HEAD)), copies, query_ref)


def project_pair(blocks, weights, gains, shards):
    rows, channels = weights.shape
    tokens = shards[0].shape[1]
    cols = rows // 3
    return pl.pallas_call(
        pair_body,
        in_specs=[smem_spec(), off_chip_spec()] + [vmem_spec()] * (1 + len(shards)),
        out_specs=[vmem_spec()] * 3,
        scratch_shapes=[
            pltpu.VMEM((2 * cols, channels), jnp.bfloat16),
            pltpu.SemaphoreType.DMA((2 * cols // ROWS,)),
        ],
        out_shape=[
            jax.ShapeDtypeStruct((2 * cols, tokens), jnp.bfloat16),
            jax.ShapeDtypeStruct((channels, tokens), jnp.bfloat16),
            jax.ShapeDtypeStruct((1, tokens), jnp.float32),
        ],
        compiler_params=params(),
        cost_estimate=pl.CostEstimate(
            flops=4 * cols * channels * tokens,
            bytes_accessed=2 * (2 * cols * channels + 2 * channels * tokens + 2 * cols * tokens),
            transcendentals=0,
        ),
        name="pair",
    )(blocks, off_chip(weights), gains, *shards)


def project_query(weights, scaled, inverse):
    rows, channels = weights.shape
    tokens = scaled.shape[1]
    cols = rows // 3
    return pl.pallas_call(
        query_body,
        in_specs=[off_chip_spec(), vmem_spec(), vmem_spec()],
        out_specs=vmem_spec(),
        scratch_shapes=[
            pltpu.VMEM((cols, channels), jnp.bfloat16),
            pltpu.SemaphoreType.DMA((cols // ROWS,)),
        ],
        out_shape=jax.ShapeDtypeStruct((cols, tokens), jnp.bfloat16),
        compiler_params=params(),
        cost_estimate=pl.CostEstimate(
            flops=2 * cols * channels * tokens,
            bytes_accessed=2 * (cols * channels + channels * tokens + cols * tokens),
            transcendentals=0,
        ),
        name="query",
    )(off_chip(weights), scaled, inverse)


def tile_lists(order_ref, ids_ref, seq_here, tiles_dev):
    half = tiles_dev // 2
    for block in range(2):
        first = jnp.int32(0)
        second = jnp.int32(0)
        away = (jnp.int32(block) != seq_here).astype(jnp.int32)
        for spot in range(tiles_dev):
            tile = order_ref[block * tiles_dev + spot]
            late = tile // tiles_dev
            rank = jnp.where(late == 0, first, second)
            ids_ref[(2 * late + away) * half + rank] = tile
            first = first + (1 - late)
            second = second + late


def attend_body(chunk, sources, goes_on, ends, seq_ref, order_ref, mask_ref, query_ref, *refs):
    count = len(sources)
    pairs, refs = refs[:count], refs[count:]
    if goes_on:
        old_stats, old_weighted, *refs = refs
    if ends:
        weight_hbm, *refs = refs
        partial_refs, refs = refs[: 4 * PIECES], refs[4 * PIECES :]
        ids_ref, bias_ref, scores_ref, heads_ref, weight_ref, arrived = refs
        copies = fetches(weight_hbm, weight_ref, arrived)
        for copy in copies:
            copy.start()
    else:
        new_stats, new_weighted, ids_ref, bias_ref, scores_ref = refs
    cols, tokens = query_ref.shape
    half = tokens // TILE
    tile_lists(order_ref, ids_ref, seq_ref[0], 2 * half)
    lane_tile = lax.broadcasted_iota(jnp.int32, (1, tokens), 1) // TILE
    for index, source in enumerate(sources):
        for spot in range(half):
            key_tile = ids_ref[source * half + spot]
            bias = jnp.zeros((1, tokens), jnp.float32)
            for query_spot in range(half):
                query_tile = ids_ref[2 * chunk * half + query_spot]
                blocked = jnp.where(mask_ref[query_tile, key_tile] == 1, 0.0, MASKED_SCORE)
                bias = jnp.where(lane_tile == query_spot, blocked, bias)
            bias_ref[index * half + spot : index * half + spot + 1, :] = bias

    def one_head(head, carry):
        rows = pl.ds(pl.multiple_of(head * HEAD, HEAD), HEAD)
        value_rows = pl.ds(pl.multiple_of(cols + head * HEAD, HEAD), HEAD)
        query = query_ref[rows, :]
        old_top = old_stats[head, 0:1, :] if goes_on else None
        top = old_top
        for index in range(count):
            block = jnp.dot(pairs[index][rows, :].T, query, preferred_element_type=jnp.float32)
            for spot in range(half):
                line = index * half + spot
                piece = block[spot * TILE : (spot + 1) * TILE, :] + bias_ref[line : line + 1, :]
                scores_ref[line * TILE : (line + 1) * TILE, :] = piece
                best = jnp.max(piece, axis=0, keepdims=True)
                top = best if top is None else jnp.maximum(top, best)
        denom = None
        weighted = None
        if goes_on:
            shrink = jnp.exp2(old_top - top)
            denom = old_stats[head, 1:2, :] * shrink
            weighted = old_weighted[rows, :] * shrink
        for index in range(count):
            powers = jnp.exp2(scores_ref[index * tokens : (index + 1) * tokens, :] - top)
            summed = jnp.sum(powers, axis=0, keepdims=True)
            term = jnp.dot(
                pairs[index][value_rows, :],
                powers.astype(jnp.bfloat16),
                preferred_element_type=jnp.float32,
            )
            denom = summed if denom is None else denom + summed
            weighted = term if weighted is None else weighted + term
        if ends:
            heads_ref[rows, :] = (weighted / denom).astype(jnp.bfloat16)
        else:
            new_stats[head, 0:1, :] = top
            new_stats[head, 1:2, :] = denom
            new_weighted[rows, :] = weighted
        return carry

    lax.fori_loop(0, cols // HEAD, one_head, 0)
    if ends:
        width = weight_ref.shape[0] // (4 * PIECES)
        for copy in copies:
            copy.wait()
        for index, out in enumerate(partial_refs):
            block = weight_ref[index * width : (index + 1) * width, :]
            out[...] = jnp.dot(
                block, heads_ref[...], preferred_element_type=jnp.float32
            ).astype(jnp.bfloat16)


def attend_call(chunk, tables, queries, sources, state=None, out_t=None):
    cols, tokens = queries.shape
    heads = cols // HEAD
    count = len(sources)
    half = tokens // TILE
    goes_on, ends = state is not None, out_t is not None
    arguments = [queries] + [array for array, _ in sources] + (list(state) if goes_on else [])
    in_specs = [vmem_spec()] * len(arguments)
    scratch = [
        pltpu.SMEM((4 * half,), jnp.int32),
        pltpu.VMEM((count * half, tokens), jnp.float32),
        pltpu.VMEM((count * tokens, tokens), jnp.float32),
    ]
    if ends:
        in_specs += [off_chip_spec()]
        arguments += [out_t]
        width = out_t.shape[0] // (4 * PIECES)
        shapes = [jax.ShapeDtypeStruct((width, tokens), jnp.bfloat16)] * (4 * PIECES)
        scratch += [
            pltpu.VMEM((cols, tokens), jnp.bfloat16),
            pltpu.VMEM(out_t.shape, jnp.bfloat16),
            pltpu.SemaphoreType.DMA((4,)),
        ]
    else:
        shapes = [
            jax.ShapeDtypeStruct((heads, 2, tokens), jnp.float32),
            jax.ShapeDtypeStruct((cols, tokens), jnp.float32),
        ]
    return pl.pallas_call(
        functools.partial(attend_body, chunk, tuple(s for _, s in sources), goes_on, ends),
        in_specs=[smem_spec()] * 3 + in_specs,
        out_specs=[vmem_spec()] * len(shapes),
        scratch_shapes=scratch,
        out_shape=shapes,
        compiler_params=params(),
        cost_estimate=pl.CostEstimate(
            flops=4 * cols * tokens * tokens * count,
            bytes_accessed=2 * cols * tokens * (2 + 2 * count),
            transcendentals=heads * tokens * tokens * count,
        ),
        name="attend",
    )(*tables, *arguments)


def summed(own, back, onward, across, at_end):
    total = own.astype(jnp.float32) + back.astype(jnp.float32) + onward.astype(jnp.float32)
    return (total + jnp.where(at_end, across.astype(jnp.float32), 0.0)).astype(jnp.bfloat16)


def place_body(seq_ref, order_ref, ends_ref, *refs):
    firsts, refs = refs[:PIECES], refs[PIECES:]
    parts, (out_ref, second_ref) = refs[:-2], refs[-2:]
    width, tokens = firsts[0].shape
    tiles_dev = 2 * tokens // TILE
    at_end = ends_ref[0] == 1
    for piece in range(PIECES):
        addends = [parts[4 * piece + index][...] for index in range(4)]
        second_ref[piece * width : (piece + 1) * width, :] = summed(*addends, at_end)
    ranks = [jnp.int32(0), jnp.int32(0)]
    for position in range(tiles_dev):
        late = order_ref[seq_ref[0] * tiles_dev + position] // tiles_dev
        spot = pl.ds(pl.multiple_of(jnp.where(late == 0, ranks[0], ranks[1]) * TILE, TILE), TILE)
        here = slice(position * TILE, (position + 1) * TILE)

        @pl.when(late == 0)
        def _(spot=spot, here=here):
            for piece in range(PIECES):
                out_ref[piece * width : (piece + 1) * width, here] = firsts[piece][:, spot]

        @pl.when(late == 1)
        def _(spot=spot, here=here):
            out_ref[:, here] = second_ref[:, spot]

        ranks[0] = ranks[0] + (1 - late)
        ranks[1] = ranks[1] + late


def place_call(seq_here, stripe_order, at_end, firsts, parts):
    width, tokens = firsts[0].shape
    channels = width * PIECES
    return pl.pallas_call(
        place_body,
        in_specs=[smem_spec()] * 3 + [vmem_spec()] * (5 * PIECES),
        out_specs=vmem_spec(),
        scratch_shapes=[pltpu.VMEM((channels, tokens), jnp.bfloat16)],
        out_shape=jax.ShapeDtypeStruct((channels, 2 * tokens), jnp.bfloat16),
        compiler_params=params(),
        cost_estimate=pl.CostEstimate(
            flops=4 * channels * tokens, bytes_accessed=14 * channels * tokens, transcendentals=0
        ),
        name="place",
    )(seq_here, stripe_order, at_end, *firsts, *[part for piece in parts for part in piece])


FORWARD = [(0, 1), (1, 2), (2, 3), (3, 0)]
BACKWARD = [(1, 0), (2, 1), (3, 2), (0, 3)]
FOLDED = [(0, 1), (1, 3), (3, 2), (2, 0)]
UNFOLDED = [(1, 0), (3, 1), (2, 3), (0, 2)]


def gather_blocks(block, here):
    before = lax.ppermute(block, "tp", FORWARD)
    after = lax.ppermute(block, "tp", BACKWARD)
    relay = jnp.where(here == 2, before, jnp.where(here == 1, after, block))
    across = lax.ppermute(relay, "tp", UNFOLDED)
    return (block, before, after, across)


def plus(a, b, chosen):
    summed = a.astype(jnp.float32) + jnp.where(chosen, b.astype(jnp.float32), 0.0)
    return summed.astype(jnp.bfloat16)


def reduce_blocks(partials, here):
    own, down, up, sent = partials
    across = lax.ppermute(sent, "tp", FOLDED)
    back = lax.ppermute(plus(down, across, here == 2), "tp", BACKWARD)
    onward = lax.ppermute(plus(up, across, here == 1), "tp", FORWARD)
    return (own, back, onward, across)


def per_device_fast(
    clip_tokens, conv_taps, norm_gain, qkv_weight, out_weight, tile_mask, stripe_order
):
    tables = (conv_taps, stripe_order, tile_mask)
    conv_taps, stripe_order, tile_mask = (off_chip(table) for table in tables)
    seq = lax.axis_index("seq")
    here = lax.axis_index("tp")
    seq_here = seq.astype(jnp.int32)[None]
    at_end = ((here == 0) | (here == 3)).astype(jnp.int32)[None]
    blocks = jnp.stack([here, (here + 3) % 4, (here + 1) % 4, (here + 2) % 4]).astype(jnp.int32)
    tables = (seq_here, stripe_order, tile_mask)
    pieces = range(PIECES)

    def gathered(blocks_here):
        by_piece = [gather_blocks(block, here) for block in blocks_here]
        return [by_piece[p][owner] for owner in range(4) for p in pieces]

    def reduced(partials):
        return [reduce_blocks(partials[p::PIECES], here) for p in pieces]

    begun = [conv_call(seq_here, stripe_order, clip_tokens, conv_taps, p) for p in pieces]
    tokens_a, before = [], []
    for _, keep, send, tokens in begun:
        got = lax.ppermute(send, "seq", [(0, 1)])
        tokens_a.append(jnp.where(seq == 0, keep, got))
        before.append(lax.ppermute(tokens, "seq", [(0, 1)]))
    kinds, cols, channels = qkv_weight.shape
    weights = qkv_weight.reshape(kinds * cols, channels)
    gains = jnp.broadcast_to(norm_gain[:, None], (channels, 128))
    out_t = prepare_out(blocks, out_weight)
    shards_a = gathered(tokens_a)

    tokens_b = []
    for p in pieces:
        keep, send = conv_call(seq_here, stripe_order, before[p], conv_taps, p, begun[p][0])
        got = lax.ppermute(send, "seq", [(1, 0)])
        tokens_b.append(jnp.where(seq == 1, keep, got))

    swap = [(0, 1), (1, 0)]
    pair_a, *normed_a = project_pair(blocks, weights, gains, shards_a)
    peer_a = lax.ppermute(pair_a, "seq", swap)
    query_a = project_query(weights, *normed_a)
    shards_b = gathered(tokens_b)
    partials_a = attend_call(0, tables, query_a, [(pair_a, 0), (peer_a, 1)], out_t=out_t)
    parts_a = reduced(partials_a)
    pair_b, *normed_b = project_pair(blocks, weights, gains, shards_b)
    peer_b = lax.ppermute(pair_b, "seq", swap)
    query_b = project_query(weights, *normed_b)
    near = [(pair_a, 0), (peer_a, 1), (pair_b, 2)]
    state = attend_call(1, tables, query_b, near)
    partials_b = attend_call(1, tables, query_b, [(peer_b, 3)], state=state, out_t=out_t)
    parts_b = reduced(partials_b)
    firsts = [summed(*part, at_end == 1) for part in parts_a]
    return place_call(seq_here, stripe_order, at_end, firsts, parts_b)


def passed_along(block, axis, distance):
    devices = range(lax.axis_size(axis))
    route = [(i - distance, i) for i in devices if i - distance in devices]
    return lax.ppermute(block, axis, route)


def from_partner(block, axis, apart):
    count = lax.axis_size(axis)
    route = []
    for low in range(count):
        high = low | 1 << apart
        if high != low and high < count:
            route += [(low, high), (high, low)]
    return lax.ppermute(block, axis, route)


def causal_conv(local_tokens, before, conv_taps):
    channels = local_tokens.shape[0]
    frames = local_tokens.shape[1] // (FH * FW)
    stacked = (
        jnp.concatenate([before, local_tokens], axis=1)
        .astype(jnp.float32)
        .reshape(channels, frames + 2, FH, FW)
    )
    padded = jnp.pad(stacked, ((0, 0), (0, 0), (1, 1), (1, 1)))
    summed = jnp.zeros((channels, frames, FH, FW), jnp.float32)
    for time_off in range(3):
        for row_off in range(3):
            for col_off in range(3):
                tap_vec = conv_taps[time_off * 9 + row_off * 3 + col_off]
                summed = (
                    summed
                    + tap_vec[:, None, None, None]
                    * padded[
                        :,
                        time_off : time_off + frames,
                        row_off : row_off + FH,
                        col_off : col_off + FW,
                    ]
                )
    return (local_tokens.astype(jnp.float32) + summed.reshape(channels, -1)).astype(jnp.bfloat16)


def stripe_tables(stripe_order, tiles_dev):
    seq_count = lax.axis_size("seq")
    seq_here = lax.axis_index("seq")
    per_source = tiles_dev // seq_count
    blocks = stripe_order.reshape(seq_count, tiles_dev)
    owners = blocks // tiles_dev
    is_mine = (owners == seq_here).astype(jnp.int32)
    rank_of = jnp.cumsum(is_mine, axis=1) - 1
    slot_ids = jnp.arange(per_source, dtype=jnp.int32)
    picked = is_mine[:, None, :] * (rank_of[:, None, :] == slot_ids[None, :, None]).astype(
        jnp.int32
    )
    local_tiles = (blocks - seq_here * tiles_dev)[:, None, :]
    send_order = jnp.sum(picked * local_tiles, axis=2).reshape(-1)
    own_row = lax.dynamic_slice_in_dim(stripe_order, seq_here * tiles_dev, tiles_dev)
    sources = own_row // tiles_dev
    position = jnp.arange(tiles_dev, dtype=jnp.int32)
    earlier = (sources[:, None] == sources[None, :]) & (position[None, :] < position[:, None])
    place_order = sources * per_source + jnp.sum(earlier.astype(jnp.int32), axis=1)
    return (send_order, place_order, own_row)


def regroup(values, send_order, place_order):
    leading = values.shape[0]
    trailing = values.shape[2:]
    in_tiles = values.reshape((leading, values.shape[1] // TILE, TILE) + trailing)
    outgoing = jnp.take(in_tiles, send_order, axis=1)
    arrived = lax.all_to_all(outgoing, "seq", split_axis=1, concat_axis=1, tiled=True)
    placed = jnp.take(arrived, place_order, axis=1)
    return placed.reshape(values.shape)


def project(mixed, norm_gain, qkv_weight):
    channels = norm_gain.shape[0]
    widened = lax.all_gather(mixed, "tp", axis=0, tiled=True).astype(jnp.float32)
    scaled = (widened * norm_gain[:, None]).astype(jnp.bfloat16)
    projected = jnp.einsum("ct,khc->kth", scaled, qkv_weight, preferred_element_type=jnp.float32)
    squares = jnp.sum(widened * widened, axis=0)
    projected, squares = (projected, squares)
    inverse = lax.rsqrt(squares / channels + EPSILON)
    return (projected * inverse[None, :, None]).astype(jnp.bfloat16)


def position_mask(tile_mask, stripe_order, own_half):
    tiles_all = tile_mask.shape[0]
    tile_ids = jnp.arange(tiles_all, dtype=jnp.int32)
    own_onehot = (own_half[:, None] == tile_ids[None, :]).astype(jnp.float32)
    order_onehot = (stripe_order[:, None] == tile_ids[None, :]).astype(jnp.float32)
    rows_mask = jnp.dot(
        own_onehot, tile_mask.astype(jnp.float32), preferred_element_type=jnp.float32
    )
    return jnp.dot(rows_mask, order_onehot.T, preferred_element_type=jnp.float32)


def attend(queries_flat, key_values, pos_mask):
    row_count = queries_flat.shape[0]
    heads_dev = queries_flat.shape[1] // HEAD
    queries = queries_flat.reshape(row_count, heads_dev, HEAD)
    score_scale = 1.0 / math.sqrt(HEAD)
    tiles_dev = row_count // TILE
    tile_ids = jnp.arange(pos_mask.shape[1], dtype=jnp.int32)
    initial = (
        jnp.full((heads_dev, row_count), MASKED_SCORE, jnp.float32),
        jnp.zeros((heads_dev, row_count), jnp.float32),
        jnp.zeros((heads_dev, row_count, HEAD), jnp.float32),
    )
    fetched = lax.all_gather(key_values, "seq", axis=1, tiled=True)
    fetched_count = fetched.shape[1]
    key_block = 512

    def advance(block_index, state_now):
        top_score, denom, weighted = state_now
        offset = block_index * key_block
        key_rows = lax.dynamic_slice_in_dim(fetched[0], offset, key_block).reshape(
            key_block, heads_dev, HEAD
        )
        values = lax.dynamic_slice_in_dim(fetched[1], offset, key_block).reshape(
            key_block, heads_dev, HEAD
        )
        tile_pos = (offset + jnp.arange(key_block, dtype=jnp.int32)) // TILE
        onehot = (tile_pos[:, None] == tile_ids[None, :]).astype(jnp.float32)
        tile_allowed = (
            jnp.einsum("qn,kn->qk", pos_mask, onehot, preferred_element_type=jnp.float32) > 0.5
        )
        visible = jnp.broadcast_to(tile_allowed[:, None, :], (tiles_dev, TILE, key_block)).reshape(
            row_count, key_block
        )
        scores = (
            jnp.einsum("qhd,khd->hqk", queries, key_rows, preferred_element_type=jnp.float32)
            * score_scale
        )
        masked = jnp.where(visible[None], scores, MASKED_SCORE)
        new_top = jnp.maximum(top_score, jnp.max(masked, axis=2))
        powers = jnp.where(visible[None], jnp.exp(masked - new_top[:, :, None]), 0.0)
        shrink = jnp.exp(top_score - new_top)
        denom = denom * shrink + jnp.sum(powers, axis=2)
        weighted = weighted * shrink[:, :, None] + jnp.einsum(
            "hqk,khd->hqd", powers.astype(jnp.bfloat16), values, preferred_element_type=jnp.float32
        )
        return (new_top, denom, weighted)

    _, denom, weighted = lax.fori_loop(0, fetched_count // key_block, advance, initial)
    finished = (weighted / denom[:, :, None]).astype(jnp.bfloat16)
    return jnp.transpose(finished, (1, 0, 2)).reshape(row_count, heads_dev * HEAD)


def per_device_general(clip_tokens, conv_taps, norm_gain, qkv_weight, out_weight, tile_mask, stripe_order):
    tiles_dev = clip_tokens.shape[1] // TILE
    send_order, place_order, own_row = stripe_tables(stripe_order, tiles_dev)
    before = passed_along(clip_tokens, "seq", 1)
    mixed = causal_conv(clip_tokens, before, conv_taps)
    mixed = regroup(mixed, send_order, place_order)
    projected = project(mixed, norm_gain, qkv_weight)
    row_count = projected.shape[1]
    group_cols = projected.shape[2]
    half_rows = row_count // 2
    side = lax.axis_index("tp") % 2
    mine_first = side == 0
    query_send = lax.dynamic_slice_in_dim(projected[0], (1 - side) * half_rows, half_rows, axis=0)
    query_mine = lax.dynamic_slice_in_dim(projected[0], side * half_rows, half_rows, axis=0)
    kv_mine = projected[1:]
    query_other, kv_other = from_partner((query_send, kv_mine), "tp", 0)
    queries = jnp.where(
        mine_first,
        jnp.concatenate([query_mine, query_other], axis=1),
        jnp.concatenate([query_other, query_mine], axis=1),
    )
    key_values = jnp.where(
        mine_first,
        jnp.concatenate([kv_mine, kv_other], axis=2),
        jnp.concatenate([kv_other, kv_mine], axis=2),
    )
    own_half = lax.dynamic_slice_in_dim(own_row, side * (tiles_dev // 2), tiles_dev // 2)
    pos_mask = position_mask(tile_mask, stripe_order, own_half)
    pair_out = attend(queries, key_values, pos_mask)
    give_cols = lax.dynamic_slice_in_dim(pair_out, (1 - side) * group_cols, group_cols, axis=1)
    keep_cols = lax.dynamic_slice_in_dim(pair_out, side * group_cols, group_cols, axis=1)
    got_cols = from_partner(give_cols, "tp", 0)
    heads_out = jnp.where(
        mine_first,
        jnp.concatenate([keep_cols, got_cols], axis=0),
        jnp.concatenate([got_cols, keep_cols], axis=0),
    )
    return lax.psum_scatter(
        jnp.einsum("qg,gc->cq", heads_out, out_weight, preferred_element_type=jnp.float32).astype(
            jnp.bfloat16
        ),
        "tp",
        scatter_dimension=0,
        tiled=True,
    )


def solution(mesh):
    in_specs = (
        P("tp", ("dp", "seq")),
        P(None, "tp"),
        P(),
        P(None, "tp", None),
        P("tp", None),
        P(),
        P(),
    )
    out_specs = P("tp", ("dp", "seq"))

    def run(clip_tokens, conv_taps, norm_gain, qkv_weight, out_weight, tile_mask, stripe_order):
        arguments = (clip_tokens, conv_taps, norm_gain, qkv_weight, out_weight, tile_mask, stripe_order)
        tokens = clip_tokens.shape[1] // (mesh.shape["dp"] * mesh.shape["seq"])
        columns = qkv_weight.shape[1] // mesh.shape["tp"]
        two_halves = mesh.shape["seq"] == 2 and tokens == 2 * FRAME
        fast = two_halves and mesh.shape["tp"] == 4 and columns % HEAD == 0

        def per_device(*local):
            if not fast:
                return per_device_general(*local)
            return per_device_fast(*local)

        step = jax.shard_map(
            per_device, mesh=mesh, in_specs=in_specs, out_specs=out_specs, check_vma=False
        )
        return step(*arguments)

    return run
```

```python
import functools
import math

import jax
import jax.numpy as jnp
from jax import lax
from jax.experimental import pallas as pl
from jax.experimental.pallas import tpu as pltpu
from jax.sharding import PartitionSpec as P


HEAD = 128
TILE = 128
FH = 16
FW = 32
FRAME = FH * FW
TAPS = 27


EPSILON = 1e-06
MASKED_SCORE = -1e30
LOG2E = math.log2(math.e)

VMEM_LIMIT = 14 * 1024 * 1024


def vmem_spec():
    return pl.BlockSpec(memory_space=pltpu.VMEM)


def off_chip_spec():
    return pl.BlockSpec(memory_space=pltpu.HBM)


def off_chip(array):
    return pltpu.with_memory_space_constraint(array, pltpu.HBM)


def smem_spec():
    return pl.BlockSpec(memory_space=pltpu.SMEM)


def params(limit=VMEM_LIMIT):
    return pltpu.CompilerParams(vmem_limit_bytes=limit)


def fetches(source, target, semaphores):
    block = target.shape[0] // semaphores.shape[0]
    return [
        pltpu.make_async_copy(
            source.at[index * block : (index + 1) * block],
            target.at[index * block : (index + 1) * block],
            semaphores.at[index],
        )
        for index in range(semaphores.shape[0])
    ]


def column_shifts(pieces, column):
    right = [jnp.where(column > 0, pltpu.roll(piece, 1, 1), 0.0) for piece in pieces]
    left = [jnp.where(column < FW - 1, pltpu.roll(piece, TILE - 1, 1), 0.0) for piece in pieces]
    return (right, pieces, left)


def rows_joined(rows, lane):
    down = [pltpu.roll(piece, FW, 1) for piece in rows[0]]
    up = [pltpu.roll(piece, TILE - FW, 1) for piece in rows[2]]
    joined = []
    for spot, middle in enumerate(rows[1]):
        before = down[spot - 1] if spot > 0 else 0.0
        after = up[spot + 1] if spot + 1 < len(up) else 0.0
        above = jnp.where(lane < FW, before, down[spot])
        below = jnp.where(lane >= TILE - FW, after, up[spot])
        joined.append(middle + (above + below))
    return joined


def pack_slots(order_ref, slots_ref, seq_here, tiles_dev, positions):
    half = tiles_dev // 2
    kept = jnp.int32(0)
    sent = jnp.int32(half)
    for position in range(positions):
        tile = order_ref[position]
        mine = tile // tiles_dev == seq_here
        stays = jnp.int32(position // tiles_dev) == seq_here
        slot = jnp.where(stays, kept, sent)

        @pl.when(mine)
        def _(tile=tile, slot=slot):
            slots_ref[tile - seq_here * tiles_dev] = slot

        step = mine.astype(jnp.int32)
        kept = kept + jnp.where(stays, step, 0)
        sent = sent + jnp.where(stays, 0, step)


GROUP = 16
CHUNKS = 4
PIECES = 2


def conv_body(with_before, first_row, seq_ref, order_ref, tokens_ref, taps_ref, part_hbm, keep_ref, send_ref, *refs):
    if with_before:
        slots_ref, taps_scr, packed, part_ref, moving = refs
        source_ref = tokens_ref
        for copy in fetches(part_hbm, part_ref, moving):
            copy.start()
    else:
        copy_ref, slots_ref, taps_scr, packed, part_ref, moving, source_ref, arrived, taps_in, taps_arrived, left = refs
    channels, tokens = packed.shape
    tiles_dev = tokens // TILE
    per_frame = FRAME // TILE
    if not with_before:
        taps_copy = pltpu.make_async_copy(
            taps_ref.at[:, first_row : first_row + channels], taps_in, taps_arrived
        )
        taps_copy.start()
        copies = fetches(tokens_ref.at[first_row : first_row + channels], source_ref, arrived)
        for copy in copies:
            copy.start()
    pack_slots(order_ref, slots_ref, seq_ref[0], tiles_dev, order_ref.shape[0])
    if not with_before:
        taps_copy.wait()
    for first in range(0, channels, TILE):
        wide = taps_ref[:, first_row + first : first_row + first + TILE] if with_before else taps_in[:, first : first + TILE]
        taps_scr[first : first + TILE, :TAPS] = wide.T
    lane = lax.broadcasted_iota(jnp.int32, (GROUP, TILE), 1)
    column = lane % FW
    if with_before:
        reads = ([(0, 0), (1, 1)], [(0, 1)])
    else:
        reads = ([(2, 0)], [(1, 0), (2, 1)])

    def advance(step, carry, base=0):
        rows = pl.ds(pl.multiple_of(base + step * GROUP, GROUP), GROUP)
        taps = taps_scr[rows, :]
        shifts = []
        for frame in range(2):
            pieces = []
            for spot in range(per_frame):
                tile = frame * per_frame + spot
                pieces.append(source_ref[rows, tile * TILE : (tile + 1) * TILE].astype(jnp.float32))
            shifts.append(column_shifts(pieces, column))
        for frame in range(2):
            sums = []
            for row_off in range(3):
                line = [None] * per_frame
                for time_off, read in reads[frame]:
                    for col_off in range(3):
                        tap = time_off * 9 + row_off * 3 + col_off
                        weight = jnp.broadcast_to(taps[:, tap : tap + 1], (GROUP, TILE))
                        for spot in range(per_frame):
                            term = weight * shifts[read][col_off][spot]
                            line[spot] = term if line[spot] is None else line[spot] + term
                sums.append(line)
            for spot, value in enumerate(rows_joined(sums, lane)):
                tile = frame * per_frame + spot
                here = slice(tile * TILE, (tile + 1) * TILE)
                if with_before:
                    value = value + part_ref[rows, here]
                else:
                    value = value + shifts[frame][1][spot]
                    part_ref[rows, here] = value
                place = pl.ds(pl.multiple_of(slots_ref[tile] * TILE, TILE), TILE)
                packed[rows, place] = value.astype(jnp.bfloat16)
        return carry

    each = channels // CHUNKS

    def block_of(index):
        return pl.ds(index * each, each)

    def part_copy(index):
        block = block_of(index)
        if with_before:
            return pltpu.make_async_copy(part_hbm.at[block], part_ref.at[block], moving.at[index])
        return pltpu.make_async_copy(part_ref.at[block], part_hbm.at[block], moving.at[index])

    def arriving(index):
        theirs = pl.ds(first_row + index * each, each)
        return pltpu.make_async_copy(
            tokens_ref.at[theirs], source_ref.at[block_of(index)], arrived.at[index]
        )

    def leaving(index):
        block = block_of(index)
        return pltpu.make_async_copy(source_ref.at[block], copy_ref.at[block], left.at[index])

    def chunk(index, carry):
        if with_before:
            part_copy(index).wait()
        else:
            arriving(index).wait()
            leaving(index).start()
        later = functools.partial(advance, base=index * each)
        carry = lax.fori_loop(0, each // GROUP, later, carry, unroll=2)
        if not with_before:

            @pl.when(index > 0)
            def _():
                part_copy(index - 1).start()

        return carry

    lax.fori_loop(0, CHUNKS, chunk, 0)
    if not with_before:
        part_copy(CHUNKS - 1).start()
    keep_ref[...] = packed[:, : tokens // 2]
    send_ref[...] = packed[:, tokens // 2 :]
    if not with_before:
        for index in range(CHUNKS):
            leaving(index).wait()
            part_copy(index).wait()


def conv_call(seq_here, stripe_order, tokens, conv_taps, piece, part=None):
    count = tokens.shape[1]
    channels = conv_taps.shape[1] // PIECES
    packed_shape = jax.ShapeDtypeStruct((channels, count // 2), jnp.bfloat16)
    with_before = part is not None
    out_shape = [packed_shape, packed_shape]
    out_specs = [vmem_spec()] * 2
    scratch = [
        pltpu.SMEM((count // TILE,), jnp.int32),
        pltpu.VMEM((channels, 128), jnp.float32),
        pltpu.VMEM((channels, count), jnp.bfloat16),
        pltpu.VMEM((channels, count), jnp.float32),
        pltpu.SemaphoreType.DMA((CHUNKS,)),
    ]
    in_specs = [smem_spec(), smem_spec(), vmem_spec(), vmem_spec(), off_chip_spec()]
    if not with_before:
        in_specs = [smem_spec(), smem_spec(), off_chip_spec(), off_chip_spec()]
        tokens = off_chip(tokens)
        sum_shape = pltpu.HBM((channels, count), jnp.float32)
        out_shape = [sum_shape] + out_shape + [pltpu.HBM((channels, count), jnp.bfloat16)]
        out_specs = [off_chip_spec(), vmem_spec(), vmem_spec(), off_chip_spec()]
        scratch += [
            pltpu.VMEM((channels, count), jnp.bfloat16),
            pltpu.SemaphoreType.DMA((CHUNKS,)),
            pltpu.VMEM((TAPS, channels), jnp.float32),
            pltpu.SemaphoreType.DMA,
            pltpu.SemaphoreType.DMA((CHUNKS,)),
        ]
    return pl.pallas_call(
        functools.partial(conv_body, with_before, piece * channels),
        in_specs=in_specs,
        out_specs=out_specs,
        scratch_shapes=scratch,
        out_shape=out_shape,
        compiler_params=params(),
        cost_estimate=pl.CostEstimate(
            flops=channels * count * TAPS, bytes_accessed=channels * count * 8, transcendentals=0
        ),
        name="conv",
    )(seq_here, stripe_order, tokens, conv_taps, *([off_chip(part)] if with_before else []))


def prepare_body(blocks_ref, out_ref, out_out):
    out_out[...] = out_ref[...].T


def prepare_out(blocks, out_weight):
    cols, channels = out_weight.shape
    count = blocks.shape[0]
    width = channels // count
    return pl.pallas_call(
        prepare_body,
        grid_spec=pltpu.PrefetchScalarGridSpec(
            num_scalar_prefetch=1,
            grid=(count,),
            in_specs=[pl.BlockSpec((cols, width), lambda j, b: (0, b[j]))],
            out_specs=pl.BlockSpec((width, cols), lambda j, b: (j, 0)),
        ),
        out_shape=jax.ShapeDtypeStruct((channels, cols), jnp.bfloat16),
        compiler_params=params(),
        cost_estimate=pl.CostEstimate(
            flops=cols * channels, bytes_accessed=4 * cols * channels, transcendentals=0
        ),
        name="prepare",
    )(blocks, out_weight)


ROWS = 256


def products(weight_ref, tokens_ref, scale, copies, out_ref):
    for index, copy in enumerate(copies):
        copy.wait()
        here = slice(index * ROWS, (index + 1) * ROWS)
        total = jnp.dot(weight_ref[here, :], tokens_ref[...], preferred_element_type=jnp.float32)
        out_ref[here, :] = (total * scale).astype(jnp.bfloat16)


def pair_body(blocks_ref, weight_hbm, gains_ref, *refs):
    shards, (pair_ref, tokens_ref, inverse_ref, weight_ref, arrived) = refs[:-5], refs[-5:]
    rows = weight_ref.shape[0]
    skipped = weight_hbm.shape[0] - rows
    copies = fetches(weight_hbm.at[skipped : skipped + rows], weight_ref, arrived)
    for copy in copies:
        copy.start()
    width, tokens = shards[0].shape
    lines = 128
    squares = jnp.zeros((1, tokens), jnp.float32)
    for index, shard in enumerate(shards):
        owner, piece = divmod(index, PIECES)
        start = (blocks_ref[owner] * PIECES + piece) * width
        for first in range(0, width, lines):
            there = pl.ds(pl.multiple_of(start + first, lines), lines)
            wide = shard[first : first + lines, :].astype(jnp.float32)
            squares = squares + jnp.sum(wide * wide, axis=0, keepdims=True)
            gain = jnp.concatenate([gains_ref[there, :]] * (tokens // 128), axis=1)
            tokens_ref[there, :] = (wide * gain).astype(jnp.bfloat16)
    inverse = lax.rsqrt(squares / (len(shards) * width) + EPSILON)
    inverse_ref[...] = inverse
    products(weight_ref, tokens_ref, inverse, copies, pair_ref)


def query_body(weight_hbm, tokens_ref, inverse_ref, query_ref, weight_ref, arrived):
    copies = fetches(weight_hbm.at[: weight_ref.shape[0]], weight_ref, arrived)
    for copy in copies:
        copy.start()
    products(weight_ref, tokens_ref, inverse_ref[...] * (LOG2E / math.sqrt(HEAD)), copies, query_ref)


def project_pair(blocks, weights, gains, shards):
    rows, channels = weights.shape
    tokens = shards[0].shape[1]
    cols = rows // 3
    return pl.pallas_call(
        pair_body,
        in_specs=[smem_spec(), off_chip_spec()] + [vmem_spec()] * (1 + len(shards)),
        out_specs=[vmem_spec()] * 3,
        scratch_shapes=[
            pltpu.VMEM((2 * cols, channels), jnp.bfloat16),
            pltpu.SemaphoreType.DMA((2 * cols // ROWS,)),
        ],
        out_shape=[
            jax.ShapeDtypeStruct((2 * cols, tokens), jnp.bfloat16),
            jax.ShapeDtypeStruct((channels, tokens), jnp.bfloat16),
            jax.ShapeDtypeStruct((1, tokens), jnp.float32),
        ],
        compiler_params=params(),
        cost_estimate=pl.CostEstimate(
            flops=4 * cols * channels * tokens,
            bytes_accessed=2 * (2 * cols * channels + 2 * channels * tokens + 2 * cols * tokens),
            transcendentals=0,
        ),
        name="pair",
    )(blocks, off_chip(weights), gains, *shards)


def project_query(weights, scaled, inverse):
    rows, channels = weights.shape
    tokens = scaled.shape[1]
    cols = rows // 3
    return pl.pallas_call(
        query_body,
        in_specs=[off_chip_spec(), vmem_spec(), vmem_spec()],
        out_specs=vmem_spec(),
        scratch_shapes=[
            pltpu.VMEM((cols, channels), jnp.bfloat16),
            pltpu.SemaphoreType.DMA((cols // ROWS,)),
        ],
        out_shape=jax.ShapeDtypeStruct((cols, tokens), jnp.bfloat16),
        compiler_params=params(),
        cost_estimate=pl.CostEstimate(
            flops=2 * cols * channels * tokens,
            bytes_accessed=2 * (cols * channels + channels * tokens + cols * tokens),
            transcendentals=0,
        ),
        name="query",
    )(off_chip(weights), scaled, inverse)


def tile_lists(order_ref, ids_ref, seq_here, tiles_dev):
    half = tiles_dev // 2
    for block in range(2):
        first = jnp.int32(0)
        second = jnp.int32(0)
        away = (jnp.int32(block) != seq_here).astype(jnp.int32)
        for spot in range(tiles_dev):
            tile = order_ref[block * tiles_dev + spot]
            late = tile // tiles_dev
            rank = jnp.where(late == 0, first, second)
            ids_ref[(2 * late + away) * half + rank] = tile
            first = first + (1 - late)
            second = second + late


def attend_body(chunk, sources, goes_on, ends, seq_ref, order_ref, mask_ref, query_ref, *refs):
    count = len(sources)
    pairs, refs = refs[:count], refs[count:]
    if goes_on:
        old_stats, old_weighted, *refs = refs
    if ends:
        weight_hbm, *refs = refs
        partial_refs, refs = refs[: 4 * PIECES], refs[4 * PIECES :]
        ids_ref, bias_ref, scores_ref, heads_ref, weight_ref, arrived = refs
        copies = fetches(weight_hbm, weight_ref, arrived)
        for copy in copies:
            copy.start()
    else:
        new_stats, new_weighted, ids_ref, bias_ref, scores_ref = refs
    cols, tokens = query_ref.shape
    half = tokens // TILE
    tile_lists(order_ref, ids_ref, seq_ref[0], 2 * half)
    lane_tile = lax.broadcasted_iota(jnp.int32, (1, tokens), 1) // TILE
    for index, source in enumerate(sources):
        for spot in range(half):
            key_tile = ids_ref[source * half + spot]
            bias = jnp.zeros((1, tokens), jnp.float32)
            for query_spot in range(half):
                query_tile = ids_ref[2 * chunk * half + query_spot]
                blocked = jnp.where(mask_ref[query_tile, key_tile] == 1, 0.0, MASKED_SCORE)
                bias = jnp.where(lane_tile == query_spot, blocked, bias)
            bias_ref[index * half + spot : index * half + spot + 1, :] = bias

    def one_head(head, carry):
        rows = pl.ds(pl.multiple_of(head * HEAD, HEAD), HEAD)
        value_rows = pl.ds(pl.multiple_of(cols + head * HEAD, HEAD), HEAD)
        query = query_ref[rows, :]
        old_top = old_stats[head, 0:1, :] if goes_on else None
        top = old_top
        for index in range(count):
            block = jnp.dot(pairs[index][rows, :].T, query, preferred_element_type=jnp.float32)
            for spot in range(half):
                line = index * half + spot
                piece = block[spot * TILE : (spot + 1) * TILE, :] + bias_ref[line : line + 1, :]
                scores_ref[line * TILE : (line + 1) * TILE, :] = piece
                best = jnp.max(piece, axis=0, keepdims=True)
                top = best if top is None else jnp.maximum(top, best)
        denom = None
        weighted = None
        if goes_on:
            shrink = jnp.exp2(old_top - top)
            denom = old_stats[head, 1:2, :] * shrink
            weighted = old_weighted[rows, :] * shrink
        for index in range(count):
            powers = jnp.exp2(scores_ref[index * tokens : (index + 1) * tokens, :] - top)
            summed = jnp.sum(powers, axis=0, keepdims=True)
            term = jnp.dot(
                pairs[index][value_rows, :],
                powers.astype(jnp.bfloat16),
                preferred_element_type=jnp.float32,
            )
            denom = summed if denom is None else denom + summed
            weighted = term if weighted is None else weighted + term
        if ends:
            heads_ref[rows, :] = (weighted / denom).astype(jnp.bfloat16)
        else:
            new_stats[head, 0:1, :] = top
            new_stats[head, 1:2, :] = denom
            new_weighted[rows, :] = weighted
        return carry

    lax.fori_loop(0, cols // HEAD, one_head, 0)
    if ends:
        width = weight_ref.shape[0] // (4 * PIECES)
        for copy in copies:
            copy.wait()
        for index, out in enumerate(partial_refs):
            block = weight_ref[index * width : (index + 1) * width, :]
            out[...] = jnp.dot(
                block, heads_ref[...], preferred_element_type=jnp.float32
            ).astype(jnp.bfloat16)


def attend_call(chunk, tables, queries, sources, state=None, out_t=None):
    cols, tokens = queries.shape
    heads = cols // HEAD
    count = len(sources)
    half = tokens // TILE
    goes_on, ends = state is not None, out_t is not None
    arguments = [queries] + [array for array, _ in sources] + (list(state) if goes_on else [])
    in_specs = [vmem_spec()] * len(arguments)
    scratch = [
        pltpu.SMEM((4 * half,), jnp.int32),
        pltpu.VMEM((count * half, tokens), jnp.float32),
        pltpu.VMEM((count * tokens, tokens), jnp.float32),
    ]
    if ends:
        in_specs += [off_chip_spec()]
        arguments += [out_t]
        width = out_t.shape[0] // (4 * PIECES)
        shapes = [jax.ShapeDtypeStruct((width, tokens), jnp.bfloat16)] * (4 * PIECES)
        scratch += [
            pltpu.VMEM((cols, tokens), jnp.bfloat16),
            pltpu.VMEM(out_t.shape, jnp.bfloat16),
            pltpu.SemaphoreType.DMA((4,)),
        ]
    else:
        shapes = [
            jax.ShapeDtypeStruct((heads, 2, tokens), jnp.float32),
            jax.ShapeDtypeStruct((cols, tokens), jnp.float32),
        ]
    return pl.pallas_call(
        functools.partial(attend_body, chunk, tuple(s for _, s in sources), goes_on, ends),
        in_specs=[smem_spec()] * 3 + in_specs,
        out_specs=[vmem_spec()] * len(shapes),
        scratch_shapes=scratch,
        out_shape=shapes,
        compiler_params=params(),
        cost_estimate=pl.CostEstimate(
            flops=4 * cols * tokens * tokens * count,
            bytes_accessed=2 * cols * tokens * (2 + 2 * count),
            transcendentals=heads * tokens * tokens * count,
        ),
        name="attend",
    )(*tables, *arguments)


def summed(own, back, onward, across, at_end):
    total = own.astype(jnp.float32) + back.astype(jnp.float32) + onward.astype(jnp.float32)
    return (total + jnp.where(at_end, across.astype(jnp.float32), 0.0)).astype(jnp.bfloat16)


def place_body(seq_ref, order_ref, ends_ref, *refs):
    firsts, refs = refs[:PIECES], refs[PIECES:]
    parts, (out_ref, second_ref) = refs[:-2], refs[-2:]
    width, tokens = firsts[0].shape
    tiles_dev = 2 * tokens // TILE
    at_end = ends_ref[0] == 1
    for piece in range(PIECES):
        addends = [parts[4 * piece + index][...] for index in range(4)]
        second_ref[piece * width : (piece + 1) * width, :] = summed(*addends, at_end)
    ranks = [jnp.int32(0), jnp.int32(0)]
    for position in range(tiles_dev):
        late = order_ref[seq_ref[0] * tiles_dev + position] // tiles_dev
        spot = pl.ds(pl.multiple_of(jnp.where(late == 0, ranks[0], ranks[1]) * TILE, TILE), TILE)
        here = slice(position * TILE, (position + 1) * TILE)

        @pl.when(late == 0)
        def _(spot=spot, here=here):
            for piece in range(PIECES):
                out_ref[piece * width : (piece + 1) * width, here] = firsts[piece][:, spot]

        @pl.when(late == 1)
        def _(spot=spot, here=here):
            out_ref[:, here] = second_ref[:, spot]

        ranks[0] = ranks[0] + (1 - late)
        ranks[1] = ranks[1] + late


def place_call(seq_here, stripe_order, at_end, firsts, parts):
    width, tokens = firsts[0].shape
    channels = width * PIECES
    return pl.pallas_call(
        place_body,
        in_specs=[smem_spec()] * 3 + [vmem_spec()] * (5 * PIECES),
        out_specs=vmem_spec(),
        scratch_shapes=[pltpu.VMEM((channels, tokens), jnp.bfloat16)],
        out_shape=jax.ShapeDtypeStruct((channels, 2 * tokens), jnp.bfloat16),
        compiler_params=params(),
        cost_estimate=pl.CostEstimate(
            flops=4 * channels * tokens, bytes_accessed=14 * channels * tokens, transcendentals=0
        ),
        name="place",
    )(seq_here, stripe_order, at_end, *firsts, *[part for piece in parts for part in piece])


FORWARD = [(0, 1), (1, 2), (2, 3), (3, 0)]
BACKWARD = [(1, 0), (2, 1), (3, 2), (0, 3)]
FOLDED = [(0, 1), (1, 3), (3, 2), (2, 0)]
UNFOLDED = [(1, 0), (3, 1), (2, 3), (0, 2)]


def gather_blocks(block, here):
    before = lax.ppermute(block, "tp", FORWARD)
    after = lax.ppermute(block, "tp", BACKWARD)
    relay = jnp.where(here == 2, before, jnp.where(here == 1, after, block))
    across = lax.ppermute(relay, "tp", UNFOLDED)
    return (block, before, after, across)


def plus(a, b, chosen):
    summed = a.astype(jnp.float32) + jnp.where(chosen, b.astype(jnp.float32), 0.0)
    return summed.astype(jnp.bfloat16)


def reduce_blocks(partials, here):
    own, down, up, sent = partials
    across = lax.ppermute(sent, "tp", FOLDED)
    back = lax.ppermute(plus(down, across, here == 2), "tp", BACKWARD)
    onward = lax.ppermute(plus(up, across, here == 1), "tp", FORWARD)
    return (own, back, onward, across)


def per_device_fast(
    clip_tokens, conv_taps, norm_gain, qkv_weight, out_weight, tile_mask, stripe_order
):
    tables = (conv_taps, stripe_order, tile_mask)
    conv_taps, stripe_order, tile_mask = (off_chip(table) for table in tables)
    seq = lax.axis_index("seq")
    here = lax.axis_index("tp")
    seq_here = seq.astype(jnp.int32)[None]
    at_end = ((here == 0) | (here == 3)).astype(jnp.int32)[None]
    blocks = jnp.stack([here, (here + 3) % 4, (here + 1) % 4, (here + 2) % 4]).astype(jnp.int32)
    tables = (seq_here, stripe_order, tile_mask)
    pieces = range(PIECES)

    def gathered(blocks_here):
        by_piece = [gather_blocks(block, here) for block in blocks_here]
        return [by_piece[p][owner] for owner in range(4) for p in pieces]

    def reduced(partials):
        return [reduce_blocks(partials[p::PIECES], here) for p in pieces]

    begun = [conv_call(seq_here, stripe_order, clip_tokens, conv_taps, p) for p in pieces]
    tokens_a, before = [], []
    for _, keep, send, tokens in begun:
        got = lax.ppermute(send, "seq", [(0, 1)])
        tokens_a.append(jnp.where(seq == 0, keep, got))
        before.append(lax.ppermute(tokens, "seq", [(0, 1)]))
    kinds, cols, channels = qkv_weight.shape
    weights = qkv_weight.reshape(kinds * cols, channels)
    gains = jnp.broadcast_to(norm_gain[:, None], (channels, 128))
    out_t = prepare_out(blocks, out_weight)
    shards_a = gathered(tokens_a)

    tokens_b = []
    for p in pieces:
        keep, send = conv_call(seq_here, stripe_order, before[p], conv_taps, p, begun[p][0])
        got = lax.ppermute(send, "seq", [(1, 0)])
        tokens_b.append(jnp.where(seq == 1, keep, got))

    swap = [(0, 1), (1, 0)]
    pair_a, *normed_a = project_pair(blocks, weights, gains, shards_a)
    peer_a = lax.ppermute(pair_a, "seq", swap)
    query_a = project_query(weights, *normed_a)
    shards_b = gathered(tokens_b)
    partials_a = attend_call(0, tables, query_a, [(pair_a, 0), (peer_a, 1)], out_t=out_t)
    parts_a = reduced(partials_a)
    pair_b, *normed_b = project_pair(blocks, weights, gains, shards_b)
    peer_b = lax.ppermute(pair_b, "seq", swap)
    query_b = project_query(weights, *normed_b)
    near = [(pair_a, 0), (peer_a, 1), (pair_b, 2)]
    state = attend_call(1, tables, query_b, near)
    partials_b = attend_call(1, tables, query_b, [(peer_b, 3)], state=state, out_t=out_t)
    parts_b = reduced(partials_b)
    firsts = [summed(*part, at_end == 1) for part in parts_a]
    return place_call(seq_here, stripe_order, at_end, firsts, parts_b)


def passed_along(block, axis, distance):
    devices = range(lax.axis_size(axis))
    route = [(i - distance, i) for i in devices if i - distance in devices]
    return lax.ppermute(block, axis, route)


def from_partner(block, axis, apart):
    count = lax.axis_size(axis)
    route = []
    for low in range(count):
        high = low | 1 << apart
        if high != low and high < count:
            route += [(low, high), (high, low)]
    return lax.ppermute(block, axis, route)


def causal_conv(local_tokens, before, conv_taps):
    channels = local_tokens.shape[0]
    frames = local_tokens.shape[1] // (FH * FW)
    stacked = (
        jnp.concatenate([before, local_tokens], axis=1)
        .astype(jnp.float32)
        .reshape(channels, frames + 2, FH, FW)
    )
    padded = jnp.pad(stacked, ((0, 0), (0, 0), (1, 1), (1, 1)))
    summed = jnp.zeros((channels, frames, FH, FW), jnp.float32)
    for time_off in range(3):
        for row_off in range(3):
            for col_off in range(3):
                tap_vec = conv_taps[time_off * 9 + row_off * 3 + col_off]
                summed = (
                    summed
                    + tap_vec[:, None, None, None]
                    * padded[
                        :,
                        time_off : time_off + frames,
                        row_off : row_off + FH,
                        col_off : col_off + FW,
                    ]
                )
    return (local_tokens.astype(jnp.float32) + summed.reshape(channels, -1)).astype(jnp.bfloat16)


def stripe_tables(stripe_order, tiles_dev):
    seq_count = lax.axis_size("seq")
    seq_here = lax.axis_index("seq")
    per_source = tiles_dev // seq_count
    blocks = stripe_order.reshape(seq_count, tiles_dev)
    owners = blocks // tiles_dev
    is_mine = (owners == seq_here).astype(jnp.int32)
    rank_of = jnp.cumsum(is_mine, axis=1) - 1
    slot_ids = jnp.arange(per_source, dtype=jnp.int32)
    picked = is_mine[:, None, :] * (rank_of[:, None, :] == slot_ids[None, :, None]).astype(
        jnp.int32
    )
    local_tiles = (blocks - seq_here * tiles_dev)[:, None, :]
    send_order = jnp.sum(picked * local_tiles, axis=2).reshape(-1)
    own_row = lax.dynamic_slice_in_dim(stripe_order, seq_here * tiles_dev, tiles_dev)
    sources = own_row // tiles_dev
    position = jnp.arange(tiles_dev, dtype=jnp.int32)
    earlier = (sources[:, None] == sources[None, :]) & (position[None, :] < position[:, None])
    place_order = sources * per_source + jnp.sum(earlier.astype(jnp.int32), axis=1)
    return (send_order, place_order, own_row)


def regroup(values, send_order, place_order):
    leading = values.shape[0]
    trailing = values.shape[2:]
    in_tiles = values.reshape((leading, values.shape[1] // TILE, TILE) + trailing)
    outgoing = jnp.take(in_tiles, send_order, axis=1)
    arrived = lax.all_to_all(outgoing, "seq", split_axis=1, concat_axis=1, tiled=True)
    placed = jnp.take(arrived, place_order, axis=1)
    return placed.reshape(values.shape)


def project(mixed, norm_gain, qkv_weight):
    channels = norm_gain.shape[0]
    widened = lax.all_gather(mixed, "tp", axis=0, tiled=True).astype(jnp.float32)
    scaled = (widened * norm_gain[:, None]).astype(jnp.bfloat16)
    projected = jnp.einsum("ct,khc->kth", scaled, qkv_weight, preferred_element_type=jnp.float32)
    squares = jnp.sum(widened * widened, axis=0)
    projected, squares = (projected, squares)
    inverse = lax.rsqrt(squares / channels + EPSILON)
    return (projected * inverse[None, :, None]).astype(jnp.bfloat16)


def position_mask(tile_mask, stripe_order, own_half):
    tiles_all = tile_mask.shape[0]
    tile_ids = jnp.arange(tiles_all, dtype=jnp.int32)
    own_onehot = (own_half[:, None] == tile_ids[None, :]).astype(jnp.float32)
    order_onehot = (stripe_order[:, None] == tile_ids[None, :]).astype(jnp.float32)
    rows_mask = jnp.dot(
        own_onehot, tile_mask.astype(jnp.float32), preferred_element_type=jnp.float32
    )
    return jnp.dot(rows_mask, order_onehot.T, preferred_element_type=jnp.float32)


def attend(queries_flat, key_values, pos_mask):
    row_count = queries_flat.shape[0]
    heads_dev = queries_flat.shape[1] // HEAD
    queries = queries_flat.reshape(row_count, heads_dev, HEAD)
    score_scale = 1.0 / math.sqrt(HEAD)
    tiles_dev = row_count // TILE
    tile_ids = jnp.arange(pos_mask.shape[1], dtype=jnp.int32)
    initial = (
        jnp.full((heads_dev, row_count), MASKED_SCORE, jnp.float32),
        jnp.zeros((heads_dev, row_count), jnp.float32),
        jnp.zeros((heads_dev, row_count, HEAD), jnp.float32),
    )
    fetched = lax.all_gather(key_values, "seq", axis=1, tiled=True)
    fetched_count = fetched.shape[1]
    key_block = 512

    def advance(block_index, state_now):
        top_score, denom, weighted = state_now
        offset = block_index * key_block
        key_rows = lax.dynamic_slice_in_dim(fetched[0], offset, key_block).reshape(
            key_block, heads_dev, HEAD
        )
        values = lax.dynamic_slice_in_dim(fetched[1], offset, key_block).reshape(
            key_block, heads_dev, HEAD
        )
        tile_pos = (offset + jnp.arange(key_block, dtype=jnp.int32)) // TILE
        onehot = (tile_pos[:, None] == tile_ids[None, :]).astype(jnp.float32)
        tile_allowed = (
            jnp.einsum("qn,kn->qk", pos_mask, onehot, preferred_element_type=jnp.float32) > 0.5
        )
        visible = jnp.broadcast_to(tile_allowed[:, None, :], (tiles_dev, TILE, key_block)).reshape(
            row_count, key_block
        )
        scores = (
            jnp.einsum("qhd,khd->hqk", queries, key_rows, preferred_element_type=jnp.float32)
            * score_scale
        )
        masked = jnp.where(visible[None], scores, MASKED_SCORE)
        new_top = jnp.maximum(top_score, jnp.max(masked, axis=2))
        powers = jnp.where(visible[None], jnp.exp(masked - new_top[:, :, None]), 0.0)
        shrink = jnp.exp(top_score - new_top)
        denom = denom * shrink + jnp.sum(powers, axis=2)
        weighted = weighted * shrink[:, :, None] + jnp.einsum(
            "hqk,khd->hqd", powers.astype(jnp.bfloat16), values, preferred_element_type=jnp.float32
        )
        return (new_top, denom, weighted)

    _, denom, weighted = lax.fori_loop(0, fetched_count // key_block, advance, initial)
    finished = (weighted / denom[:, :, None]).astype(jnp.bfloat16)
    return jnp.transpose(finished, (1, 0, 2)).reshape(row_count, heads_dev * HEAD)


def per_device_general(clip_tokens, conv_taps, norm_gain, qkv_weight, out_weight, tile_mask, stripe_order):
    tiles_dev = clip_tokens.shape[1] // TILE
    send_order, place_order, own_row = stripe_tables(stripe_order, tiles_dev)
    before = passed_along(clip_tokens, "seq", 1)
    mixed = causal_conv(clip_tokens, before, conv_taps)
    mixed = regroup(mixed, send_order, place_order)
    projected = project(mixed, norm_gain, qkv_weight)
    row_count = projected.shape[1]
    group_cols = projected.shape[2]
    half_rows = row_count // 2
    side = lax.axis_index("tp") % 2
    mine_first = side == 0
    query_send = lax.dynamic_slice_in_dim(projected[0], (1 - side) * half_rows, half_rows, axis=0)
    query_mine = lax.dynamic_slice_in_dim(projected[0], side * half_rows, half_rows, axis=0)
    kv_mine = projected[1:]
    query_other, kv_other = from_partner((query_send, kv_mine), "tp", 0)
    queries = jnp.where(
        mine_first,
        jnp.concatenate([query_mine, query_other], axis=1),
        jnp.concatenate([query_other, query_mine], axis=1),
    )
    key_values = jnp.where(
        mine_first,
        jnp.concatenate([kv_mine, kv_other], axis=2),
        jnp.concatenate([kv_other, kv_mine], axis=2),
    )
    own_half = lax.dynamic_slice_in_dim(own_row, side * (tiles_dev // 2), tiles_dev // 2)
    pos_mask = position_mask(tile_mask, stripe_order, own_half)
    pair_out = attend(queries, key_values, pos_mask)
    give_cols = lax.dynamic_slice_in_dim(pair_out, (1 - side) * group_cols, group_cols, axis=1)
    keep_cols = lax.dynamic_slice_in_dim(pair_out, side * group_cols, group_cols, axis=1)
    got_cols = from_partner(give_cols, "tp", 0)
    heads_out = jnp.where(
        mine_first,
        jnp.concatenate([keep_cols, got_cols], axis=0),
        jnp.concatenate([got_cols, keep_cols], axis=0),
    )
    return lax.psum_scatter(
        jnp.einsum("qg,gc->cq", heads_out, out_weight, preferred_element_type=jnp.float32).astype(
            jnp.bfloat16
        ),
        "tp",
        scatter_dimension=0,
        tiled=True,
    )


def solution(mesh):
    in_specs = (
        P("tp", ("dp", "seq")),
        P(None, "tp"),
        P(),
        P(None, "tp", None),
        P("tp", None),
        P(),
        P(),
    )
    out_specs = P("tp", ("dp", "seq"))

    def run(clip_tokens, conv_taps, norm_gain, qkv_weight, out_weight, tile_mask, stripe_order):
        arguments = (clip_tokens, conv_taps, norm_gain, qkv_weight, out_weight, tile_mask, stripe_order)
        tokens = clip_tokens.shape[1] // (mesh.shape["dp"] * mesh.shape["seq"])
        columns = qkv_weight.shape[1] // mesh.shape["tp"]
        two_halves = mesh.shape["seq"] == 2 and tokens == 2 * FRAME
        fast = two_halves and mesh.shape["tp"] == 4 and columns % HEAD == 0

        def per_device(*local):
            if not fast:
                return per_device_general(*local)
            return per_device_fast(*local)

        step = jax.shard_map(
            per_device, mesh=mesh, in_specs=in_specs, out_specs=out_specs, check_vma=False
        )
        return step(*arguments)

    return run
```

```python
import functools
import math

import jax
import jax.numpy as jnp
from jax import lax
from jax.experimental import pallas as pl
from jax.experimental.pallas import tpu as pltpu
from jax.sharding import PartitionSpec as P


HEAD = 128
TILE = 128
FH = 16
FW = 32
FRAME = FH * FW
TAPS = 27


EPSILON = 1e-06
MASKED_SCORE = -1e30
LOG2E = math.log2(math.e)

VMEM_LIMIT = 10 * 1024 * 1024


def vmem_spec():
    return pl.BlockSpec(memory_space=pltpu.VMEM)


def off_chip_spec():
    return pl.BlockSpec(memory_space=pltpu.HBM)


def off_chip(array):
    return pltpu.with_memory_space_constraint(array, pltpu.HBM)


def smem_spec():
    return pl.BlockSpec(memory_space=pltpu.SMEM)


def params(limit=VMEM_LIMIT):
    return pltpu.CompilerParams(vmem_limit_bytes=limit)


def fetches(source, target, semaphores):
    block = target.shape[0] // semaphores.shape[0]
    return [
        pltpu.make_async_copy(
            source.at[index * block : (index + 1) * block],
            target.at[index * block : (index + 1) * block],
            semaphores.at[index],
        )
        for index in range(semaphores.shape[0])
    ]


def column_shifts(pieces, column):
    right = [jnp.where(column > 0, pltpu.roll(piece, 1, 1), 0.0) for piece in pieces]
    left = [jnp.where(column < FW - 1, pltpu.roll(piece, TILE - 1, 1), 0.0) for piece in pieces]
    return (right, pieces, left)


def rows_joined(rows, lane):
    down = [pltpu.roll(piece, FW, 1) for piece in rows[0]]
    up = [pltpu.roll(piece, TILE - FW, 1) for piece in rows[2]]
    joined = []
    for spot, middle in enumerate(rows[1]):
        before = down[spot - 1] if spot > 0 else 0.0
        after = up[spot + 1] if spot + 1 < len(up) else 0.0
        above = jnp.where(lane < FW, before, down[spot])
        below = jnp.where(lane >= TILE - FW, after, up[spot])
        joined.append(middle + (above + below))
    return joined


def pack_slots(order_ref, slots_ref, seq_here, tiles_dev, positions):
    half = tiles_dev // 2
    kept = jnp.int32(0)
    sent = jnp.int32(half)
    for position in range(positions):
        tile = order_ref[position]
        mine = tile // tiles_dev == seq_here
        stays = jnp.int32(position // tiles_dev) == seq_here
        slot = jnp.where(stays, kept, sent)

        @pl.when(mine)
        def _(tile=tile, slot=slot):
            slots_ref[tile - seq_here * tiles_dev] = slot

        step = mine.astype(jnp.int32)
        kept = kept + jnp.where(stays, step, 0)
        sent = sent + jnp.where(stays, 0, step)


GROUP = 16
CHUNKS = 4
PIECES = 2


def conv_body(with_before, first_row, seq_ref, order_ref, tokens_ref, taps_ref, part_ref, keep_ref, send_ref, *refs):
    if with_before:
        slots_ref, taps_scr, packed = refs
        source_ref = tokens_ref
    else:
        copy_ref, slots_ref, taps_scr, packed, source_ref, arrived, taps_in, taps_arrived, left = refs
    channels, tokens = packed.shape
    tiles_dev = tokens // TILE
    per_frame = FRAME // TILE
    if not with_before:
        taps_copy = pltpu.make_async_copy(
            taps_ref.at[:, first_row : first_row + channels], taps_in, taps_arrived
        )
        taps_copy.start()
        copies = fetches(tokens_ref.at[first_row : first_row + channels], source_ref, arrived)
        for copy in copies:
            copy.start()
    pack_slots(order_ref, slots_ref, seq_ref[0], tiles_dev, order_ref.shape[0])
    if not with_before:
        taps_copy.wait()
    for first in range(0, channels, TILE):
        wide = taps_ref[:, first_row + first : first_row + first + TILE] if with_before else taps_in[:, first : first + TILE]
        taps_scr[first : first + TILE, :TAPS] = wide.T
    lane = lax.broadcasted_iota(jnp.int32, (GROUP, TILE), 1)
    column = lane % FW
    if with_before:
        reads = ([(0, 0), (1, 1)], [(0, 1)])
    else:
        reads = ([(2, 0)], [(1, 0), (2, 1)])

    def advance(step, carry, base=0):
        rows = pl.ds(pl.multiple_of(base + step * GROUP, GROUP), GROUP)
        taps = taps_scr[rows, :]
        shifts = []
        for frame in range(2):
            pieces = []
            for spot in range(per_frame):
                tile = frame * per_frame + spot
                pieces.append(source_ref[rows, tile * TILE : (tile + 1) * TILE].astype(jnp.float32))
            shifts.append(column_shifts(pieces, column))
        for frame in range(2):
            sums = []
            for row_off in range(3):
                line = [None] * per_frame
                for time_off, read in reads[frame]:
                    for col_off in range(3):
                        tap = time_off * 9 + row_off * 3 + col_off
                        weight = jnp.broadcast_to(taps[:, tap : tap + 1], (GROUP, TILE))
                        for spot in range(per_frame):
                            term = weight * shifts[read][col_off][spot]
                            line[spot] = term if line[spot] is None else line[spot] + term
                sums.append(line)
            for spot, value in enumerate(rows_joined(sums, lane)):
                tile = frame * per_frame + spot
                here = slice(tile * TILE, (tile + 1) * TILE)
                if with_before:
                    value = value + part_ref[rows, here]
                else:
                    value = value + shifts[frame][1][spot]
                    part_ref[rows, here] = value
                place = pl.ds(pl.multiple_of(slots_ref[tile] * TILE, TILE), TILE)
                packed[rows, place] = value.astype(jnp.bfloat16)
        return carry

    steps = channels // GROUP
    if with_before:
        lax.fori_loop(0, steps, advance, 0, unroll=4)
    else:
        each = steps // CHUNKS

        def leaving(begin, index):
            block = pl.ds(begin, each * GROUP)
            return pltpu.make_async_copy(source_ref.at[block], copy_ref.at[block], left.at[index])

        def chunk(index, carry):
            begin = index * each * GROUP
            pltpu.make_async_copy(
                tokens_ref.at[pl.ds(first_row + begin, each * GROUP)],
                source_ref.at[pl.ds(begin, each * GROUP)],
                arrived.at[index],
            ).wait()
            leaving(begin, index).start()
            later = functools.partial(advance, base=begin)
            return lax.fori_loop(0, each, later, carry, unroll=4)

        lax.fori_loop(0, CHUNKS, chunk, 0)
        for index in range(CHUNKS):
            leaving(index * each * GROUP, index).wait()
    keep_ref[...] = packed[:, : tokens // 2]
    send_ref[...] = packed[:, tokens // 2 :]


def conv_call(seq_here, stripe_order, tokens, conv_taps, piece, part=None):
    count = tokens.shape[1]
    channels = conv_taps.shape[1] // PIECES
    packed_shape = jax.ShapeDtypeStruct((channels, count // 2), jnp.bfloat16)
    with_before = part is not None
    out_shape = [packed_shape, packed_shape]
    out_specs = [vmem_spec()] * 2
    scratch = [
        pltpu.SMEM((count // TILE,), jnp.int32),
        pltpu.VMEM((channels, 128), jnp.float32),
        pltpu.VMEM((channels, count), jnp.bfloat16),
    ]
    in_specs = [smem_spec(), smem_spec(), vmem_spec(), vmem_spec(), vmem_spec()]
    if not with_before:
        in_specs = [smem_spec(), smem_spec(), off_chip_spec(), off_chip_spec()]
        tokens = off_chip(tokens)
        sum_shape = jax.ShapeDtypeStruct((channels, count), jnp.float32)
        out_shape = [sum_shape] + out_shape + [pltpu.HBM((channels, count), jnp.bfloat16)]
        out_specs = [vmem_spec()] * 3 + [off_chip_spec()]
        scratch += [
            pltpu.VMEM((channels, count), jnp.bfloat16),
            pltpu.SemaphoreType.DMA((CHUNKS,)),
            pltpu.VMEM((TAPS, channels), jnp.float32),
            pltpu.SemaphoreType.DMA,
            pltpu.SemaphoreType.DMA((CHUNKS,)),
        ]
    return pl.pallas_call(
        functools.partial(conv_body, with_before, piece * channels),
        in_specs=in_specs,
        out_specs=out_specs,
        scratch_shapes=scratch,
        out_shape=out_shape,
        compiler_params=params(),
        cost_estimate=pl.CostEstimate(
            flops=channels * count * TAPS, bytes_accessed=channels * count * 8, transcendentals=0
        ),
        name="conv",
    )(seq_here, stripe_order, tokens, conv_taps, *([part] if with_before else []))


def prepare_body(blocks_ref, out_ref, out_out):
    out_out[...] = out_ref[...].T


def prepare_out(blocks, out_weight):
    cols, channels = out_weight.shape
    count = blocks.shape[0]
    width = channels // count
    return pl.pallas_call(
        prepare_body,
        grid_spec=pltpu.PrefetchScalarGridSpec(
            num_scalar_prefetch=1,
            grid=(count,),
            in_specs=[pl.BlockSpec((cols, width), lambda j, b: (0, b[j]))],
            out_specs=pl.BlockSpec((width, cols), lambda j, b: (j, 0)),
        ),
        out_shape=jax.ShapeDtypeStruct((channels, cols), jnp.bfloat16),
        compiler_params=params(),
        cost_estimate=pl.CostEstimate(
            flops=cols * channels, bytes_accessed=4 * cols * channels, transcendentals=0
        ),
        name="prepare",
    )(blocks, out_weight)


ROWS = 256


def products(weight_ref, tokens_ref, scale, copies, out_ref):
    for index, copy in enumerate(copies):
        copy.wait()
        here = slice(index * ROWS, (index + 1) * ROWS)
        total = jnp.dot(weight_ref[here, :], tokens_ref[...], preferred_element_type=jnp.float32)
        out_ref[here, :] = (total * scale).astype(jnp.bfloat16)


def pair_body(blocks_ref, weight_hbm, gains_ref, *refs):
    shards, (pair_ref, tokens_ref, inverse_ref, weight_ref, arrived) = refs[:-5], refs[-5:]
    rows = weight_ref.shape[0]
    skipped = weight_hbm.shape[0] - rows
    copies = fetches(weight_hbm.at[skipped : skipped + rows], weight_ref, arrived)
    for copy in copies:
        copy.start()
    width, tokens = shards[0].shape
    lines = 128
    squares = jnp.zeros((1, tokens), jnp.float32)
    for index, shard in enumerate(shards):
        owner, piece = divmod(index, PIECES)
        start = (blocks_ref[owner] * PIECES + piece) * width
        for first in range(0, width, lines):
            there = pl.ds(pl.multiple_of(start + first, lines), lines)
            wide = shard[first : first + lines, :].astype(jnp.float32)
            squares = squares + jnp.sum(wide * wide, axis=0, keepdims=True)
            gain = jnp.concatenate([gains_ref[there, :]] * (tokens // 128), axis=1)
            tokens_ref[there, :] = (wide * gain).astype(jnp.bfloat16)
    inverse = lax.rsqrt(squares / (len(shards) * width) + EPSILON)
    inverse_ref[...] = inverse
    products(weight_ref, tokens_ref, inverse, copies, pair_ref)


def query_body(weight_hbm, tokens_ref, inverse_ref, query_ref, weight_ref, arrived):
    copies = fetches(weight_hbm.at[: weight_ref.shape[0]], weight_ref, arrived)
    for copy in copies:
        copy.start()
    products(weight_ref, tokens_ref, inverse_ref[...] * (LOG2E / math.sqrt(HEAD)), copies, query_ref)


def project_pair(blocks, weights, gains, shards):
    rows, channels = weights.shape
    tokens = shards[0].shape[1]
    cols = rows // 3
    return pl.pallas_call(
        pair_body,
        in_specs=[smem_spec(), off_chip_spec()] + [vmem_spec()] * (1 + len(shards)),
        out_specs=[vmem_spec()] * 3,
        scratch_shapes=[
            pltpu.VMEM((2 * cols, channels), jnp.bfloat16),
            pltpu.SemaphoreType.DMA((2 * cols // ROWS,)),
        ],
        out_shape=[
            jax.ShapeDtypeStruct((2 * cols, tokens), jnp.bfloat16),
            jax.ShapeDtypeStruct((channels, tokens), jnp.bfloat16),
            jax.ShapeDtypeStruct((1, tokens), jnp.float32),
        ],
        compiler_params=params(),
        cost_estimate=pl.CostEstimate(
            flops=4 * cols * channels * tokens,
            bytes_accessed=2 * (2 * cols * channels + 2 * channels * tokens + 2 * cols * tokens),
            transcendentals=0,
        ),
        name="pair",
    )(blocks, off_chip(weights), gains, *shards)


def project_query(weights, scaled, inverse):
    rows, channels = weights.shape
    tokens = scaled.shape[1]
    cols = rows // 3
    return pl.pallas_call(
        query_body,
        in_specs=[off_chip_spec(), vmem_spec(), vmem_spec()],
        out_specs=vmem_spec(),
        scratch_shapes=[
            pltpu.VMEM((cols, channels), jnp.bfloat16),
            pltpu.SemaphoreType.DMA((cols // ROWS,)),
        ],
        out_shape=jax.ShapeDtypeStruct((cols, tokens), jnp.bfloat16),
        compiler_params=params(),
        cost_estimate=pl.CostEstimate(
            flops=2 * cols * channels * tokens,
            bytes_accessed=2 * (cols * channels + channels * tokens + cols * tokens),
            transcendentals=0,
        ),
        name="query",
    )(off_chip(weights), scaled, inverse)


def tile_lists(order_ref, ids_ref, seq_here, tiles_dev):
    half = tiles_dev // 2
    for block in range(2):
        first = jnp.int32(0)
        second = jnp.int32(0)
        away = (jnp.int32(block) != seq_here).astype(jnp.int32)
        for spot in range(tiles_dev):
            tile = order_ref[block * tiles_dev + spot]
            late = tile // tiles_dev
            rank = jnp.where(late == 0, first, second)
            ids_ref[(2 * late + away) * half + rank] = tile
            first = first + (1 - late)
            second = second + late


def attend_body(chunk, sources, goes_on, ends, seq_ref, order_ref, mask_ref, query_ref, *refs):
    count = len(sources)
    pairs, refs = refs[:count], refs[count:]
    if goes_on:
        old_stats, old_weighted, *refs = refs
    if ends:
        weight_hbm, *refs = refs
        partial_refs, refs = refs[: 4 * PIECES], refs[4 * PIECES :]
        ids_ref, bias_ref, scores_ref, heads_ref, weight_ref, arrived = refs
        copies = fetches(weight_hbm, weight_ref, arrived)
        for copy in copies:
            copy.start()
    else:
        new_stats, new_weighted, ids_ref, bias_ref, scores_ref = refs
    cols, tokens = query_ref.shape
    half = tokens // TILE
    tile_lists(order_ref, ids_ref, seq_ref[0], 2 * half)
    lane_tile = lax.broadcasted_iota(jnp.int32, (1, tokens), 1) // TILE
    for index, source in enumerate(sources):
        for spot in range(half):
            key_tile = ids_ref[source * half + spot]
            bias = jnp.zeros((1, tokens), jnp.float32)
            for query_spot in range(half):
                query_tile = ids_ref[2 * chunk * half + query_spot]
                blocked = jnp.where(mask_ref[query_tile, key_tile] == 1, 0.0, MASKED_SCORE)
                bias = jnp.where(lane_tile == query_spot, blocked, bias)
            bias_ref[index * half + spot : index * half + spot + 1, :] = bias

    def one_head(head, carry):
        rows = pl.ds(pl.multiple_of(head * HEAD, HEAD), HEAD)
        value_rows = pl.ds(pl.multiple_of(cols + head * HEAD, HEAD), HEAD)
        query = query_ref[rows, :]
        old_top = old_stats[head, 0:1, :] if goes_on else None
        top = old_top
        for index in range(count):
            block = jnp.dot(pairs[index][rows, :].T, query, preferred_element_type=jnp.float32)
            for spot in range(half):
                line = index * half + spot
                piece = block[spot * TILE : (spot + 1) * TILE, :] + bias_ref[line : line + 1, :]
                scores_ref[line * TILE : (line + 1) * TILE, :] = piece
                best = jnp.max(piece, axis=0, keepdims=True)
                top = best if top is None else jnp.maximum(top, best)
        denom = None
        weighted = None
        if goes_on:
            shrink = jnp.exp2(old_top - top)
            denom = old_stats[head, 1:2, :] * shrink
            weighted = old_weighted[rows, :] * shrink
        for index in range(count):
            powers = jnp.exp2(scores_ref[index * tokens : (index + 1) * tokens, :] - top)
            summed = jnp.sum(powers, axis=0, keepdims=True)
            term = jnp.dot(
                pairs[index][value_rows, :],
                powers.astype(jnp.bfloat16),
                preferred_element_type=jnp.float32,
            )
            denom = summed if denom is None else denom + summed
            weighted = term if weighted is None else weighted + term
        if ends:
            heads_ref[rows, :] = (weighted / denom).astype(jnp.bfloat16)
        else:
            new_stats[head, 0:1, :] = top
            new_stats[head, 1:2, :] = denom
            new_weighted[rows, :] = weighted
        return carry

    lax.fori_loop(0, cols // HEAD, one_head, 0)
    if ends:
        width = weight_ref.shape[0] // (4 * PIECES)
        for copy in copies:
            copy.wait()
        for index, out in enumerate(partial_refs):
            block = weight_ref[index * width : (index + 1) * width, :]
            out[...] = jnp.dot(
                block, heads_ref[...], preferred_element_type=jnp.float32
            ).astype(jnp.bfloat16)


def attend_call(chunk, tables, queries, sources, state=None, out_t=None):
    cols, tokens = queries.shape
    heads = cols // HEAD
    count = len(sources)
    half = tokens // TILE
    goes_on, ends = state is not None, out_t is not None
    arguments = [queries] + [array for array, _ in sources] + (list(state) if goes_on else [])
    in_specs = [vmem_spec()] * len(arguments)
    scratch = [
        pltpu.SMEM((4 * half,), jnp.int32),
        pltpu.VMEM((count * half, tokens), jnp.float32),
        pltpu.VMEM((count * tokens, tokens), jnp.float32),
    ]
    if ends:
        in_specs += [off_chip_spec()]
        arguments += [out_t]
        width = out_t.shape[0] // (4 * PIECES)
        shapes = [jax.ShapeDtypeStruct((width, tokens), jnp.bfloat16)] * (4 * PIECES)
        scratch += [
            pltpu.VMEM((cols, tokens), jnp.bfloat16),
            pltpu.VMEM(out_t.shape, jnp.bfloat16),
            pltpu.SemaphoreType.DMA((4,)),
        ]
    else:
        shapes = [
            jax.ShapeDtypeStruct((heads, 2, tokens), jnp.float32),
            jax.ShapeDtypeStruct((cols, tokens), jnp.float32),
        ]
    return pl.pallas_call(
        functools.partial(attend_body, chunk, tuple(s for _, s in sources), goes_on, ends),
        in_specs=[smem_spec()] * 3 + in_specs,
        out_specs=[vmem_spec()] * len(shapes),
        scratch_shapes=scratch,
        out_shape=shapes,
        compiler_params=params(),
        cost_estimate=pl.CostEstimate(
            flops=4 * cols * tokens * tokens * count,
            bytes_accessed=2 * cols * tokens * (2 + 2 * count),
            transcendentals=heads * tokens * tokens * count,
        ),
        name="attend",
    )(*tables, *arguments)


def summed(own, back, onward, across, at_end):
    total = own.astype(jnp.float32) + back.astype(jnp.float32) + onward.astype(jnp.float32)
    return (total + jnp.where(at_end, across.astype(jnp.float32), 0.0)).astype(jnp.bfloat16)


def place_body(seq_ref, order_ref, ends_ref, *refs):
    firsts, refs = refs[:PIECES], refs[PIECES:]
    parts, (out_ref, second_ref) = refs[:-2], refs[-2:]
    width, tokens = firsts[0].shape
    tiles_dev = 2 * tokens // TILE
    at_end = ends_ref[0] == 1
    for piece in range(PIECES):
        addends = [parts[4 * piece + index][...] for index in range(4)]
        second_ref[piece * width : (piece + 1) * width, :] = summed(*addends, at_end)
    ranks = [jnp.int32(0), jnp.int32(0)]
    for position in range(tiles_dev):
        late = order_ref[seq_ref[0] * tiles_dev + position] // tiles_dev
        spot = pl.ds(pl.multiple_of(jnp.where(late == 0, ranks[0], ranks[1]) * TILE, TILE), TILE)
        here = slice(position * TILE, (position + 1) * TILE)

        @pl.when(late == 0)
        def _(spot=spot, here=here):
            for piece in range(PIECES):
                out_ref[piece * width : (piece + 1) * width, here] = firsts[piece][:, spot]

        @pl.when(late == 1)
        def _(spot=spot, here=here):
            out_ref[:, here] = second_ref[:, spot]

        ranks[0] = ranks[0] + (1 - late)
        ranks[1] = ranks[1] + late


def place_call(seq_here, stripe_order, at_end, firsts, parts):
    width, tokens = firsts[0].shape
    channels = width * PIECES
    return pl.pallas_call(
        place_body,
        in_specs=[smem_spec()] * 3 + [vmem_spec()] * (5 * PIECES),
        out_specs=vmem_spec(),
        scratch_shapes=[pltpu.VMEM((channels, tokens), jnp.bfloat16)],
        out_shape=jax.ShapeDtypeStruct((channels, 2 * tokens), jnp.bfloat16),
        compiler_params=params(),
        cost_estimate=pl.CostEstimate(
            flops=4 * channels * tokens, bytes_accessed=14 * channels * tokens, transcendentals=0
        ),
        name="place",
    )(seq_here, stripe_order, at_end, *firsts, *[part for piece in parts for part in piece])


FORWARD = [(0, 1), (1, 2), (2, 3), (3, 0)]
BACKWARD = [(1, 0), (2, 1), (3, 2), (0, 3)]
FOLDED = [(0, 1), (1, 3), (3, 2), (2, 0)]
UNFOLDED = [(1, 0), (3, 1), (2, 3), (0, 2)]


def gather_blocks(block, here):
    before = lax.ppermute(block, "tp", FORWARD)
    after = lax.ppermute(block, "tp", BACKWARD)
    relay = jnp.where(here == 2, before, jnp.where(here == 1, after, block))
    across = lax.ppermute(relay, "tp", UNFOLDED)
    return (block, before, after, across)


def plus(a, b, chosen):
    summed = a.astype(jnp.float32) + jnp.where(chosen, b.astype(jnp.float32), 0.0)
    return summed.astype(jnp.bfloat16)


def reduce_blocks(partials, here):
    own, down, up, sent = partials
    across = lax.ppermute(sent, "tp", FOLDED)
    back = lax.ppermute(plus(down, across, here == 2), "tp", BACKWARD)
    onward = lax.ppermute(plus(up, across, here == 1), "tp", FORWARD)
    return (own, back, onward, across)


def per_device_fast(
    clip_tokens, conv_taps, norm_gain, qkv_weight, out_weight, tile_mask, stripe_order
):
    tables = (conv_taps, stripe_order, tile_mask)
    conv_taps, stripe_order, tile_mask = (off_chip(table) for table in tables)
    seq = lax.axis_index("seq")
    here = lax.axis_index("tp")
    seq_here = seq.astype(jnp.int32)[None]
    at_end = ((here == 0) | (here == 3)).astype(jnp.int32)[None]
    blocks = jnp.stack([here, (here + 3) % 4, (here + 1) % 4, (here + 2) % 4]).astype(jnp.int32)
    tables = (seq_here, stripe_order, tile_mask)
    pieces = range(PIECES)

    def gathered(blocks_here):
        by_piece = [gather_blocks(block, here) for block in blocks_here]
        return [by_piece[p][owner] for owner in range(4) for p in pieces]

    def reduced(partials):
        return [reduce_blocks(partials[p::PIECES], here) for p in pieces]

    begun = [conv_call(seq_here, stripe_order, clip_tokens, conv_taps, p) for p in pieces]
    tokens_a, before = [], []
    for _, keep, send, tokens in begun:
        got = lax.ppermute(send, "seq", [(0, 1)])
        tokens_a.append(jnp.where(seq == 0, keep, got))
        before.append(lax.ppermute(tokens, "seq", [(0, 1)]))
    kinds, cols, channels = qkv_weight.shape
    weights = qkv_weight.reshape(kinds * cols, channels)
    gains = jnp.broadcast_to(norm_gain[:, None], (channels, 128))
    out_t = prepare_out(blocks, out_weight)
    shards_a = gathered(tokens_a)

    tokens_b = []
    for p in pieces:
        keep, send = conv_call(seq_here, stripe_order, before[p], conv_taps, p, begun[p][0])
        got = lax.ppermute(send, "seq", [(1, 0)])
        tokens_b.append(jnp.where(seq == 1, keep, got))

    swap = [(0, 1), (1, 0)]
    pair_a, *normed_a = project_pair(blocks, weights, gains, shards_a)
    peer_a = lax.ppermute(pair_a, "seq", swap)
    query_a = project_query(weights, *normed_a)
    shards_b = gathered(tokens_b)
    partials_a = attend_call(0, tables, query_a, [(pair_a, 0), (peer_a, 1)], out_t=out_t)
    parts_a = reduced(partials_a)
    pair_b, *normed_b = project_pair(blocks, weights, gains, shards_b)
    peer_b = lax.ppermute(pair_b, "seq", swap)
    query_b = project_query(weights, *normed_b)
    near = [(pair_a, 0), (peer_a, 1), (pair_b, 2)]
    state = attend_call(1, tables, query_b, near)
    partials_b = attend_call(1, tables, query_b, [(peer_b, 3)], state=state, out_t=out_t)
    parts_b = reduced(partials_b)
    firsts = [summed(*part, at_end == 1) for part in parts_a]
    return place_call(seq_here, stripe_order, at_end, firsts, parts_b)


def passed_along(block, axis, distance):
    devices = range(lax.axis_size(axis))
    route = [(i - distance, i) for i in devices if i - distance in devices]
    return lax.ppermute(block, axis, route)


def from_partner(block, axis, apart):
    count = lax.axis_size(axis)
    route = []
    for low in range(count):
        high = low | 1 << apart
        if high != low and high < count:
            route += [(low, high), (high, low)]
    return lax.ppermute(block, axis, route)


def causal_conv(local_tokens, before, conv_taps):
    channels = local_tokens.shape[0]
    frames = local_tokens.shape[1] // (FH * FW)
    stacked = (
        jnp.concatenate([before, local_tokens], axis=1)
        .astype(jnp.float32)
        .reshape(channels, frames + 2, FH, FW)
    )
    padded = jnp.pad(stacked, ((0, 0), (0, 0), (1, 1), (1, 1)))
    summed = jnp.zeros((channels, frames, FH, FW), jnp.float32)
    for time_off in range(3):
        for row_off in range(3):
            for col_off in range(3):
                tap_vec = conv_taps[time_off * 9 + row_off * 3 + col_off]
                summed = (
                    summed
                    + tap_vec[:, None, None, None]
                    * padded[
                        :,
                        time_off : time_off + frames,
                        row_off : row_off + FH,
                        col_off : col_off + FW,
                    ]
                )
    return (local_tokens.astype(jnp.float32) + summed.reshape(channels, -1)).astype(jnp.bfloat16)


def stripe_tables(stripe_order, tiles_dev):
    seq_count = lax.axis_size("seq")
    seq_here = lax.axis_index("seq")
    per_source = tiles_dev // seq_count
    blocks = stripe_order.reshape(seq_count, tiles_dev)
    owners = blocks // tiles_dev
    is_mine = (owners == seq_here).astype(jnp.int32)
    rank_of = jnp.cumsum(is_mine, axis=1) - 1
    slot_ids = jnp.arange(per_source, dtype=jnp.int32)
    picked = is_mine[:, None, :] * (rank_of[:, None, :] == slot_ids[None, :, None]).astype(
        jnp.int32
    )
    local_tiles = (blocks - seq_here * tiles_dev)[:, None, :]
    send_order = jnp.sum(picked * local_tiles, axis=2).reshape(-1)
    own_row = lax.dynamic_slice_in_dim(stripe_order, seq_here * tiles_dev, tiles_dev)
    sources = own_row // tiles_dev
    position = jnp.arange(tiles_dev, dtype=jnp.int32)
    earlier = (sources[:, None] == sources[None, :]) & (position[None, :] < position[:, None])
    place_order = sources * per_source + jnp.sum(earlier.astype(jnp.int32), axis=1)
    return (send_order, place_order, own_row)


def regroup(values, send_order, place_order):
    leading = values.shape[0]
    trailing = values.shape[2:]
    in_tiles = values.reshape((leading, values.shape[1] // TILE, TILE) + trailing)
    outgoing = jnp.take(in_tiles, send_order, axis=1)
    arrived = lax.all_to_all(outgoing, "seq", split_axis=1, concat_axis=1, tiled=True)
    placed = jnp.take(arrived, place_order, axis=1)
    return placed.reshape(values.shape)


def project(mixed, norm_gain, qkv_weight):
    channels = norm_gain.shape[0]
    widened = lax.all_gather(mixed, "tp", axis=0, tiled=True).astype(jnp.float32)
    scaled = (widened * norm_gain[:, None]).astype(jnp.bfloat16)
    projected = jnp.einsum("ct,khc->kth", scaled, qkv_weight, preferred_element_type=jnp.float32)
    squares = jnp.sum(widened * widened, axis=0)
    projected, squares = (projected, squares)
    inverse = lax.rsqrt(squares / channels + EPSILON)
    return (projected * inverse[None, :, None]).astype(jnp.bfloat16)


def position_mask(tile_mask, stripe_order, own_half):
    tiles_all = tile_mask.shape[0]
    tile_ids = jnp.arange(tiles_all, dtype=jnp.int32)
    own_onehot = (own_half[:, None] == tile_ids[None, :]).astype(jnp.float32)
    order_onehot = (stripe_order[:, None] == tile_ids[None, :]).astype(jnp.float32)
    rows_mask = jnp.dot(
        own_onehot, tile_mask.astype(jnp.float32), preferred_element_type=jnp.float32
    )
    return jnp.dot(rows_mask, order_onehot.T, preferred_element_type=jnp.float32)


def attend(queries_flat, key_values, pos_mask):
    row_count = queries_flat.shape[0]
    heads_dev = queries_flat.shape[1] // HEAD
    queries = queries_flat.reshape(row_count, heads_dev, HEAD)
    score_scale = 1.0 / math.sqrt(HEAD)
    tiles_dev = row_count // TILE
    tile_ids = jnp.arange(pos_mask.shape[1], dtype=jnp.int32)
    initial = (
        jnp.full((heads_dev, row_count), MASKED_SCORE, jnp.float32),
        jnp.zeros((heads_dev, row_count), jnp.float32),
        jnp.zeros((heads_dev, row_count, HEAD), jnp.float32),
    )
    fetched = lax.all_gather(key_values, "seq", axis=1, tiled=True)
    fetched_count = fetched.shape[1]
    key_block = 512

    def advance(block_index, state_now):
        top_score, denom, weighted = state_now
        offset = block_index * key_block
        key_rows = lax.dynamic_slice_in_dim(fetched[0], offset, key_block).reshape(
            key_block, heads_dev, HEAD
        )
        values = lax.dynamic_slice_in_dim(fetched[1], offset, key_block).reshape(
            key_block, heads_dev, HEAD
        )
        tile_pos = (offset + jnp.arange(key_block, dtype=jnp.int32)) // TILE
        onehot = (tile_pos[:, None] == tile_ids[None, :]).astype(jnp.float32)
        tile_allowed = (
            jnp.einsum("qn,kn->qk", pos_mask, onehot, preferred_element_type=jnp.float32) > 0.5
        )
        visible = jnp.broadcast_to(tile_allowed[:, None, :], (tiles_dev, TILE, key_block)).reshape(
            row_count, key_block
        )
        scores = (
            jnp.einsum("qhd,khd->hqk", queries, key_rows, preferred_element_type=jnp.float32)
            * score_scale
        )
        masked = jnp.where(visible[None], scores, MASKED_SCORE)
        new_top = jnp.maximum(top_score, jnp.max(masked, axis=2))
        powers = jnp.where(visible[None], jnp.exp(masked - new_top[:, :, None]), 0.0)
        shrink = jnp.exp(top_score - new_top)
        denom = denom * shrink + jnp.sum(powers, axis=2)
        weighted = weighted * shrink[:, :, None] + jnp.einsum(
            "hqk,khd->hqd", powers.astype(jnp.bfloat16), values, preferred_element_type=jnp.float32
        )
        return (new_top, denom, weighted)

    _, denom, weighted = lax.fori_loop(0, fetched_count // key_block, advance, initial)
    finished = (weighted / denom[:, :, None]).astype(jnp.bfloat16)
    return jnp.transpose(finished, (1, 0, 2)).reshape(row_count, heads_dev * HEAD)


def per_device_general(clip_tokens, conv_taps, norm_gain, qkv_weight, out_weight, tile_mask, stripe_order):
    tiles_dev = clip_tokens.shape[1] // TILE
    send_order, place_order, own_row = stripe_tables(stripe_order, tiles_dev)
    before = passed_along(clip_tokens, "seq", 1)
    mixed = causal_conv(clip_tokens, before, conv_taps)
    mixed = regroup(mixed, send_order, place_order)
    projected = project(mixed, norm_gain, qkv_weight)
    row_count = projected.shape[1]
    group_cols = projected.shape[2]
    half_rows = row_count // 2
    side = lax.axis_index("tp") % 2
    mine_first = side == 0
    query_send = lax.dynamic_slice_in_dim(projected[0], (1 - side) * half_rows, half_rows, axis=0)
    query_mine = lax.dynamic_slice_in_dim(projected[0], side * half_rows, half_rows, axis=0)
    kv_mine = projected[1:]
    query_other, kv_other = from_partner((query_send, kv_mine), "tp", 0)
    queries = jnp.where(
        mine_first,
        jnp.concatenate([query_mine, query_other], axis=1),
        jnp.concatenate([query_other, query_mine], axis=1),
    )
    key_values = jnp.where(
        mine_first,
        jnp.concatenate([kv_mine, kv_other], axis=2),
        jnp.concatenate([kv_other, kv_mine], axis=2),
    )
    own_half = lax.dynamic_slice_in_dim(own_row, side * (tiles_dev // 2), tiles_dev // 2)
    pos_mask = position_mask(tile_mask, stripe_order, own_half)
    pair_out = attend(queries, key_values, pos_mask)
    give_cols = lax.dynamic_slice_in_dim(pair_out, (1 - side) * group_cols, group_cols, axis=1)
    keep_cols = lax.dynamic_slice_in_dim(pair_out, side * group_cols, group_cols, axis=1)
    got_cols = from_partner(give_cols, "tp", 0)
    heads_out = jnp.where(
        mine_first,
        jnp.concatenate([keep_cols, got_cols], axis=0),
        jnp.concatenate([got_cols, keep_cols], axis=0),
    )
    return lax.psum_scatter(
        jnp.einsum("qg,gc->cq", heads_out, out_weight, preferred_element_type=jnp.float32).astype(
            jnp.bfloat16
        ),
        "tp",
        scatter_dimension=0,
        tiled=True,
    )


def solution(mesh):
    in_specs = (
        P("tp", ("dp", "seq")),
        P(None, "tp"),
        P(),
        P(None, "tp", None),
        P("tp", None),
        P(),
        P(),
    )
    out_specs = P("tp", ("dp", "seq"))

    def run(clip_tokens, conv_taps, norm_gain, qkv_weight, out_weight, tile_mask, stripe_order):
        arguments = (clip_tokens, conv_taps, norm_gain, qkv_weight, out_weight, tile_mask, stripe_order)
        tokens = clip_tokens.shape[1] // (mesh.shape["dp"] * mesh.shape["seq"])
        columns = qkv_weight.shape[1] // mesh.shape["tp"]
        two_halves = mesh.shape["seq"] == 2 and tokens == 2 * FRAME
        fast = two_halves and mesh.shape["tp"] == 4 and columns % HEAD == 0

        def per_device(*local):
            if not fast:
                return per_device_general(*local)
            return per_device_fast(*local)

        step = jax.shard_map(
            per_device, mesh=mesh, in_specs=in_specs, out_specs=out_specs, check_vma=False
        )
        return step(*arguments)

    return run
```
